128 devices in a mesh: slab: 8 (over y, x_hi), brick: 16 (over x_lo, z, core).
Axes of the slice: x: 4 (x_hi: 2, x_lo: 2; x = x_hi * 2 + x_lo), y: 4, z: 4, core: 2. Of those that a mesh axis runs over, the one named last changes fastest.
Arguments:
- k_coeffs: float32 [16, 32, 16, 128], P('slab', 'brick'), may hold values from -0.3 to 0.4
- v_basis: float32 [32768, 128], P(('slab', 'brick')), may hold values from -4 to 4
Outputs:
- basis_x: float32 [16, 32, 16, 128], P('slab', 'brick')
- coupling: float32 [128, 128], replicated
- basis_v: float32 [32768, 128], P(('slab', 'brick'))
The draws below stay inside these ranges and needn't reach their ends.
All inputs are finite; a program needn't handle non-finite values.
Results may differ from the reference program's by a relative error of at most 0.0001.
Values sent between devices are 32-bit elements; how exact they have to be, the bound alone decides.
No kernel may reach another device: no remote copies, remote signals or barrier semaphores. Data moves between devices by JAX's collectives and lax.ppermute only.
A program may use at most 64 MiB of HBM per device.

```python
import math
import jax
import jax.numpy as jnp
from jax import lax

R = 128
NVX = 32
NV = 32768
NZ = 16
NX = 16
NY = 32


VMAX = 6.0


def node_velocities(indices):
    spacing = 2.0 * VMAX / NVX
    first_index = indices // (NVX * NVX)
    second = indices // NVX % NVX
    third_index = indices % NVX
    coords = jnp.stack([first_index, second, third_index]).astype(jnp.float32)
    return -VMAX + (coords + 0.5) * spacing


def draw_v_basis(key, part):
    velocity = node_velocities(jnp.arange(NV, dtype=jnp.int32))
    square = jnp.sum(velocity * velocity, axis=0)
    gaussian = jnp.exp(-0.5 * square)
    smooth = jnp.stack([gaussian, velocity[0] * gaussian, velocity[1] * gaussian, velocity[2] * gaussian, (square - 3.0) * gaussian], axis=1)
    rough_part = jnp.clip(jax.random.normal(key, (NV, R - 5), jnp.float32), -4.0, 4.0) * jnp.exp(-0.25 * square)[:, None]
    columns = jnp.concatenate([smooth, rough_part], axis=1)
    weight_v = (2.0 * VMAX / NVX) ** 3
    identity = jnp.eye(R, dtype=jnp.float32)
    for sweep_index in range(2):
        gram_matrix = lax.dot_general(columns, columns, (((0,), (0,)), ((), ())), precision=lax.Precision.HIGHEST) * weight_v
        factor = jnp.linalg.cholesky(gram_matrix)
        inverse = jax.scipy.linalg.solve_triangular(factor, identity, lower=True)
        columns = jnp.dot(columns, inverse.T, precision=lax.Precision.HIGHEST)
    return columns.astype(jnp.float32)


def draw_k_coeffs(key, part):
    subkeys = jax.random.split(key, 3)
    rough_part = jnp.clip(jax.random.normal(subkeys[0], (NX, NY, NZ, R), jnp.float32), -5.0, 5.0) * 0.05
    density = jnp.exp(jax.random.uniform(subkeys[1], (NX, NY, NZ), jnp.float32, math.log(0.03), math.log(0.3)))
    row_scale = jnp.concatenate([jnp.zeros((1,), jnp.float32), jnp.full((4,), 0.6, jnp.float32), jnp.ones((R - 5,), jnp.float32)])
    return (rough_part * row_scale).at[..., 0].set(density).astype(jnp.float32)


def setup_inputs(seed: int = 0) -> dict:
    arg_keys = jax.random.split(jax.random.key(seed), 3)
    return {
        "k_coeffs": draw_k_coeffs(jax.random.fold_in(arg_keys[2], 71), 0),
        "v_basis": draw_v_basis(jax.random.fold_in(arg_keys[2], 71), 0),
    }


CFL = 0.9
VMAX = 6.0
COLLIDE = 0.3
RHO_MIN = 0.25
TEMP_MIN = 0.25
PRECISE = lax.Precision.HIGHEST

def velocities(indices):
    spacing = 2.0 * VMAX / NVX
    first_index = indices // (NVX * NVX)
    second = indices // NVX % NVX
    third_index = indices % NVX
    coords = jnp.stack([first_index, second, third_index]).astype(jnp.float32)
    return -VMAX + (coords + 0.5) * spacing

def maxwell(cell_params, velocity):
    distance = (velocity[0][None, :] - cell_params[1][:, None]) ** 2
    distance = distance + (velocity[1][None, :] - cell_params[2][:, None]) ** 2
    distance = distance + (velocity[2][None, :] - cell_params[3][:, None]) ** 2
    amplitude = cell_params[0] * (2.0 * math.pi * cell_params[4]) ** (-1.5)
    return amplitude[:, None] * jnp.exp(distance * (-0.5 / cell_params[4])[:, None])

def cell_state(vectors, coeffs):
    moments = lax.dot_general(vectors, coeffs, (((1,), (1,)), ((), ())), precision=PRECISE)
    density = jnp.maximum(moments[0], RHO_MIN)
    drift_speed = moments[1:4] / density[None, :]
    temper = jnp.maximum((moments[4] / density - jnp.sum(drift_speed * drift_speed, axis=0)) / 3.0, TEMP_MIN)
    return jnp.concatenate([density[None], drift_speed, temper[None]], axis=0)

def transport_flux(backward, forward, transport):
    flux = jnp.zeros_like(backward[0])
    for axis_id in range(3):
        flux = flux + jnp.dot(backward[axis_id], transport[axis_id], precision=PRECISE)
        flux = flux + jnp.dot(forward[axis_id], transport[3 + axis_id], precision=PRECISE)
    return flux

def products(left_side, backward, forward, maxwell_proj):
    pieces = [lax.dot_general(left_side, item, (((0,), (0,)), ((), ())), precision=PRECISE) for item in backward + forward + [maxwell_proj]]
    return jnp.stack(pieces)

def coupling_step(coupling_hat, minus_side, plus_side, projected, transport, time_step):
    drift_sum = jnp.zeros_like(coupling_hat)
    for axis_id in range(3):
        drift_sum = drift_sum + jnp.dot(jnp.dot(minus_side[axis_id], coupling_hat, precision=PRECISE), transport[axis_id], precision=PRECISE)
        drift_sum = drift_sum + jnp.dot(jnp.dot(plus_side[axis_id], coupling_hat, precision=PRECISE), transport[3 + axis_id], precision=PRECISE)
    return coupling_hat + time_step * drift_sum - COLLIDE * (projected - coupling_hat)

def velocity_step(velocity_part, minus_side, plus_side, back_proj, positive, negative, time_step):
    drift_sum = jnp.zeros_like(velocity_part)
    for axis_id in range(3):
        drift_sum = drift_sum + positive[axis_id][:, None] * jnp.dot(velocity_part, minus_side[axis_id].T, precision=PRECISE)
        drift_sum = drift_sum + negative[axis_id][:, None] * jnp.dot(velocity_part, plus_side[axis_id].T, precision=PRECISE)
    return velocity_part - time_step * drift_sum + COLLIDE * (back_proj - velocity_part)

def slopes(field):
    rank_size = field.shape[3]
    lengths = (NX, NY, NZ)
    backward = [((field - jnp.roll(field, 1, axis=axis_id)) * lengths[axis_id]).reshape(-1, rank_size) for axis_id in range(3)]
    forward = [((jnp.roll(field, -1, axis=axis_id) - field) * lengths[axis_id]).reshape(-1, rank_size) for axis_id in range(3)]
    return (backward, forward)

def reference(k_coeffs, v_basis):
    rank_size = k_coeffs.shape[3]
    cell_count = NX * NY * NZ
    time_step = CFL / (VMAX * (NX + NY + NZ))
    weight_x = 1.0 / cell_count
    weight_v = (2.0 * VMAX / NVX) ** 3
    velocity = velocities(jnp.arange(NV, dtype=jnp.int32))
    positive = jnp.maximum(velocity, 0.0)
    negative = jnp.minimum(velocity, 0.0)
    weights = jnp.stack([jnp.ones_like(velocity[0]), velocity[0], velocity[1], velocity[2], jnp.sum(velocity * velocity, axis=0)])
    vectors = jnp.dot(weights, v_basis, precision=PRECISE) * weight_v
    transport = jnp.stack([lax.dot_general(v_basis * (side[axis_id] * weight_v)[:, None], v_basis, (((0,), (0,)), ((), ())), precision=PRECISE) for side in (positive, negative) for axis_id in range(3)])
    coeff_flat = k_coeffs.reshape(cell_count, rank_size)
    cell_params = cell_state(vectors, coeff_flat)
    block_rows = math.gcd(NV, 2048)
    block_total = NV // block_rows
    vel_blocks = velocity.reshape(3, block_total, block_rows).transpose(1, 0, 2)
    basis_blocks = v_basis.reshape(block_total, block_rows, rank_size)

    def add_block(accumulated, pair):
        return (accumulated + jnp.dot(maxwell(cell_params, pair[0]), pair[1], precision=PRECISE) * weight_v, None)
    maxwell_proj = lax.scan(add_block, jnp.zeros((cell_count, rank_size), jnp.float32), (vel_blocks, basis_blocks))[0]
    backward, forward = slopes(k_coeffs)
    advanced = coeff_flat - time_step * transport_flux(backward, forward, transport) + COLLIDE * (maxwell_proj - coeff_flat)
    gram_matrix = lax.dot_general(advanced, advanced, (((0,), (0,)), ((), ())), precision=PRECISE) * weight_x
    factor = jnp.linalg.cholesky(gram_matrix)
    identity = jnp.eye(rank_size, dtype=jnp.float32)
    inverse = jax.scipy.linalg.solve_triangular(factor, identity, lower=True)
    basis_new = jnp.dot(advanced, inverse.T, precision=PRECISE)
    backward, forward = slopes(basis_new.reshape(NX, NY, NZ, rank_size))
    reduced = products(basis_new, backward, forward, maxwell_proj) * weight_x
    coupling_mid = coupling_step(factor.T, reduced[0:3], reduced[3:6], reduced[6], transport, time_step)

    def back_block(vblock):
        return lax.dot_general(maxwell(cell_params, vblock), basis_new, (((0,), (0,)), ((), ())), precision=PRECISE) * weight_x
    back_proj = lax.map(back_block, vel_blocks).reshape(NV, rank_size)
    velocity_part = jnp.dot(v_basis, coupling_mid.T, precision=PRECISE)
    velocity_new = velocity_step(velocity_part, reduced[0:3], reduced[3:6], back_proj, positive, negative, time_step)
    gram_v = lax.dot_general(velocity_new, velocity_new, (((0,), (0,)), ((), ())), precision=PRECISE) * weight_v
    coupling = jnp.linalg.cholesky(gram_v)
    inverse_v = jax.scipy.linalg.solve_triangular(coupling, identity, lower=True)
    vbasis_new = jnp.dot(velocity_new, inverse_v.T, precision=PRECISE)
    return (basis_new.reshape(NX, NY, NZ, rank_size), coupling, vbasis_new)
```

```python
import math

import jax
import jax.numpy as jnp
from jax import lax
from jax.sharding import PartitionSpec as P

NVX = 32


CFL = 0.9
VMAX = 6.0
COLLIDE = 0.3
RHO_MIN = 0.25
TEMP_MIN = 0.25
PRECISE = lax.Precision.HIGHEST
FINE = lax.Precision.HIGHEST
SPACING = 2.0 * VMAX / NVX
WEIGHT_V = SPACING**3


def contract(left, right, left_dim, right_dim, precision=PRECISE):
    return lax.dot_general(
        left, right, (((left_dim,), (right_dim,)), ((), ())), precision=precision
    )


def exchange(array, axis):
    return lax.all_to_all(array, axis, 0, 0, tiled=True)


def to_all(array, axis):
    copies = lax.axis_size(axis)
    return exchange(jnp.broadcast_to(array[None], (copies,) + array.shape), axis)


def velocities(indices):
    coords = jnp.stack([indices // (NVX * NVX), indices // NVX % NVX, indices % NVX])
    return -VMAX + (coords.astype(jnp.float32) + 0.5) * SPACING


def cell_state(moments):
    density = jnp.maximum(moments[0], RHO_MIN)
    drift = [moments[axis_id] / density for axis_id in (1, 2, 3)]
    square = drift[0] * drift[0] + drift[1] * drift[1] + drift[2] * drift[2]
    temper = jnp.maximum((moments[4] / density - square) / 3.0, TEMP_MIN)
    return density, drift, temper


def sum_over_devices(array):
    slabs, bricks = lax.axis_size("slab"), lax.axis_size("brick")
    devices = slabs * bricks

    def from_peer(values, mask):
        pairs = [(i, i ^ mask) for i in range(devices)]
        return lax.ppermute(values, ("slab", "brick"), pairs)

    step = 1
    array = array + from_peer(array, step)
    step = 2
    while step < devices:
        if step * 4 <= devices:
            one, two, three = (from_peer(array, step * k) for k in (1, 2, 3))
            array = (array + one) + (two + three)
            step *= 4
        else:
            array = array + from_peer(array, step)
            step *= 2
    return array


def invert_factor(gram):
    factor = jnp.linalg.cholesky(gram)
    identity = jnp.eye(gram.shape[0], dtype=jnp.float32)
    return factor, jax.scipy.linalg.solve_triangular(factor, identity, lower=True)


def local(k_coeffs, v_basis):
    cells_x, cells_y, cells_z, rank = k_coeffs.shape
    cells = cells_x * cells_y * cells_z
    slabs, bricks = lax.axis_size("slab"), lax.axis_size("brick")
    slab, brick = lax.axis_index("slab"), lax.axis_index("brick")
    lengths = (cells_x * slabs, cells_y * bricks, cells_z)
    time_step = CFL / (VMAX * sum(lengths))
    weight_x = 1.0 / (lengths[0] * lengths[1] * lengths[2])
    rows = v_basis.shape[0]
    slab_cells = cells * bricks
    up = [(i, (i + 1) % slabs) for i in range(slabs)]
    down = [(i, (i - 1) % slabs) for i in range(slabs)]

    k_below = lax.ppermute(k_coeffs[-1:], "slab", up)
    k_above = lax.ppermute(k_coeffs[:1], "slab", down)

    nodes = to_all(v_basis, "slab")
    owner = jnp.arange(slabs, dtype=jnp.int32)[:, None] * bricks + brick
    ids = owner * rows + jnp.arange(rows, dtype=jnp.int32)[None]
    velocity = velocities(ids.reshape(-1))
    positive = jnp.maximum(velocity, 0.0) * WEIGHT_V
    negative = jnp.minimum(velocity, 0.0) * WEIGHT_V
    nodes_flat = nodes.reshape(slabs * rows, rank)
    ones = jnp.ones_like(velocity[0])
    weights = jnp.stack(
        [ones, velocity[0], velocity[1], velocity[2], jnp.sum(velocity * velocity, axis=0)]
        + [jnp.zeros_like(ones)] * 3
    )
    vectors_part = contract(weights, nodes_flat, 1, 0) * WEIGHT_V
    weighted = jnp.concatenate(
        [nodes_flat * side[axis_id][:, None] for axis_id in range(3) for side in (positive, negative)],
        axis=1,
    )
    transport_part = contract(weighted, nodes_flat, 0, 0)
    slice_rows = 6 * rank // bricks
    own_cells = k_coeffs.reshape(cells, rank)
    first = exchange(
        jnp.concatenate(
            [
                jnp.broadcast_to(own_cells[None], (bricks, cells, rank)),
                jnp.broadcast_to(vectors_part[None], (bricks, 8, rank)),
                transport_part.reshape(bricks, slice_rows, rank),
            ],
            axis=1,
        ),
        "brick",
    )
    k_slab = first[:, :cells]
    vectors = jnp.sum(first[:, cells : cells + 8], axis=0)
    transport_slice = jnp.sum(first[:, cells + 8 :], axis=0)

    k_flat = k_slab.reshape(slab_cells, rank)
    moments = contract(vectors, k_flat, 1, 1)
    density, drift, temper = cell_state([moments[i : i + 1] for i in range(5)])
    across = velocities((brick * rows + jnp.arange(rows, dtype=jnp.int32)))
    distance = (across[1][:, None] - drift[1]) ** 2 + (across[2][:, None] - drift[2]) ** 2
    plane = jnp.exp(distance * (-0.5 / temper))
    columns = contract(k_flat, vectors, 1, 1)
    density, drift, temper = cell_state([columns[:, i : i + 1] for i in range(5)])
    first_velocity = velocities(owner[:, 0] * rows)[0]
    amplitude = density * (2.0 * math.pi * temper) ** (-1.5)
    line = amplitude * jnp.exp((first_velocity[None, :] - drift[0]) ** 2 * (-0.5 / temper))

    node_columns = jnp.concatenate([nodes[i] for i in range(slabs)], axis=1)
    planes = contract(plane, node_columns, 0, 0)
    mproj_part = sum(
        line[:, i : i + 1] * planes[:, i * rank : (i + 1) * rank] for i in range(slabs)
    )
    second = exchange(
        jnp.concatenate(
            [
                mproj_part.reshape(bricks, cells, rank),
                jnp.broadcast_to(transport_slice[None], (bricks, slice_rows, rank)),
            ],
            axis=1,
        ),
        "brick",
    )
    maxwell_proj = jnp.sum(second[:, :cells], axis=0) * WEIGHT_V
    transport = second[:, cells:].reshape(6 * rank, rank)

    slab_grid = k_slab.reshape(bricks, cells_x, cells_y, cells_z, rank)
    left = lax.dynamic_index_in_dim(slab_grid, (brick - 1) % bricks, 0, keepdims=False)
    right = lax.dynamic_index_in_dim(slab_grid, (brick + 1) % bricks, 0, keepdims=False)
    lower = [
        jnp.concatenate([k_below, k_coeffs[:-1]], axis=0),
        jnp.concatenate([left[:, -1:], k_coeffs[:, :-1]], axis=1),
        jnp.roll(k_coeffs, 1, axis=2),
    ]
    upper = [
        jnp.concatenate([k_coeffs[1:], k_above], axis=0),
        jnp.concatenate([k_coeffs[:, 1:], right[:, :1]], axis=1),
        jnp.roll(k_coeffs, -1, axis=2),
    ]
    steps = []
    for axis_id in range(3):
        steps.append(((k_coeffs - lower[axis_id]) * lengths[axis_id]).reshape(cells, rank))
        steps.append(((upper[axis_id] - k_coeffs) * lengths[axis_id]).reshape(cells, rank))
    flux = contract(jnp.concatenate(steps, axis=1), transport, 1, 0)
    advanced = own_cells - time_step * flux + COLLIDE * (maxwell_proj - own_cells)

    grid = advanced.reshape(cells_x, cells_y, cells_z, rank)
    below = lax.ppermute(grid[-1:], "slab", up)
    shifted = jnp.concatenate([below, grid[:-1]], axis=0).reshape(cells, rank)
    own_products = contract(advanced, jnp.concatenate([shifted, maxwell_proj], axis=1), 0, 0)
    part_rows = rank // bricks
    third = exchange(
        jnp.concatenate(
            [
                jnp.broadcast_to(advanced[None], (bricks, cells, rank)),
                own_products[:, :rank].reshape(bricks, part_rows, rank),
                own_products[:, rank:].reshape(bricks, part_rows, rank),
            ],
            axis=1,
        ),
        "brick",
    )
    slab_advanced = third[:, :cells]
    summed = jnp.sum(third[:, cells:], axis=0)
    adv_grid = slab_advanced.reshape(bricks, cells_x, cells_y, cells_z, rank)
    before = jnp.concatenate([adv_grid[-1:, :, -1:], adv_grid[:-1, :, -1:]], axis=0)
    shift_y = jnp.concatenate([before, adv_grid[:, :, :-1]], axis=2)
    shift_z = jnp.roll(adv_grid, 1, axis=3)
    adv_flat = slab_advanced.reshape(slab_cells, rank)
    slab_products = contract(
        adv_flat,
        jnp.concatenate(
            [adv_flat, shift_y.reshape(slab_cells, rank), shift_z.reshape(slab_cells, rank)], axis=1
        ),
        0,
        0,
    )
    own_rows = lax.dynamic_slice_in_dim(slab_products, brick * part_rows, part_rows, 0)
    pieces = jnp.concatenate(
        [own_rows[:, :rank], summed, own_rows[:, rank : 2 * rank], own_rows[:, 2 * rank :]], axis=0
    )
    scaled = jnp.concatenate([line[:, i : i + 1] * adv_flat for i in range(slabs)], axis=1)
    back = contract(plane, scaled, 1, 0)
    fourth = exchange(
        jnp.concatenate(
            [
                jnp.stack([back[:, i * rank : (i + 1) * rank] for i in range(slabs)]),
                jnp.broadcast_to(pieces[None], (slabs,) + pieces.shape),
            ],
            axis=1,
        ),
        "slab",
    )
    totals = jnp.sum(fourth, axis=0)
    back_own = totals[:rows]
    reduced = to_all(totals[rows:] * weight_x, "brick")
    reduced = [
        reduced[:, i * part_rows : (i + 1) * part_rows].reshape(rank, rank) for i in range(5)
    ]
    gram, shift_x, projected = reduced[0], reduced[1], reduced[2]
    shifts = [shift_x, reduced[3], reduced[4]]

    factor, inverse = invert_factor(gram)
    upper_factor = factor.T
    basis_new = contract(advanced, inverse, 1, 1)
    sides = [item for shift in shifts for item in (shift, shift.T)]
    solved = contract(inverse, jnp.concatenate(sides + [projected], axis=1), 1, 0)
    blocks = [solved[:, i * rank : (i + 1) * rank] for i in range(7)]
    moved = []
    for axis_id in range(3):
        moved.append((upper_factor - blocks[2 * axis_id]) * lengths[axis_id])
        moved.append((blocks[2 * axis_id + 1] - upper_factor) * lengths[axis_id])
    middle = (
        upper_factor
        + time_step * contract(jnp.concatenate(moved, axis=1), transport, 1, 0)
        - COLLIDE * (blocks[6] - upper_factor)
    )
    turned = [contract(blocks[2 * axis_id], inverse, 1, 1) for axis_id in range(3)]
    now = contract(v_basis, middle, 1, 1)
    kept = jnp.concatenate([item for q in turned for item in (q.T, q)], axis=1)
    applied = contract(now, kept, 1, 0)
    back_proj = contract(back_own, inverse, 1, 1) * weight_x
    own_ids = (slab * bricks + brick) * rows + jnp.arange(rows, dtype=jnp.int32)
    own_velocity = velocities(own_ids)
    drift_sum = jnp.zeros_like(now)
    for axis_id in range(3):
        speed = own_velocity[axis_id][:, None] * lengths[axis_id]
        minus = applied[:, 2 * axis_id * rank : (2 * axis_id + 1) * rank]
        plus = applied[:, (2 * axis_id + 1) * rank : (2 * axis_id + 2) * rank]
        drift_sum = drift_sum + jnp.maximum(speed, 0.0) * (now - minus)
        drift_sum = drift_sum + jnp.minimum(speed, 0.0) * (plus - now)
    velocity_new = now - time_step * drift_sum + COLLIDE * (back_proj - now)

    gram_v = sum_over_devices(contract(velocity_new, velocity_new, 0, 0) * WEIGHT_V)
    coupling, inverse_v = invert_factor(gram_v)
    vbasis_new = contract(velocity_new, inverse_v, 1, 1)
    return (basis_new.reshape(cells_x, cells_y, cells_z, rank), coupling, vbasis_new)


def solution(mesh):
    placed = (P("slab", "brick", None, None), P(("slab", "brick"), None))
    return jax.shard_map(
        local,
        mesh=mesh,
        in_specs=placed,
        out_specs=(P("slab", "brick", None, None), P(), P(("slab", "brick"), None)),
        check_vma=False,
    )
```

```python
import functools
import math

import jax
import jax.numpy as jnp
from jax import lax
from jax.experimental import pallas as pl
from jax.experimental.pallas import tpu as pltpu
from jax.sharding import PartitionSpec as P

NVX = 32


CFL = 0.9
VMAX = 6.0
COLLIDE = 0.3
RHO_MIN = 0.25
TEMP_MIN = 0.25
PRECISE = lax.Precision.HIGHEST
FINE = lax.Precision.HIGH
SPACING = 2.0 * VMAX / NVX
WEIGHT_V = SPACING**3
PANEL = 16


def contract(left, right, left_dim, right_dim, precision=PRECISE):
    return lax.dot_general(
        left, right, (((left_dim,), (right_dim,)), ((), ())), precision=precision
    )


def exchange(array, axis):
    return lax.all_to_all(array, axis, 0, 0, tiled=True)


def to_all(array, axis):
    copies = lax.axis_size(axis)
    return exchange(jnp.broadcast_to(array[None], (copies,) + array.shape), axis)


def velocities(indices):
    coords = jnp.stack([indices // (NVX * NVX), indices // NVX % NVX, indices % NVX])
    return -VMAX + (coords.astype(jnp.float32) + 0.5) * SPACING


def cell_state(moments):
    density = jnp.maximum(moments[0], RHO_MIN)
    drift = [moments[axis_id] / density for axis_id in (1, 2, 3)]
    square = drift[0] * drift[0] + drift[1] * drift[1] + drift[2] * drift[2]
    temper = jnp.maximum((moments[4] / density - square) / 3.0, TEMP_MIN)
    return density, drift, temper


def sum_over_devices(array):
    slabs, bricks = lax.axis_size("slab"), lax.axis_size("brick")
    devices = slabs * bricks

    def from_peer(values, mask):
        pairs = [(i, i ^ mask) for i in range(devices)]
        return lax.ppermute(values, ("slab", "brick"), pairs)

    step = 1
    array = array + from_peer(array, step)
    step = 2
    while step < devices:
        if step * 4 <= devices:
            one, two, three = (from_peer(array, step * k) for k in (1, 2, 3))
            array = (array + one) + (two + three)
            step *= 4
        else:
            array = array + from_peer(array, step)
            step *= 2
    return array


def three_parts(array):
    high = array.astype(jnp.bfloat16).astype(jnp.float32)
    rest = array - high
    middle = rest.astype(jnp.bfloat16).astype(jnp.float32)
    return high, middle, rest - middle


def two_parts(array):
    high = array.astype(jnp.bfloat16)
    return high, (array - high.astype(jnp.float32)).astype(jnp.bfloat16)


def factor_into(gram, work_ref, upper_ref, inverse_ref):
    size = gram.shape[0]
    rows = lax.broadcasted_iota(jnp.int32, (size, size), 0)
    cols = lax.broadcasted_iota(jnp.int32, (size, size), 1)
    work_ref[:, :size] = gram
    work_ref[:, size:] = jnp.where(rows == cols, 1.0, 0.0)
    panel_row = lax.broadcasted_iota(jnp.int32, (PANEL, size), 0)
    panel_col = lax.broadcasted_iota(jnp.int32, (PANEL, size), 1)
    for start in range(0, size, PANEL):
        stop = start + PANEL
        panel = work_ref[start:stop, :]
        spread = [
            jnp.broadcast_to(panel[:, start + t : start + t + 1], (PANEL, size))
            for t in range(PANEL)
        ]
        pivots = jnp.zeros((PANEL, size), jnp.float32)
        for t in range(PANEL):
            pivot = jnp.broadcast_to(spread[t][t : t + 1, :], (PANEL, size))
            pivots = jnp.where(panel_row == t, pivot, pivots)
            if t == PANEL - 1:
                break
            ratio = jnp.where(panel_row > t, spread[t] * (1.0 / pivot), 0.0)
            for u in range(t + 1, PANEL):
                spread[u] = spread[u] - ratio * jnp.broadcast_to(
                    spread[u][t : t + 1, :], (PANEL, size)
                )
            panel = panel - jnp.concatenate([ratio, ratio], axis=1) * jnp.broadcast_to(
                panel[t : t + 1, :], (PANEL, 2 * size)
            )
        scale = lax.rsqrt(pivots)
        panel = panel * jnp.concatenate([scale, scale], axis=1)
        left = jnp.where(panel_col >= panel_row + start, panel[:, :size], 0.0)
        right = panel[:, size:]
        upper_ref[start:stop, :] = left
        inverse_ref[start:stop, :] = right
        if stop < size:
            high, middle, low = three_parts(jnp.concatenate([left, right], axis=1))
            lhs = [high, high, middle, middle, high, low]
            rhs = [high, middle, high, middle, low, high]
            update = lax.dot_general(
                jnp.concatenate([part[:, :size] for part in lhs], axis=0).astype(jnp.bfloat16),
                jnp.concatenate(rhs, axis=0).astype(jnp.bfloat16),
                (((0,), (0,)), ((), ())),
                preferred_element_type=jnp.float32,
            )
            work_ref[stop:, :] = work_ref[stop:, :] - update[stop:, :]


def transport_kernel(nodes_ref, columns_ref, speeds_ref, out_ref):
    groups, rows, rank = nodes_ref.shape
    bricks = out_ref.shape[0]
    factors = [jnp.broadcast_to(columns_ref[:, i : i + 1], (rows, rank)) for i in range(4)]
    sums = [jnp.zeros((rank, rank), jnp.float32) for _ in range(6)]
    for group in range(groups):
        nodes = nodes_ref[group]
        weighted = jnp.concatenate([nodes] + [nodes * factor for factor in factors], axis=1)
        high, low = two_parts(weighted)
        node_high, node_low = high[:, :rank], low[:, :rank]
        product = lax.dot_general(
            jnp.concatenate([node_high, node_high, node_low], axis=0),
            jnp.concatenate([high, low, high], axis=0),
            (((0,), (0,)), ((), ())),
            preferred_element_type=jnp.float32,
        )
        plain = product[:, :rank]
        speed = jnp.broadcast_to(speeds_ref[group : group + 1, :], (rank, rank))
        sums[0] = sums[0] + jnp.maximum(speed, 0.0) * plain
        sums[1] = sums[1] + jnp.minimum(speed, 0.0) * plain
        for i in range(4):
            sums[2 + i] = sums[2 + i] + product[:, (i + 1) * rank : (i + 2) * rank]
    height = rank // bricks
    for i in range(6):
        out_ref[:, i * height : (i + 1) * height, :] = (sums[i] * WEIGHT_V).reshape(
            bricks, height, rank
        )


def advance_kernel(parts_ref, steps_ref, cells_ref, payload_ref, advanced_ref, *, time_step):
    cells, rank = cells_ref.shape
    bricks = parts_ref.shape[0]
    height = rank // bricks
    maxwell_proj = parts_ref[0, :cells, :]
    for i in range(1, bricks):
        maxwell_proj = maxwell_proj + parts_ref[i, :cells, :]
    maxwell_proj = maxwell_proj * WEIGHT_V
    flux = jnp.zeros((cells, rank), jnp.float32)
    for i in range(6):
        block = parts_ref[:, cells + i * height : cells + (i + 1) * height, :].reshape(rank, rank)
        flux = flux + contract(steps_ref[i], block, 1, 0)
    own = cells_ref[...]
    advanced = own - time_step * flux + COLLIDE * (maxwell_proj - own)
    advanced_ref[...] = advanced
    payload_ref[:, :cells, :] = jnp.broadcast_to(advanced[None], (bricks, cells, rank))
    projected = contract(advanced, maxwell_proj, 0, 0)
    payload_ref[:, cells:, :] = projected.reshape(bricks, height, rank)


def middle_kernel(
    pieces_ref,
    transport_ref,
    basis_ref,
    back_ref,
    advanced_ref,
    speeds_ref,
    basis_x_ref,
    velocity_ref,
    gram_ref,
    work_ref,
    upper_ref,
    inverse_ref,
    *,
    lengths,
    time_step,
    weight_x,
):
    bricks, _, rank = pieces_ref.shape
    rows = basis_ref.shape[0]
    height = rank // bricks

    def piece(ref, i):
        return ref[:, i * height : (i + 1) * height, :].reshape(rank, rank)

    factor_into(piece(pieces_ref, 0) * weight_x, work_ref, upper_ref, inverse_ref)
    upper, inverse = upper_ref[...], inverse_ref[...]
    basis_x_ref[...] = contract(advanced_ref[...], inverse, 1, 1)
    change = jnp.zeros((rank, rank), jnp.float32)
    turned = []
    for i in range(3):
        shift = piece(pieces_ref, 1 + i) * weight_x
        straight = contract(inverse, shift, 1, 0)
        crossed = contract(inverse, shift, 1, 1)
        if i == 0:
            straight, crossed = crossed, straight
        turned.append(contract(straight, inverse, 1, 1))
        change = change + lengths[i] * (
            contract(upper - straight, piece(transport_ref, 2 * i), 1, 0)
            + contract(crossed - upper, piece(transport_ref, 2 * i + 1), 1, 0)
        )
    projected = contract(inverse, piece(pieces_ref, 4) * weight_x, 1, 0)
    middle = upper + time_step * change - COLLIDE * (projected - upper)
    now = contract(basis_ref[...], middle, 1, 1)
    drift_sum = jnp.zeros((rows, rank), jnp.float32)
    for i in range(3):
        speed = jnp.broadcast_to(speeds_ref[:, i : i + 1], (rows, rank)) * lengths[i]
        minus = contract(now, turned[i], 1, 1)
        plus = contract(now, turned[i], 1, 0)
        drift_sum = drift_sum + jnp.maximum(speed, 0.0) * (now - minus)
        drift_sum = drift_sum + jnp.minimum(speed, 0.0) * (plus - now)
    back_proj = contract(back_ref[...] * weight_x, inverse, 1, 1)
    updated = now - time_step * drift_sum + COLLIDE * (back_proj - now)
    velocity_ref[...] = updated
    gram_ref[...] = contract(updated, updated, 0, 0) * WEIGHT_V


def last_kernel(gram_ref, velocity_ref, coupling_ref, basis_ref, work_ref, upper_ref, inverse_ref):
    factor_into(gram_ref[...], work_ref, upper_ref, inverse_ref)
    coupling_ref[...] = upper_ref[...].T
    basis_ref[...] = contract(velocity_ref[...], inverse_ref[...], 1, 1)


def f32(*shape):
    return jax.ShapeDtypeStruct(shape, jnp.float32)


def factor_scratch(rank):
    shapes = ((rank, 2 * rank), (rank, rank), (rank, rank))
    return [pltpu.VMEM(shape, jnp.float32) for shape in shapes]


def local(k_coeffs, v_basis):
    cells_x, cells_y, cells_z, rank = k_coeffs.shape
    cells = cells_x * cells_y * cells_z
    slabs, bricks = lax.axis_size("slab"), lax.axis_size("brick")
    devices = slabs * bricks
    slab, brick = lax.axis_index("slab"), lax.axis_index("brick")
    lengths = (cells_x * slabs, cells_y * bricks, cells_z)
    time_step = CFL / (VMAX * sum(lengths))
    weight_x = 1.0 / (lengths[0] * lengths[1] * lengths[2])
    rows = v_basis.shape[0]
    slab_cells = cells * bricks
    half = slab_cells // cells_x
    height = rank // bricks
    up = [(i, (i + 1) % slabs) for i in range(slabs)]
    down = [(i, (i - 1) % slabs) for i in range(slabs)]
    own_cells = k_coeffs.reshape(cells, rank)

    own_ids = (slab * bricks + brick) * rows + jnp.arange(rows, dtype=jnp.int32)
    own_velocity = velocities(own_ids)
    ones = jnp.ones_like(own_velocity[0])
    weights = jnp.stack(
        [ones, own_velocity[0], own_velocity[1], own_velocity[2]]
        + [jnp.sum(own_velocity * own_velocity, axis=0)]
        + [jnp.zeros_like(ones)] * 3
    )
    vectors_part = contract(weights, v_basis, 1, 0) * WEIGHT_V
    vectors_all = exchange(
        jnp.broadcast_to(vectors_part[None], (devices, 8, rank)), ("slab", "brick")
    )
    nodes = to_all(v_basis, "slab")
    k_slab = to_all(own_cells, "brick")
    vectors = jnp.sum(vectors_all, axis=0)
    k_below = lax.ppermute(k_coeffs[-1:], "slab", up)
    k_above = lax.ppermute(k_coeffs[:1], "slab", down)

    across = velocities(brick * rows + jnp.arange(rows, dtype=jnp.int32))
    columns = [f(across[i]) for i in (1, 2) for f in (lambda v: jnp.maximum(v, 0.0), lambda v: jnp.minimum(v, 0.0))]
    columns = jnp.stack(columns + [jnp.zeros_like(ones)] * 4, axis=1)
    owner = jnp.arange(slabs, dtype=jnp.int32) * bricks + brick
    first_velocity = velocities(owner * rows)[0]
    transport_part = pl.pallas_call(
        transport_kernel, out_shape=f32(bricks, 6 * height, rank), name="transport"
    )(nodes, columns, jnp.broadcast_to(first_velocity[:, None], (slabs, rank)))
    transport_slice = jnp.sum(exchange(transport_part, "brick"), axis=0)

    k_flat = k_slab.reshape(slab_cells, rank)
    moments = contract(vectors, k_flat, 1, 1)
    density, drift, temper = cell_state([moments[i : i + 1] for i in range(5)])
    distance = (across[1][:, None] - drift[1]) ** 2 + (across[2][:, None] - drift[2]) ** 2
    plane = jnp.exp(distance * (-0.5 / temper))
    moments = contract(k_flat, vectors, 1, 1)
    density, drift, temper = cell_state([moments[:, i : i + 1] for i in range(5)])
    amplitude = density * (2.0 * math.pi * temper) ** (-1.5)
    line = amplitude * jnp.exp((first_velocity[None, :] - drift[0]) ** 2 * (-0.5 / temper))

    node_columns = jnp.concatenate([nodes[i] for i in range(slabs)], axis=1)
    planes = contract(plane, node_columns, 0, 0, FINE)
    mproj_part = sum(
        line[:, i : i + 1] * planes[:, i * rank : (i + 1) * rank] for i in range(slabs)
    )
    second = exchange(
        jnp.concatenate(
            [
                mproj_part.reshape(bricks, cells, rank),
                jnp.broadcast_to(transport_slice[None], (bricks, 6 * height, rank)),
            ],
            axis=1,
        ),
        "brick",
    )

    slab_grid = k_slab.reshape(bricks, cells_x, cells_y, cells_z, rank)
    left = lax.dynamic_index_in_dim(slab_grid, (brick - 1) % bricks, 0, keepdims=False)
    right = lax.dynamic_index_in_dim(slab_grid, (brick + 1) % bricks, 0, keepdims=False)
    lower = [
        jnp.concatenate([k_below, k_coeffs[:-1]], axis=0),
        jnp.concatenate([left[:, -1:], k_coeffs[:, :-1]], axis=1),
        jnp.roll(k_coeffs, 1, axis=2),
    ]
    upper = [
        jnp.concatenate([k_coeffs[1:], k_above], axis=0),
        jnp.concatenate([k_coeffs[:, 1:], right[:, :1]], axis=1),
        jnp.roll(k_coeffs, -1, axis=2),
    ]
    steps = []
    for axis_id in range(3):
        steps.append(((k_coeffs - lower[axis_id]) * lengths[axis_id]).reshape(cells, rank))
        steps.append(((upper[axis_id] - k_coeffs) * lengths[axis_id]).reshape(cells, rank))
    payload, advanced = pl.pallas_call(
        functools.partial(advance_kernel, time_step=time_step),
        out_shape=(f32(bricks, cells + height, rank), f32(cells, rank)),
        name="advance",
    )(second, jnp.stack(steps), own_cells)
    third = exchange(payload, "brick")

    slab_advanced = third[:, :cells]
    projected_rows = jnp.sum(third[:, cells:], axis=0)
    adv_grid = slab_advanced.reshape(bricks, cells_x, cells_y, cells_z, rank)
    planes_x = [adv_grid[:, i].reshape(half, rank) for i in range(cells_x)]
    choose = brick * height + jnp.arange(height, dtype=jnp.int32)
    choose = (choose[:, None] == jnp.arange(rank, dtype=jnp.int32)[None]).astype(jnp.float32)
    chosen = contract(choose, planes_x[-1], 1, 1)
    chosen_below = lax.ppermute(chosen, "slab", up)
    before = jnp.concatenate([adv_grid[-1:, :, -1:], adv_grid[:-1, :, -1:]], axis=0)
    shift_y = jnp.concatenate([before, adv_grid[:, :, :-1]], axis=2).reshape(slab_cells, rank)
    shift_z = jnp.roll(adv_grid, 1, axis=3).reshape(slab_cells, rank)
    adv_flat = slab_advanced.reshape(slab_cells, rank)

    def own_rows(left_side, right_side):
        whole = contract(left_side, right_side, 0, 0)
        return lax.dynamic_slice_in_dim(whole, brick * height, height, 0)

    crossing = contract(chosen_below, planes_x[0], 1, 0)
    for i in range(1, cells_x):
        crossing = crossing + own_rows(planes_x[i - 1], planes_x[i])
    pieces = jnp.concatenate(
        [
            own_rows(adv_flat, adv_flat),
            crossing,
            own_rows(adv_flat, shift_y),
            own_rows(adv_flat, shift_z),
            projected_rows,
        ],
        axis=0,
    )
    reduced = to_all(jnp.sum(to_all(pieces, "slab"), axis=0), "brick")

    scaled = jnp.concatenate([line[:, i : i + 1] * adv_flat for i in range(slabs)], axis=1)
    back = contract(plane, scaled, 1, 0, FINE)
    fourth = exchange(
        jnp.stack([back[:, i * rank : (i + 1) * rank] for i in range(slabs)]), "slab"
    )
    back_own = jnp.sum(fourth, axis=0)

    speeds = jnp.stack(list(own_velocity) + [jnp.zeros_like(ones)] * 5, axis=1)
    basis_new, velocity_new, gram_part = pl.pallas_call(
        functools.partial(
            middle_kernel, lengths=lengths, time_step=time_step, weight_x=weight_x
        ),
        out_shape=(f32(cells, rank), f32(rows, rank), f32(rank, rank)),
        scratch_shapes=factor_scratch(rank),
        name="middle",
    )(reduced, second[:, cells:], v_basis, back_own, advanced, speeds)
    gram_v = sum_over_devices(gram_part)
    coupling, vbasis_new = pl.pallas_call(
        last_kernel,
        out_shape=(f32(rank, rank), f32(rows, rank)),
        scratch_shapes=factor_scratch(rank),
        name="last",
    )(gram_v, velocity_new)
    return (basis_new.reshape(cells_x, cells_y, cells_z, rank), coupling, vbasis_new)


def solution(mesh):
    placed = (P("slab", "brick", None, None), P(("slab", "brick"), None))
    return jax.shard_map(
        local,
        mesh=mesh,
        in_specs=placed,
        out_specs=(P("slab", "brick", None, None), P(), P(("slab", "brick"), None)),
        check_vma=False,
    )
```

```python
import functools
import math

import jax
import jax.numpy as jnp
from jax import lax
from jax.experimental import pallas as pl
from jax.experimental.pallas import tpu as pltpu
from jax.sharding import PartitionSpec as P

NVX = 32


CFL = 0.9
VMAX = 6.0
COLLIDE = 0.3
RHO_MIN = 0.25
TEMP_MIN = 0.25
PRECISE = lax.Precision.HIGHEST
FINE = lax.Precision.HIGH
SPACING = 2.0 * VMAX / NVX
WEIGHT_V = SPACING**3
PANEL = 16


def contract(left, right, left_dim, right_dim, precision=PRECISE):
    return lax.dot_general(
        left, right, (((left_dim,), (right_dim,)), ((), ())), precision=precision
    )


def exchange(array, axis):
    return lax.all_to_all(array, axis, 0, 0, tiled=True)


def to_all(array, axis):
    copies = lax.axis_size(axis)
    return exchange(jnp.broadcast_to(array[None], (copies,) + array.shape), axis)


def velocities(indices):
    coords = jnp.stack([indices // (NVX * NVX), indices // NVX % NVX, indices % NVX])
    return -VMAX + (coords.astype(jnp.float32) + 0.5) * SPACING


def cell_state(moments):
    density = jnp.maximum(moments[0], RHO_MIN)
    drift = [moments[axis_id] / density for axis_id in (1, 2, 3)]
    square = drift[0] * drift[0] + drift[1] * drift[1] + drift[2] * drift[2]
    temper = jnp.maximum((moments[4] / density - square) / 3.0, TEMP_MIN)
    return density, drift, temper


def from_peer(values, axis, mask):
    return lax.ppermute(values, axis, [(i, i ^ mask) for i in range(lax.axis_size(axis))])


def sum_over(array, axis, groups):
    for masks in groups:
        parts = [array] + [from_peer(array, axis, mask) for mask in masks]
        array = sum_pairs(parts)
    return array


def sum_pairs(parts):
    if len(parts) == 1:
        return parts[0]
    half = len(parts) // 2
    return sum_pairs(parts[:half]) + sum_pairs(parts[half:])


def gather_relative(array, axis, groups):
    array = array[None]
    for masks in groups:
        array = jnp.concatenate([array] + [from_peer(array, axis, mask) for mask in masks], axis=0)
    return array


BRICK_GROUPS = ((1,), (2, 4, 6), (8,))
SLAB_GROUPS = ((1,), (2, 4, 6))


def three_parts(array):
    high = array.astype(jnp.bfloat16).astype(jnp.float32)
    rest = array - high
    middle = rest.astype(jnp.bfloat16).astype(jnp.float32)
    return high, middle, rest - middle


def two_parts(array):
    high = array.astype(jnp.bfloat16)
    return high, (array - high.astype(jnp.float32)).astype(jnp.bfloat16)


def factor_into(gram, work_ref, upper_ref, inverse_ref):
    size = gram.shape[0]
    rows = lax.broadcasted_iota(jnp.int32, (size, size), 0)
    cols = lax.broadcasted_iota(jnp.int32, (size, size), 1)
    work_ref[:, :size] = gram
    work_ref[:, size:] = jnp.where(rows == cols, 1.0, 0.0)
    panel_row = lax.broadcasted_iota(jnp.int32, (PANEL, size), 0)
    panel_col = lax.broadcasted_iota(jnp.int32, (PANEL, size), 1)
    for start in range(0, size, PANEL):
        stop = start + PANEL
        panel = work_ref[start:stop, :]
        spread = [
            jnp.broadcast_to(panel[:, start + t : start + t + 1], (PANEL, size))
            for t in range(PANEL)
        ]
        pivots = jnp.zeros((PANEL, size), jnp.float32)
        for t in range(PANEL):
            pivot = jnp.broadcast_to(spread[t][t : t + 1, :], (PANEL, size))
            pivots = jnp.where(panel_row == t, pivot, pivots)
            if t == PANEL - 1:
                break
            ratio = jnp.where(panel_row > t, spread[t] * (1.0 / pivot), 0.0)
            for u in range(t + 1, PANEL):
                spread[u] = spread[u] - ratio * jnp.broadcast_to(
                    spread[u][t : t + 1, :], (PANEL, size)
                )
            panel = panel - jnp.concatenate([ratio, ratio], axis=1) * jnp.broadcast_to(
                panel[t : t + 1, :], (PANEL, 2 * size)
            )
        scale = lax.rsqrt(pivots)
        panel = panel * jnp.concatenate([scale, scale], axis=1)
        left = jnp.where(panel_col >= panel_row + start, panel[:, :size], 0.0)
        right = panel[:, size:]
        upper_ref[start:stop, :] = left
        inverse_ref[start:stop, :] = right
        if stop < size:
            high, middle, low = three_parts(jnp.concatenate([left, right], axis=1))
            lhs = [high, high, middle, middle, high, low]
            rhs = [high, middle, high, middle, low, high]
            update = lax.dot_general(
                jnp.concatenate([part[:, :size] for part in lhs], axis=0).astype(jnp.bfloat16),
                jnp.concatenate(rhs, axis=0).astype(jnp.bfloat16),
                (((0,), (0,)), ((), ())),
                preferred_element_type=jnp.float32,
            )
            work_ref[stop:, :] = work_ref[stop:, :] - update[stop:, :]


def transport_kernel(nodes_ref, columns_ref, speeds_ref, weights_ref, out_ref, vectors_ref):
    groups, rows, rank = nodes_ref.shape
    bricks = out_ref.shape[0]
    factors = [jnp.broadcast_to(columns_ref[:, i : i + 1], (rows, rank)) for i in range(4)]
    sums = [jnp.zeros((rank, rank), jnp.float32) for _ in range(6)]
    vectors = jnp.zeros(vectors_ref.shape, jnp.float32)
    for group in range(groups):
        nodes = nodes_ref[group]
        weighted = jnp.concatenate([nodes] + [nodes * factor for factor in factors], axis=1)
        high, low = two_parts(weighted)
        node_high, node_low = high[:, :rank], low[:, :rank]
        product = lax.dot_general(
            jnp.concatenate([node_high, node_high, node_low], axis=0),
            jnp.concatenate([high, low, high], axis=0),
            (((0,), (0,)), ((), ())),
            preferred_element_type=jnp.float32,
        )
        vectors = vectors + contract(weights_ref[group], nodes, 1, 0)
        plain = product[:, :rank]
        speed = jnp.broadcast_to(speeds_ref[group : group + 1, :], (rank, rank))
        sums[0] = sums[0] + jnp.maximum(speed, 0.0) * plain
        sums[1] = sums[1] + jnp.minimum(speed, 0.0) * plain
        for i in range(4):
            sums[2 + i] = sums[2 + i] + product[:, (i + 1) * rank : (i + 2) * rank]
    vectors_ref[...] = vectors * WEIGHT_V
    height = rank // bricks
    for i in range(6):
        out_ref[:, i * height : (i + 1) * height, :] = (sums[i] * WEIGHT_V).reshape(
            bricks, height, rank
        )


def maxwell_kernel(
    brick_ref, cells_ref, vectors_ref, nodes_ref, first_ref, across_ref, part_ref, line_ref, state_ref
):
    bricks, cells, rank = cells_ref.shape
    groups, rows, _ = nodes_ref.shape
    total = bricks * cells
    brick = brick_ref[0]
    k_flat = jnp.concatenate([cells_ref[i ^ brick] for i in range(bricks)], axis=0)
    moments = contract(vectors_ref[...], k_flat, 1, 1)
    density, drift, temper = cell_state([moments[i : i + 1] for i in range(5)])
    slope = -0.5 / temper
    amplitude = density * jnp.exp(-1.5 * jnp.log(2.0 * math.pi * temper))
    first = jnp.broadcast_to(first_ref[:, :1], (groups, total))
    line = amplitude * jnp.exp((first - drift[0]) ** 2 * slope)
    state = jnp.concatenate([drift[1], drift[2], slope] + [amplitude] * 5, axis=0)
    state_ref[...] = state
    both = jnp.concatenate([line, state], axis=0).T
    line_cols = both[:, :groups]
    line_ref[...] = line_cols
    distance = (across_ref[0:1, :] - both[:, groups : groups + 1]) ** 2
    distance = distance + (across_ref[1:2, :] - both[:, groups + 1 : groups + 2]) ** 2
    high, low = two_parts(jnp.exp(distance * both[:, groups + 2 : groups + 3]))
    lhs = jnp.concatenate([high, high, low], axis=1)
    result = jnp.zeros((total, rank), jnp.float32)
    for group in range(0, groups, 2):
        node_high, node_low = two_parts(
            jnp.concatenate([nodes_ref[group], nodes_ref[group + 1]], axis=1)
        )
        product = lax.dot_general(
            lhs,
            jnp.concatenate([node_high, node_low, node_high], axis=0),
            (((1,), (0,)), ((), ())),
            preferred_element_type=jnp.float32,
        )
        result = result + line_cols[:, group : group + 1] * product[:, :rank]
        result = result + line_cols[:, group + 1 : group + 2] * product[:, rank:]
    part_ref[...] = result.reshape(bricks, cells, rank)


def back_kernel(parts_ref, line_ref, state_ref, across_ref, out_ref):
    bricks, _, rank = parts_ref.shape
    groups, rows, _ = out_ref.shape
    total = line_ref.shape[0]
    cells = total // bricks
    advanced = parts_ref[:, :cells, :].reshape(total, rank)
    distance = (across_ref[:, 0:1] - state_ref[0:1, :]) ** 2
    distance = distance + (across_ref[:, 1:2] - state_ref[1:2, :]) ** 2
    high, low = two_parts(jnp.exp(distance * state_ref[2:3, :]))
    lhs = jnp.concatenate([high, high, low], axis=1)
    for group in range(0, groups, 2):
        scaled = [line_ref[:, i : i + 1] * advanced for i in (group, group + 1)]
        part_high, part_low = two_parts(jnp.concatenate(scaled, axis=1))
        product = lax.dot_general(
            lhs,
            jnp.concatenate([part_high, part_low, part_high], axis=0),
            (((1,), (0,)), ((), ())),
            preferred_element_type=jnp.float32,
        )
        out_ref[group] = product[:, :rank]
        out_ref[group + 1] = product[:, rank:]


def advance_kernel(parts_ref, steps_ref, cells_ref, payload_ref, advanced_ref, *, time_step):
    cells, rank = cells_ref.shape
    bricks = parts_ref.shape[0]
    height = rank // bricks
    maxwell_proj = parts_ref[0, :cells, :]
    for i in range(1, bricks):
        maxwell_proj = maxwell_proj + parts_ref[i, :cells, :]
    maxwell_proj = maxwell_proj * WEIGHT_V
    flux = jnp.zeros((cells, rank), jnp.float32)
    for i in range(6):
        block = parts_ref[:, cells + i * height : cells + (i + 1) * height, :].reshape(rank, rank)
        flux = flux + contract(steps_ref[i], block, 1, 0)
    own = cells_ref[...]
    advanced = own - time_step * flux + COLLIDE * (maxwell_proj - own)
    advanced_ref[...] = advanced
    payload_ref[:, :cells, :] = jnp.broadcast_to(advanced[None], (bricks, cells, rank))
    projected = contract(advanced, maxwell_proj, 0, 0)
    payload_ref[:, cells:, :] = projected.reshape(bricks, height, rank)


def middle_kernel(
    brick_ref,
    pieces_ref,
    transport_ref,
    basis_ref,
    back_ref,
    advanced_ref,
    speeds_ref,
    basis_x_ref,
    velocity_ref,
    gram_ref,
    work_ref,
    upper_ref,
    inverse_ref,
    *,
    lengths,
    time_step,
    weight_x,
):
    bricks, _, rank = pieces_ref.shape
    rows = basis_ref.shape[0]
    height = rank // bricks
    cells = advanced_ref.shape[0]
    brick = brick_ref[0]

    def piece(ref, i):
        if ref is transport_ref:
            start = cells + i * height
            return ref[:, start : start + height, :].reshape(rank, rank)
        rows_of = [ref[j ^ brick, i * height : (i + 1) * height, :] for j in range(bricks)]
        return jnp.concatenate(rows_of, axis=0)

    factor_into(piece(pieces_ref, 0) * weight_x, work_ref, upper_ref, inverse_ref)
    upper, inverse = upper_ref[...], inverse_ref[...]
    basis_x_ref[...] = contract(advanced_ref[...], inverse, 1, 1)
    change = jnp.zeros((rank, rank), jnp.float32)
    turned = []
    for i in range(3):
        shift = piece(pieces_ref, 1 + i) * weight_x
        straight = contract(inverse, shift, 1, 0)
        crossed = contract(inverse, shift, 1, 1)
        if i == 0:
            straight, crossed = crossed, straight
        turned.append(contract(straight, inverse, 1, 1))
        change = change + lengths[i] * (
            contract(upper - straight, piece(transport_ref, 2 * i), 1, 0)
            + contract(crossed - upper, piece(transport_ref, 2 * i + 1), 1, 0)
        )
    projected = contract(inverse, piece(pieces_ref, 4) * weight_x, 1, 0)
    middle = upper + time_step * change - COLLIDE * (projected - upper)
    now = contract(basis_ref[...], middle, 1, 1)
    drift_sum = jnp.zeros((rows, rank), jnp.float32)
    for i in range(3):
        speed = jnp.broadcast_to(speeds_ref[:, i : i + 1], (rows, rank)) * lengths[i]
        minus = contract(now, turned[i], 1, 1)
        plus = contract(now, turned[i], 1, 0)
        drift_sum = drift_sum + jnp.maximum(speed, 0.0) * (now - minus)
        drift_sum = drift_sum + jnp.minimum(speed, 0.0) * (plus - now)
    back = back_ref[0]
    for i in range(1, back_ref.shape[0]):
        back = back + back_ref[i]
    back_proj = contract(back * weight_x, inverse, 1, 1)
    updated = now - time_step * drift_sum + COLLIDE * (back_proj - now)
    velocity_ref[...] = updated
    gram_ref[...] = contract(updated, updated, 0, 0) * WEIGHT_V


def last_kernel(gram_ref, velocity_ref, coupling_ref, basis_ref, work_ref, upper_ref, inverse_ref):
    factor_into(gram_ref[...], work_ref, upper_ref, inverse_ref)
    coupling_ref[...] = upper_ref[...].T
    basis_ref[...] = contract(velocity_ref[...], inverse_ref[...], 1, 1)


def f32(*shape):
    return jax.ShapeDtypeStruct(shape, jnp.float32)


def factor_scratch(rank):
    shapes = ((rank, 2 * rank), (rank, rank), (rank, rank))
    return [pltpu.VMEM(shape, jnp.float32) for shape in shapes]


def local(k_coeffs, v_basis):
    cells_x, cells_y, cells_z, rank = k_coeffs.shape
    cells = cells_x * cells_y * cells_z
    slabs, bricks = lax.axis_size("slab"), lax.axis_size("brick")
    devices = slabs * bricks
    slab, brick = lax.axis_index("slab"), lax.axis_index("brick")
    lengths = (cells_x * slabs, cells_y * bricks, cells_z)
    time_step = CFL / (VMAX * sum(lengths))
    weight_x = 1.0 / (lengths[0] * lengths[1] * lengths[2])
    rows = v_basis.shape[0]
    slab_cells = cells * bricks
    half = slab_cells // cells_x
    height = rank // bricks
    up = [(i, (i + 1) % slabs) for i in range(slabs)]
    down = [(i, (i - 1) % slabs) for i in range(slabs)]
    own_cells = k_coeffs.reshape(cells, rank)

    own_ids = (slab * bricks + brick) * rows + jnp.arange(rows, dtype=jnp.int32)
    own_velocity = velocities(own_ids)
    ones = jnp.ones_like(own_velocity[0])
    slab_owner = jnp.arange(slabs, dtype=jnp.int32)[:, None] * bricks + brick
    slab_velocity = velocities(slab_owner * rows + jnp.arange(rows, dtype=jnp.int32)[None])
    weights = jnp.stack(
        [jnp.ones_like(slab_velocity[0]), slab_velocity[0], slab_velocity[1], slab_velocity[2]]
        + [jnp.sum(slab_velocity * slab_velocity, axis=0)]
        + [jnp.zeros_like(slab_velocity[0])] * 3,
        axis=1,
    )
    nodes = to_all(v_basis, "slab")
    k_slab = gather_relative(own_cells, "brick", BRICK_GROUPS)
    k_below = lax.ppermute(k_coeffs[-1:], "slab", up)
    k_above = lax.ppermute(k_coeffs[:1], "slab", down)

    across = velocities(brick * rows + jnp.arange(rows, dtype=jnp.int32))
    columns = [f(across[i]) for i in (1, 2) for f in (lambda v: jnp.maximum(v, 0.0), lambda v: jnp.minimum(v, 0.0))]
    columns = jnp.stack(columns + [jnp.zeros_like(ones)] * 4, axis=1)
    owner = jnp.arange(slabs, dtype=jnp.int32) * bricks + brick
    first_velocity = velocities(owner * rows)[0]
    first_speeds = jnp.broadcast_to(first_velocity[:, None], (slabs, rank))
    transport_part, vectors_part = pl.pallas_call(
        transport_kernel,
        out_shape=(f32(bricks, 6 * height, rank), f32(8, rank)),
        name="transport",
    )(nodes, columns, first_speeds, weights)
    vectors = sum_over(vectors_part, "brick", BRICK_GROUPS)
    transport_slice = jnp.sum(exchange(transport_part, "brick"), axis=0)

    brick_id = brick.astype(jnp.int32)[None]
    vector_specs = [pl.BlockSpec(memory_space=pltpu.SMEM)]
    whole = pl.BlockSpec(memory_space=pltpu.VMEM)
    mproj_part, line, state = pl.pallas_call(
        maxwell_kernel,
        out_shape=(f32(bricks, cells, rank), f32(slab_cells, slabs), f32(8, slab_cells)),
        in_specs=vector_specs + [whole] * 5,
        name="maxwell",
    )(brick_id, k_slab, vectors, nodes, first_speeds, across[1:])
    second = exchange(
        jnp.concatenate(
            [mproj_part, jnp.broadcast_to(transport_slice[None], (bricks, 6 * height, rank))],
            axis=1,
        ),
        "brick",
    )

    slab_grid = k_slab.reshape(bricks, cells_x, cells_y, cells_z, rank)
    left = ((brick - 1) % bricks) ^ brick
    right = ((brick + 1) % bricks) ^ brick
    left = lax.dynamic_index_in_dim(slab_grid, left, 0, keepdims=False)
    right = lax.dynamic_index_in_dim(slab_grid, right, 0, keepdims=False)
    lower = [
        jnp.concatenate([k_below, k_coeffs[:-1]], axis=0),
        jnp.concatenate([left[:, -1:], k_coeffs[:, :-1]], axis=1),
        jnp.roll(k_coeffs, 1, axis=2),
    ]
    upper = [
        jnp.concatenate([k_coeffs[1:], k_above], axis=0),
        jnp.concatenate([k_coeffs[:, 1:], right[:, :1]], axis=1),
        jnp.roll(k_coeffs, -1, axis=2),
    ]
    steps = []
    for axis_id in range(3):
        steps.append(((k_coeffs - lower[axis_id]) * lengths[axis_id]).reshape(cells, rank))
        steps.append(((upper[axis_id] - k_coeffs) * lengths[axis_id]).reshape(cells, rank))
    payload, advanced = pl.pallas_call(
        functools.partial(advance_kernel, time_step=time_step),
        out_shape=(f32(bricks, cells + height, rank), f32(cells, rank)),
        name="advance",
    )(second, jnp.stack(steps), own_cells)
    third = exchange(payload, "brick")

    slab_advanced = third[:, :cells]
    projected_rows = jnp.sum(third[:, cells:], axis=0)
    adv_grid = slab_advanced.reshape(bricks, cells_x, cells_y, cells_z, rank)
    planes_x = [adv_grid[:, i].reshape(half, rank) for i in range(cells_x)]
    choose = brick * height + jnp.arange(height, dtype=jnp.int32)
    choose = (choose[:, None] == jnp.arange(rank, dtype=jnp.int32)[None]).astype(jnp.float32)
    chosen = contract(choose, planes_x[-1], 1, 1)
    chosen_below = lax.ppermute(chosen, "slab", up)
    before = jnp.concatenate([adv_grid[-1:, :, -1:], adv_grid[:-1, :, -1:]], axis=0)
    shift_y = jnp.concatenate([before, adv_grid[:, :, :-1]], axis=2).reshape(slab_cells, rank)
    shift_z = jnp.roll(adv_grid, 1, axis=3).reshape(slab_cells, rank)
    adv_flat = slab_advanced.reshape(slab_cells, rank)

    def own_rows(left_side, right_side):
        whole = contract(left_side, right_side, 0, 0)
        return lax.dynamic_slice_in_dim(whole, brick * height, height, 0)

    crossing = contract(chosen_below, planes_x[0], 1, 0)
    for i in range(1, cells_x):
        crossing = crossing + own_rows(planes_x[i - 1], planes_x[i])
    pieces = jnp.concatenate(
        [
            own_rows(adv_flat, adv_flat),
            crossing,
            own_rows(adv_flat, shift_y),
            own_rows(adv_flat, shift_z),
            projected_rows,
        ],
        axis=0,
    )
    pieces = sum_over(pieces, "slab", SLAB_GROUPS)
    reduced = gather_relative(pieces, "brick", BRICK_GROUPS)

    back = pl.pallas_call(back_kernel, out_shape=f32(slabs, rows, rank), name="back")(
        third, line, state, across[1:].T
    )
    fourth = exchange(back, "slab")

    speeds = jnp.stack(list(own_velocity) + [jnp.zeros_like(ones)] * 5, axis=1)
    basis_new, velocity_new, gram_part = pl.pallas_call(
        functools.partial(
            middle_kernel, lengths=lengths, time_step=time_step, weight_x=weight_x
        ),
        out_shape=(f32(cells, rank), f32(rows, rank), f32(rank, rank)),
        in_specs=vector_specs + [whole] * 6,
        scratch_shapes=factor_scratch(rank),
        name="middle",
    )(brick_id, reduced, second, v_basis, fourth, advanced, speeds)
    gram_v = sum_over(sum_over(gram_part, "brick", BRICK_GROUPS), "slab", SLAB_GROUPS)
    coupling, vbasis_new = pl.pallas_call(
        last_kernel,
        out_shape=(f32(rank, rank), f32(rows, rank)),
        scratch_shapes=factor_scratch(rank),
        name="last",
    )(gram_v, velocity_new)
    return (basis_new.reshape(cells_x, cells_y, cells_z, rank), coupling, vbasis_new)


def solution(mesh):
    placed = (P("slab", "brick", None, None), P(("slab", "brick"), None))
    return jax.shard_map(
        local,
        mesh=mesh,
        in_specs=placed,
        out_specs=(P("slab", "brick", None, None), P(), P(("slab", "brick"), None)),
        check_vma=False,
    )
```

```python
import functools
import math

import jax
import jax.numpy as jnp
from jax import lax
from jax.experimental import pallas as pl
from jax.experimental.pallas import tpu as pltpu
from jax.sharding import PartitionSpec as P

NVX = 32


CFL = 0.9
VMAX = 6.0
COLLIDE = 0.3
RHO_MIN = 0.25
TEMP_MIN = 0.25
PRECISE = lax.Precision.HIGHEST
FINE = lax.Precision.HIGH
SPACING = 2.0 * VMAX / NVX
WEIGHT_V = SPACING**3
PANEL = 16


def contract(left, right, left_dim, right_dim, precision=PRECISE):
    return lax.dot_general(
        left, right, (((left_dim,), (right_dim,)), ((), ())), precision=precision
    )


def exchange(array, axis):
    return lax.all_to_all(array, axis, 0, 0, tiled=True)


def to_all(array, axis):
    copies = lax.axis_size(axis)
    return exchange(jnp.broadcast_to(array[None], (copies,) + array.shape), axis)


def velocities(indices):
    coords = jnp.stack([indices // (NVX * NVX), indices // NVX % NVX, indices % NVX])
    return -VMAX + (coords.astype(jnp.float32) + 0.5) * SPACING


def cell_state(moments):
    density = jnp.maximum(moments[0], RHO_MIN)
    drift = [moments[axis_id] / density for axis_id in (1, 2, 3)]
    square = drift[0] * drift[0] + drift[1] * drift[1] + drift[2] * drift[2]
    temper = jnp.maximum((moments[4] / density - square) / 3.0, TEMP_MIN)
    return density, drift, temper


def from_peer(values, axis, mask):
    peers = lax.axis_size(axis)
    return lax.ppermute(values, axis, [(i, i ^ mask) for i in range(peers)])


def sum_over(array, axis, groups):
    for masks in groups:
        parts = [array] + [from_peer(array, axis, mask) for mask in masks]
        array = sum_pairs(parts)
    return array


def sum_pairs(parts):
    if len(parts) == 1:
        return parts[0]
    half = len(parts) // 2
    return sum_pairs(parts[:half]) + sum_pairs(parts[half:])


def gather_relative(array, axis, groups):
    array = array[None]
    for masks in groups:
        array = jnp.concatenate([array] + [from_peer(array, axis, mask) for mask in masks], axis=0)
    return array


BRICK_GROUPS = ((1,), (2, 4, 6), (8,))
SLAB_GROUPS = ((1,), (2, 4, 6))
ALL_GROUPS = ((1,), (2, 4, 6), (8, 16, 24), (32, 64, 96))


def three_parts(array):
    high = array.astype(jnp.bfloat16).astype(jnp.float32)
    rest = array - high
    middle = rest.astype(jnp.bfloat16).astype(jnp.float32)
    return high, middle, rest - middle


def two_parts(array):
    high = array.astype(jnp.bfloat16)
    return high, (array - high.astype(jnp.float32)).astype(jnp.bfloat16)


def factor_into(gram, work_ref, upper_ref, inverse_ref):
    size = gram.shape[0]
    rows = lax.broadcasted_iota(jnp.int32, (size, size), 0)
    cols = lax.broadcasted_iota(jnp.int32, (size, size), 1)
    work_ref[:, :size] = gram
    work_ref[:, size:] = jnp.where(rows == cols, 1.0, 0.0)
    panel_row = lax.broadcasted_iota(jnp.int32, (PANEL, size), 0)
    panel_col = lax.broadcasted_iota(jnp.int32, (PANEL, size), 1)
    for start in range(0, size, PANEL):
        stop = start + PANEL
        panel = work_ref[start:stop, :]
        spread = [
            jnp.broadcast_to(panel[:, start + t : start + t + 1], (PANEL, size))
            for t in range(PANEL)
        ]
        pivots = jnp.zeros((PANEL, size), jnp.float32)
        for t in range(PANEL):
            pivot = jnp.broadcast_to(spread[t][t : t + 1, :], (PANEL, size))
            pivots = jnp.where(panel_row == t, pivot, pivots)
            if t == PANEL - 1:
                break
            ratio = jnp.where(panel_row > t, spread[t] * (1.0 / pivot), 0.0)
            for u in range(t + 1, PANEL):
                spread[u] = spread[u] - ratio * jnp.broadcast_to(
                    spread[u][t : t + 1, :], (PANEL, size)
                )
            panel = panel - jnp.concatenate([ratio, ratio], axis=1) * jnp.broadcast_to(
                panel[t : t + 1, :], (PANEL, 2 * size)
            )
        scale = lax.rsqrt(pivots)
        panel = panel * jnp.concatenate([scale, scale], axis=1)
        left = jnp.where(panel_col >= panel_row + start, panel[:, :size], 0.0)
        right = panel[:, size:]
        upper_ref[start:stop, :] = left
        inverse_ref[start:stop, :] = right
        if stop < size:
            high, middle, low = three_parts(jnp.concatenate([left, right], axis=1))
            lhs = [high, high, middle, middle, high, low]
            rhs = [high, middle, high, middle, low, high]
            update = lax.dot_general(
                jnp.concatenate([part[:, :size] for part in lhs], axis=0).astype(jnp.bfloat16),
                jnp.concatenate(rhs, axis=0).astype(jnp.bfloat16),
                (((0,), (0,)), ((), ())),
                preferred_element_type=jnp.float32,
            )
            work_ref[stop:, :] = work_ref[stop:, :] - update[stop:, :]


def transport_kernel(nodes_ref, columns_ref, speeds_ref, weights_ref, out_ref):
    groups, rows, rank = nodes_ref.shape
    bricks = out_ref.shape[0]
    factors = [jnp.broadcast_to(columns_ref[:, i : i + 1], (rows, rank)) for i in range(4)]
    sums = [jnp.zeros((rank, rank), jnp.float32) for _ in range(6)]
    vectors = jnp.zeros((8, rank), jnp.float32)
    for group in range(groups):
        nodes = nodes_ref[group]
        weighted = jnp.concatenate([nodes] + [nodes * factor for factor in factors], axis=1)
        high, low = two_parts(weighted)
        node_high, node_low = high[:, :rank], low[:, :rank]
        product = lax.dot_general(
            jnp.concatenate([node_high, node_high, node_low], axis=0),
            jnp.concatenate([high, low, high], axis=0),
            (((0,), (0,)), ((), ())),
            preferred_element_type=jnp.float32,
        )
        vectors = vectors + contract(weights_ref[group], nodes, 1, 0)
        plain = product[:, :rank]
        speed = jnp.broadcast_to(speeds_ref[group : group + 1, :], (rank, rank))
        sums[0] = sums[0] + jnp.maximum(speed, 0.0) * plain
        sums[1] = sums[1] + jnp.minimum(speed, 0.0) * plain
        for i in range(4):
            sums[2 + i] = sums[2 + i] + product[:, (i + 1) * rank : (i + 2) * rank]
    out_ref[:, :8, :] = jnp.broadcast_to((vectors * WEIGHT_V)[None], (bricks, 8, rank))
    height = rank // bricks
    for i in range(6):
        start = 8 + i * height
        out_ref[:, start : start + height, :] = (sums[i] * WEIGHT_V).reshape(
            bricks, height, rank
        )


def maxwell_kernel(
    brick_ref, cells_ref, integrals_ref, nodes_ref, first_ref, across_ref, part_ref, line_ref, state_ref
):
    bricks, cells, rank = cells_ref.shape
    groups, rows, _ = nodes_ref.shape
    total = bricks * cells
    brick = brick_ref[0]
    k_flat = jnp.concatenate([cells_ref[i ^ brick] for i in range(bricks)], axis=0)
    integrals = integrals_ref[0]
    for i in range(1, bricks):
        integrals = integrals + integrals_ref[i]
    height = integrals.shape[0] - 8
    part_ref[:, cells:, :] = jnp.broadcast_to(integrals[8:][None], (bricks, height, rank))
    moments = contract(integrals[:8], k_flat, 1, 1)
    density, drift, temper = cell_state([moments[i : i + 1] for i in range(5)])
    slope = -0.5 / temper
    amplitude = density * jnp.exp(-1.5 * jnp.log(2.0 * math.pi * temper))
    first = jnp.broadcast_to(first_ref[:, :1], (groups, total))
    line = amplitude * jnp.exp((first - drift[0]) ** 2 * slope)
    state = jnp.concatenate([drift[1], drift[2], slope] + [amplitude] * 5, axis=0)
    state_ref[...] = state
    both = jnp.concatenate([line, state], axis=0).T
    line_cols = both[:, :groups]
    line_ref[...] = line_cols
    distance = (across_ref[0:1, :] - both[:, groups : groups + 1]) ** 2
    distance = distance + (across_ref[1:2, :] - both[:, groups + 1 : groups + 2]) ** 2
    high, low = two_parts(jnp.exp(distance * both[:, groups + 2 : groups + 3]))
    lhs = jnp.concatenate([high, high, low], axis=1)
    result = jnp.zeros((total, rank), jnp.float32)
    for group in range(0, groups, 2):
        node_high, node_low = two_parts(
            jnp.concatenate([nodes_ref[group], nodes_ref[group + 1]], axis=1)
        )
        product = lax.dot_general(
            lhs,
            jnp.concatenate([node_high, node_low, node_high], axis=0),
            (((1,), (0,)), ((), ())),
            preferred_element_type=jnp.float32,
        )
        result = result + line_cols[:, group : group + 1] * product[:, :rank]
        result = result + line_cols[:, group + 1 : group + 2] * product[:, rank:]
    part_ref[:, :cells, :] = result.reshape(bricks, cells, rank)


def back_kernel(parts_ref, line_ref, state_ref, across_ref, out_ref):
    bricks, _, rank = parts_ref.shape
    groups, rows, _ = out_ref.shape
    total = line_ref.shape[0]
    cells = total // bricks
    advanced = parts_ref[:, :cells, :].reshape(total, rank)
    distance = (across_ref[:, 0:1] - state_ref[0:1, :]) ** 2
    distance = distance + (across_ref[:, 1:2] - state_ref[1:2, :]) ** 2
    high, low = two_parts(jnp.exp(distance * state_ref[2:3, :]))
    lhs = jnp.concatenate([high, high, low], axis=1)
    for group in range(0, groups, 2):
        scaled = [line_ref[:, i : i + 1] * advanced for i in (group, group + 1)]
        part_high, part_low = two_parts(jnp.concatenate(scaled, axis=1))
        product = lax.dot_general(
            lhs,
            jnp.concatenate([part_high, part_low, part_high], axis=0),
            (((1,), (0,)), ((), ())),
            preferred_element_type=jnp.float32,
        )
        out_ref[group] = product[:, :rank]
        out_ref[group + 1] = product[:, rank:]


def advance_kernel(parts_ref, steps_ref, cells_ref, payload_ref, advanced_ref, *, time_step):
    cells, rank = cells_ref.shape
    bricks = parts_ref.shape[0]
    height = rank // bricks
    maxwell_proj = parts_ref[0, :cells, :]
    for i in range(1, bricks):
        maxwell_proj = maxwell_proj + parts_ref[i, :cells, :]
    maxwell_proj = maxwell_proj * WEIGHT_V
    flux = jnp.zeros((cells, rank), jnp.float32)
    for i in range(6):
        block = parts_ref[:, cells + i * height : cells + (i + 1) * height, :].reshape(rank, rank)
        flux = flux + contract(steps_ref[i], block, 1, 0)
    own = cells_ref[...]
    advanced = own - time_step * flux + COLLIDE * (maxwell_proj - own)
    advanced_ref[...] = advanced
    payload_ref[:, :cells, :] = jnp.broadcast_to(advanced[None], (bricks, cells, rank))
    projected = contract(advanced, maxwell_proj, 0, 0)
    payload_ref[:, cells:, :] = projected.reshape(bricks, height, rank)


def middle_kernel(
    brick_ref,
    pieces_ref,
    transport_ref,
    basis_ref,
    back_ref,
    advanced_ref,
    speeds_ref,
    basis_x_ref,
    velocity_ref,
    gram_ref,
    work_ref,
    upper_ref,
    inverse_ref,
    *,
    lengths,
    time_step,
    weight_x,
):
    bricks, _, rank = pieces_ref.shape
    rows = basis_ref.shape[0]
    height = rank // bricks
    cells = advanced_ref.shape[0]
    brick = brick_ref[0]

    def piece(ref, i):
        if ref is transport_ref:
            start = cells + i * height
            return ref[:, start : start + height, :].reshape(rank, rank)
        rows_of = [ref[j ^ brick, i * height : (i + 1) * height, :] for j in range(bricks)]
        return jnp.concatenate(rows_of, axis=0)

    factor_into(piece(pieces_ref, 0) * weight_x, work_ref, upper_ref, inverse_ref)
    upper, inverse = upper_ref[...], inverse_ref[...]
    basis_x_ref[...] = contract(advanced_ref[...], inverse, 1, 1)
    change = jnp.zeros((rank, rank), jnp.float32)
    turned = []
    for i in range(3):
        shift = piece(pieces_ref, 1 + i) * weight_x
        straight = contract(inverse, shift, 1, 0)
        crossed = contract(inverse, shift, 1, 1)
        if i == 0:
            straight, crossed = crossed, straight
        turned.append(contract(straight, inverse, 1, 1))
        change = change + lengths[i] * (
            contract(upper - straight, piece(transport_ref, 2 * i), 1, 0)
            + contract(crossed - upper, piece(transport_ref, 2 * i + 1), 1, 0)
        )
    projected = contract(inverse, piece(pieces_ref, 4) * weight_x, 1, 0)
    middle = upper + time_step * change - COLLIDE * (projected - upper)
    now = contract(basis_ref[...], middle, 1, 1)
    drift_sum = jnp.zeros((rows, rank), jnp.float32)
    for i in range(3):
        speed = jnp.broadcast_to(speeds_ref[:, i : i + 1], (rows, rank)) * lengths[i]
        minus = contract(now, turned[i], 1, 1)
        plus = contract(now, turned[i], 1, 0)
        drift_sum = drift_sum + jnp.maximum(speed, 0.0) * (now - minus)
        drift_sum = drift_sum + jnp.minimum(speed, 0.0) * (plus - now)
    back = back_ref[0]
    for i in range(1, back_ref.shape[0]):
        back = back + back_ref[i]
    back_proj = contract(back * weight_x, inverse, 1, 1)
    updated = now - time_step * drift_sum + COLLIDE * (back_proj - now)
    velocity_ref[...] = updated
    gram_ref[...] = contract(updated, updated, 0, 0) * WEIGHT_V


def last_kernel(gram_ref, velocity_ref, coupling_ref, basis_ref, work_ref, upper_ref, inverse_ref):
    factor_into(gram_ref[...], work_ref, upper_ref, inverse_ref)
    coupling_ref[...] = upper_ref[...].T
    basis_ref[...] = contract(velocity_ref[...], inverse_ref[...], 1, 1)


def f32(*shape):
    return jax.ShapeDtypeStruct(shape, jnp.float32)


def factor_scratch(rank):
    shapes = ((rank, 2 * rank), (rank, rank), (rank, rank))
    return [pltpu.VMEM(shape, jnp.float32) for shape in shapes]


def local(k_coeffs, v_basis):
    cells_x, cells_y, cells_z, rank = k_coeffs.shape
    cells = cells_x * cells_y * cells_z
    slabs, bricks = lax.axis_size("slab"), lax.axis_size("brick")
    devices = slabs * bricks
    slab, brick = lax.axis_index("slab"), lax.axis_index("brick")
    lengths = (cells_x * slabs, cells_y * bricks, cells_z)
    time_step = CFL / (VMAX * sum(lengths))
    weight_x = 1.0 / (lengths[0] * lengths[1] * lengths[2])
    rows = v_basis.shape[0]
    slab_cells = cells * bricks
    half = slab_cells // cells_x
    height = rank // bricks
    up = [(i, (i + 1) % slabs) for i in range(slabs)]
    down = [(i, (i - 1) % slabs) for i in range(slabs)]
    own_cells = k_coeffs.reshape(cells, rank)

    own_ids = (slab * bricks + brick) * rows + jnp.arange(rows, dtype=jnp.int32)
    own_velocity = velocities(own_ids)
    ones = jnp.ones_like(own_velocity[0])
    slab_owner = jnp.arange(slabs, dtype=jnp.int32)[:, None] * bricks + brick
    slab_velocity = velocities(slab_owner * rows + jnp.arange(rows, dtype=jnp.int32)[None])
    weights = jnp.stack(
        [jnp.ones_like(slab_velocity[0]), slab_velocity[0], slab_velocity[1], slab_velocity[2]]
        + [jnp.sum(slab_velocity * slab_velocity, axis=0)]
        + [jnp.zeros_like(slab_velocity[0])] * 3,
        axis=1,
    )
    nodes = to_all(v_basis, "slab")
    k_slab = gather_relative(own_cells, "brick", BRICK_GROUPS)
    k_edges, k_slab = lax.optimization_barrier((k_coeffs, k_slab))
    k_below = lax.ppermute(k_edges[-1:], "slab", up)
    k_above = lax.ppermute(k_edges[:1], "slab", down)

    across = velocities(brick * rows + jnp.arange(rows, dtype=jnp.int32))
    columns = [f(across[i]) for i in (1, 2) for f in (lambda v: jnp.maximum(v, 0.0), lambda v: jnp.minimum(v, 0.0))]
    columns = jnp.stack(columns + [jnp.zeros_like(ones)] * 4, axis=1)
    owner = jnp.arange(slabs, dtype=jnp.int32) * bricks + brick
    first_velocity = velocities(owner * rows)[0]
    first_speeds = jnp.broadcast_to(first_velocity[:, None], (slabs, rank))
    transport_part = pl.pallas_call(
        transport_kernel, out_shape=f32(bricks, 8 + 6 * height, rank), name="transport"
    )(nodes, columns, first_speeds, weights)
    integrals = exchange(transport_part, "brick")

    brick_id = brick.astype(jnp.int32)[None]
    vector_specs = [pl.BlockSpec(memory_space=pltpu.SMEM)]
    whole = pl.BlockSpec(memory_space=pltpu.VMEM)
    payload, line, state = pl.pallas_call(
        maxwell_kernel,
        out_shape=(
            f32(bricks, cells + 6 * height, rank),
            f32(slab_cells, slabs),
            f32(8, slab_cells),
        ),
        in_specs=vector_specs + [whole] * 5,
        name="maxwell",
    )(brick_id, k_slab, integrals, nodes, first_speeds, across[1:])
    second = exchange(payload, "brick")

    slab_grid = k_slab.reshape(bricks, cells_x, cells_y, cells_z, rank)
    left = ((brick - 1) % bricks) ^ brick
    right = ((brick + 1) % bricks) ^ brick
    left = lax.dynamic_index_in_dim(slab_grid, left, 0, keepdims=False)
    right = lax.dynamic_index_in_dim(slab_grid, right, 0, keepdims=False)
    lower = [
        jnp.concatenate([k_below, k_coeffs[:-1]], axis=0),
        jnp.concatenate([left[:, -1:], k_coeffs[:, :-1]], axis=1),
        jnp.roll(k_coeffs, 1, axis=2),
    ]
    upper = [
        jnp.concatenate([k_coeffs[1:], k_above], axis=0),
        jnp.concatenate([k_coeffs[:, 1:], right[:, :1]], axis=1),
        jnp.roll(k_coeffs, -1, axis=2),
    ]
    steps = []
    for axis_id in range(3):
        steps.append(((k_coeffs - lower[axis_id]) * lengths[axis_id]).reshape(cells, rank))
        steps.append(((upper[axis_id] - k_coeffs) * lengths[axis_id]).reshape(cells, rank))
    payload, advanced = pl.pallas_call(
        functools.partial(advance_kernel, time_step=time_step),
        out_shape=(f32(bricks, cells + height, rank), f32(cells, rank)),
        name="advance",
    )(second, jnp.stack(steps), own_cells)
    third = exchange(payload, "brick")

    slab_advanced = third[:, :cells]
    projected_rows = jnp.sum(third[:, cells:], axis=0)
    adv_grid = slab_advanced.reshape(bricks, cells_x, cells_y, cells_z, rank)
    planes_x = [adv_grid[:, i].reshape(half, rank) for i in range(cells_x)]
    choose = brick * height + jnp.arange(height, dtype=jnp.int32)
    choose = (choose[:, None] == jnp.arange(rank, dtype=jnp.int32)[None]).astype(jnp.float32)
    chosen = contract(choose, planes_x[-1], 1, 1)
    chosen_below = lax.ppermute(chosen, "slab", up)
    back = pl.pallas_call(back_kernel, out_shape=f32(slabs, rows, rank), name="back")(
        third, line, state, across[1:].T
    )
    back, slab_advanced = lax.optimization_barrier((back, slab_advanced))
    fourth = exchange(back, "slab")

    adv_grid = slab_advanced.reshape(bricks, cells_x, cells_y, cells_z, rank)
    planes_x = [adv_grid[:, i].reshape(half, rank) for i in range(cells_x)]
    before = jnp.concatenate([adv_grid[-1:, :, -1:], adv_grid[:-1, :, -1:]], axis=0)
    shift_y = jnp.concatenate([before, adv_grid[:, :, :-1]], axis=2).reshape(slab_cells, rank)
    shift_z = jnp.roll(adv_grid, 1, axis=3).reshape(slab_cells, rank)
    adv_flat = slab_advanced.reshape(slab_cells, rank)

    def own_rows(left_side, right_side):
        whole = contract(left_side, right_side, 0, 0)
        return lax.dynamic_slice_in_dim(whole, brick * height, height, 0)

    crossing = contract(chosen_below, planes_x[0], 1, 0)
    for i in range(1, cells_x):
        crossing = crossing + own_rows(planes_x[i - 1], planes_x[i])
    pieces = jnp.concatenate(
        [
            own_rows(adv_flat, adv_flat),
            crossing,
            own_rows(adv_flat, shift_y),
            own_rows(adv_flat, shift_z),
            projected_rows,
        ],
        axis=0,
    )
    pieces = sum_over(pieces, "slab", SLAB_GROUPS)
    reduced = gather_relative(pieces, "brick", BRICK_GROUPS)

    speeds = jnp.stack(list(own_velocity) + [jnp.zeros_like(ones)] * 5, axis=1)
    basis_new, velocity_new, gram_part = pl.pallas_call(
        functools.partial(
            middle_kernel, lengths=lengths, time_step=time_step, weight_x=weight_x
        ),
        out_shape=(f32(cells, rank), f32(rows, rank), f32(rank, rank)),
        in_specs=vector_specs + [whole] * 6,
        scratch_shapes=factor_scratch(rank),
        name="middle",
    )(brick_id, reduced, second, v_basis, fourth, advanced, speeds)
    gram_v = sum_over(gram_part, ("slab", "brick"), ALL_GROUPS)
    coupling, vbasis_new = pl.pallas_call(
        last_kernel,
        out_shape=(f32(rank, rank), f32(rows, rank)),
        scratch_shapes=factor_scratch(rank),
        name="last",
    )(gram_v, velocity_new)
    return (basis_new.reshape(cells_x, cells_y, cells_z, rank), coupling, vbasis_new)


def solution(mesh):
    placed = (P("slab", "brick", None, None), P(("slab", "brick"), None))
    return jax.shard_map(
        local,
        mesh=mesh,
        in_specs=placed,
        out_specs=(P("slab", "brick", None, None), P(), P(("slab", "brick"), None)),
        check_vma=False,
    )
```

```python
import functools
import math

import jax
import jax.numpy as jnp
from jax import lax
from jax.experimental import pallas as pl
from jax.experimental.pallas import tpu as pltpu
from jax.sharding import PartitionSpec as P

NVX = 32


CFL = 0.9
VMAX = 6.0
COLLIDE = 0.3
RHO_MIN = 0.25
TEMP_MIN = 0.25
PRECISE = lax.Precision.HIGHEST
FINE = lax.Precision.HIGH
SPACING = 2.0 * VMAX / NVX
WEIGHT_V = SPACING**3
PANEL = 16


def contract(left, right, left_dim, right_dim, precision=PRECISE):
    return lax.dot_general(
        left, right, (((left_dim,), (right_dim,)), ((), ())), precision=precision
    )


def exchange(array, axis):
    return lax.all_to_all(array, axis, 0, 0, tiled=True)


def to_all(array, axis):
    copies = lax.axis_size(axis)
    return exchange(jnp.broadcast_to(array[None], (copies,) + array.shape), axis)


def velocities(indices):
    coords = jnp.stack([indices // (NVX * NVX), indices // NVX % NVX, indices % NVX])
    return -VMAX + (coords.astype(jnp.float32) + 0.5) * SPACING


def cell_state(moments):
    density = jnp.maximum(moments[0], RHO_MIN)
    drift = [moments[axis_id] / density for axis_id in (1, 2, 3)]
    square = drift[0] * drift[0] + drift[1] * drift[1] + drift[2] * drift[2]
    temper = jnp.maximum((moments[4] / density - square) / 3.0, TEMP_MIN)
    return density, drift, temper


def from_peer(values, axis, mask):
    axes = axis if isinstance(axis, tuple) else (axis,)
    peers = math.prod(lax.axis_size(name) for name in axes)
    return lax.ppermute(values, axis, [(i, i ^ mask) for i in range(peers)])


def sum_over(array, axis, groups):
    for masks in groups:
        parts = [array] + [from_peer(array, axis, mask) for mask in masks]
        array = sum_pairs(parts)
    return array


def sum_pairs(parts):
    if len(parts) == 1:
        return parts[0]
    half = len(parts) // 2
    return sum_pairs(parts[:half]) + sum_pairs(parts[half:])


def gather_relative(array, axis, groups):
    return gather_more(array[None], axis, groups)


def gather_more(array, axis, groups):
    for masks in groups:
        array = jnp.concatenate([array] + [from_peer(array, axis, mask) for mask in masks], axis=0)
    return array


BRICK_GROUPS = ((1,), (2, 4, 6), (8,))
ALL_GROUPS = ((1,), (2, 4, 6), (8, 16, 24), (32, 64, 96))


def three_parts(array):
    high = array.astype(jnp.bfloat16).astype(jnp.float32)
    rest = array - high
    middle = rest.astype(jnp.bfloat16).astype(jnp.float32)
    return high, middle, rest - middle


def two_parts(array):
    high = array.astype(jnp.bfloat16)
    return high, (array - high.astype(jnp.float32)).astype(jnp.bfloat16)


def factor_into(gram, work_ref, upper_ref, inverse_ref):
    size = gram.shape[0]
    rows = lax.broadcasted_iota(jnp.int32, (size, size), 0)
    cols = lax.broadcasted_iota(jnp.int32, (size, size), 1)
    work_ref[:, :size] = gram
    work_ref[:, size:] = jnp.where(rows == cols, 1.0, 0.0)
    panel_row = lax.broadcasted_iota(jnp.int32, (PANEL, size), 0)
    panel_col = lax.broadcasted_iota(jnp.int32, (PANEL, size), 1)
    for start in range(0, size, PANEL):
        stop = start + PANEL
        panel = work_ref[start:stop, :]
        spread = [
            jnp.broadcast_to(panel[:, start + t : start + t + 1], (PANEL, size))
            for t in range(PANEL)
        ]
        pivots = jnp.zeros((PANEL, size), jnp.float32)
        for t in range(PANEL):
            pivot = jnp.broadcast_to(spread[t][t : t + 1, :], (PANEL, size))
            pivots = jnp.where(panel_row == t, pivot, pivots)
            if t == PANEL - 1:
                break
            ratio = jnp.where(panel_row > t, spread[t] * (1.0 / pivot), 0.0)
            for u in range(t + 1, PANEL):
                spread[u] = spread[u] - ratio * jnp.broadcast_to(
                    spread[u][t : t + 1, :], (PANEL, size)
                )
            panel = panel - jnp.concatenate([ratio, ratio], axis=1) * jnp.broadcast_to(
                panel[t : t + 1, :], (PANEL, 2 * size)
            )
        scale = lax.rsqrt(pivots)
        panel = panel * jnp.concatenate([scale, scale], axis=1)
        left = jnp.where(panel_col >= panel_row + start, panel[:, :size], 0.0)
        right = panel[:, size:]
        upper_ref[start:stop, :] = left
        inverse_ref[start:stop, :] = right
        if stop < size:
            high, middle, low = three_parts(jnp.concatenate([left, right], axis=1))
            lhs = [high, high, middle, middle, high, low]
            rhs = [high, middle, high, middle, low, high]
            update = lax.dot_general(
                jnp.concatenate([part[:, :size] for part in lhs], axis=0).astype(jnp.bfloat16),
                jnp.concatenate(rhs, axis=0).astype(jnp.bfloat16),
                (((0,), (0,)), ((), ())),
                preferred_element_type=jnp.float32,
            )
            work_ref[stop:, :] = work_ref[stop:, :] - update[stop:, :]


def transport_kernel(nodes_ref, columns_ref, speeds_ref, weights_ref, out_ref):
    groups, rows, rank = nodes_ref.shape
    bricks = out_ref.shape[0]
    factors = [jnp.broadcast_to(columns_ref[:, i : i + 1], (rows, rank)) for i in range(4)]
    sums = [jnp.zeros((rank, rank), jnp.float32) for _ in range(6)]
    vectors = jnp.zeros((8, rank), jnp.float32)
    for group in range(groups):
        nodes = nodes_ref[group]
        weighted = jnp.concatenate([nodes] + [nodes * factor for factor in factors], axis=1)
        high, low = two_parts(weighted)
        node_high, node_low = high[:, :rank], low[:, :rank]
        product = lax.dot_general(
            jnp.concatenate([node_high, node_high, node_low], axis=0),
            jnp.concatenate([high, low, high], axis=0),
            (((0,), (0,)), ((), ())),
            preferred_element_type=jnp.float32,
        )
        vectors = vectors + contract(weights_ref[group], nodes, 1, 0)
        plain = product[:, :rank]
        speed = jnp.broadcast_to(speeds_ref[group : group + 1, :], (rank, rank))
        sums[0] = sums[0] + jnp.maximum(speed, 0.0) * plain
        sums[1] = sums[1] + jnp.minimum(speed, 0.0) * plain
        for i in range(4):
            sums[2 + i] = sums[2 + i] + product[:, (i + 1) * rank : (i + 2) * rank]
    out_ref[:, :8, :] = jnp.broadcast_to((vectors * WEIGHT_V)[None], (bricks, 8, rank))
    height = rank // bricks
    for i in range(6):
        start = 8 + i * height
        out_ref[:, start : start + height, :] = (sums[i] * WEIGHT_V).reshape(
            bricks, height, rank
        )


def maxwell_kernel(
    brick_ref, cells_ref, integrals_ref, nodes_ref, first_ref, across_ref, part_ref, line_ref, state_ref
):
    bricks, cells, rank = cells_ref.shape
    groups, rows, _ = nodes_ref.shape
    total = bricks * cells
    brick = brick_ref[0]
    k_flat = jnp.concatenate([cells_ref[i ^ brick] for i in range(bricks)], axis=0)
    integrals = integrals_ref[0]
    for i in range(1, bricks):
        integrals = integrals + integrals_ref[i]
    height = integrals.shape[0] - 8
    part_ref[:, cells:, :] = jnp.broadcast_to(integrals[8:][None], (bricks, height, rank))
    moments = contract(integrals[:8], k_flat, 1, 1)
    density, drift, temper = cell_state([moments[i : i + 1] for i in range(5)])
    slope = -0.5 / temper
    amplitude = density * jnp.exp(-1.5 * jnp.log(2.0 * math.pi * temper))
    first = jnp.broadcast_to(first_ref[:, :1], (groups, total))
    line = amplitude * jnp.exp((first - drift[0]) ** 2 * slope)
    state = jnp.concatenate([drift[1], drift[2], slope] + [amplitude] * 5, axis=0)
    state_ref[...] = state
    both = jnp.concatenate([line, state], axis=0).T
    line_cols = both[:, :groups]
    line_ref[...] = line_cols
    distance = (across_ref[0:1, :] - both[:, groups : groups + 1]) ** 2
    distance = distance + (across_ref[1:2, :] - both[:, groups + 1 : groups + 2]) ** 2
    high, low = two_parts(jnp.exp(distance * both[:, groups + 2 : groups + 3]))
    lhs = jnp.concatenate([high, high, low], axis=1)
    result = jnp.zeros((total, rank), jnp.float32)
    for group in range(0, groups, 2):
        node_high, node_low = two_parts(
            jnp.concatenate([nodes_ref[group], nodes_ref[group + 1]], axis=1)
        )
        product = lax.dot_general(
            lhs,
            jnp.concatenate([node_high, node_low, node_high], axis=0),
            (((1,), (0,)), ((), ())),
            preferred_element_type=jnp.float32,
        )
        result = result + line_cols[:, group : group + 1] * product[:, :rank]
        result = result + line_cols[:, group + 1 : group + 2] * product[:, rank:]
    part_ref[:, :cells, :] = result.reshape(bricks, cells, rank)


def back_kernel(parts_ref, line_ref, state_ref, across_ref, out_ref):
    bricks, _, rank = parts_ref.shape
    groups, rows, _ = out_ref.shape
    total = line_ref.shape[0]
    cells = total // bricks
    advanced = parts_ref[:, :cells, :].reshape(total, rank)
    distance = (across_ref[:, 0:1] - state_ref[0:1, :]) ** 2
    distance = distance + (across_ref[:, 1:2] - state_ref[1:2, :]) ** 2
    high, low = two_parts(jnp.exp(distance * state_ref[2:3, :]))
    lhs = jnp.concatenate([high, high, low], axis=1)
    for group in range(0, groups, 2):
        scaled = [line_ref[:, i : i + 1] * advanced for i in (group, group + 1)]
        part_high, part_low = two_parts(jnp.concatenate(scaled, axis=1))
        product = lax.dot_general(
            lhs,
            jnp.concatenate([part_high, part_low, part_high], axis=0),
            (((1,), (0,)), ((), ())),
            preferred_element_type=jnp.float32,
        )
        out_ref[group] = product[:, :rank]
        out_ref[group + 1] = product[:, rank:]


def advance_kernel(parts_ref, steps_ref, cells_ref, payload_ref, advanced_ref, *, time_step):
    cells, rank = cells_ref.shape
    bricks = parts_ref.shape[0]
    height = rank // bricks
    maxwell_proj = parts_ref[0, :cells, :]
    for i in range(1, bricks):
        maxwell_proj = maxwell_proj + parts_ref[i, :cells, :]
    maxwell_proj = maxwell_proj * WEIGHT_V
    flux = jnp.zeros((cells, rank), jnp.float32)
    for i in range(6):
        block = parts_ref[:, cells + i * height : cells + (i + 1) * height, :].reshape(rank, rank)
        flux = flux + contract(steps_ref[i], block, 1, 0)
    own = cells_ref[...]
    advanced = own - time_step * flux + COLLIDE * (maxwell_proj - own)
    advanced_ref[...] = advanced
    payload_ref[:, :cells, :] = jnp.broadcast_to(advanced[None], (bricks, cells, rank))
    projected = contract(advanced, maxwell_proj, 0, 0)
    payload_ref[:, cells:, :] = projected.reshape(bricks, height, rank)


def middle_kernel(
    brick_ref,
    pieces_ref,
    transport_ref,
    basis_ref,
    back_ref,
    advanced_ref,
    speeds_ref,
    basis_x_ref,
    velocity_ref,
    gram_ref,
    work_ref,
    upper_ref,
    inverse_ref,
    *,
    lengths,
    time_step,
    weight_x,
):
    bricks, _, rank = pieces_ref.shape
    rows = basis_ref.shape[0]
    height = rank // bricks
    cells = advanced_ref.shape[0]
    masks = [j ^ brick_ref[0] for j in range(bricks)]
    slots = [((m >> 1) & 3) * 4 + (m & 1) * 2 + (m >> 3) for m in masks]

    def piece(ref, i):
        if ref is transport_ref:
            start = cells + i * height
            return ref[:, start : start + height, :].reshape(rank, rank)
        rows_of = [ref[slot, i * height : (i + 1) * height, :] for slot in slots]
        return jnp.concatenate(rows_of, axis=0)

    factor_into(piece(pieces_ref, 0) * weight_x, work_ref, upper_ref, inverse_ref)
    upper, inverse = upper_ref[...], inverse_ref[...]
    basis_x_ref[...] = contract(advanced_ref[...], inverse, 1, 1)
    change = jnp.zeros((rank, rank), jnp.float32)
    turned = []
    for i in range(3):
        shift = piece(pieces_ref, 1 + i) * weight_x
        straight = contract(inverse, shift, 1, 0)
        crossed = contract(inverse, shift, 1, 1)
        if i == 0:
            straight, crossed = crossed, straight
        turned.append(contract(straight, inverse, 1, 1))
        change = change + lengths[i] * (
            contract(upper - straight, piece(transport_ref, 2 * i), 1, 0)
            + contract(crossed - upper, piece(transport_ref, 2 * i + 1), 1, 0)
        )
    projected = contract(inverse, piece(pieces_ref, 4) * weight_x, 1, 0)
    middle = upper + time_step * change - COLLIDE * (projected - upper)
    now = contract(basis_ref[...], middle, 1, 1)
    drift_sum = jnp.zeros((rows, rank), jnp.float32)
    for i in range(3):
        speed = jnp.broadcast_to(speeds_ref[:, i : i + 1], (rows, rank)) * lengths[i]
        minus = contract(now, turned[i], 1, 1)
        plus = contract(now, turned[i], 1, 0)
        drift_sum = drift_sum + jnp.maximum(speed, 0.0) * (now - minus)
        drift_sum = drift_sum + jnp.minimum(speed, 0.0) * (plus - now)
    back = back_ref[0]
    for i in range(1, back_ref.shape[0]):
        back = back + back_ref[i]
    back_proj = contract(back * weight_x, inverse, 1, 1)
    updated = now - time_step * drift_sum + COLLIDE * (back_proj - now)
    velocity_ref[...] = updated
    gram_ref[...] = contract(updated, updated, 0, 0) * WEIGHT_V


def last_kernel(gram_ref, velocity_ref, coupling_ref, basis_ref, work_ref, upper_ref, inverse_ref):
    factor_into(gram_ref[...], work_ref, upper_ref, inverse_ref)
    coupling_ref[...] = upper_ref[...].T
    basis_ref[...] = contract(velocity_ref[...], inverse_ref[...], 1, 1)


def f32(*shape):
    return jax.ShapeDtypeStruct(shape, jnp.float32)


def factor_scratch(rank):
    shapes = ((rank, 2 * rank), (rank, rank), (rank, rank))
    return [pltpu.VMEM(shape, jnp.float32) for shape in shapes]


def local(k_coeffs, v_basis):
    cells_x, cells_y, cells_z, rank = k_coeffs.shape
    cells = cells_x * cells_y * cells_z
    slabs, bricks = lax.axis_size("slab"), lax.axis_size("brick")
    devices = slabs * bricks
    slab, brick = lax.axis_index("slab"), lax.axis_index("brick")
    lengths = (cells_x * slabs, cells_y * bricks, cells_z)
    time_step = CFL / (VMAX * sum(lengths))
    weight_x = 1.0 / (lengths[0] * lengths[1] * lengths[2])
    rows = v_basis.shape[0]
    slab_cells = cells * bricks
    half = slab_cells // cells_x
    height = rank // bricks
    up = [(i, (i + 1) % slabs) for i in range(slabs)]
    down = [(i, (i - 1) % slabs) for i in range(slabs)]
    own_cells = k_coeffs.reshape(cells, rank)

    own_ids = (slab * bricks + brick) * rows + jnp.arange(rows, dtype=jnp.int32)
    own_velocity = velocities(own_ids)
    ones = jnp.ones_like(own_velocity[0])
    slab_owner = jnp.arange(slabs, dtype=jnp.int32)[:, None] * bricks + brick
    slab_velocity = velocities(slab_owner * rows + jnp.arange(rows, dtype=jnp.int32)[None])
    weights = jnp.stack(
        [jnp.ones_like(slab_velocity[0]), slab_velocity[0], slab_velocity[1], slab_velocity[2]]
        + [jnp.sum(slab_velocity * slab_velocity, axis=0)]
        + [jnp.zeros_like(slab_velocity[0])] * 3,
        axis=1,
    )
    nodes = to_all(v_basis, "slab")
    k_slab = gather_relative(own_cells, "brick", BRICK_GROUPS)
    k_edges, k_slab = lax.optimization_barrier((k_coeffs, k_slab))
    k_below = lax.ppermute(k_edges[-1:], "slab", up)
    k_above = lax.ppermute(k_edges[:1], "slab", down)

    across = velocities(brick * rows + jnp.arange(rows, dtype=jnp.int32))
    columns = [f(across[i]) for i in (1, 2) for f in (lambda v: jnp.maximum(v, 0.0), lambda v: jnp.minimum(v, 0.0))]
    columns = jnp.stack(columns + [jnp.zeros_like(ones)] * 4, axis=1)
    owner = jnp.arange(slabs, dtype=jnp.int32) * bricks + brick
    first_velocity = velocities(owner * rows)[0]
    first_speeds = jnp.broadcast_to(first_velocity[:, None], (slabs, rank))
    transport_part = pl.pallas_call(
        transport_kernel, out_shape=f32(bricks, 8 + 6 * height, rank), name="transport"
    )(nodes, columns, first_speeds, weights)
    integrals = exchange(transport_part, "brick")

    brick_id = brick.astype(jnp.int32)[None]
    vector_specs = [pl.BlockSpec(memory_space=pltpu.SMEM)]
    whole = pl.BlockSpec(memory_space=pltpu.VMEM)
    payload, line, state = pl.pallas_call(
        maxwell_kernel,
        out_shape=(
            f32(bricks, cells + 6 * height, rank),
            f32(slab_cells, slabs),
            f32(8, slab_cells),
        ),
        in_specs=vector_specs + [whole] * 5,
        name="maxwell",
    )(brick_id, k_slab, integrals, nodes, first_speeds, across[1:])
    second = exchange(payload, "brick")

    slab_grid = k_slab.reshape(bricks, cells_x, cells_y, cells_z, rank)
    left = ((brick - 1) % bricks) ^ brick
    right = ((brick + 1) % bricks) ^ brick
    left = lax.dynamic_index_in_dim(slab_grid, left, 0, keepdims=False)
    right = lax.dynamic_index_in_dim(slab_grid, right, 0, keepdims=False)
    lower = [
        jnp.concatenate([k_below, k_coeffs[:-1]], axis=0),
        jnp.concatenate([left[:, -1:], k_coeffs[:, :-1]], axis=1),
        jnp.roll(k_coeffs, 1, axis=2),
    ]
    upper = [
        jnp.concatenate([k_coeffs[1:], k_above], axis=0),
        jnp.concatenate([k_coeffs[:, 1:], right[:, :1]], axis=1),
        jnp.roll(k_coeffs, -1, axis=2),
    ]
    steps = []
    for axis_id in range(3):
        steps.append(((k_coeffs - lower[axis_id]) * lengths[axis_id]).reshape(cells, rank))
        steps.append(((upper[axis_id] - k_coeffs) * lengths[axis_id]).reshape(cells, rank))
    payload, advanced = pl.pallas_call(
        functools.partial(advance_kernel, time_step=time_step),
        out_shape=(f32(bricks, cells + height, rank), f32(cells, rank)),
        name="advance",
    )(second, jnp.stack(steps), own_cells)
    third = exchange(payload, "brick")

    slab_advanced = third[:, :cells]
    projected_rows = jnp.sum(third[:, cells:], axis=0)
    adv_grid = slab_advanced.reshape(bricks, cells_x, cells_y, cells_z, rank)
    planes_x = [adv_grid[:, i].reshape(half, rank) for i in range(cells_x)]
    choose = brick * height + jnp.arange(height, dtype=jnp.int32)
    choose = (choose[:, None] == jnp.arange(rank, dtype=jnp.int32)[None]).astype(jnp.float32)
    chosen = contract(choose, planes_x[-1], 1, 1)
    chosen_below = lax.ppermute(chosen, "slab", up)
    adv_grid = slab_advanced.reshape(bricks, cells_x, cells_y, cells_z, rank)
    planes_x = [adv_grid[:, i].reshape(half, rank) for i in range(cells_x)]
    before = jnp.concatenate([adv_grid[-1:, :, -1:], adv_grid[:-1, :, -1:]], axis=0)
    shift_y = jnp.concatenate([before, adv_grid[:, :, :-1]], axis=2).reshape(slab_cells, rank)
    shift_z = jnp.roll(adv_grid, 1, axis=3).reshape(slab_cells, rank)
    adv_flat = slab_advanced.reshape(slab_cells, rank)

    def own_rows(left_side, right_side):
        whole = contract(left_side, right_side, 0, 0)
        return lax.dynamic_slice_in_dim(whole, brick * height, height, 0)

    crossing = contract(chosen_below, planes_x[0], 1, 0)
    for i in range(1, cells_x):
        crossing = crossing + own_rows(planes_x[i - 1], planes_x[i])
    pieces = jnp.concatenate(
        [
            own_rows(adv_flat, adv_flat),
            crossing,
            own_rows(adv_flat, shift_y),
            own_rows(adv_flat, shift_z),
            projected_rows,
        ],
        axis=0,
    )
    pieces, third_after = lax.optimization_barrier((pieces, third))
    back = pl.pallas_call(back_kernel, out_shape=f32(slabs, rows, rank), name="back")(
        third_after, line, state, across[1:].T
    )
    fourth = exchange(back, "slab")

    both = ("slab", "brick")
    lower_x, upper_x, cross_x = (from_peer(pieces, both, mask) for mask in (8, 16, 24))
    reduced = jnp.stack([pieces + upper_x, lower_x + cross_x])
    reduced = sum_over(reduced, both, ((32, 64, 96),))
    reduced = gather_more(reduced, both, ((1,), (2, 4, 6)))

    speeds = jnp.stack(list(own_velocity) + [jnp.zeros_like(ones)] * 5, axis=1)
    basis_new, velocity_new, gram_part = pl.pallas_call(
        functools.partial(
            middle_kernel, lengths=lengths, time_step=time_step, weight_x=weight_x
        ),
        out_shape=(f32(cells, rank), f32(rows, rank), f32(rank, rank)),
        in_specs=vector_specs + [whole] * 6,
        scratch_shapes=factor_scratch(rank),
        name="middle",
    )(brick_id, reduced, second, v_basis, fourth, advanced, speeds)
    gram_v = sum_over(gram_part, ("slab", "brick"), ALL_GROUPS)
    coupling, vbasis_new = pl.pallas_call(
        last_kernel,
        out_shape=(f32(rank, rank), f32(rows, rank)),
        scratch_shapes=factor_scratch(rank),
        name="last",
    )(gram_v, velocity_new)
    return (basis_new.reshape(cells_x, cells_y, cells_z, rank), coupling, vbasis_new)


def solution(mesh):
    placed = (P("slab", "brick", None, None), P(("slab", "brick"), None))
    return jax.shard_map(
        local,
        mesh=mesh,
        in_specs=placed,
        out_specs=(P("slab", "brick", None, None), P(), P(("slab", "brick"), None)),
        check_vma=False,
    )
```

```python
import functools
import math

import jax
import jax.numpy as jnp
from jax import lax
from jax.experimental import pallas as pl
from jax.experimental.pallas import tpu as pltpu
from jax.sharding import PartitionSpec as P

NVX = 32


CFL = 0.9
VMAX = 6.0
COLLIDE = 0.3
RHO_MIN = 0.25
TEMP_MIN = 0.25
PRECISE = lax.Precision.HIGHEST
FINE = lax.Precision.HIGH
SPACING = 2.0 * VMAX / NVX
WEIGHT_V = SPACING**3
PANEL = 16
VMEM_BYTES = 24 * 2**20


def contract(left, right, left_dim, right_dim, precision=PRECISE):
    return lax.dot_general(
        left, right, (((left_dim,), (right_dim,)), ((), ())), precision=precision
    )


def exchange(array, axis):
    return lax.all_to_all(array, axis, 0, 0, tiled=True)


def to_all(array, axis):
    copies = lax.axis_size(axis)
    return exchange(jnp.broadcast_to(array[None], (copies,) + array.shape), axis)


def velocities(indices):
    coords = jnp.stack([indices // (NVX * NVX), indices // NVX % NVX, indices % NVX])
    return -VMAX + (coords.astype(jnp.float32) + 0.5) * SPACING


def cell_state(moments):
    density = jnp.maximum(moments[0], RHO_MIN)
    drift = [moments[axis_id] / density for axis_id in (1, 2, 3)]
    square = drift[0] * drift[0] + drift[1] * drift[1] + drift[2] * drift[2]
    temper = jnp.maximum((moments[4] / density - square) / 3.0, TEMP_MIN)
    return density, drift, temper


def from_peer(values, axis, mask):
    axes = axis if isinstance(axis, tuple) else (axis,)
    peers = math.prod(lax.axis_size(name) for name in axes)
    return lax.ppermute(values, axis, [(i, i ^ mask) for i in range(peers)])


def sum_over(array, axis, groups):
    for masks in groups:
        parts = [array] + [from_peer(array, axis, mask) for mask in masks]
        array = sum_pairs(parts)
    return array


def sum_pairs(parts):
    if len(parts) == 1:
        return parts[0]
    half = len(parts) // 2
    return sum_pairs(parts[:half]) + sum_pairs(parts[half:])


def gather_relative(array, axis, groups):
    return gather_more(array[None], axis, groups)


def gather_more(array, axis, groups):
    for masks in groups:
        array = jnp.concatenate([array] + [from_peer(array, axis, mask) for mask in masks], axis=0)
    return array


BRICK_GROUPS = ((1,), (2, 4, 6), (8,))
ALL_GROUPS = ((1,), (2, 4, 6), (8, 16, 24), (32, 64, 96))


def three_parts(array):
    high = array.astype(jnp.bfloat16).astype(jnp.float32)
    rest = array - high
    middle = rest.astype(jnp.bfloat16).astype(jnp.float32)
    return high, middle, rest - middle


def two_parts(array):
    high = array.astype(jnp.bfloat16)
    return high, (array - high.astype(jnp.float32)).astype(jnp.bfloat16)


def factor_into(gram, work_ref, upper_ref, inverse_ref):
    size = gram.shape[0]
    rows = lax.broadcasted_iota(jnp.int32, (size, size), 0)
    cols = lax.broadcasted_iota(jnp.int32, (size, size), 1)
    work_ref[:, :size] = gram
    work_ref[:, size:] = jnp.where(rows == cols, 1.0, 0.0)
    panel_row = lax.broadcasted_iota(jnp.int32, (PANEL, size), 0)
    panel_col = lax.broadcasted_iota(jnp.int32, (PANEL, size), 1)
    for start in range(0, size, PANEL):
        stop = start + PANEL
        panel = work_ref[start:stop, :]
        spread = [
            jnp.broadcast_to(panel[:, start + t : start + t + 1], (PANEL, size))
            for t in range(PANEL)
        ]
        pivots = jnp.zeros((PANEL, size), jnp.float32)
        for t in range(PANEL):
            pivot = jnp.broadcast_to(spread[t][t : t + 1, :], (PANEL, size))
            pivots = jnp.where(panel_row == t, pivot, pivots)
            if t == PANEL - 1:
                break
            ratio = jnp.where(panel_row > t, spread[t] * (1.0 / pivot), 0.0)
            for u in range(t + 1, PANEL):
                spread[u] = spread[u] - ratio * jnp.broadcast_to(
                    spread[u][t : t + 1, :], (PANEL, size)
                )
            panel = panel - jnp.concatenate([ratio, ratio], axis=1) * jnp.broadcast_to(
                panel[t : t + 1, :], (PANEL, 2 * size)
            )
        scale = lax.rsqrt(pivots)
        panel = panel * jnp.concatenate([scale, scale], axis=1)
        left = jnp.where(panel_col >= panel_row + start, panel[:, :size], 0.0)
        right = panel[:, size:]
        upper_ref[start:stop, :] = left
        inverse_ref[start:stop, :] = right
        if stop < size:
            high, middle, low = three_parts(jnp.concatenate([left, right], axis=1))
            lhs = [high, high, middle, middle, high, low]
            rhs = [high, middle, high, middle, low, high]
            update = lax.dot_general(
                jnp.concatenate([part[:, :size] for part in lhs], axis=0).astype(jnp.bfloat16),
                jnp.concatenate(rhs, axis=0).astype(jnp.bfloat16),
                (((0,), (0,)), ((), ())),
                preferred_element_type=jnp.float32,
            )
            work_ref[stop:, :] = work_ref[stop:, :] - update[stop:, :]


def transport_kernel(nodes_ref, columns_ref, speeds_ref, weights_ref, out_ref):
    groups, rows, rank = nodes_ref.shape
    bricks = out_ref.shape[0]
    factors = [jnp.broadcast_to(columns_ref[:, i : i + 1], (rows, rank)) for i in range(4)]
    sums = [jnp.zeros((rank, rank), jnp.float32) for _ in range(6)]
    vectors = jnp.zeros((8, rank), jnp.float32)
    for group in range(groups):
        nodes = nodes_ref[group]
        weighted = jnp.concatenate([nodes] + [nodes * factor for factor in factors], axis=1)
        high, low = two_parts(weighted)
        node_high, node_low = high[:, :rank], low[:, :rank]
        product = lax.dot_general(
            jnp.concatenate([node_high, node_high, node_low], axis=0),
            jnp.concatenate([high, low, high], axis=0),
            (((0,), (0,)), ((), ())),
            preferred_element_type=jnp.float32,
        )
        vectors = vectors + contract(weights_ref[group], nodes, 1, 0)
        plain = product[:, :rank]
        speed = jnp.broadcast_to(speeds_ref[group : group + 1, :], (rank, rank))
        sums[0] = sums[0] + jnp.maximum(speed, 0.0) * plain
        sums[1] = sums[1] + jnp.minimum(speed, 0.0) * plain
        for i in range(4):
            sums[2 + i] = sums[2 + i] + product[:, (i + 1) * rank : (i + 2) * rank]
    out_ref[:, :8, :] = jnp.broadcast_to((vectors * WEIGHT_V)[None], (bricks, 8, rank))
    height = rank // bricks
    for i in range(6):
        start = 8 + i * height
        out_ref[:, start : start + height, :] = (sums[i] * WEIGHT_V).reshape(
            bricks, height, rank
        )


def maxwell_kernel(
    brick_ref, cells_ref, integrals_ref, nodes_ref, first_ref, across_ref, part_ref, line_ref, state_ref
):
    bricks, cells, rank = cells_ref.shape
    groups, rows, _ = nodes_ref.shape
    total = bricks * cells
    brick = brick_ref[0]
    k_flat = jnp.concatenate([cells_ref[i ^ brick] for i in range(bricks)], axis=0)
    integrals = integrals_ref[0]
    for i in range(1, bricks):
        integrals = integrals + integrals_ref[i]
    height = integrals.shape[0] - 8
    part_ref[:, cells:, :] = jnp.broadcast_to(integrals[8:][None], (bricks, height, rank))
    moments = contract(integrals[:8], k_flat, 1, 1)
    density, drift, temper = cell_state([moments[i : i + 1] for i in range(5)])
    slope = -0.5 / temper
    amplitude = density * jnp.exp(-1.5 * jnp.log(2.0 * math.pi * temper))
    first = jnp.broadcast_to(first_ref[:, :1], (groups, total))
    line = amplitude * jnp.exp((first - drift[0]) ** 2 * slope)
    state = jnp.concatenate([drift[1], drift[2], slope] + [amplitude] * 5, axis=0)
    state_ref[...] = state
    both = jnp.concatenate([line, state], axis=0).T
    line_cols = both[:, :groups]
    line_ref[...] = line_cols
    distance = (across_ref[0:1, :] - both[:, groups : groups + 1]) ** 2
    distance = distance + (across_ref[1:2, :] - both[:, groups + 1 : groups + 2]) ** 2
    high, low = two_parts(jnp.exp(distance * both[:, groups + 2 : groups + 3]))
    lhs = jnp.concatenate([high, high, low], axis=1)
    result = jnp.zeros((total, rank), jnp.float32)
    for group in range(0, groups, 2):
        node_high, node_low = two_parts(
            jnp.concatenate([nodes_ref[group], nodes_ref[group + 1]], axis=1)
        )
        product = lax.dot_general(
            lhs,
            jnp.concatenate([node_high, node_low, node_high], axis=0),
            (((1,), (0,)), ((), ())),
            preferred_element_type=jnp.float32,
        )
        result = result + line_cols[:, group : group + 1] * product[:, :rank]
        result = result + line_cols[:, group + 1 : group + 2] * product[:, rank:]
    part_ref[:, :cells, :] = result.reshape(bricks, cells, rank)


def back_kernel(parts_ref, line_ref, state_ref, across_ref, out_ref):
    bricks, _, rank = parts_ref.shape
    groups, rows, _ = out_ref.shape
    total = line_ref.shape[0]
    cells = total // bricks
    advanced = parts_ref[:, :cells, :].reshape(total, rank)
    distance = (across_ref[:, 0:1] - state_ref[0:1, :]) ** 2
    distance = distance + (across_ref[:, 1:2] - state_ref[1:2, :]) ** 2
    high, low = two_parts(jnp.exp(distance * state_ref[2:3, :]))
    lhs = jnp.concatenate([high, high, low], axis=1)
    for group in range(0, groups, 2):
        scaled = [line_ref[:, i : i + 1] * advanced for i in (group, group + 1)]
        part_high, part_low = two_parts(jnp.concatenate(scaled, axis=1))
        product = lax.dot_general(
            lhs,
            jnp.concatenate([part_high, part_low, part_high], axis=0),
            (((1,), (0,)), ((), ())),
            preferred_element_type=jnp.float32,
        )
        out_ref[group] = product[:, :rank]
        out_ref[group + 1] = product[:, rank:]


def advance_kernel(parts_ref, steps_ref, cells_ref, payload_ref, advanced_ref, *, time_step):
    cells, rank = cells_ref.shape
    bricks = parts_ref.shape[0]
    height = rank // bricks
    maxwell_proj = parts_ref[0, :cells, :]
    for i in range(1, bricks):
        maxwell_proj = maxwell_proj + parts_ref[i, :cells, :]
    maxwell_proj = maxwell_proj * WEIGHT_V
    flux = jnp.zeros((cells, rank), jnp.float32)
    for i in range(6):
        block = parts_ref[:, cells + i * height : cells + (i + 1) * height, :].reshape(rank, rank)
        flux = flux + contract(steps_ref[i], block, 1, 0)
    own = cells_ref[...]
    advanced = own - time_step * flux + COLLIDE * (maxwell_proj - own)
    advanced_ref[...] = advanced
    payload_ref[:, :cells, :] = jnp.broadcast_to(advanced[None], (bricks, cells, rank))
    projected = contract(advanced, maxwell_proj, 0, 0)
    payload_ref[:, cells:, :] = projected.reshape(bricks, height, rank)


def middle_kernel(
    brick_ref,
    pieces_ref,
    transport_ref,
    basis_ref,
    back_ref,
    advanced_ref,
    speeds_ref,
    basis_x_ref,
    velocity_ref,
    gram_ref,
    work_ref,
    upper_ref,
    inverse_ref,
    *,
    lengths,
    time_step,
    weight_x,
):
    bricks, _, rank = pieces_ref.shape
    rows = basis_ref.shape[0]
    height = rank // bricks
    cells = advanced_ref.shape[0]
    masks = [j ^ brick_ref[0] for j in range(bricks)]
    slots = [((m >> 1) & 3) * 4 + (m & 1) * 2 + (m >> 3) for m in masks]

    def piece(ref, i):
        if ref is transport_ref:
            start = cells + i * height
            return ref[:, start : start + height, :].reshape(rank, rank)
        rows_of = [ref[slot, i * height : (i + 1) * height, :] for slot in slots]
        return jnp.concatenate(rows_of, axis=0)

    factor_into(piece(pieces_ref, 0) * weight_x, work_ref, upper_ref, inverse_ref)
    upper, inverse = upper_ref[...], inverse_ref[...]
    basis_x_ref[...] = contract(advanced_ref[...], inverse, 1, 1)
    change = jnp.zeros((rank, rank), jnp.float32)
    turned = []
    for i in range(3):
        shift = piece(pieces_ref, 1 + i) * weight_x
        straight = contract(inverse, shift, 1, 0)
        crossed = contract(inverse, shift, 1, 1)
        if i == 0:
            straight, crossed = crossed, straight
        turned.append(contract(straight, inverse, 1, 1))
        change = change + lengths[i] * (
            contract(upper - straight, piece(transport_ref, 2 * i), 1, 0)
            + contract(crossed - upper, piece(transport_ref, 2 * i + 1), 1, 0)
        )
    projected = contract(inverse, piece(pieces_ref, 4) * weight_x, 1, 0)
    middle = upper + time_step * change - COLLIDE * (projected - upper)
    now = contract(basis_ref[...], middle, 1, 1)
    drift_sum = jnp.zeros((rows, rank), jnp.float32)
    for i in range(3):
        speed = jnp.broadcast_to(speeds_ref[:, i : i + 1], (rows, rank)) * lengths[i]
        minus = contract(now, turned[i], 1, 1)
        plus = contract(now, turned[i], 1, 0)
        drift_sum = drift_sum + jnp.maximum(speed, 0.0) * (now - minus)
        drift_sum = drift_sum + jnp.minimum(speed, 0.0) * (plus - now)
    back = back_ref[0]
    for i in range(1, back_ref.shape[0]):
        back = back + back_ref[i]
    back_proj = contract(back * weight_x, inverse, 1, 1)
    updated = now - time_step * drift_sum + COLLIDE * (back_proj - now)
    velocity_ref[...] = updated
    gram_ref[...] = contract(updated, updated, 0, 0) * WEIGHT_V


def last_kernel(gram_ref, velocity_ref, coupling_ref, basis_ref, work_ref, upper_ref, inverse_ref):
    factor_into(gram_ref[...], work_ref, upper_ref, inverse_ref)
    coupling_ref[...] = upper_ref[...].T
    basis_ref[...] = contract(velocity_ref[...], inverse_ref[...], 1, 1)


def f32(*shape):
    return jax.ShapeDtypeStruct(shape, jnp.float32)


def factor_scratch(rank):
    shapes = ((rank, 2 * rank), (rank, rank), (rank, rank))
    return [pltpu.VMEM(shape, jnp.float32) for shape in shapes]


def local(k_coeffs, v_basis):
    cells_x, cells_y, cells_z, rank = k_coeffs.shape
    cells = cells_x * cells_y * cells_z
    slabs, bricks = lax.axis_size("slab"), lax.axis_size("brick")
    devices = slabs * bricks
    slab, brick = lax.axis_index("slab"), lax.axis_index("brick")
    lengths = (cells_x * slabs, cells_y * bricks, cells_z)
    time_step = CFL / (VMAX * sum(lengths))
    weight_x = 1.0 / (lengths[0] * lengths[1] * lengths[2])
    rows = v_basis.shape[0]
    slab_cells = cells * bricks
    half = slab_cells // cells_x
    height = rank // bricks
    up = [(i, (i + 1) % slabs) for i in range(slabs)]
    down = [(i, (i - 1) % slabs) for i in range(slabs)]
    own_cells = k_coeffs.reshape(cells, rank)

    own_ids = (slab * bricks + brick) * rows + jnp.arange(rows, dtype=jnp.int32)
    own_velocity = velocities(own_ids)
    ones = jnp.ones_like(own_velocity[0])
    slab_owner = jnp.arange(slabs, dtype=jnp.int32)[:, None] * bricks + brick
    slab_velocity = velocities(slab_owner * rows + jnp.arange(rows, dtype=jnp.int32)[None])
    weights = jnp.stack(
        [jnp.ones_like(slab_velocity[0]), slab_velocity[0], slab_velocity[1], slab_velocity[2]]
        + [jnp.sum(slab_velocity * slab_velocity, axis=0)]
        + [jnp.zeros_like(slab_velocity[0])] * 3,
        axis=1,
    )
    nodes = to_all(v_basis, "slab")
    k_slab = gather_relative(own_cells, "brick", BRICK_GROUPS)
    k_edges, k_slab = lax.optimization_barrier((k_coeffs, k_slab))
    k_below = lax.ppermute(k_edges[-1:], "slab", up)
    k_above = lax.ppermute(k_edges[:1], "slab", down)

    across = velocities(brick * rows + jnp.arange(rows, dtype=jnp.int32))
    columns = [f(across[i]) for i in (1, 2) for f in (lambda v: jnp.maximum(v, 0.0), lambda v: jnp.minimum(v, 0.0))]
    columns = jnp.stack(columns + [jnp.zeros_like(ones)] * 4, axis=1)
    owner = jnp.arange(slabs, dtype=jnp.int32) * bricks + brick
    first_velocity = velocities(owner * rows)[0]
    first_speeds = jnp.broadcast_to(first_velocity[:, None], (slabs, rank))
    transport_part = pl.pallas_call(
        transport_kernel, out_shape=f32(bricks, 8 + 6 * height, rank), name="transport", compiler_params=pltpu.CompilerParams(vmem_limit_bytes=VMEM_BYTES)
    )(nodes, columns, first_speeds, weights)
    integrals = exchange(transport_part, "brick")

    brick_id = brick.astype(jnp.int32)[None]
    vector_specs = [pl.BlockSpec(memory_space=pltpu.SMEM)]
    whole = pl.BlockSpec(memory_space=pltpu.VMEM)
    payload, line, state = pl.pallas_call(
        maxwell_kernel,
        out_shape=(
            f32(bricks, cells + 6 * height, rank),
            f32(slab_cells, slabs),
            f32(8, slab_cells),
        ),
        in_specs=vector_specs + [whole] * 5,
        name="maxwell", compiler_params=pltpu.CompilerParams(vmem_limit_bytes=VMEM_BYTES),
    )(brick_id, k_slab, integrals, nodes, first_speeds, across[1:])
    second = exchange(payload, "brick")

    slab_grid = k_slab.reshape(bricks, cells_x, cells_y, cells_z, rank)
    left = ((brick - 1) % bricks) ^ brick
    right = ((brick + 1) % bricks) ^ brick
    left = lax.dynamic_index_in_dim(slab_grid, left, 0, keepdims=False)
    right = lax.dynamic_index_in_dim(slab_grid, right, 0, keepdims=False)
    lower = [
        jnp.concatenate([k_below, k_coeffs[:-1]], axis=0),
        jnp.concatenate([left[:, -1:], k_coeffs[:, :-1]], axis=1),
        jnp.roll(k_coeffs, 1, axis=2),
    ]
    upper = [
        jnp.concatenate([k_coeffs[1:], k_above], axis=0),
        jnp.concatenate([k_coeffs[:, 1:], right[:, :1]], axis=1),
        jnp.roll(k_coeffs, -1, axis=2),
    ]
    steps = []
    for axis_id in range(3):
        steps.append(((k_coeffs - lower[axis_id]) * lengths[axis_id]).reshape(cells, rank))
        steps.append(((upper[axis_id] - k_coeffs) * lengths[axis_id]).reshape(cells, rank))
    payload, advanced = pl.pallas_call(
        functools.partial(advance_kernel, time_step=time_step),
        out_shape=(f32(bricks, cells + height, rank), f32(cells, rank)),
        name="advance", compiler_params=pltpu.CompilerParams(vmem_limit_bytes=VMEM_BYTES),
    )(second, jnp.stack(steps), own_cells)
    third = exchange(payload, "brick")

    slab_advanced = third[:, :cells]
    projected_rows = jnp.sum(third[:, cells:], axis=0)
    adv_grid = slab_advanced.reshape(bricks, cells_x, cells_y, cells_z, rank)
    planes_x = [adv_grid[:, i].reshape(half, rank) for i in range(cells_x)]
    choose = brick * height + jnp.arange(height, dtype=jnp.int32)
    choose = (choose[:, None] == jnp.arange(rank, dtype=jnp.int32)[None]).astype(jnp.float32)
    chosen = contract(choose, planes_x[-1], 1, 1)
    chosen_below = lax.ppermute(chosen, "slab", up)
    adv_grid = slab_advanced.reshape(bricks, cells_x, cells_y, cells_z, rank)
    planes_x = [adv_grid[:, i].reshape(half, rank) for i in range(cells_x)]
    before = jnp.concatenate([adv_grid[-1:, :, -1:], adv_grid[:-1, :, -1:]], axis=0)
    shift_y = jnp.concatenate([before, adv_grid[:, :, :-1]], axis=2).reshape(slab_cells, rank)
    shift_z = jnp.roll(adv_grid, 1, axis=3).reshape(slab_cells, rank)
    adv_flat = slab_advanced.reshape(slab_cells, rank)

    def own_rows(left_side, right_side):
        whole = contract(left_side, right_side, 0, 0)
        return lax.dynamic_slice_in_dim(whole, brick * height, height, 0)

    crossing = contract(chosen_below, planes_x[0], 1, 0)
    for i in range(1, cells_x):
        crossing = crossing + own_rows(planes_x[i - 1], planes_x[i])
    pieces = jnp.concatenate(
        [
            own_rows(adv_flat, adv_flat),
            crossing,
            own_rows(adv_flat, shift_y),
            own_rows(adv_flat, shift_z),
            projected_rows,
        ],
        axis=0,
    )
    pieces, third_after = lax.optimization_barrier((pieces, third))
    back = pl.pallas_call(back_kernel, out_shape=f32(slabs, rows, rank), name="back", compiler_params=pltpu.CompilerParams(vmem_limit_bytes=VMEM_BYTES))(
        third_after, line, state, across[1:].T
    )
    fourth = exchange(back, "slab")

    both = ("slab", "brick")
    lower_x, upper_x, cross_x = (from_peer(pieces, both, mask) for mask in (8, 16, 24))
    reduced = jnp.stack([pieces + upper_x, lower_x + cross_x])
    reduced = sum_over(reduced, both, ((32, 64, 96),))
    reduced = gather_more(reduced, both, ((1,), (2, 4, 6)))

    speeds = jnp.stack(list(own_velocity) + [jnp.zeros_like(ones)] * 5, axis=1)
    basis_new, velocity_new, gram_part = pl.pallas_call(
        functools.partial(
            middle_kernel, lengths=lengths, time_step=time_step, weight_x=weight_x
        ),
        out_shape=(f32(cells, rank), f32(rows, rank), f32(rank, rank)),
        in_specs=vector_specs + [whole] * 6,
        scratch_shapes=factor_scratch(rank),
        name="middle", compiler_params=pltpu.CompilerParams(vmem_limit_bytes=VMEM_BYTES),
    )(brick_id, reduced, second, v_basis, fourth, advanced, speeds)
    gram_v = sum_over(gram_part, ("slab", "brick"), ALL_GROUPS)
    coupling, vbasis_new = pl.pallas_call(
        last_kernel,
        out_shape=(f32(rank, rank), f32(rows, rank)),
        scratch_shapes=factor_scratch(rank),
        name="last", compiler_params=pltpu.CompilerParams(vmem_limit_bytes=VMEM_BYTES),
    )(gram_v, velocity_new)
    return (basis_new.reshape(cells_x, cells_y, cells_z, rank), coupling, vbasis_new)


def solution(mesh):
    placed = (P("slab", "brick", None, None), P(("slab", "brick"), None))
    return jax.shard_map(
        local,
        mesh=mesh,
        in_specs=placed,
        out_specs=(P("slab", "brick", None, None), P(), P(("slab", "brick"), None)),
        check_vma=False,
    )
```

```python
import functools
import math

import jax
import jax.numpy as jnp
from jax import lax
from jax.experimental import pallas as pl
from jax.experimental.pallas import tpu as pltpu
from jax.sharding import PartitionSpec as P

NVX = 32


CFL = 0.9
VMAX = 6.0
COLLIDE = 0.3
RHO_MIN = 0.25
TEMP_MIN = 0.25
PRECISE = lax.Precision.HIGHEST
FINE = lax.Precision.HIGH
SPACING = 2.0 * VMAX / NVX
WEIGHT_V = SPACING**3
PANEL = 16
VMEM_BYTES = 24 * 2**20


def contract(left, right, left_dim, right_dim, precision=PRECISE):
    return lax.dot_general(
        left, right, (((left_dim,), (right_dim,)), ((), ())), precision=precision
    )


def exchange(array, axis):
    return lax.all_to_all(array, axis, 0, 0, tiled=True)


def to_all(array, axis):
    copies = lax.axis_size(axis)
    return exchange(jnp.broadcast_to(array[None], (copies,) + array.shape), axis)


def velocities(indices):
    coords = jnp.stack([indices // (NVX * NVX), indices // NVX % NVX, indices % NVX])
    return -VMAX + (coords.astype(jnp.float32) + 0.5) * SPACING


def cell_state(moments):
    density = jnp.maximum(moments[0], RHO_MIN)
    drift = [moments[axis_id] / density for axis_id in (1, 2, 3)]
    square = drift[0] * drift[0] + drift[1] * drift[1] + drift[2] * drift[2]
    temper = jnp.maximum((moments[4] / density - square) / 3.0, TEMP_MIN)
    return density, drift, temper


def from_peer(values, axis, mask):
    axes = axis if isinstance(axis, tuple) else (axis,)
    peers = math.prod(lax.axis_size(name) for name in axes)
    return lax.ppermute(values, axis, [(i, i ^ mask) for i in range(peers)])


def sum_over(array, axis, groups):
    for masks in groups:
        parts = [array] + [from_peer(array, axis, mask) for mask in masks]
        array = sum_pairs(parts)
    return array


def sum_pairs(parts):
    if len(parts) == 1:
        return parts[0]
    half = len(parts) // 2
    return sum_pairs(parts[:half]) + sum_pairs(parts[half:])


def gather_relative(array, axis, groups):
    return gather_more(array[None], axis, groups)


def gather_more(array, axis, groups):
    for masks in groups:
        array = jnp.concatenate([array] + [from_peer(array, axis, mask) for mask in masks], axis=0)
    return array


BRICK_GROUPS = ((1,), (2, 4, 6), (8,))
ALL_GROUPS = ((1,), (2, 4, 6), (8, 16, 24), (32, 64, 96))


def three_parts(array):
    high = array.astype(jnp.bfloat16).astype(jnp.float32)
    rest = array - high
    middle = rest.astype(jnp.bfloat16).astype(jnp.float32)
    return high, middle, rest - middle


def two_parts(array):
    high = array.astype(jnp.bfloat16)
    return high, (array - high.astype(jnp.float32)).astype(jnp.bfloat16)


def factor_into(gram, work_ref, upper_ref, inverse_ref):
    size = gram.shape[0]
    rows = lax.broadcasted_iota(jnp.int32, (size, size), 0)
    cols = lax.broadcasted_iota(jnp.int32, (size, size), 1)
    work_ref[:, :size] = gram
    work_ref[:, size:] = jnp.where(rows == cols, 1.0, 0.0)
    panel_row = lax.broadcasted_iota(jnp.int32, (PANEL, size), 0)
    panel_col = lax.broadcasted_iota(jnp.int32, (PANEL, size), 1)
    for start in range(0, size, PANEL):
        stop = start + PANEL
        panel = work_ref[start:stop, :]
        spread = [
            jnp.broadcast_to(panel[:, start + t : start + t + 1], (PANEL, size))
            for t in range(PANEL)
        ]
        pivots = jnp.zeros((PANEL, size), jnp.float32)
        for t in range(PANEL):
            pivot = jnp.broadcast_to(spread[t][t : t + 1, :], (PANEL, size))
            pivots = jnp.where(panel_row == t, pivot, pivots)
            if t == PANEL - 1:
                break
            ratio = jnp.where(panel_row > t, spread[t] * (1.0 / pivot), 0.0)
            for u in range(t + 1, PANEL):
                spread[u] = spread[u] - ratio * jnp.broadcast_to(
                    spread[u][t : t + 1, :], (PANEL, size)
                )
            panel = panel - jnp.concatenate([ratio, ratio], axis=1) * jnp.broadcast_to(
                panel[t : t + 1, :], (PANEL, 2 * size)
            )
        scale = lax.rsqrt(pivots)
        panel = panel * jnp.concatenate([scale, scale], axis=1)
        left = jnp.where(panel_col >= panel_row + start, panel[:, :size], 0.0)
        right = panel[:, size:]
        upper_ref[start:stop, :] = left
        inverse_ref[start:stop, :] = right
        if stop < size:
            high, middle, low = three_parts(jnp.concatenate([left, right], axis=1))
            lhs = [high, high, middle, middle, high, low]
            rhs = [high, middle, high, middle, low, high]
            update = lax.dot_general(
                jnp.concatenate([part[:, :size] for part in lhs], axis=0).astype(jnp.bfloat16),
                jnp.concatenate(rhs, axis=0).astype(jnp.bfloat16),
                (((0,), (0,)), ((), ())),
                preferred_element_type=jnp.float32,
            )
            work_ref[stop:, :] = work_ref[stop:, :] - update[stop:, :]


def contract_three(left, right, left_dim, right_dim):
    left_high, left_low = two_parts(left)
    right_high, right_low = two_parts(right)
    dims = (((left_dim,), (right_dim,)), ((), ()))

    def product(one, other):
        return lax.dot_general(one, other, dims, preferred_element_type=jnp.float32)

    small = product(left_high, right_low) + product(left_low, right_high)
    return product(left_high, right_high) + small


def transport_kernel(nodes_ref, columns_ref, speeds_ref, weights_ref, out_ref):
    groups, rows, rank = nodes_ref.shape
    bricks = out_ref.shape[0]
    factors = [jnp.broadcast_to(columns_ref[:, i : i + 1], (rows, rank)) for i in range(4)]
    sums = [jnp.zeros((rank, rank), jnp.float32) for _ in range(6)]
    vectors = jnp.zeros((8, rank), jnp.float32)
    for group in range(groups):
        nodes = nodes_ref[group]
        weighted = jnp.concatenate([nodes] + [nodes * factor for factor in factors], axis=1)
        high, low = two_parts(weighted)
        node_high, node_low = high[:, :rank], low[:, :rank]
        product = lax.dot_general(
            jnp.concatenate([node_high, node_high, node_low], axis=0),
            jnp.concatenate([high, low, high], axis=0),
            (((0,), (0,)), ((), ())),
            preferred_element_type=jnp.float32,
        )
        vectors = vectors + contract(weights_ref[group], nodes, 1, 0)
        plain = product[:, :rank]
        speed = jnp.broadcast_to(speeds_ref[group : group + 1, :], (rank, rank))
        sums[0] = sums[0] + jnp.maximum(speed, 0.0) * plain
        sums[1] = sums[1] + jnp.minimum(speed, 0.0) * plain
        for i in range(4):
            sums[2 + i] = sums[2 + i] + product[:, (i + 1) * rank : (i + 2) * rank]
    out_ref[:, :8, :] = jnp.broadcast_to((vectors * WEIGHT_V)[None], (bricks, 8, rank))
    height = rank // bricks
    for i in range(6):
        start = 8 + i * height
        out_ref[:, start : start + height, :] = (sums[i] * WEIGHT_V).reshape(
            bricks, height, rank
        )


def maxwell_kernel(
    brick_ref, cells_ref, integrals_ref, nodes_ref, first_ref, across_ref, part_ref, line_ref, state_ref
):
    bricks, cells, rank = cells_ref.shape
    groups, rows, _ = nodes_ref.shape
    total = bricks * cells
    brick = brick_ref[0]
    k_flat = jnp.concatenate([cells_ref[i ^ brick] for i in range(bricks)], axis=0)
    integrals = integrals_ref[0]
    for i in range(1, bricks):
        integrals = integrals + integrals_ref[i]
    height = integrals.shape[0] - 8
    part_ref[:, cells:, :] = jnp.broadcast_to(integrals[8:][None], (bricks, height, rank))
    moments = contract(integrals[:8], k_flat, 1, 1)
    density, drift, temper = cell_state([moments[i : i + 1] for i in range(5)])
    slope = -0.5 / temper
    amplitude = density * jnp.exp(-1.5 * jnp.log(2.0 * math.pi * temper))
    first = jnp.broadcast_to(first_ref[:, :1], (groups, total))
    line = amplitude * jnp.exp((first - drift[0]) ** 2 * slope)
    state = jnp.concatenate([drift[1], drift[2], slope] + [amplitude] * 5, axis=0)
    state_ref[...] = state
    both = jnp.concatenate([line, state], axis=0).T
    line_cols = both[:, :groups]
    line_ref[...] = line_cols
    distance = (across_ref[0:1, :] - both[:, groups : groups + 1]) ** 2
    distance = distance + (across_ref[1:2, :] - both[:, groups + 1 : groups + 2]) ** 2
    high, low = two_parts(jnp.exp(distance * both[:, groups + 2 : groups + 3]))
    lhs = jnp.concatenate([high, high, low], axis=1)
    result = jnp.zeros((total, rank), jnp.float32)
    for group in range(0, groups, 2):
        node_high, node_low = two_parts(
            jnp.concatenate([nodes_ref[group], nodes_ref[group + 1]], axis=1)
        )
        product = lax.dot_general(
            lhs,
            jnp.concatenate([node_high, node_low, node_high], axis=0),
            (((1,), (0,)), ((), ())),
            preferred_element_type=jnp.float32,
        )
        result = result + line_cols[:, group : group + 1] * product[:, :rank]
        result = result + line_cols[:, group + 1 : group + 2] * product[:, rank:]
    part_ref[:, :cells, :] = result.reshape(bricks, cells, rank)


def products_kernel(
    brick_ref, parts_ref, pieces_ref, chosen_ref, work_ref, *, cells_x, cells_y, cells_z
):
    bricks, _, rank = parts_ref.shape
    height = rank // bricks
    cells = cells_x * cells_y * cells_z
    total = bricks * cells
    advanced = parts_ref[:, :cells, :].reshape(total, rank)
    last_plane = parts_ref[:, cells - cells // cells_x : cells, :].reshape(-1, rank)
    start = pl.multiple_of(brick_ref[0] * height, height)
    chosen_row = lax.broadcasted_iota(jnp.int32, (height, rank), 0) + start
    chosen_col = lax.broadcasted_iota(jnp.int32, (height, rank), 1)
    chosen_ref[...] = contract(jnp.where(chosen_row == chosen_col, 1.0, 0.0), last_plane, 1, 1)
    row = lax.broadcasted_iota(jnp.int32, (total, rank), 0)
    plane = cells_y * cells_z

    def shifted(amount):
        return pltpu.roll(advanced, amount % total, 0)

    along_x = jnp.where(row // plane % cells_x < cells_x - 1, shifted(-plane), 0.0)
    wrap = cells - (cells_y - 1) * cells_z
    along_y = jnp.where(row // cells_z % cells_y > 0, shifted(cells_z), shifted(wrap))
    along_z = jnp.where(row % cells_z > 0, shifted(1), shifted(1 - cells_z))
    left_high, left_low = two_parts(advanced)
    high, low = two_parts(jnp.concatenate([along_x, along_y, along_z], axis=1))
    work_ref[:, :rank] = contract(advanced, advanced, 0, 0)
    work_ref[:, rank:] = lax.dot_general(
        jnp.concatenate([left_high, left_high, left_low], axis=0),
        jnp.concatenate([high, low, high], axis=0),
        (((0,), (0,)), ((), ())),
        preferred_element_type=jnp.float32,
    )
    own = work_ref[pl.ds(start, height), :]
    for i in range(4):
        pieces_ref[i * height : (i + 1) * height, :] = own[:, i * rank : (i + 1) * rank]
    projected = parts_ref[0, cells:, :]
    for i in range(1, bricks):
        projected = projected + parts_ref[i, cells:, :]
    pieces_ref[4 * height :, :] = projected


def back_kernel(parts_ref, line_ref, state_ref, across_ref, out_ref):
    bricks, _, rank = parts_ref.shape
    groups, rows, _ = out_ref.shape
    total = line_ref.shape[0]
    cells = total // bricks
    advanced = parts_ref[:, :cells, :].reshape(total, rank)
    distance = (across_ref[:, 0:1] - state_ref[0:1, :]) ** 2
    distance = distance + (across_ref[:, 1:2] - state_ref[1:2, :]) ** 2
    high, low = two_parts(jnp.exp(distance * state_ref[2:3, :]))
    lhs = jnp.concatenate([high, high, low], axis=1)
    for group in range(0, groups, 2):
        scaled = [line_ref[:, i : i + 1] * advanced for i in (group, group + 1)]
        part_high, part_low = two_parts(jnp.concatenate(scaled, axis=1))
        product = lax.dot_general(
            lhs,
            jnp.concatenate([part_high, part_low, part_high], axis=0),
            (((1,), (0,)), ((), ())),
            preferred_element_type=jnp.float32,
        )
        out_ref[group] = product[:, :rank]
        out_ref[group + 1] = product[:, rank:]


def advance_kernel(parts_ref, steps_ref, cells_ref, payload_ref, advanced_ref, *, time_step):
    cells, rank = cells_ref.shape
    bricks = parts_ref.shape[0]
    height = rank // bricks
    maxwell_proj = parts_ref[0, :cells, :]
    for i in range(1, bricks):
        maxwell_proj = maxwell_proj + parts_ref[i, :cells, :]
    maxwell_proj = maxwell_proj * WEIGHT_V
    flux = jnp.zeros((cells, rank), jnp.float32)
    for i in range(6):
        block = parts_ref[:, cells + i * height : cells + (i + 1) * height, :].reshape(rank, rank)
        flux = flux + contract(steps_ref[i], block, 1, 0)
    own = cells_ref[...]
    advanced = own - time_step * flux + COLLIDE * (maxwell_proj - own)
    advanced_ref[...] = advanced
    payload_ref[:, :cells, :] = jnp.broadcast_to(advanced[None], (bricks, cells, rank))
    projected = contract(advanced, maxwell_proj, 0, 0)
    payload_ref[:, cells:, :] = projected.reshape(bricks, height, rank)


def middle_kernel(
    brick_ref,
    pieces_ref,
    transport_ref,
    basis_ref,
    back_ref,
    advanced_ref,
    speeds_ref,
    basis_x_ref,
    velocity_ref,
    gram_ref,
    work_ref,
    upper_ref,
    inverse_ref,
    *,
    lengths,
    time_step,
    weight_x,
):
    bricks, _, rank = pieces_ref.shape
    rows = basis_ref.shape[0]
    height = rank // bricks
    cells = advanced_ref.shape[0]
    masks = [j ^ brick_ref[0] for j in range(bricks)]
    slots = [((m >> 1) & 3) * 4 + (m & 1) * 2 + (m >> 3) for m in masks]

    def piece(ref, i):
        if ref is transport_ref:
            start = cells + i * height
            return ref[:, start : start + height, :].reshape(rank, rank)
        rows_of = [ref[slot, i * height : (i + 1) * height, :] for slot in slots]
        return jnp.concatenate(rows_of, axis=0)

    factor_into(piece(pieces_ref, 0) * weight_x, work_ref, upper_ref, inverse_ref)
    upper, inverse = upper_ref[...], inverse_ref[...]
    basis_x_ref[...] = contract(advanced_ref[...], inverse, 1, 1)
    change = jnp.zeros((rank, rank), jnp.float32)
    turned = []
    for i in range(3):
        shift = piece(pieces_ref, 1 + i) * weight_x
        straight = contract(inverse, shift, 1, 0)
        crossed = contract(inverse, shift, 1, 1)
        if i == 0:
            straight, crossed = crossed, straight
        turned.append(contract(straight, inverse, 1, 1))
        change = change + lengths[i] * (
            contract_three(upper - straight, piece(transport_ref, 2 * i), 1, 0)
            + contract_three(crossed - upper, piece(transport_ref, 2 * i + 1), 1, 0)
        )
    projected = contract(inverse, piece(pieces_ref, 4) * weight_x, 1, 0)
    middle = upper + time_step * change - COLLIDE * (projected - upper)
    now = contract(basis_ref[...], middle, 1, 1)
    drift_sum = jnp.zeros((rows, rank), jnp.float32)
    for i in range(3):
        speed = jnp.broadcast_to(speeds_ref[:, i : i + 1], (rows, rank)) * lengths[i]
        minus = contract_three(now, turned[i], 1, 1)
        plus = contract_three(now, turned[i], 1, 0)
        drift_sum = drift_sum + jnp.maximum(speed, 0.0) * (now - minus)
        drift_sum = drift_sum + jnp.minimum(speed, 0.0) * (plus - now)
    back = back_ref[0]
    for i in range(1, back_ref.shape[0]):
        back = back + back_ref[i]
    back_proj = contract(back * weight_x, inverse, 1, 1)
    updated = now - time_step * drift_sum + COLLIDE * (back_proj - now)
    velocity_ref[...] = updated
    gram_ref[...] = contract(updated, updated, 0, 0) * WEIGHT_V


def last_kernel(gram_ref, velocity_ref, coupling_ref, basis_ref, work_ref, upper_ref, inverse_ref):
    factor_into(gram_ref[...], work_ref, upper_ref, inverse_ref)
    coupling_ref[...] = upper_ref[...].T
    basis_ref[...] = contract(velocity_ref[...], inverse_ref[...], 1, 1)


def f32(*shape):
    return jax.ShapeDtypeStruct(shape, jnp.float32)


def factor_scratch(rank):
    shapes = ((rank, 2 * rank), (rank, rank), (rank, rank))
    return [pltpu.VMEM(shape, jnp.float32) for shape in shapes]


def local(k_coeffs, v_basis):
    cells_x, cells_y, cells_z, rank = k_coeffs.shape
    cells = cells_x * cells_y * cells_z
    slabs, bricks = lax.axis_size("slab"), lax.axis_size("brick")
    devices = slabs * bricks
    slab, brick = lax.axis_index("slab"), lax.axis_index("brick")
    lengths = (cells_x * slabs, cells_y * bricks, cells_z)
    time_step = CFL / (VMAX * sum(lengths))
    weight_x = 1.0 / (lengths[0] * lengths[1] * lengths[2])
    rows = v_basis.shape[0]
    slab_cells = cells * bricks
    half = slab_cells // cells_x
    height = rank // bricks
    up = [(i, (i + 1) % slabs) for i in range(slabs)]
    down = [(i, (i - 1) % slabs) for i in range(slabs)]
    own_cells = k_coeffs.reshape(cells, rank)

    own_ids = (slab * bricks + brick) * rows + jnp.arange(rows, dtype=jnp.int32)
    own_velocity = velocities(own_ids)
    ones = jnp.ones_like(own_velocity[0])
    slab_owner = jnp.arange(slabs, dtype=jnp.int32)[:, None] * bricks + brick
    slab_velocity = velocities(slab_owner * rows + jnp.arange(rows, dtype=jnp.int32)[None])
    weights = jnp.stack(
        [jnp.ones_like(slab_velocity[0]), slab_velocity[0], slab_velocity[1], slab_velocity[2]]
        + [jnp.sum(slab_velocity * slab_velocity, axis=0)]
        + [jnp.zeros_like(slab_velocity[0])] * 3,
        axis=1,
    )
    nodes = to_all(v_basis, "slab")
    k_slab = gather_relative(own_cells, "brick", BRICK_GROUPS)
    k_edges, k_slab = lax.optimization_barrier((k_coeffs, k_slab))
    k_below = lax.ppermute(k_edges[-1:], "slab", up)
    k_above = lax.ppermute(k_edges[:1], "slab", down)

    across = velocities(brick * rows + jnp.arange(rows, dtype=jnp.int32))
    columns = [f(across[i]) for i in (1, 2) for f in (lambda v: jnp.maximum(v, 0.0), lambda v: jnp.minimum(v, 0.0))]
    columns = jnp.stack(columns + [jnp.zeros_like(ones)] * 4, axis=1)
    owner = jnp.arange(slabs, dtype=jnp.int32) * bricks + brick
    first_velocity = velocities(owner * rows)[0]
    first_speeds = jnp.broadcast_to(first_velocity[:, None], (slabs, rank))
    transport_part = pl.pallas_call(
        transport_kernel, out_shape=f32(bricks, 8 + 6 * height, rank), name="transport", compiler_params=pltpu.CompilerParams(vmem_limit_bytes=VMEM_BYTES)
    )(nodes, columns, first_speeds, weights)
    integrals = exchange(transport_part, "brick")

    brick_id = brick.astype(jnp.int32)[None]
    vector_specs = [pl.BlockSpec(memory_space=pltpu.SMEM)]
    whole = pl.BlockSpec(memory_space=pltpu.VMEM)
    payload, line, state = pl.pallas_call(
        maxwell_kernel,
        out_shape=(
            f32(bricks, cells + 6 * height, rank),
            f32(slab_cells, slabs),
            f32(8, slab_cells),
        ),
        in_specs=vector_specs + [whole] * 5,
        name="maxwell", compiler_params=pltpu.CompilerParams(vmem_limit_bytes=VMEM_BYTES),
    )(brick_id, k_slab, integrals, nodes, first_speeds, across[1:])
    second = exchange(payload, "brick")

    slab_grid = k_slab.reshape(bricks, cells_x, cells_y, cells_z, rank)
    left = ((brick - 1) % bricks) ^ brick
    right = ((brick + 1) % bricks) ^ brick
    left = lax.dynamic_index_in_dim(slab_grid, left, 0, keepdims=False)
    right = lax.dynamic_index_in_dim(slab_grid, right, 0, keepdims=False)
    lower = [
        jnp.concatenate([k_below, k_coeffs[:-1]], axis=0),
        jnp.concatenate([left[:, -1:], k_coeffs[:, :-1]], axis=1),
        jnp.roll(k_coeffs, 1, axis=2),
    ]
    upper = [
        jnp.concatenate([k_coeffs[1:], k_above], axis=0),
        jnp.concatenate([k_coeffs[:, 1:], right[:, :1]], axis=1),
        jnp.roll(k_coeffs, -1, axis=2),
    ]
    steps = []
    for axis_id in range(3):
        steps.append(((k_coeffs - lower[axis_id]) * lengths[axis_id]).reshape(cells, rank))
        steps.append(((upper[axis_id] - k_coeffs) * lengths[axis_id]).reshape(cells, rank))
    payload, advanced = pl.pallas_call(
        functools.partial(advance_kernel, time_step=time_step),
        out_shape=(f32(bricks, cells + height, rank), f32(cells, rank)),
        name="advance", compiler_params=pltpu.CompilerParams(vmem_limit_bytes=VMEM_BYTES),
    )(second, jnp.stack(steps), own_cells)
    third = exchange(payload, "brick")

    pieces, chosen = pl.pallas_call(
        functools.partial(products_kernel, cells_x=cells_x, cells_y=cells_y, cells_z=cells_z),
        out_shape=(f32(5 * height, rank), f32(height, half)),
        in_specs=vector_specs + [whole],
        scratch_shapes=[pltpu.VMEM((rank, 4 * rank), jnp.float32)],
        name="products",
        compiler_params=pltpu.CompilerParams(vmem_limit_bytes=VMEM_BYTES),
    )(brick_id, third)
    chosen, third_after = lax.optimization_barrier((chosen, third))
    chosen_below = lax.ppermute(chosen, "slab", up)
    first_plane = third[:, : cells // cells_x].reshape(half, rank)

    back = pl.pallas_call(back_kernel, out_shape=f32(slabs, rows, rank), name="back", compiler_params=pltpu.CompilerParams(vmem_limit_bytes=VMEM_BYTES))(
        third_after, line, state, across[1:].T
    )

    pieces = pieces + jnp.pad(
        contract(chosen_below, first_plane, 1, 0), ((height, 3 * height), (0, 0))
    )
    pieces, back = lax.optimization_barrier((pieces, back))
    fourth = exchange(back, "slab")
    both = ("slab", "brick")
    lower_x, upper_x, cross_x = (from_peer(pieces, both, mask) for mask in (8, 16, 24))
    reduced = jnp.stack([pieces + upper_x, lower_x + cross_x])
    reduced = sum_over(reduced, both, ((32, 64, 96),))
    reduced = gather_more(reduced, both, ((1,), (2, 4, 6)))

    speeds = jnp.stack(list(own_velocity) + [jnp.zeros_like(ones)] * 5, axis=1)
    basis_new, velocity_new, gram_part = pl.pallas_call(
        functools.partial(
            middle_kernel, lengths=lengths, time_step=time_step, weight_x=weight_x
        ),
        out_shape=(f32(cells, rank), f32(rows, rank), f32(rank, rank)),
        in_specs=vector_specs + [whole] * 6,
        scratch_shapes=factor_scratch(rank),
        name="middle", compiler_params=pltpu.CompilerParams(vmem_limit_bytes=VMEM_BYTES),
    )(brick_id, reduced, second, v_basis, fourth, advanced, speeds)
    gram_v = sum_over(gram_part, ("slab", "brick"), ALL_GROUPS)
    coupling, vbasis_new = pl.pallas_call(
        last_kernel,
        out_shape=(f32(rank, rank), f32(rows, rank)),
        scratch_shapes=factor_scratch(rank),
        name="last", compiler_params=pltpu.CompilerParams(vmem_limit_bytes=VMEM_BYTES),
    )(gram_v, velocity_new)
    return (basis_new.reshape(cells_x, cells_y, cells_z, rank), coupling, vbasis_new)


def solution(mesh):
    placed = (P("slab", "brick", None, None), P(("slab", "brick"), None))
    return jax.shard_map(
        local,
        mesh=mesh,
        in_specs=placed,
        out_specs=(P("slab", "brick", None, None), P(), P(("slab", "brick"), None)),
        check_vma=False,
    )
```

```python
import functools
import math

import jax
import jax.numpy as jnp
from jax import lax
from jax.experimental import pallas as pl
from jax.experimental.pallas import tpu as pltpu
from jax.sharding import PartitionSpec as P

NVX = 32


CFL = 0.9
VMAX = 6.0
COLLIDE = 0.3
RHO_MIN = 0.25
TEMP_MIN = 0.25
PRECISE = lax.Precision.HIGHEST
FINE = lax.Precision.HIGH
SPACING = 2.0 * VMAX / NVX
WEIGHT_V = SPACING**3
PANEL = 16
VMEM_BYTES = 24 * 2**20


def contract(left, right, left_dim, right_dim, precision=PRECISE):
    return lax.dot_general(
        left, right, (((left_dim,), (right_dim,)), ((), ())), precision=precision
    )


def exchange(array, axis):
    return lax.all_to_all(array, axis, 0, 0, tiled=True)


def to_all(array, axis):
    copies = lax.axis_size(axis)
    return exchange(jnp.broadcast_to(array[None], (copies,) + array.shape), axis)


def velocities(indices):
    coords = jnp.stack([indices // (NVX * NVX), indices // NVX % NVX, indices % NVX])
    return -VMAX + (coords.astype(jnp.float32) + 0.5) * SPACING


def cell_state(moments):
    density = jnp.maximum(moments[0], RHO_MIN)
    drift = [moments[axis_id] / density for axis_id in (1, 2, 3)]
    square = drift[0] * drift[0] + drift[1] * drift[1] + drift[2] * drift[2]
    temper = jnp.maximum((moments[4] / density - square) / 3.0, TEMP_MIN)
    return density, drift, temper


def from_peer(values, axis, mask):
    axes = axis if isinstance(axis, tuple) else (axis,)
    peers = math.prod(lax.axis_size(name) for name in axes)
    return lax.ppermute(values, axis, [(i, i ^ mask) for i in range(peers)])


def sum_over(array, axis, groups):
    for masks in groups:
        parts = [array] + [from_peer(array, axis, mask) for mask in masks]
        array = sum_pairs(parts)
    return array


def sum_pairs(parts):
    if len(parts) == 1:
        return parts[0]
    half = len(parts) // 2
    return sum_pairs(parts[:half]) + sum_pairs(parts[half:])


def gather_relative(array, axis, groups):
    return gather_more(array[None], axis, groups)


def gather_more(array, axis, groups):
    for masks in groups:
        array = jnp.concatenate([array] + [from_peer(array, axis, mask) for mask in masks], axis=0)
    return array


BRICK_GROUPS = ((1,), (2, 4, 6), (8,))
ALL_GROUPS = ((1,), (2, 4, 6), (8, 16, 24), (32, 64, 96))


def three_parts(array):
    high = array.astype(jnp.bfloat16).astype(jnp.float32)
    rest = array - high
    middle = rest.astype(jnp.bfloat16).astype(jnp.float32)
    return high, middle, rest - middle


def two_parts(array):
    high = array.astype(jnp.bfloat16)
    return high, (array - high.astype(jnp.float32)).astype(jnp.bfloat16)


def factor_into(gram, work_ref, upper_ref, inverse_ref):
    size = gram.shape[0]
    rows = lax.broadcasted_iota(jnp.int32, (size, size), 0)
    cols = lax.broadcasted_iota(jnp.int32, (size, size), 1)
    work_ref[:, :size] = gram
    work_ref[:, size:] = jnp.where(rows == cols, 1.0, 0.0)
    panel_row = lax.broadcasted_iota(jnp.int32, (PANEL, size), 0)
    panel_col = lax.broadcasted_iota(jnp.int32, (PANEL, size), 1)
    for start in range(0, size, PANEL):
        stop = start + PANEL
        panel = work_ref[start:stop, :]
        spread = [
            jnp.broadcast_to(panel[:, start + t : start + t + 1], (PANEL, size))
            for t in range(PANEL)
        ]
        pivots = jnp.zeros((PANEL, size), jnp.float32)
        for t in range(PANEL):
            pivot = jnp.broadcast_to(spread[t][t : t + 1, :], (PANEL, size))
            pivots = jnp.where(panel_row == t, pivot, pivots)
            if t == PANEL - 1:
                break
            ratio = jnp.where(panel_row > t, spread[t] * (1.0 / pivot), 0.0)
            for u in range(t + 1, PANEL):
                spread[u] = spread[u] - ratio * jnp.broadcast_to(
                    spread[u][t : t + 1, :], (PANEL, size)
                )
            panel = panel - jnp.concatenate([ratio, ratio], axis=1) * jnp.broadcast_to(
                panel[t : t + 1, :], (PANEL, 2 * size)
            )
        scale = lax.rsqrt(pivots)
        panel = panel * jnp.concatenate([scale, scale], axis=1)
        left = jnp.where(panel_col >= panel_row + start, panel[:, :size], 0.0)
        right = panel[:, size:]
        upper_ref[start:stop, :] = left
        inverse_ref[start:stop, :] = right
        if stop < size:
            high, middle, low = three_parts(jnp.concatenate([left, right], axis=1))
            lhs = [high, high, middle, middle, high, low]
            rhs = [high, middle, high, middle, low, high]
            update = lax.dot_general(
                jnp.concatenate([part[:, :size] for part in lhs], axis=0).astype(jnp.bfloat16),
                jnp.concatenate(rhs, axis=0).astype(jnp.bfloat16),
                (((0,), (0,)), ((), ())),
                preferred_element_type=jnp.float32,
            )
            work_ref[stop:, :] = work_ref[stop:, :] - update[stop:, :]


def contract_three(left, right, left_dim, right_dim):
    left_high, left_low = two_parts(left)
    right_high, right_low = two_parts(right)
    dims = (((left_dim,), (right_dim,)), ((), ()))

    def product(one, other):
        return lax.dot_general(one, other, dims, preferred_element_type=jnp.float32)

    small = product(left_high, right_low) + product(left_low, right_high)
    return product(left_high, right_high) + small


def repeat_kernel(source_ref, out_ref, sems):
    copies = [
        pltpu.make_async_copy(source_ref, out_ref.at[i], sems.at[i])
        for i in range(out_ref.shape[0])
    ]
    for copy in copies:
        copy.start()
    for copy in copies:
        copy.wait()


def transport_kernel(nodes_ref, columns_ref, speeds_ref, weights_ref, out_ref):
    groups, rows, rank = nodes_ref.shape
    bricks = out_ref.shape[0]
    factors = [jnp.broadcast_to(columns_ref[:, i : i + 1], (rows, rank)) for i in range(4)]
    sums = [jnp.zeros((rank, rank), jnp.float32) for _ in range(6)]
    vectors = jnp.zeros((8, rank), jnp.float32)
    for group in range(groups):
        nodes = nodes_ref[group]
        weighted = jnp.concatenate([nodes] + [nodes * factor for factor in factors], axis=1)
        high, low = two_parts(weighted)
        node_high, node_low = high[:, :rank], low[:, :rank]
        product = lax.dot_general(
            jnp.concatenate([node_high, node_high, node_low], axis=0),
            jnp.concatenate([high, low, high], axis=0),
            (((0,), (0,)), ((), ())),
            preferred_element_type=jnp.float32,
        )
        vectors = vectors + contract(weights_ref[group], nodes, 1, 0)
        plain = product[:, :rank]
        speed = jnp.broadcast_to(speeds_ref[group : group + 1, :], (rank, rank))
        sums[0] = sums[0] + jnp.maximum(speed, 0.0) * plain
        sums[1] = sums[1] + jnp.minimum(speed, 0.0) * plain
        for i in range(4):
            sums[2 + i] = sums[2 + i] + product[:, (i + 1) * rank : (i + 2) * rank]
    out_ref[:, :8, :] = jnp.broadcast_to((vectors * WEIGHT_V)[None], (bricks, 8, rank))
    height = rank // bricks
    for i in range(6):
        start = 8 + i * height
        out_ref[:, start : start + height, :] = (sums[i] * WEIGHT_V).reshape(
            bricks, height, rank
        )


def maxwell_kernel(
    brick_ref, cells_ref, integrals_ref, nodes_ref, first_ref, across_ref, part_ref, line_ref, state_ref
):
    bricks, cells, rank = cells_ref.shape
    groups, rows, _ = nodes_ref.shape
    total = bricks * cells
    brick = brick_ref[0]
    k_flat = jnp.concatenate([cells_ref[i ^ brick] for i in range(bricks)], axis=0)
    integrals = integrals_ref[0]
    for i in range(1, bricks):
        integrals = integrals + integrals_ref[i]
    height = integrals.shape[0] - 8
    part_ref[:, cells:, :] = jnp.broadcast_to(integrals[8:][None], (bricks, height, rank))
    moments = contract(integrals[:8], k_flat, 1, 1)
    density, drift, temper = cell_state([moments[i : i + 1] for i in range(5)])
    slope = -0.5 / temper
    amplitude = density * jnp.exp(-1.5 * jnp.log(2.0 * math.pi * temper))
    first = jnp.broadcast_to(first_ref[:, :1], (groups, total))
    line = amplitude * jnp.exp((first - drift[0]) ** 2 * slope)
    state = jnp.concatenate([drift[1], drift[2], slope] + [amplitude] * 5, axis=0)
    state_ref[...] = state
    both = jnp.concatenate([line, state], axis=0).T
    line_cols = both[:, :groups]
    line_ref[...] = line_cols
    distance = (across_ref[0:1, :] - both[:, groups : groups + 1]) ** 2
    distance = distance + (across_ref[1:2, :] - both[:, groups + 1 : groups + 2]) ** 2
    high, low = two_parts(jnp.exp(distance * both[:, groups + 2 : groups + 3]))
    lhs = jnp.concatenate([high, high, low], axis=1)
    result = jnp.zeros((total, rank), jnp.float32)
    for group in range(0, groups, 2):
        node_high, node_low = two_parts(
            jnp.concatenate([nodes_ref[group], nodes_ref[group + 1]], axis=1)
        )
        product = lax.dot_general(
            lhs,
            jnp.concatenate([node_high, node_low, node_high], axis=0),
            (((1,), (0,)), ((), ())),
            preferred_element_type=jnp.float32,
        )
        result = result + line_cols[:, group : group + 1] * product[:, :rank]
        result = result + line_cols[:, group + 1 : group + 2] * product[:, rank:]
    part_ref[:, :cells, :] = result.reshape(bricks, cells, rank)


def products_kernel(
    brick_ref, parts_ref, pieces_ref, chosen_ref, work_ref, *, cells_x, cells_y, cells_z
):
    bricks, _, rank = parts_ref.shape
    height = rank // bricks
    cells = cells_x * cells_y * cells_z
    total = bricks * cells
    advanced = parts_ref[:, :cells, :].reshape(total, rank)
    last_plane = parts_ref[:, cells - cells // cells_x : cells, :].reshape(-1, rank)
    start = pl.multiple_of(brick_ref[0] * height, height)
    chosen_row = lax.broadcasted_iota(jnp.int32, (height, rank), 0) + start
    chosen_col = lax.broadcasted_iota(jnp.int32, (height, rank), 1)
    chosen_ref[...] = contract(jnp.where(chosen_row == chosen_col, 1.0, 0.0), last_plane, 1, 1)
    row = lax.broadcasted_iota(jnp.int32, (total, rank), 0)
    plane = cells_y * cells_z

    def shifted(amount):
        return pltpu.roll(advanced, amount % total, 0)

    along_x = jnp.where(row // plane % cells_x < cells_x - 1, shifted(-plane), 0.0)
    wrap = cells - (cells_y - 1) * cells_z
    along_y = jnp.where(row // cells_z % cells_y > 0, shifted(cells_z), shifted(wrap))
    along_z = jnp.where(row % cells_z > 0, shifted(1), shifted(1 - cells_z))
    left_high, left_low = two_parts(advanced)
    high, low = two_parts(jnp.concatenate([along_x, along_y, along_z], axis=1))
    work_ref[:, :rank] = contract(advanced, advanced, 0, 0)
    work_ref[:, rank:] = lax.dot_general(
        jnp.concatenate([left_high, left_high, left_low], axis=0),
        jnp.concatenate([high, low, high], axis=0),
        (((0,), (0,)), ((), ())),
        preferred_element_type=jnp.float32,
    )
    own = work_ref[pl.ds(start, height), :]
    for i in range(4):
        pieces_ref[i * height : (i + 1) * height, :] = own[:, i * rank : (i + 1) * rank]
    projected = parts_ref[0, cells:, :]
    for i in range(1, bricks):
        projected = projected + parts_ref[i, cells:, :]
    pieces_ref[4 * height :, :] = projected


def back_kernel(parts_ref, line_ref, state_ref, across_ref, out_ref):
    bricks, _, rank = parts_ref.shape
    groups, rows, _ = out_ref.shape
    total = line_ref.shape[0]
    cells = total // bricks
    advanced = parts_ref[:, :cells, :].reshape(total, rank)
    distance = (across_ref[:, 0:1] - state_ref[0:1, :]) ** 2
    distance = distance + (across_ref[:, 1:2] - state_ref[1:2, :]) ** 2
    high, low = two_parts(jnp.exp(distance * state_ref[2:3, :]))
    lhs = jnp.concatenate([high, high, low], axis=1)
    for group in range(0, groups, 2):
        scaled = [line_ref[:, i : i + 1] * advanced for i in (group, group + 1)]
        part_high, part_low = two_parts(jnp.concatenate(scaled, axis=1))
        product = lax.dot_general(
            lhs,
            jnp.concatenate([part_high, part_low, part_high], axis=0),
            (((1,), (0,)), ((), ())),
            preferred_element_type=jnp.float32,
        )
        out_ref[group] = product[:, :rank]
        out_ref[group + 1] = product[:, rank:]


def advance_kernel(parts_ref, steps_ref, cells_ref, payload_ref, advanced_ref, *, time_step):
    cells, rank = cells_ref.shape
    bricks = parts_ref.shape[0]
    height = rank // bricks
    maxwell_proj = parts_ref[0, :cells, :]
    for i in range(1, bricks):
        maxwell_proj = maxwell_proj + parts_ref[i, :cells, :]
    maxwell_proj = maxwell_proj * WEIGHT_V
    flux = jnp.zeros((cells, rank), jnp.float32)
    for i in range(6):
        block = parts_ref[:, cells + i * height : cells + (i + 1) * height, :].reshape(rank, rank)
        flux = flux + contract(steps_ref[i], block, 1, 0)
    own = cells_ref[...]
    advanced = own - time_step * flux + COLLIDE * (maxwell_proj - own)
    advanced_ref[...] = advanced
    payload_ref[:, :cells, :] = jnp.broadcast_to(advanced[None], (bricks, cells, rank))
    projected = contract(advanced, maxwell_proj, 0, 0)
    payload_ref[:, cells:, :] = projected.reshape(bricks, height, rank)


def middle_kernel(
    brick_ref,
    pieces_ref,
    transport_ref,
    basis_ref,
    back_ref,
    advanced_ref,
    speeds_ref,
    basis_x_ref,
    velocity_ref,
    gram_ref,
    work_ref,
    upper_ref,
    inverse_ref,
    *,
    lengths,
    time_step,
    weight_x,
):
    bricks, _, rank = pieces_ref.shape
    rows = basis_ref.shape[0]
    height = rank // bricks
    cells = advanced_ref.shape[0]
    masks = [j ^ brick_ref[0] for j in range(bricks)]
    slots = [((m >> 1) & 3) * 4 + (m & 1) * 2 + (m >> 3) for m in masks]

    def piece(ref, i):
        if ref is transport_ref:
            start = cells + i * height
            return ref[:, start : start + height, :].reshape(rank, rank)
        rows_of = [ref[slot, i * height : (i + 1) * height, :] for slot in slots]
        return jnp.concatenate(rows_of, axis=0)

    factor_into(piece(pieces_ref, 0) * weight_x, work_ref, upper_ref, inverse_ref)
    upper, inverse = upper_ref[...], inverse_ref[...]
    basis_x_ref[...] = contract(advanced_ref[...], inverse, 1, 1)
    change = jnp.zeros((rank, rank), jnp.float32)
    turned = []
    for i in range(3):
        shift = piece(pieces_ref, 1 + i) * weight_x
        straight = contract(inverse, shift, 1, 0)
        crossed = contract(inverse, shift, 1, 1)
        if i == 0:
            straight, crossed = crossed, straight
        turned.append(contract(straight, inverse, 1, 1))
        change = change + lengths[i] * (
            contract_three(upper - straight, piece(transport_ref, 2 * i), 1, 0)
            + contract_three(crossed - upper, piece(transport_ref, 2 * i + 1), 1, 0)
        )
    projected = contract(inverse, piece(pieces_ref, 4) * weight_x, 1, 0)
    middle = upper + time_step * change - COLLIDE * (projected - upper)
    now = contract(basis_ref[...], middle, 1, 1)
    drift_sum = jnp.zeros((rows, rank), jnp.float32)
    for i in range(3):
        speed = jnp.broadcast_to(speeds_ref[:, i : i + 1], (rows, rank)) * lengths[i]
        minus = contract_three(now, turned[i], 1, 1)
        plus = contract_three(now, turned[i], 1, 0)
        drift_sum = drift_sum + jnp.maximum(speed, 0.0) * (now - minus)
        drift_sum = drift_sum + jnp.minimum(speed, 0.0) * (plus - now)
    back = back_ref[0]
    for i in range(1, back_ref.shape[0]):
        back = back + back_ref[i]
    back_proj = contract(back * weight_x, inverse, 1, 1)
    updated = now - time_step * drift_sum + COLLIDE * (back_proj - now)
    velocity_ref[...] = updated
    gram_ref[...] = contract(updated, updated, 0, 0) * WEIGHT_V


def last_kernel(gram_ref, velocity_ref, coupling_ref, basis_ref, work_ref, upper_ref, inverse_ref):
    factor_into(gram_ref[...], work_ref, upper_ref, inverse_ref)
    coupling_ref[...] = upper_ref[...].T
    basis_ref[...] = contract(velocity_ref[...], inverse_ref[...], 1, 1)


def f32(*shape):
    return jax.ShapeDtypeStruct(shape, jnp.float32)


def factor_scratch(rank):
    shapes = ((rank, 2 * rank), (rank, rank), (rank, rank))
    return [pltpu.VMEM(shape, jnp.float32) for shape in shapes]


def local(k_coeffs, v_basis):
    cells_x, cells_y, cells_z, rank = k_coeffs.shape
    cells = cells_x * cells_y * cells_z
    slabs, bricks = lax.axis_size("slab"), lax.axis_size("brick")
    devices = slabs * bricks
    slab, brick = lax.axis_index("slab"), lax.axis_index("brick")
    lengths = (cells_x * slabs, cells_y * bricks, cells_z)
    time_step = CFL / (VMAX * sum(lengths))
    weight_x = 1.0 / (lengths[0] * lengths[1] * lengths[2])
    rows = v_basis.shape[0]
    slab_cells = cells * bricks
    half = slab_cells // cells_x
    height = rank // bricks
    up = [(i, (i + 1) % slabs) for i in range(slabs)]
    down = [(i, (i - 1) % slabs) for i in range(slabs)]
    own_cells = k_coeffs.reshape(cells, rank)

    own_ids = (slab * bricks + brick) * rows + jnp.arange(rows, dtype=jnp.int32)
    own_velocity = velocities(own_ids)
    ones = jnp.ones_like(own_velocity[0])
    slab_owner = jnp.arange(slabs, dtype=jnp.int32)[:, None] * bricks + brick
    slab_velocity = velocities(slab_owner * rows + jnp.arange(rows, dtype=jnp.int32)[None])
    weights = jnp.stack(
        [jnp.ones_like(slab_velocity[0]), slab_velocity[0], slab_velocity[1], slab_velocity[2]]
        + [jnp.sum(slab_velocity * slab_velocity, axis=0)]
        + [jnp.zeros_like(slab_velocity[0])] * 3,
        axis=1,
    )
    nodes = exchange(
        pl.pallas_call(
            repeat_kernel,
            out_shape=f32(slabs, rows, rank),
            in_specs=[pl.BlockSpec(memory_space=pl.ANY)],
            out_specs=pl.BlockSpec(memory_space=pl.ANY),
            scratch_shapes=[pltpu.SemaphoreType.DMA((slabs,))],
            name="repeat",
        )(v_basis),
        "slab",
    )
    k_slab = gather_relative(own_cells, "brick", BRICK_GROUPS)
    k_edges, k_slab = lax.optimization_barrier((k_coeffs, k_slab))
    k_below = lax.ppermute(k_edges[-1:], "slab", up)
    k_above = lax.ppermute(k_edges[:1], "slab", down)

    across = velocities(brick * rows + jnp.arange(rows, dtype=jnp.int32))
    columns = [f(across[i]) for i in (1, 2) for f in (lambda v: jnp.maximum(v, 0.0), lambda v: jnp.minimum(v, 0.0))]
    columns = jnp.stack(columns + [jnp.zeros_like(ones)] * 4, axis=1)
    owner = jnp.arange(slabs, dtype=jnp.int32) * bricks + brick
    first_velocity = velocities(owner * rows)[0]
    first_speeds = jnp.broadcast_to(first_velocity[:, None], (slabs, rank))
    transport_part = pl.pallas_call(
        transport_kernel, out_shape=f32(bricks, 8 + 6 * height, rank), name="transport", compiler_params=pltpu.CompilerParams(vmem_limit_bytes=VMEM_BYTES)
    )(nodes, columns, first_speeds, weights)
    integrals = exchange(transport_part, "brick")

    brick_id = brick.astype(jnp.int32)[None]
    vector_specs = [pl.BlockSpec(memory_space=pltpu.SMEM)]
    whole = pl.BlockSpec(memory_space=pltpu.VMEM)
    payload, line, state = pl.pallas_call(
        maxwell_kernel,
        out_shape=(
            f32(bricks, cells + 6 * height, rank),
            f32(slab_cells, slabs),
            f32(8, slab_cells),
        ),
        in_specs=vector_specs + [whole] * 5,
        name="maxwell", compiler_params=pltpu.CompilerParams(vmem_limit_bytes=VMEM_BYTES),
    )(brick_id, k_slab, integrals, nodes, first_speeds, across[1:])
    second = exchange(payload, "brick")

    slab_grid = k_slab.reshape(bricks, cells_x, cells_y, cells_z, rank)
    left = ((brick - 1) % bricks) ^ brick
    right = ((brick + 1) % bricks) ^ brick
    left = lax.dynamic_index_in_dim(slab_grid, left, 0, keepdims=False)
    right = lax.dynamic_index_in_dim(slab_grid, right, 0, keepdims=False)
    lower = [
        jnp.concatenate([k_below, k_coeffs[:-1]], axis=0),
        jnp.concatenate([left[:, -1:], k_coeffs[:, :-1]], axis=1),
        jnp.roll(k_coeffs, 1, axis=2),
    ]
    upper = [
        jnp.concatenate([k_coeffs[1:], k_above], axis=0),
        jnp.concatenate([k_coeffs[:, 1:], right[:, :1]], axis=1),
        jnp.roll(k_coeffs, -1, axis=2),
    ]
    steps = []
    for axis_id in range(3):
        steps.append(((k_coeffs - lower[axis_id]) * lengths[axis_id]).reshape(cells, rank))
        steps.append(((upper[axis_id] - k_coeffs) * lengths[axis_id]).reshape(cells, rank))
    payload, advanced = pl.pallas_call(
        functools.partial(advance_kernel, time_step=time_step),
        out_shape=(f32(bricks, cells + height, rank), f32(cells, rank)),
        name="advance", compiler_params=pltpu.CompilerParams(vmem_limit_bytes=VMEM_BYTES),
    )(second, jnp.stack(steps), own_cells)
    third = exchange(payload, "brick")

    pieces, chosen = pl.pallas_call(
        functools.partial(products_kernel, cells_x=cells_x, cells_y=cells_y, cells_z=cells_z),
        out_shape=(f32(5 * height, rank), f32(height, half)),
        in_specs=vector_specs + [whole],
        scratch_shapes=[pltpu.VMEM((rank, 4 * rank), jnp.float32)],
        name="products",
        compiler_params=pltpu.CompilerParams(vmem_limit_bytes=VMEM_BYTES),
    )(brick_id, third)
    chosen, third_after = lax.optimization_barrier((chosen, third))
    chosen_below = lax.ppermute(chosen, "slab", up)
    first_plane = third[:, : cells // cells_x].reshape(half, rank)

    back = pl.pallas_call(back_kernel, out_shape=f32(slabs, rows, rank), name="back", compiler_params=pltpu.CompilerParams(vmem_limit_bytes=VMEM_BYTES))(
        third_after, line, state, across[1:].T
    )

    pieces = pieces + jnp.pad(
        contract(chosen_below, first_plane, 1, 0), ((height, 3 * height), (0, 0))
    )
    pieces, back = lax.optimization_barrier((pieces, back))
    fourth = exchange(back, "slab")
    both = ("slab", "brick")
    lower_x, upper_x, cross_x = (from_peer(pieces, both, mask) for mask in (8, 16, 24))
    reduced = jnp.stack([pieces + upper_x, lower_x + cross_x])
    reduced = sum_over(reduced, both, ((32, 64, 96),))
    reduced = gather_more(reduced, both, ((1,),))
    later, fourth = lax.optimization_barrier((reduced, fourth))
    peers_z = [from_peer(part, both, mask) for part, mask in ((reduced, 2), (later, 4), (reduced, 6))]
    reduced = jnp.concatenate([reduced] + peers_z, axis=0)

    speeds = jnp.stack(list(own_velocity) + [jnp.zeros_like(ones)] * 5, axis=1)
    basis_new, velocity_new, gram_part = pl.pallas_call(
        functools.partial(
            middle_kernel, lengths=lengths, time_step=time_step, weight_x=weight_x
        ),
        out_shape=(f32(cells, rank), f32(rows, rank), f32(rank, rank)),
        in_specs=vector_specs + [whole] * 6,
        scratch_shapes=factor_scratch(rank),
        name="middle", compiler_params=pltpu.CompilerParams(vmem_limit_bytes=VMEM_BYTES),
    )(brick_id, reduced, second, v_basis, fourth, advanced, speeds)
    gram_v = sum_over(gram_part, ("slab", "brick"), ALL_GROUPS)
    coupling, vbasis_new = pl.pallas_call(
        last_kernel,
        out_shape=(f32(rank, rank), f32(rows, rank)),
        scratch_shapes=factor_scratch(rank),
        name="last", compiler_params=pltpu.CompilerParams(vmem_limit_bytes=VMEM_BYTES),
    )(gram_v, velocity_new)
    return (basis_new.reshape(cells_x, cells_y, cells_z, rank), coupling, vbasis_new)


def solution(mesh):
    placed = (P("slab", "brick", None, None), P(("slab", "brick"), None))
    return jax.shard_map(
        local,
        mesh=mesh,
        in_specs=placed,
        out_specs=(P("slab", "brick", None, None), P(), P(("slab", "brick"), None)),
        check_vma=False,
    )
```

```python
import functools
import math

import jax
import jax.numpy as jnp
from jax import lax
from jax.experimental import pallas as pl
from jax.experimental.pallas import tpu as pltpu
from jax.sharding import PartitionSpec as P

NVX = 32


CFL = 0.9
VMAX = 6.0
COLLIDE = 0.3
RHO_MIN = 0.25
TEMP_MIN = 0.25
PRECISE = lax.Precision.HIGHEST
FINE = lax.Precision.HIGH
SPACING = 2.0 * VMAX / NVX
WEIGHT_V = SPACING**3
PANEL = 16
VMEM_BYTES = 24 * 2**20


def contract(left, right, left_dim, right_dim, precision=PRECISE):
    return lax.dot_general(
        left, right, (((left_dim,), (right_dim,)), ((), ())), precision=precision
    )


def exchange(array, axis):
    return lax.all_to_all(array, axis, 0, 0, tiled=True)


def to_all(array, axis):
    copies = lax.axis_size(axis)
    return exchange(jnp.broadcast_to(array[None], (copies,) + array.shape), axis)


def velocities(indices):
    coords = jnp.stack([indices // (NVX * NVX), indices // NVX % NVX, indices % NVX])
    return -VMAX + (coords.astype(jnp.float32) + 0.5) * SPACING


def cell_state(moments):
    density = jnp.maximum(moments[0], RHO_MIN)
    drift = [moments[axis_id] / density for axis_id in (1, 2, 3)]
    square = drift[0] * drift[0] + drift[1] * drift[1] + drift[2] * drift[2]
    temper = jnp.maximum((moments[4] / density - square) / 3.0, TEMP_MIN)
    return density, drift, temper


def from_peer(values, axis, mask):
    axes = axis if isinstance(axis, tuple) else (axis,)
    peers = math.prod(lax.axis_size(name) for name in axes)
    return lax.ppermute(values, axis, [(i, i ^ mask) for i in range(peers)])


def sum_over(array, axis, groups):
    for masks in groups:
        parts = [array] + [from_peer(array, axis, mask) for mask in masks]
        array = sum_pairs(parts)
    return array


def sum_pairs(parts):
    if len(parts) == 1:
        return parts[0]
    half = len(parts) // 2
    return sum_pairs(parts[:half]) + sum_pairs(parts[half:])


def gather_relative(array, axis, groups):
    return gather_more(array[None], axis, groups)


def gather_more(array, axis, groups):
    for masks in groups:
        array = jnp.concatenate([array] + [from_peer(array, axis, mask) for mask in masks], axis=0)
    return array


BRICK_GROUPS = ((1,), (2, 4, 6), (8,))
ALL_GROUPS = ((1,), (2, 4, 6), (8, 16, 24), (32, 64, 96))


def three_parts(array):
    high = array.astype(jnp.bfloat16).astype(jnp.float32)
    rest = array - high
    middle = rest.astype(jnp.bfloat16).astype(jnp.float32)
    return high, middle, rest - middle


def two_parts(array):
    high = array.astype(jnp.bfloat16)
    return high, (array - high.astype(jnp.float32)).astype(jnp.bfloat16)


def factor_into(gram, work_ref, upper_ref, inverse_ref):
    size = gram.shape[0]
    rows = lax.broadcasted_iota(jnp.int32, (size, size), 0)
    cols = lax.broadcasted_iota(jnp.int32, (size, size), 1)
    work_ref[:, :size] = gram
    work_ref[:, size:] = jnp.where(rows == cols, 1.0, 0.0)
    panel_row = lax.broadcasted_iota(jnp.int32, (PANEL, size), 0)
    panel_col = lax.broadcasted_iota(jnp.int32, (PANEL, size), 1)
    for start in range(0, size, PANEL):
        stop = start + PANEL
        panel = work_ref[start:stop, :]
        spread = [
            jnp.broadcast_to(panel[:, start + t : start + t + 1], (PANEL, size))
            for t in range(PANEL)
        ]
        pivots = jnp.zeros((PANEL, size), jnp.float32)
        for t in range(PANEL):
            pivot = jnp.broadcast_to(spread[t][t : t + 1, :], (PANEL, size))
            pivots = jnp.where(panel_row == t, pivot, pivots)
            if t == PANEL - 1:
                break
            ratio = jnp.where(panel_row > t, spread[t] * (1.0 / pivot), 0.0)
            for u in range(t + 1, PANEL):
                spread[u] = spread[u] - ratio * jnp.broadcast_to(
                    spread[u][t : t + 1, :], (PANEL, size)
                )
            panel = panel - jnp.concatenate([ratio, ratio], axis=1) * jnp.broadcast_to(
                panel[t : t + 1, :], (PANEL, 2 * size)
            )
        scale = lax.rsqrt(pivots)
        panel = panel * jnp.concatenate([scale, scale], axis=1)
        left = jnp.where(panel_col >= panel_row + start, panel[:, :size], 0.0)
        right = panel[:, size:]
        upper_ref[start:stop, :] = left
        inverse_ref[start:stop, :] = right
        if stop < size:
            high, middle, low = three_parts(jnp.concatenate([left, right], axis=1))
            lhs = [high, high, middle, middle, high, low]
            rhs = [high, middle, high, middle, low, high]
            update = lax.dot_general(
                jnp.concatenate([part[:, :size] for part in lhs], axis=0).astype(jnp.bfloat16),
                jnp.concatenate(rhs, axis=0).astype(jnp.bfloat16),
                (((0,), (0,)), ((), ())),
                preferred_element_type=jnp.float32,
            )
            work_ref[stop:, :] = work_ref[stop:, :] - update[stop:, :]


def repeat_kernel(source_ref, out_ref, sems):
    copies = [
        pltpu.make_async_copy(source_ref, out_ref.at[i], sems.at[i])
        for i in range(out_ref.shape[0])
    ]
    for copy in copies:
        copy.start()
    for copy in copies:
        copy.wait()


def contract_three(left, right, left_dim, right_dim):
    left_high, left_low = two_parts(left)
    right_high, right_low = two_parts(right)
    dims = (((left_dim,), (right_dim,)), ((), ()))

    def product(one, other):
        return lax.dot_general(one, other, dims, preferred_element_type=jnp.float32)

    small = product(left_high, right_low) + product(left_low, right_high)
    return product(left_high, right_high) + small


def transport_kernel(nodes_ref, columns_ref, speeds_ref, weights_ref, out_ref):
    groups, rows, rank = nodes_ref.shape
    bricks = out_ref.shape[0]
    factors = [jnp.broadcast_to(columns_ref[:, i : i + 1], (rows, rank)) for i in range(4)]
    sums = [jnp.zeros((rank, rank), jnp.float32) for _ in range(6)]
    vectors = jnp.zeros((8, rank), jnp.float32)
    for group in range(groups):
        nodes = nodes_ref[group]
        weighted = jnp.concatenate([nodes] + [nodes * factor for factor in factors], axis=1)
        high, low = two_parts(weighted)
        node_high, node_low = high[:, :rank], low[:, :rank]
        product = lax.dot_general(
            jnp.concatenate([node_high, node_high, node_low], axis=0),
            jnp.concatenate([high, low, high], axis=0),
            (((0,), (0,)), ((), ())),
            preferred_element_type=jnp.float32,
        )
        vectors = vectors + contract(weights_ref[group], nodes, 1, 0)
        plain = product[:, :rank]
        speed = jnp.broadcast_to(speeds_ref[group : group + 1, :], (rank, rank))
        sums[0] = sums[0] + jnp.maximum(speed, 0.0) * plain
        sums[1] = sums[1] + jnp.minimum(speed, 0.0) * plain
        for i in range(4):
            sums[2 + i] = sums[2 + i] + product[:, (i + 1) * rank : (i + 2) * rank]
    out_ref[:, :8, :] = jnp.broadcast_to((vectors * WEIGHT_V)[None], (bricks, 8, rank))
    height = rank // bricks
    for i in range(6):
        start = 8 + i * height
        out_ref[:, start : start + height, :] = (sums[i] * WEIGHT_V).reshape(
            bricks, height, rank
        )


def maxwell_kernel(
    brick_ref, cells_ref, integrals_ref, nodes_ref, first_ref, across_ref, part_ref, line_ref, state_ref
):
    bricks, cells, rank = cells_ref.shape
    groups, rows, _ = nodes_ref.shape
    total = bricks * cells
    brick = brick_ref[0]
    k_flat = jnp.concatenate([cells_ref[i ^ brick] for i in range(bricks)], axis=0)
    integrals = integrals_ref[0]
    for i in range(1, bricks):
        integrals = integrals + integrals_ref[i]
    height = integrals.shape[0] - 8
    part_ref[:, cells:, :] = jnp.broadcast_to(integrals[8:][None], (bricks, height, rank))
    moments = contract(integrals[:8], k_flat, 1, 1)
    density, drift, temper = cell_state([moments[i : i + 1] for i in range(5)])
    slope = -0.5 / temper
    amplitude = density * jnp.exp(-1.5 * jnp.log(2.0 * math.pi * temper))
    first = jnp.broadcast_to(first_ref[:, :1], (groups, total))
    line = amplitude * jnp.exp((first - drift[0]) ** 2 * slope)
    state = jnp.concatenate([drift[1], drift[2], slope] + [amplitude] * 5, axis=0)
    state_ref[...] = state
    both = jnp.concatenate([line, state], axis=0).T
    line_cols = both[:, :groups]
    line_ref[...] = line_cols
    distance = (across_ref[0:1, :] - both[:, groups : groups + 1]) ** 2
    distance = distance + (across_ref[1:2, :] - both[:, groups + 1 : groups + 2]) ** 2
    high, low = two_parts(jnp.exp(distance * both[:, groups + 2 : groups + 3]))
    lhs = jnp.concatenate([high, high, low], axis=1)
    result = jnp.zeros((total, rank), jnp.float32)
    for group in range(0, groups, 2):
        node_high, node_low = two_parts(
            jnp.concatenate([nodes_ref[group], nodes_ref[group + 1]], axis=1)
        )
        product = lax.dot_general(
            lhs,
            jnp.concatenate([node_high, node_low, node_high], axis=0),
            (((1,), (0,)), ((), ())),
            preferred_element_type=jnp.float32,
        )
        result = result + line_cols[:, group : group + 1] * product[:, :rank]
        result = result + line_cols[:, group + 1 : group + 2] * product[:, rank:]
    part_ref[:, :cells, :] = result.reshape(bricks, cells, rank)


def products_kernel(
    brick_ref, parts_ref, pieces_ref, chosen_ref, work_ref, *, cells_x, cells_y, cells_z
):
    bricks, _, rank = parts_ref.shape
    height = rank // bricks
    cells = cells_x * cells_y * cells_z
    total = bricks * cells
    advanced = parts_ref[:, :cells, :].reshape(total, rank)
    last_plane = parts_ref[:, cells - cells // cells_x : cells, :].reshape(-1, rank)
    start = pl.multiple_of(brick_ref[0] * height, height)
    chosen_row = lax.broadcasted_iota(jnp.int32, (height, rank), 0) + start
    chosen_col = lax.broadcasted_iota(jnp.int32, (height, rank), 1)
    chosen_ref[...] = contract(jnp.where(chosen_row == chosen_col, 1.0, 0.0), last_plane, 1, 1)
    row = lax.broadcasted_iota(jnp.int32, (total, rank), 0)
    plane = cells_y * cells_z

    def shifted(amount):
        return pltpu.roll(advanced, amount % total, 0)

    along_x = jnp.where(row // plane % cells_x < cells_x - 1, shifted(-plane), 0.0)
    wrap = cells - (cells_y - 1) * cells_z
    along_y = jnp.where(row // cells_z % cells_y > 0, shifted(cells_z), shifted(wrap))
    along_z = jnp.where(row % cells_z > 0, shifted(1), shifted(1 - cells_z))
    left_high, left_low = two_parts(advanced)
    high, low = two_parts(jnp.concatenate([along_x, along_y, along_z], axis=1))
    work_ref[:, :rank] = contract(advanced, advanced, 0, 0)
    work_ref[:, rank:] = lax.dot_general(
        jnp.concatenate([left_high, left_high, left_low], axis=0),
        jnp.concatenate([high, low, high], axis=0),
        (((0,), (0,)), ((), ())),
        preferred_element_type=jnp.float32,
    )
    own = work_ref[pl.ds(start, height), :]
    for i in range(4):
        pieces_ref[i * height : (i + 1) * height, :] = own[:, i * rank : (i + 1) * rank]
    projected = parts_ref[0, cells:, :]
    for i in range(1, bricks):
        projected = projected + parts_ref[i, cells:, :]
    pieces_ref[4 * height :, :] = projected


def back_kernel(parts_ref, line_ref, state_ref, across_ref, out_ref):
    bricks, _, rank = parts_ref.shape
    groups, rows, _ = out_ref.shape
    total = line_ref.shape[0]
    cells = total // bricks
    advanced = parts_ref[:, :cells, :].reshape(total, rank)
    distance = (across_ref[:, 0:1] - state_ref[0:1, :]) ** 2
    distance = distance + (across_ref[:, 1:2] - state_ref[1:2, :]) ** 2
    high, low = two_parts(jnp.exp(distance * state_ref[2:3, :]))
    lhs = jnp.concatenate([high, high, low], axis=1)
    for group in range(0, groups, 2):
        scaled = [line_ref[:, i : i + 1] * advanced for i in (group, group + 1)]
        part_high, part_low = two_parts(jnp.concatenate(scaled, axis=1))
        product = lax.dot_general(
            lhs,
            jnp.concatenate([part_high, part_low, part_high], axis=0),
            (((1,), (0,)), ((), ())),
            preferred_element_type=jnp.float32,
        )
        out_ref[group] = product[:, :rank]
        out_ref[group + 1] = product[:, rank:]


def advance_kernel(parts_ref, steps_ref, cells_ref, payload_ref, advanced_ref, *, time_step):
    cells, rank = cells_ref.shape
    bricks = parts_ref.shape[0]
    height = rank // bricks
    maxwell_proj = parts_ref[0, :cells, :]
    for i in range(1, bricks):
        maxwell_proj = maxwell_proj + parts_ref[i, :cells, :]
    maxwell_proj = maxwell_proj * WEIGHT_V
    flux = jnp.zeros((cells, rank), jnp.float32)
    for i in range(6):
        block = parts_ref[:, cells + i * height : cells + (i + 1) * height, :].reshape(rank, rank)
        flux = flux + contract(steps_ref[i], block, 1, 0)
    own = cells_ref[...]
    advanced = own - time_step * flux + COLLIDE * (maxwell_proj - own)
    advanced_ref[...] = advanced
    payload_ref[:, :cells, :] = jnp.broadcast_to(advanced[None], (bricks, cells, rank))
    projected = contract(advanced, maxwell_proj, 0, 0)
    payload_ref[:, cells:, :] = projected.reshape(bricks, height, rank)


def middle_kernel(
    brick_ref,
    pieces_ref,
    transport_ref,
    basis_ref,
    advanced_ref,
    speeds_ref,
    basis_x_ref,
    velocity_ref,
    inverse_ref,
    work_ref,
    upper_ref,
    *,
    lengths,
    time_step,
    weight_x,
):
    bricks, _, rank = pieces_ref.shape
    rows = basis_ref.shape[0]
    height = rank // bricks
    cells = advanced_ref.shape[0]
    masks = [j ^ brick_ref[0] for j in range(bricks)]
    slots = [((m >> 1) & 3) * 4 + (m & 1) * 2 + (m >> 3) for m in masks]

    def piece(ref, i):
        if ref is transport_ref:
            start = cells + i * height
            return ref[:, start : start + height, :].reshape(rank, rank)
        rows_of = [ref[slot, i * height : (i + 1) * height, :] for slot in slots]
        return jnp.concatenate(rows_of, axis=0)

    factor_into(piece(pieces_ref, 0) * weight_x, work_ref, upper_ref, inverse_ref)
    upper, inverse = upper_ref[...], inverse_ref[...]
    basis_x_ref[...] = contract(advanced_ref[...], inverse, 1, 1)
    change = jnp.zeros((rank, rank), jnp.float32)
    turned = []
    for i in range(3):
        shift = piece(pieces_ref, 1 + i) * weight_x
        straight = contract(inverse, shift, 1, 0)
        crossed = contract(inverse, shift, 1, 1)
        if i == 0:
            straight, crossed = crossed, straight
        turned.append(contract(straight, inverse, 1, 1))
        change = change + lengths[i] * (
            contract_three(upper - straight, piece(transport_ref, 2 * i), 1, 0)
            + contract_three(crossed - upper, piece(transport_ref, 2 * i + 1), 1, 0)
        )
    projected = contract(inverse, piece(pieces_ref, 4) * weight_x, 1, 0)
    middle = upper + time_step * change - COLLIDE * (projected - upper)
    now = contract(basis_ref[...], middle, 1, 1)
    drift_sum = jnp.zeros((rows, rank), jnp.float32)
    for i in range(3):
        speed = jnp.broadcast_to(speeds_ref[:, i : i + 1], (rows, rank)) * lengths[i]
        minus = contract_three(now, turned[i], 1, 1)
        plus = contract_three(now, turned[i], 1, 0)
        drift_sum = drift_sum + jnp.maximum(speed, 0.0) * (now - minus)
        drift_sum = drift_sum + jnp.minimum(speed, 0.0) * (plus - now)
    velocity_ref[...] = now - time_step * drift_sum - COLLIDE * now


def update_kernel(back_ref, velocity_ref, inverse_ref, updated_ref, gram_ref, *, weight_x):
    back = back_ref[0]
    for i in range(1, back_ref.shape[0]):
        back = back + back_ref[i]
    back_proj = contract(back * weight_x, inverse_ref[...], 1, 1)
    updated = velocity_ref[...] + COLLIDE * back_proj
    updated_ref[...] = updated
    gram_ref[...] = contract(updated, updated, 0, 0) * WEIGHT_V


def last_kernel(gram_ref, velocity_ref, coupling_ref, basis_ref, work_ref, upper_ref, inverse_ref):
    factor_into(gram_ref[...], work_ref, upper_ref, inverse_ref)
    coupling_ref[...] = upper_ref[...].T
    basis_ref[...] = contract(velocity_ref[...], inverse_ref[...], 1, 1)


def f32(*shape):
    return jax.ShapeDtypeStruct(shape, jnp.float32)


def factor_scratch(rank):
    shapes = ((rank, 2 * rank), (rank, rank), (rank, rank))
    return [pltpu.VMEM(shape, jnp.float32) for shape in shapes]


def local(k_coeffs, v_basis):
    cells_x, cells_y, cells_z, rank = k_coeffs.shape
    cells = cells_x * cells_y * cells_z
    slabs, bricks = lax.axis_size("slab"), lax.axis_size("brick")
    devices = slabs * bricks
    slab, brick = lax.axis_index("slab"), lax.axis_index("brick")
    lengths = (cells_x * slabs, cells_y * bricks, cells_z)
    time_step = CFL / (VMAX * sum(lengths))
    weight_x = 1.0 / (lengths[0] * lengths[1] * lengths[2])
    rows = v_basis.shape[0]
    slab_cells = cells * bricks
    half = slab_cells // cells_x
    height = rank // bricks
    up = [(i, (i + 1) % slabs) for i in range(slabs)]
    down = [(i, (i - 1) % slabs) for i in range(slabs)]
    own_cells = k_coeffs.reshape(cells, rank)

    own_ids = (slab * bricks + brick) * rows + jnp.arange(rows, dtype=jnp.int32)
    own_velocity = velocities(own_ids)
    ones = jnp.ones_like(own_velocity[0])
    slab_owner = jnp.arange(slabs, dtype=jnp.int32)[:, None] * bricks + brick
    slab_velocity = velocities(slab_owner * rows + jnp.arange(rows, dtype=jnp.int32)[None])
    weights = jnp.stack(
        [jnp.ones_like(slab_velocity[0]), slab_velocity[0], slab_velocity[1], slab_velocity[2]]
        + [jnp.sum(slab_velocity * slab_velocity, axis=0)]
        + [jnp.zeros_like(slab_velocity[0])] * 3,
        axis=1,
    )
    nodes = exchange(
        pl.pallas_call(
            repeat_kernel,
            out_shape=f32(slabs, rows, rank),
            out_specs=pl.BlockSpec(memory_space=pl.ANY),
            scratch_shapes=[pltpu.SemaphoreType.DMA((slabs,))],
            name="repeat",
            compiler_params=pltpu.CompilerParams(vmem_limit_bytes=VMEM_BYTES),
        )(v_basis),
        "slab",
    )
    k_slab = gather_relative(own_cells, "brick", BRICK_GROUPS)
    k_edges, k_slab = lax.optimization_barrier((k_coeffs, k_slab))
    k_below = lax.ppermute(k_edges[-1:], "slab", up)
    k_above = lax.ppermute(k_edges[:1], "slab", down)

    across = velocities(brick * rows + jnp.arange(rows, dtype=jnp.int32))
    columns = [f(across[i]) for i in (1, 2) for f in (lambda v: jnp.maximum(v, 0.0), lambda v: jnp.minimum(v, 0.0))]
    columns = jnp.stack(columns + [jnp.zeros_like(ones)] * 4, axis=1)
    owner = jnp.arange(slabs, dtype=jnp.int32) * bricks + brick
    first_velocity = velocities(owner * rows)[0]
    first_speeds = jnp.broadcast_to(first_velocity[:, None], (slabs, rank))
    transport_part = pl.pallas_call(
        transport_kernel, out_shape=f32(bricks, 8 + 6 * height, rank), name="transport", compiler_params=pltpu.CompilerParams(vmem_limit_bytes=VMEM_BYTES)
    )(nodes, columns, first_speeds, weights)
    integrals = exchange(transport_part, "brick")

    brick_id = brick.astype(jnp.int32)[None]
    vector_specs = [pl.BlockSpec(memory_space=pltpu.SMEM)]
    whole = pl.BlockSpec(memory_space=pltpu.VMEM)
    payload, line, state = pl.pallas_call(
        maxwell_kernel,
        out_shape=(
            f32(bricks, cells + 6 * height, rank),
            f32(slab_cells, slabs),
            f32(8, slab_cells),
        ),
        in_specs=vector_specs + [whole] * 5,
        name="maxwell", compiler_params=pltpu.CompilerParams(vmem_limit_bytes=VMEM_BYTES),
    )(brick_id, k_slab, integrals, nodes, first_speeds, across[1:])
    second = exchange(payload, "brick")

    slab_grid = k_slab.reshape(bricks, cells_x, cells_y, cells_z, rank)
    left = ((brick - 1) % bricks) ^ brick
    right = ((brick + 1) % bricks) ^ brick
    left = lax.dynamic_index_in_dim(slab_grid, left, 0, keepdims=False)
    right = lax.dynamic_index_in_dim(slab_grid, right, 0, keepdims=False)
    lower = [
        jnp.concatenate([k_below, k_coeffs[:-1]], axis=0),
        jnp.concatenate([left[:, -1:], k_coeffs[:, :-1]], axis=1),
        jnp.roll(k_coeffs, 1, axis=2),
    ]
    upper = [
        jnp.concatenate([k_coeffs[1:], k_above], axis=0),
        jnp.concatenate([k_coeffs[:, 1:], right[:, :1]], axis=1),
        jnp.roll(k_coeffs, -1, axis=2),
    ]
    steps = []
    for axis_id in range(3):
        steps.append(((k_coeffs - lower[axis_id]) * lengths[axis_id]).reshape(cells, rank))
        steps.append(((upper[axis_id] - k_coeffs) * lengths[axis_id]).reshape(cells, rank))
    payload, advanced = pl.pallas_call(
        functools.partial(advance_kernel, time_step=time_step),
        out_shape=(f32(bricks, cells + height, rank), f32(cells, rank)),
        name="advance", compiler_params=pltpu.CompilerParams(vmem_limit_bytes=VMEM_BYTES),
    )(second, jnp.stack(steps), own_cells)
    third = exchange(payload, "brick")

    pieces, chosen = pl.pallas_call(
        functools.partial(products_kernel, cells_x=cells_x, cells_y=cells_y, cells_z=cells_z),
        out_shape=(f32(5 * height, rank), f32(height, half)),
        in_specs=vector_specs + [whole],
        scratch_shapes=[pltpu.VMEM((rank, 4 * rank), jnp.float32)],
        name="products",
        compiler_params=pltpu.CompilerParams(vmem_limit_bytes=VMEM_BYTES),
    )(brick_id, third)
    chosen, third_after = lax.optimization_barrier((chosen, third))
    chosen_below = lax.ppermute(chosen, "slab", up)
    first_plane = third[:, : cells // cells_x].reshape(half, rank)

    back = pl.pallas_call(back_kernel, out_shape=f32(slabs, rows, rank), name="back", compiler_params=pltpu.CompilerParams(vmem_limit_bytes=VMEM_BYTES))(
        third_after, line, state, across[1:].T
    )

    pieces = pieces + jnp.pad(
        contract(chosen_below, first_plane, 1, 0), ((height, 3 * height), (0, 0))
    )
    pieces, back = lax.optimization_barrier((pieces, back))
    fourth = exchange(back, "slab")
    both = ("slab", "brick")
    lower_x, upper_x, cross_x = (from_peer(pieces, both, mask) for mask in (8, 16, 24))
    reduced = jnp.stack([pieces + upper_x, lower_x + cross_x])
    reduced = sum_over(reduced, both, ((32, 64, 96),))
    reduced = gather_more(reduced, both, ((1,), (2, 4, 6)))

    speeds = jnp.stack(list(own_velocity) + [jnp.zeros_like(ones)] * 5, axis=1)
    basis_new, velocity_part, inverse = pl.pallas_call(
        functools.partial(
            middle_kernel, lengths=lengths, time_step=time_step, weight_x=weight_x
        ),
        out_shape=(f32(cells, rank), f32(rows, rank), f32(rank, rank)),
        in_specs=vector_specs + [whole] * 5,
        scratch_shapes=factor_scratch(rank)[:2],
        name="middle",
        compiler_params=pltpu.CompilerParams(vmem_limit_bytes=VMEM_BYTES),
    )(brick_id, reduced, second, v_basis, advanced, speeds)
    velocity_new, gram_part = pl.pallas_call(
        functools.partial(update_kernel, weight_x=weight_x),
        out_shape=(f32(rows, rank), f32(rank, rank)),
        name="update",
        compiler_params=pltpu.CompilerParams(vmem_limit_bytes=VMEM_BYTES),
    )(fourth, velocity_part, inverse)
    gram_v = sum_over(gram_part, ("slab", "brick"), ALL_GROUPS)
    coupling, vbasis_new = pl.pallas_call(
        last_kernel,
        out_shape=(f32(rank, rank), f32(rows, rank)),
        scratch_shapes=factor_scratch(rank),
        name="last", compiler_params=pltpu.CompilerParams(vmem_limit_bytes=VMEM_BYTES),
    )(gram_v, velocity_new)
    return (basis_new.reshape(cells_x, cells_y, cells_z, rank), coupling, vbasis_new)


def solution(mesh):
    placed = (P("slab", "brick", None, None), P(("slab", "brick"), None))
    return jax.shard_map(
        local,
        mesh=mesh,
        in_specs=placed,
        out_specs=(P("slab", "brick", None, None), P(), P(("slab", "brick"), None)),
        check_vma=False,
    )
```

```python
import functools
import math

import jax
import jax.numpy as jnp
from jax import lax
from jax.experimental import pallas as pl
from jax.experimental.pallas import tpu as pltpu
from jax.sharding import PartitionSpec as P

NVX = 32


CFL = 0.9
VMAX = 6.0
COLLIDE = 0.3
RHO_MIN = 0.25
TEMP_MIN = 0.25
PRECISE = lax.Precision.HIGHEST
FINE = lax.Precision.HIGH
SPACING = 2.0 * VMAX / NVX
WEIGHT_V = SPACING**3
PANEL = 16
VMEM_BYTES = 24 * 2**20


def contract(left, right, left_dim, right_dim, precision=PRECISE):
    return lax.dot_general(
        left, right, (((left_dim,), (right_dim,)), ((), ())), precision=precision
    )


def exchange(array, axis):
    return lax.all_to_all(array, axis, 0, 0, tiled=True)


def to_all(array, axis):
    copies = lax.axis_size(axis)
    return exchange(jnp.broadcast_to(array[None], (copies,) + array.shape), axis)


def velocities(indices):
    coords = jnp.stack([indices // (NVX * NVX), indices // NVX % NVX, indices % NVX])
    return -VMAX + (coords.astype(jnp.float32) + 0.5) * SPACING


def cell_state(moments):
    density = jnp.maximum(moments[0], RHO_MIN)
    drift = [moments[axis_id] / density for axis_id in (1, 2, 3)]
    square = drift[0] * drift[0] + drift[1] * drift[1] + drift[2] * drift[2]
    temper = jnp.maximum((moments[4] / density - square) / 3.0, TEMP_MIN)
    return density, drift, temper


def from_peer(values, axis, mask):
    axes = axis if isinstance(axis, tuple) else (axis,)
    peers = math.prod(lax.axis_size(name) for name in axes)
    return lax.ppermute(values, axis, [(i, i ^ mask) for i in range(peers)])


def sum_over(array, axis, groups):
    for masks in groups:
        parts = [array] + [from_peer(array, axis, mask) for mask in masks]
        array = sum_pairs(parts)
    return array


def sum_pairs(parts):
    if len(parts) == 1:
        return parts[0]
    half = len(parts) // 2
    return sum_pairs(parts[:half]) + sum_pairs(parts[half:])


def gather_relative(array, axis, groups):
    return gather_more(array[None], axis, groups)


def gather_more(array, axis, groups):
    for masks in groups:
        array = jnp.concatenate([array] + [from_peer(array, axis, mask) for mask in masks], axis=0)
    return array


BRICK_GROUPS = ((1,), (2, 4, 6), (8,))
ALL_GROUPS = ((1,), (2, 4, 6), (8, 16, 24), (32, 64, 96))


def three_parts(array):
    high = array.astype(jnp.bfloat16).astype(jnp.float32)
    rest = array - high
    middle = rest.astype(jnp.bfloat16).astype(jnp.float32)
    return high, middle, rest - middle


def two_parts(array):
    high = array.astype(jnp.bfloat16)
    return high, (array - high.astype(jnp.float32)).astype(jnp.bfloat16)


def factor_into(gram, work_ref, upper_ref, inverse_ref):
    size = gram.shape[0]
    rows = lax.broadcasted_iota(jnp.int32, (size, size), 0)
    cols = lax.broadcasted_iota(jnp.int32, (size, size), 1)
    work_ref[:, :size] = gram
    work_ref[:, size:] = jnp.where(rows == cols, 1.0, 0.0)
    panel_row = lax.broadcasted_iota(jnp.int32, (PANEL, size), 0)
    panel_col = lax.broadcasted_iota(jnp.int32, (PANEL, size), 1)
    for start in range(0, size, PANEL):
        stop = start + PANEL
        panel = work_ref[start:stop, :]
        spread = [
            jnp.broadcast_to(panel[:, start + t : start + t + 1], (PANEL, size))
            for t in range(PANEL)
        ]
        pivots = jnp.zeros((PANEL, size), jnp.float32)
        for t in range(PANEL):
            pivot = jnp.broadcast_to(spread[t][t : t + 1, :], (PANEL, size))
            pivots = jnp.where(panel_row == t, pivot, pivots)
            if t == PANEL - 1:
                break
            ratio = jnp.where(panel_row > t, spread[t] * (1.0 / pivot), 0.0)
            for u in range(t + 1, PANEL):
                spread[u] = spread[u] - ratio * jnp.broadcast_to(
                    spread[u][t : t + 1, :], (PANEL, size)
                )
            panel = panel - jnp.concatenate([ratio, ratio], axis=1) * jnp.broadcast_to(
                panel[t : t + 1, :], (PANEL, 2 * size)
            )
        scale = lax.rsqrt(pivots)
        panel = panel * jnp.concatenate([scale, scale], axis=1)
        left = jnp.where(panel_col >= panel_row + start, panel[:, :size], 0.0)
        right = panel[:, size:]
        upper_ref[start:stop, :] = left
        inverse_ref[start:stop, :] = right
        if stop < size:
            high, middle, low = three_parts(jnp.concatenate([left, right], axis=1))
            lhs = [high, high, middle, middle, high, low]
            rhs = [high, middle, high, middle, low, high]
            update = lax.dot_general(
                jnp.concatenate([part[:, :size] for part in lhs], axis=0).astype(jnp.bfloat16),
                jnp.concatenate(rhs, axis=0).astype(jnp.bfloat16),
                (((0,), (0,)), ((), ())),
                preferred_element_type=jnp.float32,
            )
            work_ref[stop:, :] = work_ref[stop:, :] - update[stop:, :]


def repeat_kernel(source_ref, out_ref, sems):
    copies = [
        pltpu.make_async_copy(source_ref, out_ref.at[i], sems.at[i])
        for i in range(out_ref.shape[0])
    ]
    for copy in copies:
        copy.start()
    for copy in copies:
        copy.wait()


def contract_three(left, right, left_dim, right_dim):
    left_high, left_low = two_parts(left)
    right_high, right_low = two_parts(right)
    dims = (((left_dim,), (right_dim,)), ((), ()))

    def product(one, other):
        return lax.dot_general(one, other, dims, preferred_element_type=jnp.float32)

    small = product(left_high, right_low) + product(left_low, right_high)
    return product(left_high, right_high) + small


def transport_kernel(nodes_ref, columns_ref, speeds_ref, weights_ref, out_ref):
    groups, rows, rank = nodes_ref.shape
    bricks = out_ref.shape[0]
    factors = [jnp.broadcast_to(columns_ref[:, i : i + 1], (rows, rank)) for i in range(4)]
    sums = [jnp.zeros((rank, rank), jnp.float32) for _ in range(6)]
    vectors = jnp.zeros((8, rank), jnp.float32)
    for group in range(groups):
        nodes = nodes_ref[group]
        weighted = jnp.concatenate([nodes] + [nodes * factor for factor in factors], axis=1)
        high, low = two_parts(weighted)
        node_high, node_low = high[:, :rank], low[:, :rank]
        product = lax.dot_general(
            jnp.concatenate([node_high, node_high, node_low], axis=0),
            jnp.concatenate([high, low, high], axis=0),
            (((0,), (0,)), ((), ())),
            preferred_element_type=jnp.float32,
        )
        vectors = vectors + contract(weights_ref[group], nodes, 1, 0)
        plain = product[:, :rank]
        speed = jnp.broadcast_to(speeds_ref[group : group + 1, :], (rank, rank))
        sums[0] = sums[0] + jnp.maximum(speed, 0.0) * plain
        sums[1] = sums[1] + jnp.minimum(speed, 0.0) * plain
        for i in range(4):
            sums[2 + i] = sums[2 + i] + product[:, (i + 1) * rank : (i + 2) * rank]
    row = lax.broadcasted_iota(jnp.int32, (rank, rank), 0)
    col = lax.broadcasted_iota(jnp.int32, (rank, rank), 1)
    block_row = lax.broadcasted_iota(jnp.int32, (8, rank), 0)
    height = rank // bricks
    for i in range(3):
        plus, minus = sums[2 * i], sums[2 * i + 1]
        diagonal = jnp.sum(jnp.where(row == col, minus, 0.0), axis=0, keepdims=True)
        vectors = vectors + jnp.where(block_row == 5 + i, diagonal, 0.0)
        packed = jnp.where(col >= row, plus, minus) * WEIGHT_V
        start = 8 + i * height
        out_ref[:, start : start + height, :] = packed.reshape(bricks, height, rank)
    out_ref[:, :8, :] = jnp.broadcast_to((vectors * WEIGHT_V)[None], (bricks, 8, rank))


def maxwell_kernel(
    brick_ref,
    cells_ref,
    integrals_ref,
    nodes_ref,
    first_ref,
    across_ref,
    part_ref,
    line_ref,
    state_ref,
    vectors_ref,
):
    bricks, cells, rank = cells_ref.shape
    groups, rows, _ = nodes_ref.shape
    total = bricks * cells
    brick = brick_ref[0]
    k_flat = jnp.concatenate([cells_ref[i ^ brick] for i in range(bricks)], axis=0)
    integrals = integrals_ref[0]
    for i in range(1, bricks):
        integrals = integrals + integrals_ref[i]
    height = integrals.shape[0] - 8
    part_ref[:, cells:, :] = jnp.broadcast_to(integrals[8:][None], (bricks, height, rank))
    vectors_ref[...] = integrals[:8]
    moments = contract(integrals[:8], k_flat, 1, 1)
    density, drift, temper = cell_state([moments[i : i + 1] for i in range(5)])
    slope = -0.5 / temper
    amplitude = density * jnp.exp(-1.5 * jnp.log(2.0 * math.pi * temper))
    first = jnp.broadcast_to(first_ref[:, :1], (groups, total))
    line = amplitude * jnp.exp((first - drift[0]) ** 2 * slope)
    state = jnp.concatenate([drift[1], drift[2], slope] + [amplitude] * 5, axis=0)
    state_ref[...] = state
    both = jnp.concatenate([line, state], axis=0).T
    line_cols = both[:, :groups]
    line_ref[...] = line_cols
    distance = (across_ref[0:1, :] - both[:, groups : groups + 1]) ** 2
    distance = distance + (across_ref[1:2, :] - both[:, groups + 1 : groups + 2]) ** 2
    high, low = two_parts(jnp.exp(distance * both[:, groups + 2 : groups + 3]))
    lhs = jnp.concatenate([high, high, low], axis=1)
    result = jnp.zeros((total, rank), jnp.float32)
    for group in range(0, groups, 2):
        node_high, node_low = two_parts(
            jnp.concatenate([nodes_ref[group], nodes_ref[group + 1]], axis=1)
        )
        product = lax.dot_general(
            lhs,
            jnp.concatenate([node_high, node_low, node_high], axis=0),
            (((1,), (0,)), ((), ())),
            preferred_element_type=jnp.float32,
        )
        result = result + line_cols[:, group : group + 1] * product[:, :rank]
        result = result + line_cols[:, group + 1 : group + 2] * product[:, rank:]
    part_ref[:, :cells, :] = result.reshape(bricks, cells, rank)


def products_kernel(
    brick_ref, parts_ref, pieces_ref, chosen_ref, work_ref, *, cells_x, cells_y, cells_z
):
    bricks, _, rank = parts_ref.shape
    height = rank // bricks
    cells = cells_x * cells_y * cells_z
    total = bricks * cells
    advanced = parts_ref[:, :cells, :].reshape(total, rank)
    last_plane = parts_ref[:, cells - cells // cells_x : cells, :].reshape(-1, rank)
    start = pl.multiple_of(brick_ref[0] * height, height)
    chosen_row = lax.broadcasted_iota(jnp.int32, (height, rank), 0) + start
    chosen_col = lax.broadcasted_iota(jnp.int32, (height, rank), 1)
    chosen_ref[...] = contract(jnp.where(chosen_row == chosen_col, 1.0, 0.0), last_plane, 1, 1)
    row = lax.broadcasted_iota(jnp.int32, (total, rank), 0)
    plane = cells_y * cells_z

    def shifted(amount):
        return pltpu.roll(advanced, amount % total, 0)

    along_x = jnp.where(row // plane % cells_x < cells_x - 1, shifted(-plane), 0.0)
    wrap = cells - (cells_y - 1) * cells_z
    along_y = jnp.where(row // cells_z % cells_y > 0, shifted(cells_z), shifted(wrap))
    along_z = jnp.where(row % cells_z > 0, shifted(1), shifted(1 - cells_z))
    left_high, left_low = two_parts(advanced)
    high, low = two_parts(jnp.concatenate([along_x, along_y, along_z], axis=1))
    work_ref[:, :rank] = contract(advanced, advanced, 0, 0)
    work_ref[:, rank:] = lax.dot_general(
        jnp.concatenate([left_high, left_high, left_low], axis=0),
        jnp.concatenate([high, low, high], axis=0),
        (((0,), (0,)), ((), ())),
        preferred_element_type=jnp.float32,
    )
    own = work_ref[pl.ds(start, height), :]
    for i in range(4):
        pieces_ref[i * height : (i + 1) * height, :] = own[:, i * rank : (i + 1) * rank]
    projected = parts_ref[0, cells:, :]
    for i in range(1, bricks):
        projected = projected + parts_ref[i, cells:, :]
    pieces_ref[4 * height :, :] = projected


def back_kernel(parts_ref, line_ref, state_ref, across_ref, out_ref):
    bricks, _, rank = parts_ref.shape
    groups, rows, _ = out_ref.shape
    total = line_ref.shape[0]
    cells = total // bricks
    advanced = parts_ref[:, :cells, :].reshape(total, rank)
    distance = (across_ref[:, 0:1] - state_ref[0:1, :]) ** 2
    distance = distance + (across_ref[:, 1:2] - state_ref[1:2, :]) ** 2
    high, low = two_parts(jnp.exp(distance * state_ref[2:3, :]))
    lhs = jnp.concatenate([high, high, low], axis=1)
    for group in range(0, groups, 2):
        scaled = [line_ref[:, i : i + 1] * advanced for i in (group, group + 1)]
        part_high, part_low = two_parts(jnp.concatenate(scaled, axis=1))
        product = lax.dot_general(
            lhs,
            jnp.concatenate([part_high, part_low, part_high], axis=0),
            (((1,), (0,)), ((), ())),
            preferred_element_type=jnp.float32,
        )
        out_ref[group] = product[:, :rank]
        out_ref[group + 1] = product[:, rank:]


def advance_kernel(
    parts_ref,
    steps_ref,
    cells_ref,
    vectors_ref,
    payload_ref,
    advanced_ref,
    transport_ref,
    *,
    time_step,
):
    cells, rank = cells_ref.shape
    bricks = parts_ref.shape[0]
    height = rank // bricks
    maxwell_proj = parts_ref[0, :cells, :]
    for i in range(1, bricks):
        maxwell_proj = maxwell_proj + parts_ref[i, :cells, :]
    maxwell_proj = maxwell_proj * WEIGHT_V
    flux = jnp.zeros((cells, rank), jnp.float32)
    row = lax.broadcasted_iota(jnp.int32, (rank, rank), 0)
    col = lax.broadcasted_iota(jnp.int32, (rank, rank), 1)
    for i in range(3):
        start = cells + i * height
        packed = parts_ref[:, start : start + height, :].reshape(rank, rank)
        turned = packed.T
        plus = jnp.where(col >= row, packed, turned)
        minus = jnp.where(col < row, packed, turned)
        minus = jnp.where(col == row, vectors_ref[5 + i : 6 + i, :], minus)
        transport_ref[2 * i] = plus
        transport_ref[2 * i + 1] = minus
        flux = flux + contract(steps_ref[2 * i], plus, 1, 0)
        flux = flux + contract(steps_ref[2 * i + 1], minus, 1, 0)
    own = cells_ref[...]
    advanced = own - time_step * flux + COLLIDE * (maxwell_proj - own)
    advanced_ref[...] = advanced
    payload_ref[:, :cells, :] = jnp.broadcast_to(advanced[None], (bricks, cells, rank))
    projected = contract(advanced, maxwell_proj, 0, 0)
    payload_ref[:, cells:, :] = projected.reshape(bricks, height, rank)


def middle_kernel(
    brick_ref,
    pieces_ref,
    transport_ref,
    basis_ref,
    advanced_ref,
    speeds_ref,
    basis_x_ref,
    velocity_ref,
    inverse_ref,
    work_ref,
    upper_ref,
    *,
    lengths,
    time_step,
    weight_x,
):
    bricks, _, rank = pieces_ref.shape
    rows = basis_ref.shape[0]
    height = rank // bricks
    masks = [j ^ brick_ref[0] for j in range(bricks)]
    slots = [((m >> 1) & 3) * 4 + (m & 1) * 2 + (m >> 3) for m in masks]

    def piece(ref, i):
        if ref is transport_ref:
            return ref[i]
        rows_of = [ref[slot, i * height : (i + 1) * height, :] for slot in slots]
        return jnp.concatenate(rows_of, axis=0)

    factor_into(piece(pieces_ref, 0) * weight_x, work_ref, upper_ref, inverse_ref)
    upper, inverse = upper_ref[...], inverse_ref[...]
    basis_x_ref[...] = contract(advanced_ref[...], inverse, 1, 1)
    change = jnp.zeros((rank, rank), jnp.float32)
    turned = []
    for i in range(3):
        shift = piece(pieces_ref, 1 + i) * weight_x
        straight = contract(inverse, shift, 1, 0)
        crossed = contract(inverse, shift, 1, 1)
        if i == 0:
            straight, crossed = crossed, straight
        turned.append(contract(straight, inverse, 1, 1))
        change = change + lengths[i] * (
            contract_three(upper - straight, piece(transport_ref, 2 * i), 1, 0)
            + contract_three(crossed - upper, piece(transport_ref, 2 * i + 1), 1, 0)
        )
    projected = contract(inverse, piece(pieces_ref, 4) * weight_x, 1, 0)
    middle = upper + time_step * change - COLLIDE * (projected - upper)
    now = contract(basis_ref[...], middle, 1, 1)
    drift_sum = jnp.zeros((rows, rank), jnp.float32)
    for i in range(3):
        speed = jnp.broadcast_to(speeds_ref[:, i : i + 1], (rows, rank)) * lengths[i]
        minus = contract_three(now, turned[i], 1, 1)
        plus = contract_three(now, turned[i], 1, 0)
        drift_sum = drift_sum + jnp.maximum(speed, 0.0) * (now - minus)
        drift_sum = drift_sum + jnp.minimum(speed, 0.0) * (plus - now)
    velocity_ref[...] = now - time_step * drift_sum - COLLIDE * now


def update_kernel(back_ref, velocity_ref, inverse_ref, updated_ref, gram_ref, *, weight_x):
    back = back_ref[0]
    for i in range(1, back_ref.shape[0]):
        back = back + back_ref[i]
    back_proj = contract(back * weight_x, inverse_ref[...], 1, 1)
    updated = velocity_ref[...] + COLLIDE * back_proj
    updated_ref[...] = updated
    gram_ref[...] = contract(updated, updated, 0, 0) * WEIGHT_V


def last_kernel(gram_ref, velocity_ref, coupling_ref, basis_ref, work_ref, upper_ref, inverse_ref):
    factor_into(gram_ref[...], work_ref, upper_ref, inverse_ref)
    coupling_ref[...] = upper_ref[...].T
    basis_ref[...] = contract(velocity_ref[...], inverse_ref[...], 1, 1)


def f32(*shape):
    return jax.ShapeDtypeStruct(shape, jnp.float32)


def factor_scratch(rank):
    shapes = ((rank, 2 * rank), (rank, rank), (rank, rank))
    return [pltpu.VMEM(shape, jnp.float32) for shape in shapes]


def local(k_coeffs, v_basis):
    cells_x, cells_y, cells_z, rank = k_coeffs.shape
    cells = cells_x * cells_y * cells_z
    slabs, bricks = lax.axis_size("slab"), lax.axis_size("brick")
    devices = slabs * bricks
    slab, brick = lax.axis_index("slab"), lax.axis_index("brick")
    lengths = (cells_x * slabs, cells_y * bricks, cells_z)
    time_step = CFL / (VMAX * sum(lengths))
    weight_x = 1.0 / (lengths[0] * lengths[1] * lengths[2])
    rows = v_basis.shape[0]
    slab_cells = cells * bricks
    half = slab_cells // cells_x
    height = rank // bricks
    up = [(i, (i + 1) % slabs) for i in range(slabs)]
    down = [(i, (i - 1) % slabs) for i in range(slabs)]
    own_cells = k_coeffs.reshape(cells, rank)

    own_ids = (slab * bricks + brick) * rows + jnp.arange(rows, dtype=jnp.int32)
    own_velocity = velocities(own_ids)
    ones = jnp.ones_like(own_velocity[0])
    slab_owner = jnp.arange(slabs, dtype=jnp.int32)[:, None] * bricks + brick
    slab_velocity = velocities(slab_owner * rows + jnp.arange(rows, dtype=jnp.int32)[None])
    weights = jnp.stack(
        [jnp.ones_like(slab_velocity[0]), slab_velocity[0], slab_velocity[1], slab_velocity[2]]
        + [jnp.sum(slab_velocity * slab_velocity, axis=0)]
        + [jnp.zeros_like(slab_velocity[0])] * 3,
        axis=1,
    )
    nodes = exchange(
        pl.pallas_call(
            repeat_kernel,
            out_shape=f32(slabs, rows, rank),
            out_specs=pl.BlockSpec(memory_space=pl.ANY),
            scratch_shapes=[pltpu.SemaphoreType.DMA((slabs,))],
            name="repeat",
            compiler_params=pltpu.CompilerParams(vmem_limit_bytes=VMEM_BYTES),
        )(v_basis),
        "slab",
    )
    k_slab = gather_relative(own_cells, "brick", BRICK_GROUPS)
    k_edges, k_slab = lax.optimization_barrier((k_coeffs, k_slab))
    k_below = lax.ppermute(k_edges[-1:], "slab", up)
    k_above = lax.ppermute(k_edges[:1], "slab", down)

    across = velocities(brick * rows + jnp.arange(rows, dtype=jnp.int32))
    columns = [f(across[i]) for i in (1, 2) for f in (lambda v: jnp.maximum(v, 0.0), lambda v: jnp.minimum(v, 0.0))]
    columns = jnp.stack(columns + [jnp.zeros_like(ones)] * 4, axis=1)
    owner = jnp.arange(slabs, dtype=jnp.int32) * bricks + brick
    first_velocity = velocities(owner * rows)[0]
    first_speeds = jnp.broadcast_to(first_velocity[:, None], (slabs, rank))
    transport_part = pl.pallas_call(
        transport_kernel, out_shape=f32(bricks, 8 + 3 * height, rank), name="transport", compiler_params=pltpu.CompilerParams(vmem_limit_bytes=VMEM_BYTES)
    )(nodes, columns, first_speeds, weights)
    integrals = exchange(transport_part, "brick")

    brick_id = brick.astype(jnp.int32)[None]
    vector_specs = [pl.BlockSpec(memory_space=pltpu.SMEM)]
    whole = pl.BlockSpec(memory_space=pltpu.VMEM)
    payload, line, state, vectors = pl.pallas_call(
        maxwell_kernel,
        out_shape=(
            f32(bricks, cells + 3 * height, rank),
            f32(slab_cells, slabs),
            f32(8, slab_cells),
            f32(8, rank),
        ),
        in_specs=vector_specs + [whole] * 5,
        name="maxwell", compiler_params=pltpu.CompilerParams(vmem_limit_bytes=VMEM_BYTES),
    )(brick_id, k_slab, integrals, nodes, first_speeds, across[1:])
    second = exchange(payload, "brick")

    slab_grid = k_slab.reshape(bricks, cells_x, cells_y, cells_z, rank)
    left = ((brick - 1) % bricks) ^ brick
    right = ((brick + 1) % bricks) ^ brick
    left = lax.dynamic_index_in_dim(slab_grid, left, 0, keepdims=False)
    right = lax.dynamic_index_in_dim(slab_grid, right, 0, keepdims=False)
    lower = [
        jnp.concatenate([k_below, k_coeffs[:-1]], axis=0),
        jnp.concatenate([left[:, -1:], k_coeffs[:, :-1]], axis=1),
        jnp.roll(k_coeffs, 1, axis=2),
    ]
    upper = [
        jnp.concatenate([k_coeffs[1:], k_above], axis=0),
        jnp.concatenate([k_coeffs[:, 1:], right[:, :1]], axis=1),
        jnp.roll(k_coeffs, -1, axis=2),
    ]
    steps = []
    for axis_id in range(3):
        steps.append(((k_coeffs - lower[axis_id]) * lengths[axis_id]).reshape(cells, rank))
        steps.append(((upper[axis_id] - k_coeffs) * lengths[axis_id]).reshape(cells, rank))
    payload, advanced, transport = pl.pallas_call(
        functools.partial(advance_kernel, time_step=time_step),
        out_shape=(
            f32(bricks, cells + height, rank),
            f32(cells, rank),
            f32(6, rank, rank),
        ),
        name="advance", compiler_params=pltpu.CompilerParams(vmem_limit_bytes=VMEM_BYTES),
    )(second, jnp.stack(steps), own_cells, vectors)
    third = exchange(payload, "brick")

    pieces, chosen = pl.pallas_call(
        functools.partial(products_kernel, cells_x=cells_x, cells_y=cells_y, cells_z=cells_z),
        out_shape=(f32(5 * height, rank), f32(height, half)),
        in_specs=vector_specs + [whole],
        scratch_shapes=[pltpu.VMEM((rank, 4 * rank), jnp.float32)],
        name="products",
        compiler_params=pltpu.CompilerParams(vmem_limit_bytes=VMEM_BYTES),
    )(brick_id, third)
    chosen, third_after = lax.optimization_barrier((chosen, third))
    chosen_below = lax.ppermute(chosen, "slab", up)
    first_plane = third[:, : cells // cells_x].reshape(half, rank)

    back = pl.pallas_call(back_kernel, out_shape=f32(slabs, rows, rank), name="back", compiler_params=pltpu.CompilerParams(vmem_limit_bytes=VMEM_BYTES))(
        third_after, line, state, across[1:].T
    )

    pieces = pieces + jnp.pad(
        contract(chosen_below, first_plane, 1, 0), ((height, 3 * height), (0, 0))
    )
    pieces, back = lax.optimization_barrier((pieces, back))
    fourth = exchange(back, "slab")
    both = ("slab", "brick")
    lower_x, upper_x, cross_x = (from_peer(pieces, both, mask) for mask in (8, 16, 24))
    reduced = jnp.stack([pieces + upper_x, lower_x + cross_x])
    reduced = sum_over(reduced, both, ((32, 64, 96),))
    reduced = gather_more(reduced, both, ((1,), (2, 4, 6)))

    speeds = jnp.stack(list(own_velocity) + [jnp.zeros_like(ones)] * 5, axis=1)
    basis_new, velocity_part, inverse = pl.pallas_call(
        functools.partial(
            middle_kernel, lengths=lengths, time_step=time_step, weight_x=weight_x
        ),
        out_shape=(f32(cells, rank), f32(rows, rank), f32(rank, rank)),
        in_specs=vector_specs + [whole] * 5,
        scratch_shapes=factor_scratch(rank)[:2],
        name="middle",
        compiler_params=pltpu.CompilerParams(vmem_limit_bytes=VMEM_BYTES),
    )(brick_id, reduced, transport, v_basis, advanced, speeds)
    velocity_new, gram_part = pl.pallas_call(
        functools.partial(update_kernel, weight_x=weight_x),
        out_shape=(f32(rows, rank), f32(rank, rank)),
        name="update",
        compiler_params=pltpu.CompilerParams(vmem_limit_bytes=VMEM_BYTES),
    )(fourth, velocity_part, inverse)
    gram_v = sum_over(gram_part, ("slab", "brick"), ALL_GROUPS)
    coupling, vbasis_new = pl.pallas_call(
        last_kernel,
        out_shape=(f32(rank, rank), f32(rows, rank)),
        scratch_shapes=factor_scratch(rank),
        name="last", compiler_params=pltpu.CompilerParams(vmem_limit_bytes=VMEM_BYTES),
    )(gram_v, velocity_new)
    return (basis_new.reshape(cells_x, cells_y, cells_z, rank), coupling, vbasis_new)


def solution(mesh):
    placed = (P("slab", "brick", None, None), P(("slab", "brick"), None))
    return jax.shard_map(
        local,
        mesh=mesh,
        in_specs=placed,
        out_specs=(P("slab", "brick", None, None), P(), P(("slab", "brick"), None)),
        check_vma=False,
    )
```

```python
import functools
import math

import jax
import jax.numpy as jnp
from jax import lax
from jax.experimental import pallas as pl
from jax.experimental.pallas import tpu as pltpu
from jax.sharding import PartitionSpec as P

NVX = 32


CFL = 0.9
VMAX = 6.0
COLLIDE = 0.3
RHO_MIN = 0.25
TEMP_MIN = 0.25
PRECISE = lax.Precision.HIGHEST
FINE = lax.Precision.HIGH
SPACING = 2.0 * VMAX / NVX
WEIGHT_V = SPACING**3
PANEL = 16
VMEM_BYTES = 24 * 2**20


def contract(left, right, left_dim, right_dim, precision=PRECISE):
    return lax.dot_general(
        left, right, (((left_dim,), (right_dim,)), ((), ())), precision=precision
    )


def exchange(array, axis):
    return lax.all_to_all(array, axis, 0, 0, tiled=True)


def to_all(array, axis):
    copies = lax.axis_size(axis)
    return exchange(jnp.broadcast_to(array[None], (copies,) + array.shape), axis)


def velocities(indices):
    coords = jnp.stack([indices // (NVX * NVX), indices // NVX % NVX, indices % NVX])
    return -VMAX + (coords.astype(jnp.float32) + 0.5) * SPACING


def cell_state(moments):
    density = jnp.maximum(moments[0], RHO_MIN)
    drift = [moments[axis_id] / density for axis_id in (1, 2, 3)]
    square = drift[0] * drift[0] + drift[1] * drift[1] + drift[2] * drift[2]
    temper = jnp.maximum((moments[4] / density - square) / 3.0, TEMP_MIN)
    return density, drift, temper


def from_peer(values, axis, mask):
    axes = axis if isinstance(axis, tuple) else (axis,)
    peers = math.prod(lax.axis_size(name) for name in axes)
    return lax.ppermute(values, axis, [(i, i ^ mask) for i in range(peers)])


def sum_over(array, axis, groups):
    for masks in groups:
        parts = [array] + [from_peer(array, axis, mask) for mask in masks]
        array = sum_pairs(parts)
    return array


def sum_pairs(parts):
    if len(parts) == 1:
        return parts[0]
    half = len(parts) // 2
    return sum_pairs(parts[:half]) + sum_pairs(parts[half:])


def gather_relative(array, axis, groups):
    return gather_more(array[None], axis, groups)


def gather_more(array, axis, groups):
    for masks in groups:
        array = jnp.concatenate([array] + [from_peer(array, axis, mask) for mask in masks], axis=0)
    return array


BRICK_GROUPS = ((1,), (2, 4, 6), (8,))
ALL_GROUPS = ((1,), (2, 4, 6), (8, 16, 24), (32, 64, 96))


def three_parts(array):
    high = array.astype(jnp.bfloat16).astype(jnp.float32)
    rest = array - high
    middle = rest.astype(jnp.bfloat16).astype(jnp.float32)
    return high, middle, rest - middle


def two_parts(array):
    high = array.astype(jnp.bfloat16)
    return high, (array - high.astype(jnp.float32)).astype(jnp.bfloat16)


def factor_into(gram, work_ref, upper_ref, inverse_ref):
    size = gram.shape[0]
    rows = lax.broadcasted_iota(jnp.int32, (size, size), 0)
    cols = lax.broadcasted_iota(jnp.int32, (size, size), 1)
    work_ref[:, :size] = gram
    work_ref[:, size:] = jnp.where(rows == cols, 1.0, 0.0)
    panel_row = lax.broadcasted_iota(jnp.int32, (PANEL, size), 0)
    panel_col = lax.broadcasted_iota(jnp.int32, (PANEL, size), 1)
    for start in range(0, size, PANEL):
        stop = start + PANEL
        panel = work_ref[start:stop, :]
        spread = [
            jnp.broadcast_to(panel[:, start + t : start + t + 1], (PANEL, size))
            for t in range(PANEL)
        ]
        pivots = jnp.zeros((PANEL, size), jnp.float32)
        for t in range(PANEL):
            pivot = jnp.broadcast_to(spread[t][t : t + 1, :], (PANEL, size))
            pivots = jnp.where(panel_row == t, pivot, pivots)
            if t == PANEL - 1:
                break
            ratio = jnp.where(panel_row > t, spread[t] * (1.0 / pivot), 0.0)
            for u in range(t + 1, PANEL):
                spread[u] = spread[u] - ratio * jnp.broadcast_to(
                    spread[u][t : t + 1, :], (PANEL, size)
                )
            panel = panel - jnp.concatenate([ratio, ratio], axis=1) * jnp.broadcast_to(
                panel[t : t + 1, :], (PANEL, 2 * size)
            )
        scale = lax.rsqrt(pivots)
        panel = panel * jnp.concatenate([scale, scale], axis=1)
        left = jnp.where(panel_col >= panel_row + start, panel[:, :size], 0.0)
        right = panel[:, size:]
        upper_ref[start:stop, :] = left
        inverse_ref[start:stop, :] = right
        if stop < size:
            high, middle, low = three_parts(jnp.concatenate([left, right], axis=1))
            lhs = [high, high, middle, middle, high, low]
            rhs = [high, middle, high, middle, low, high]
            update = lax.dot_general(
                jnp.concatenate([part[:, :size] for part in lhs], axis=0).astype(jnp.bfloat16),
                jnp.concatenate(rhs, axis=0).astype(jnp.bfloat16),
                (((0,), (0,)), ((), ())),
                preferred_element_type=jnp.float32,
            )
            work_ref[stop:, :] = work_ref[stop:, :] - update[stop:, :]


def repeat_kernel(below_ref, source_ref, cells_ref, out_ref, sems):
    rows = source_ref.shape[0]
    plane = out_ref.shape[1] - rows
    last = cells_ref.shape[0] - plane
    copies = []
    for i in range(out_ref.shape[0]):
        start = pl.multiple_of(jnp.where(below_ref[0] == i, 0, last), 8)
        copies.append(pltpu.make_async_copy(source_ref, out_ref.at[i, :rows], sems.at[0, i]))
        copies.append(
            pltpu.make_async_copy(
                cells_ref.at[pl.ds(start, plane)], out_ref.at[i, rows:], sems.at[1, i]
            )
        )
    for copy in copies:
        copy.start()
    for copy in copies:
        copy.wait()


def contract_three(left, right, left_dim, right_dim):
    left_high, left_low = two_parts(left)
    right_high, right_low = two_parts(right)
    dims = (((left_dim,), (right_dim,)), ((), ()))

    def product(one, other):
        return lax.dot_general(one, other, dims, preferred_element_type=jnp.float32)

    small = product(left_high, right_low) + product(left_low, right_high)
    return product(left_high, right_high) + small


def transport_kernel(nodes_ref, columns_ref, speeds_ref, weights_ref, out_ref):
    groups, _, rank = nodes_ref.shape
    rows = columns_ref.shape[0]
    bricks = out_ref.shape[0]
    factors = [jnp.broadcast_to(columns_ref[:, i : i + 1], (rows, rank)) for i in range(4)]
    sums = [jnp.zeros((rank, rank), jnp.float32) for _ in range(6)]
    vectors = jnp.zeros((8, rank), jnp.float32)
    for group in range(groups):
        nodes = nodes_ref[group, :rows]
        weighted = jnp.concatenate([nodes] + [nodes * factor for factor in factors], axis=1)
        high, low = two_parts(weighted)
        node_high, node_low = high[:, :rank], low[:, :rank]
        product = lax.dot_general(
            jnp.concatenate([node_high, node_high, node_low], axis=0),
            jnp.concatenate([high, low, high], axis=0),
            (((0,), (0,)), ((), ())),
            preferred_element_type=jnp.float32,
        )
        vectors = vectors + contract(weights_ref[group], nodes, 1, 0)
        plain = product[:, :rank]
        speed = jnp.broadcast_to(speeds_ref[group : group + 1, :], (rank, rank))
        sums[0] = sums[0] + jnp.maximum(speed, 0.0) * plain
        sums[1] = sums[1] + jnp.minimum(speed, 0.0) * plain
        for i in range(4):
            sums[2 + i] = sums[2 + i] + product[:, (i + 1) * rank : (i + 2) * rank]
    row = lax.broadcasted_iota(jnp.int32, (rank, rank), 0)
    col = lax.broadcasted_iota(jnp.int32, (rank, rank), 1)
    block_row = lax.broadcasted_iota(jnp.int32, (8, rank), 0)
    height = rank // bricks
    for i in range(3):
        plus, minus = sums[2 * i], sums[2 * i + 1]
        diagonal = jnp.sum(jnp.where(row == col, minus, 0.0), axis=0, keepdims=True)
        vectors = vectors + jnp.where(block_row == 5 + i, diagonal, 0.0)
        packed = jnp.where(col >= row, plus, minus) * WEIGHT_V
        start = 8 + i * height
        out_ref[:, start : start + height, :] = packed.reshape(bricks, height, rank)
    out_ref[:, :8, :] = jnp.broadcast_to((vectors * WEIGHT_V)[None], (bricks, 8, rank))


def maxwell_kernel(
    brick_ref,
    cells_ref,
    integrals_ref,
    nodes_ref,
    first_ref,
    across_ref,
    part_ref,
    line_ref,
    state_ref,
    vectors_ref,
):
    bricks, cells, rank = cells_ref.shape
    groups, rows = nodes_ref.shape[0], across_ref.shape[1]
    total = bricks * cells
    brick = brick_ref[0]
    k_flat = jnp.concatenate([cells_ref[i ^ brick] for i in range(bricks)], axis=0)
    integrals = integrals_ref[0]
    for i in range(1, bricks):
        integrals = integrals + integrals_ref[i]
    height = integrals.shape[0] - 8
    part_ref[:, cells:, :] = jnp.broadcast_to(integrals[8:][None], (bricks, height, rank))
    vectors_ref[...] = integrals[:8]
    moments = contract(integrals[:8], k_flat, 1, 1)
    density, drift, temper = cell_state([moments[i : i + 1] for i in range(5)])
    slope = -0.5 / temper
    amplitude = density * jnp.exp(-1.5 * jnp.log(2.0 * math.pi * temper))
    first = jnp.broadcast_to(first_ref[:, :1], (groups, total))
    line = amplitude * jnp.exp((first - drift[0]) ** 2 * slope)
    state = jnp.concatenate([drift[1], drift[2], slope] + [amplitude] * 5, axis=0)
    state_ref[...] = state
    both = jnp.concatenate([line, state], axis=0).T
    line_cols = both[:, :groups]
    line_ref[...] = line_cols
    distance = (across_ref[0:1, :] - both[:, groups : groups + 1]) ** 2
    distance = distance + (across_ref[1:2, :] - both[:, groups + 1 : groups + 2]) ** 2
    high, low = two_parts(jnp.exp(distance * both[:, groups + 2 : groups + 3]))
    lhs = jnp.concatenate([high, high, low], axis=1)
    result = jnp.zeros((total, rank), jnp.float32)
    for group in range(0, groups, 2):
        node_high, node_low = two_parts(
            jnp.concatenate([nodes_ref[i, :rows] for i in (group, group + 1)], axis=1)
        )
        product = lax.dot_general(
            lhs,
            jnp.concatenate([node_high, node_low, node_high], axis=0),
            (((1,), (0,)), ((), ())),
            preferred_element_type=jnp.float32,
        )
        result = result + line_cols[:, group : group + 1] * product[:, :rank]
        result = result + line_cols[:, group + 1 : group + 2] * product[:, rank:]
    part_ref[:, :cells, :] = result.reshape(bricks, cells, rank)


def products_kernel(
    brick_ref, parts_ref, pieces_ref, chosen_ref, work_ref, *, cells_x, cells_y, cells_z
):
    bricks, _, rank = parts_ref.shape
    height = rank // bricks
    cells = cells_x * cells_y * cells_z
    total = bricks * cells
    advanced = parts_ref[:, :cells, :].reshape(total, rank)
    last_plane = parts_ref[:, cells - cells // cells_x : cells, :].reshape(-1, rank)
    start = pl.multiple_of(brick_ref[0] * height, height)
    chosen_row = lax.broadcasted_iota(jnp.int32, (height, rank), 0) + start
    chosen_col = lax.broadcasted_iota(jnp.int32, (height, rank), 1)
    chosen_ref[...] = contract(jnp.where(chosen_row == chosen_col, 1.0, 0.0), last_plane, 1, 1)
    row = lax.broadcasted_iota(jnp.int32, (total, rank), 0)
    plane = cells_y * cells_z

    def shifted(amount):
        return pltpu.roll(advanced, amount % total, 0)

    along_x = jnp.where(row // plane % cells_x < cells_x - 1, shifted(-plane), 0.0)
    wrap = cells - (cells_y - 1) * cells_z
    along_y = jnp.where(row // cells_z % cells_y > 0, shifted(cells_z), shifted(wrap))
    along_z = jnp.where(row % cells_z > 0, shifted(1), shifted(1 - cells_z))
    left_high, left_low = two_parts(advanced)
    high, low = two_parts(jnp.concatenate([along_x, along_y, along_z], axis=1))
    work_ref[:, :rank] = contract(advanced, advanced, 0, 0)
    work_ref[:, rank:] = lax.dot_general(
        jnp.concatenate([left_high, left_high, left_low], axis=0),
        jnp.concatenate([high, low, high], axis=0),
        (((0,), (0,)), ((), ())),
        preferred_element_type=jnp.float32,
    )
    own = work_ref[pl.ds(start, height), :]
    for i in range(4):
        pieces_ref[i * height : (i + 1) * height, :] = own[:, i * rank : (i + 1) * rank]
    projected = parts_ref[0, cells:, :]
    for i in range(1, bricks):
        projected = projected + parts_ref[i, cells:, :]
    pieces_ref[4 * height :, :] = projected


def back_kernel(parts_ref, line_ref, state_ref, across_ref, out_ref):
    bricks, _, rank = parts_ref.shape
    groups, rows, _ = out_ref.shape
    total = line_ref.shape[0]
    cells = total // bricks
    advanced = parts_ref[:, :cells, :].reshape(total, rank)
    distance = (across_ref[:, 0:1] - state_ref[0:1, :]) ** 2
    distance = distance + (across_ref[:, 1:2] - state_ref[1:2, :]) ** 2
    high, low = two_parts(jnp.exp(distance * state_ref[2:3, :]))
    lhs = jnp.concatenate([high, high, low], axis=1)
    for group in range(0, groups, 2):
        scaled = [line_ref[:, i : i + 1] * advanced for i in (group, group + 1)]
        part_high, part_low = two_parts(jnp.concatenate(scaled, axis=1))
        product = lax.dot_general(
            lhs,
            jnp.concatenate([part_high, part_low, part_high], axis=0),
            (((1,), (0,)), ((), ())),
            preferred_element_type=jnp.float32,
        )
        out_ref[group] = product[:, :rank]
        out_ref[group + 1] = product[:, rank:]


def advance_kernel(
    parts_ref,
    steps_ref,
    cells_ref,
    vectors_ref,
    payload_ref,
    advanced_ref,
    transport_ref,
    *,
    time_step,
):
    cells, rank = cells_ref.shape
    bricks = parts_ref.shape[0]
    height = rank // bricks
    maxwell_proj = parts_ref[0, :cells, :]
    for i in range(1, bricks):
        maxwell_proj = maxwell_proj + parts_ref[i, :cells, :]
    maxwell_proj = maxwell_proj * WEIGHT_V
    flux = jnp.zeros((cells, rank), jnp.float32)
    row = lax.broadcasted_iota(jnp.int32, (rank, rank), 0)
    col = lax.broadcasted_iota(jnp.int32, (rank, rank), 1)
    for i in range(3):
        start = cells + i * height
        packed = parts_ref[:, start : start + height, :].reshape(rank, rank)
        turned = packed.T
        plus = jnp.where(col >= row, packed, turned)
        minus = jnp.where(col < row, packed, turned)
        minus = jnp.where(col == row, vectors_ref[5 + i : 6 + i, :], minus)
        transport_ref[2 * i] = plus
        transport_ref[2 * i + 1] = minus
        flux = flux + contract(steps_ref[2 * i], plus, 1, 0)
        flux = flux + contract(steps_ref[2 * i + 1], minus, 1, 0)
    own = cells_ref[...]
    advanced = own - time_step * flux + COLLIDE * (maxwell_proj - own)
    advanced_ref[...] = advanced
    payload_ref[:, :cells, :] = jnp.broadcast_to(advanced[None], (bricks, cells, rank))
    projected = contract(advanced, maxwell_proj, 0, 0)
    payload_ref[:, cells:, :] = projected.reshape(bricks, height, rank)


def middle_kernel(
    brick_ref,
    pieces_ref,
    transport_ref,
    basis_ref,
    advanced_ref,
    speeds_ref,
    basis_x_ref,
    velocity_ref,
    inverse_ref,
    work_ref,
    upper_ref,
    *,
    lengths,
    time_step,
    weight_x,
):
    bricks, _, rank = pieces_ref.shape
    rows = basis_ref.shape[0]
    height = rank // bricks
    masks = [j ^ brick_ref[0] for j in range(bricks)]
    slots = [((m >> 1) & 3) * 4 + (m & 1) * 2 + (m >> 3) for m in masks]

    def piece(ref, i):
        if ref is transport_ref:
            return ref[i]
        rows_of = [ref[slot, i * height : (i + 1) * height, :] for slot in slots]
        return jnp.concatenate(rows_of, axis=0)

    factor_into(piece(pieces_ref, 0) * weight_x, work_ref, upper_ref, inverse_ref)
    upper, inverse = upper_ref[...], inverse_ref[...]
    basis_x_ref[...] = contract(advanced_ref[...], inverse, 1, 1)
    change = jnp.zeros((rank, rank), jnp.float32)
    turned = []
    for i in range(3):
        shift = piece(pieces_ref, 1 + i) * weight_x
        straight = contract(inverse, shift, 1, 0)
        crossed = contract(inverse, shift, 1, 1)
        if i == 0:
            straight, crossed = crossed, straight
        turned.append(contract(straight, inverse, 1, 1))
        change = change + lengths[i] * (
            contract_three(upper - straight, piece(transport_ref, 2 * i), 1, 0)
            + contract_three(crossed - upper, piece(transport_ref, 2 * i + 1), 1, 0)
        )
    projected = contract(inverse, piece(pieces_ref, 4) * weight_x, 1, 0)
    middle = upper + time_step * change - COLLIDE * (projected - upper)
    now = contract(basis_ref[...], middle, 1, 1)
    drift_sum = jnp.zeros((rows, rank), jnp.float32)
    for i in range(3):
        speed = jnp.broadcast_to(speeds_ref[:, i : i + 1], (rows, rank)) * lengths[i]
        minus = contract_three(now, turned[i], 1, 1)
        plus = contract_three(now, turned[i], 1, 0)
        drift_sum = drift_sum + jnp.maximum(speed, 0.0) * (now - minus)
        drift_sum = drift_sum + jnp.minimum(speed, 0.0) * (plus - now)
    velocity_ref[...] = now - time_step * drift_sum - COLLIDE * now


def update_kernel(back_ref, velocity_ref, inverse_ref, updated_ref, gram_ref, *, weight_x):
    back = back_ref[0]
    for i in range(1, back_ref.shape[0]):
        back = back + back_ref[i]
    back_proj = contract(back * weight_x, inverse_ref[...], 1, 1)
    updated = velocity_ref[...] + COLLIDE * back_proj
    updated_ref[...] = updated
    gram_ref[...] = contract(updated, updated, 0, 0) * WEIGHT_V


def last_kernel(gram_ref, velocity_ref, coupling_ref, basis_ref, work_ref, upper_ref, inverse_ref):
    factor_into(gram_ref[...], work_ref, upper_ref, inverse_ref)
    coupling_ref[...] = upper_ref[...].T
    basis_ref[...] = contract(velocity_ref[...], inverse_ref[...], 1, 1)


def f32(*shape):
    return jax.ShapeDtypeStruct(shape, jnp.float32)


def factor_scratch(rank):
    shapes = ((rank, 2 * rank), (rank, rank), (rank, rank))
    return [pltpu.VMEM(shape, jnp.float32) for shape in shapes]


def local(k_coeffs, v_basis):
    cells_x, cells_y, cells_z, rank = k_coeffs.shape
    cells = cells_x * cells_y * cells_z
    slabs, bricks = lax.axis_size("slab"), lax.axis_size("brick")
    devices = slabs * bricks
    slab, brick = lax.axis_index("slab"), lax.axis_index("brick")
    lengths = (cells_x * slabs, cells_y * bricks, cells_z)
    time_step = CFL / (VMAX * sum(lengths))
    weight_x = 1.0 / (lengths[0] * lengths[1] * lengths[2])
    rows = v_basis.shape[0]
    slab_cells = cells * bricks
    half = slab_cells // cells_x
    height = rank // bricks
    up = [(i, (i + 1) % slabs) for i in range(slabs)]
    own_cells = k_coeffs.reshape(cells, rank)

    own_ids = (slab * bricks + brick) * rows + jnp.arange(rows, dtype=jnp.int32)
    own_velocity = velocities(own_ids)
    ones = jnp.ones_like(own_velocity[0])
    slab_owner = jnp.arange(slabs, dtype=jnp.int32)[:, None] * bricks + brick
    slab_velocity = velocities(slab_owner * rows + jnp.arange(rows, dtype=jnp.int32)[None])
    weights = jnp.stack(
        [jnp.ones_like(slab_velocity[0]), slab_velocity[0], slab_velocity[1], slab_velocity[2]]
        + [jnp.sum(slab_velocity * slab_velocity, axis=0)]
        + [jnp.zeros_like(slab_velocity[0])] * 3,
        axis=1,
    )
    plane = cells // cells_x
    vector_specs = [pl.BlockSpec(memory_space=pltpu.SMEM)]
    whole = pl.BlockSpec(memory_space=pltpu.VMEM)
    nodes = exchange(
        pl.pallas_call(
            repeat_kernel,
            out_shape=f32(slabs, rows + plane, rank),
            in_specs=vector_specs + [whole] * 2,
            out_specs=pl.BlockSpec(memory_space=pl.ANY),
            scratch_shapes=[pltpu.SemaphoreType.DMA((2, slabs))],
            name="repeat",
            compiler_params=pltpu.CompilerParams(vmem_limit_bytes=VMEM_BYTES),
        )(((slab + slabs - 1) % slabs).astype(jnp.int32)[None], v_basis, own_cells),
        "slab",
    )
    k_slab = gather_relative(own_cells, "brick", BRICK_GROUPS)
    below, above = ((slab + shift) % slabs for shift in (slabs - 1, 1))
    k_below, k_above = (
        lax.dynamic_slice(nodes, (peer, rows, 0), (1, plane, rank)).reshape(k_coeffs[:1].shape)
        for peer in (below, above)
    )

    across = velocities(brick * rows + jnp.arange(rows, dtype=jnp.int32))
    columns = [f(across[i]) for i in (1, 2) for f in (lambda v: jnp.maximum(v, 0.0), lambda v: jnp.minimum(v, 0.0))]
    columns = jnp.stack(columns + [jnp.zeros_like(ones)] * 4, axis=1)
    owner = jnp.arange(slabs, dtype=jnp.int32) * bricks + brick
    first_velocity = velocities(owner * rows)[0]
    first_speeds = jnp.broadcast_to(first_velocity[:, None], (slabs, rank))
    transport_part = pl.pallas_call(
        transport_kernel, out_shape=f32(bricks, 8 + 3 * height, rank), name="transport", compiler_params=pltpu.CompilerParams(vmem_limit_bytes=VMEM_BYTES)
    )(nodes, columns, first_speeds, weights)
    integrals = exchange(transport_part, "brick")

    brick_id = brick.astype(jnp.int32)[None]
    payload, line, state, vectors = pl.pallas_call(
        maxwell_kernel,
        out_shape=(
            f32(bricks, cells + 3 * height, rank),
            f32(slab_cells, slabs),
            f32(8, slab_cells),
            f32(8, rank),
        ),
        in_specs=vector_specs + [whole] * 5,
        name="maxwell", compiler_params=pltpu.CompilerParams(vmem_limit_bytes=VMEM_BYTES),
    )(brick_id, k_slab, integrals, nodes, first_speeds, across[1:])
    second = exchange(payload, "brick")

    slab_grid = k_slab.reshape(bricks, cells_x, cells_y, cells_z, rank)
    left = ((brick - 1) % bricks) ^ brick
    right = ((brick + 1) % bricks) ^ brick
    left = lax.dynamic_index_in_dim(slab_grid, left, 0, keepdims=False)
    right = lax.dynamic_index_in_dim(slab_grid, right, 0, keepdims=False)
    lower = [
        jnp.concatenate([k_below, k_coeffs[:-1]], axis=0),
        jnp.concatenate([left[:, -1:], k_coeffs[:, :-1]], axis=1),
        jnp.roll(k_coeffs, 1, axis=2),
    ]
    upper = [
        jnp.concatenate([k_coeffs[1:], k_above], axis=0),
        jnp.concatenate([k_coeffs[:, 1:], right[:, :1]], axis=1),
        jnp.roll(k_coeffs, -1, axis=2),
    ]
    steps = []
    for axis_id in range(3):
        steps.append(((k_coeffs - lower[axis_id]) * lengths[axis_id]).reshape(cells, rank))
        steps.append(((upper[axis_id] - k_coeffs) * lengths[axis_id]).reshape(cells, rank))
    payload, advanced, transport = pl.pallas_call(
        functools.partial(advance_kernel, time_step=time_step),
        out_shape=(
            f32(bricks, cells + height, rank),
            f32(cells, rank),
            f32(6, rank, rank),
        ),
        name="advance", compiler_params=pltpu.CompilerParams(vmem_limit_bytes=VMEM_BYTES),
    )(second, jnp.stack(steps), own_cells, vectors)
    third = exchange(payload, "brick")

    pieces, chosen = pl.pallas_call(
        functools.partial(products_kernel, cells_x=cells_x, cells_y=cells_y, cells_z=cells_z),
        out_shape=(f32(5 * height, rank), f32(height, half)),
        in_specs=vector_specs + [whole],
        scratch_shapes=[pltpu.VMEM((rank, 4 * rank), jnp.float32)],
        name="products",
        compiler_params=pltpu.CompilerParams(vmem_limit_bytes=VMEM_BYTES),
    )(brick_id, third)
    chosen, third_after = lax.optimization_barrier((chosen, third))
    chosen_below = lax.ppermute(chosen, "slab", up)
    first_plane = third[:, : cells // cells_x].reshape(half, rank)

    back = pl.pallas_call(back_kernel, out_shape=f32(slabs, rows, rank), name="back", compiler_params=pltpu.CompilerParams(vmem_limit_bytes=VMEM_BYTES))(
        third_after, line, state, across[1:].T
    )

    pieces = pieces + jnp.pad(
        contract(chosen_below, first_plane, 1, 0), ((height, 3 * height), (0, 0))
    )
    pieces, back = lax.optimization_barrier((pieces, back))
    fourth = exchange(back, "slab")
    both = ("slab", "brick")
    lower_x, upper_x, cross_x = (from_peer(pieces, both, mask) for mask in (8, 16, 24))
    reduced = jnp.stack([pieces + upper_x, lower_x + cross_x])
    reduced = sum_over(reduced, both, ((32, 64, 96),))
    reduced = gather_more(reduced, both, ((1,), (2, 4, 6)))

    speeds = jnp.stack(list(own_velocity) + [jnp.zeros_like(ones)] * 5, axis=1)
    basis_new, velocity_part, inverse = pl.pallas_call(
        functools.partial(
            middle_kernel, lengths=lengths, time_step=time_step, weight_x=weight_x
        ),
        out_shape=(f32(cells, rank), f32(rows, rank), f32(rank, rank)),
        in_specs=vector_specs + [whole] * 5,
        scratch_shapes=factor_scratch(rank)[:2],
        name="middle",
        compiler_params=pltpu.CompilerParams(vmem_limit_bytes=VMEM_BYTES),
    )(brick_id, reduced, transport, v_basis, advanced, speeds)
    velocity_new, gram_part = pl.pallas_call(
        functools.partial(update_kernel, weight_x=weight_x),
        out_shape=(f32(rows, rank), f32(rank, rank)),
        name="update",
        compiler_params=pltpu.CompilerParams(vmem_limit_bytes=VMEM_BYTES),
    )(fourth, velocity_part, inverse)
    gram_v = sum_over(gram_part, ("slab", "brick"), ALL_GROUPS)
    coupling, vbasis_new = pl.pallas_call(
        last_kernel,
        out_shape=(f32(rank, rank), f32(rows, rank)),
        scratch_shapes=factor_scratch(rank),
        name="last", compiler_params=pltpu.CompilerParams(vmem_limit_bytes=VMEM_BYTES),
    )(gram_v, velocity_new)
    return (basis_new.reshape(cells_x, cells_y, cells_z, rank), coupling, vbasis_new)


def solution(mesh):
    placed = (P("slab", "brick", None, None), P(("slab", "brick"), None))
    return jax.shard_map(
        local,
        mesh=mesh,
        in_specs=placed,
        out_specs=(P("slab", "brick", None, None), P(), P(("slab", "brick"), None)),
        check_vma=False,
    )
```

```python
import functools
import math

import jax
import jax.numpy as jnp
from jax import lax
from jax.experimental import pallas as pl
from jax.experimental.pallas import tpu as pltpu
from jax.sharding import PartitionSpec as P

NVX = 32


CFL = 0.9
VMAX = 6.0
COLLIDE = 0.3
RHO_MIN = 0.25
TEMP_MIN = 0.25
PRECISE = lax.Precision.HIGHEST
FINE = lax.Precision.HIGH
SPACING = 2.0 * VMAX / NVX
WEIGHT_V = SPACING**3
PANEL = 16
VMEM_BYTES = 24 * 2**20


def contract(left, right, left_dim, right_dim, precision=PRECISE):
    return lax.dot_general(
        left, right, (((left_dim,), (right_dim,)), ((), ())), precision=precision
    )


def exchange(array, axis):
    return lax.all_to_all(array, axis, 0, 0, tiled=True)


def to_all(array, axis):
    copies = lax.axis_size(axis)
    return exchange(jnp.broadcast_to(array[None], (copies,) + array.shape), axis)


def velocities(indices):
    coords = jnp.stack([indices // (NVX * NVX), indices // NVX % NVX, indices % NVX])
    return -VMAX + (coords.astype(jnp.float32) + 0.5) * SPACING


def cell_state(moments):
    density = jnp.maximum(moments[0], RHO_MIN)
    drift = [moments[axis_id] / density for axis_id in (1, 2, 3)]
    square = drift[0] * drift[0] + drift[1] * drift[1] + drift[2] * drift[2]
    temper = jnp.maximum((moments[4] / density - square) / 3.0, TEMP_MIN)
    return density, drift, temper


def from_peer(values, axis, mask):
    axes = axis if isinstance(axis, tuple) else (axis,)
    peers = math.prod(lax.axis_size(name) for name in axes)
    return lax.ppermute(values, axis, [(i, i ^ mask) for i in range(peers)])


def sum_over(array, axis, groups):
    for masks in groups:
        parts = [array] + [from_peer(array, axis, mask) for mask in masks]
        array = sum_pairs(parts)
    return array


def sum_pairs(parts):
    if len(parts) == 1:
        return parts[0]
    half = len(parts) // 2
    return sum_pairs(parts[:half]) + sum_pairs(parts[half:])


def gather_relative(array, axis, groups):
    return gather_more(array[None], axis, groups)


def gather_more(array, axis, groups):
    for masks in groups:
        array = jnp.concatenate([array] + [from_peer(array, axis, mask) for mask in masks], axis=0)
    return array


def slot_of(mask):
    return (mask & 1) * 8 + ((mask >> 1) & 3) * 2 + (mask >> 3)


BRICK_GROUPS = ((8,), (2, 4, 6), (1,))
ALL_GROUPS = ((1,), (2, 4, 6), (8, 16, 24), (32, 64, 96))


def three_parts(array):
    high = array.astype(jnp.bfloat16).astype(jnp.float32)
    rest = array - high
    middle = rest.astype(jnp.bfloat16).astype(jnp.float32)
    return high, middle, rest - middle


def two_parts(array):
    high = array.astype(jnp.bfloat16)
    return high, (array - high.astype(jnp.float32)).astype(jnp.bfloat16)


def factor_into(gram, work_ref, upper_ref, inverse_ref):
    size = gram.shape[0]
    rows = lax.broadcasted_iota(jnp.int32, (size, size), 0)
    cols = lax.broadcasted_iota(jnp.int32, (size, size), 1)
    work_ref[:, :size] = gram
    work_ref[:, size:] = jnp.where(rows == cols, 1.0, 0.0)
    panel_row = lax.broadcasted_iota(jnp.int32, (PANEL, size), 0)
    panel_col = lax.broadcasted_iota(jnp.int32, (PANEL, size), 1)
    for start in range(0, size, PANEL):
        stop = start + PANEL
        panel = work_ref[start:stop, :]
        spread = [
            jnp.broadcast_to(panel[:, start + t : start + t + 1], (PANEL, size))
            for t in range(PANEL)
        ]
        pivots = jnp.zeros((PANEL, size), jnp.float32)
        for t in range(PANEL):
            pivot = jnp.broadcast_to(spread[t][t : t + 1, :], (PANEL, size))
            pivots = jnp.where(panel_row == t, pivot, pivots)
            if t == PANEL - 1:
                break
            ratio = jnp.where(panel_row > t, spread[t] * (1.0 / pivot), 0.0)
            for u in range(t + 1, PANEL):
                spread[u] = spread[u] - ratio * jnp.broadcast_to(
                    spread[u][t : t + 1, :], (PANEL, size)
                )
            panel = panel - jnp.concatenate([ratio, ratio], axis=1) * jnp.broadcast_to(
                panel[t : t + 1, :], (PANEL, 2 * size)
            )
        scale = lax.rsqrt(pivots)
        panel = panel * jnp.concatenate([scale, scale], axis=1)
        left = jnp.where(panel_col >= panel_row + start, panel[:, :size], 0.0)
        right = panel[:, size:]
        upper_ref[start:stop, :] = left
        inverse_ref[start:stop, :] = right
        if stop < size:
            high, middle, low = three_parts(jnp.concatenate([left, right], axis=1))
            lhs = [high, high, middle, middle, high, low]
            rhs = [high, middle, high, middle, low, high]
            update = lax.dot_general(
                jnp.concatenate([part[:, :size] for part in lhs], axis=0).astype(jnp.bfloat16),
                jnp.concatenate(rhs, axis=0).astype(jnp.bfloat16),
                (((0,), (0,)), ((), ())),
                preferred_element_type=jnp.float32,
            )
            work_ref[stop:, :] = work_ref[stop:, :] - update[stop:, :]


def repeat_kernel(below_ref, source_ref, cells_ref, out_ref, sems):
    rows = source_ref.shape[0]
    plane = out_ref.shape[1] - rows
    last = cells_ref.shape[0] - plane
    copies = []
    for i in range(out_ref.shape[0]):
        start = pl.multiple_of(jnp.where(below_ref[0] == i, 0, last), 8)
        copies.append(pltpu.make_async_copy(source_ref, out_ref.at[i, :rows], sems.at[0, i]))
        copies.append(
            pltpu.make_async_copy(
                cells_ref.at[pl.ds(start, plane)], out_ref.at[i, rows:], sems.at[1, i]
            )
        )
    for copy in copies:
        copy.start()
    for copy in copies:
        copy.wait()


def contract_three(left, right, left_dim, right_dim):
    left_high, left_low = two_parts(left)
    right_high, right_low = two_parts(right)
    dims = (((left_dim,), (right_dim,)), ((), ()))

    def product(one, other):
        return lax.dot_general(one, other, dims, preferred_element_type=jnp.float32)

    small = product(left_high, right_low) + product(left_low, right_high)
    return product(left_high, right_high) + small


def transport_kernel(nodes_ref, columns_ref, speeds_ref, weights_ref, out_ref):
    groups, _, rank = nodes_ref.shape
    rows = columns_ref.shape[0]
    bricks = out_ref.shape[0]
    factors = [jnp.broadcast_to(columns_ref[:, i : i + 1], (rows, rank)) for i in range(4)]
    sums = [jnp.zeros((rank, rank), jnp.float32) for _ in range(6)]
    vectors = jnp.zeros((8, rank), jnp.float32)
    for group in range(groups):
        nodes = nodes_ref[group, :rows]
        weighted = jnp.concatenate([nodes] + [nodes * factor for factor in factors], axis=1)
        high, low = two_parts(weighted)
        node_high, node_low = high[:, :rank], low[:, :rank]
        product = lax.dot_general(
            jnp.concatenate([node_high, node_high, node_low], axis=0),
            jnp.concatenate([high, low, high], axis=0),
            (((0,), (0,)), ((), ())),
            preferred_element_type=jnp.float32,
        )
        vectors = vectors + contract(weights_ref[group], nodes, 1, 0)
        plain = product[:, :rank]
        speed = jnp.broadcast_to(speeds_ref[group : group + 1, :], (rank, rank))
        sums[0] = sums[0] + jnp.maximum(speed, 0.0) * plain
        sums[1] = sums[1] + jnp.minimum(speed, 0.0) * plain
        for i in range(4):
            sums[2 + i] = sums[2 + i] + product[:, (i + 1) * rank : (i + 2) * rank]
    row = lax.broadcasted_iota(jnp.int32, (rank, rank), 0)
    col = lax.broadcasted_iota(jnp.int32, (rank, rank), 1)
    block_row = lax.broadcasted_iota(jnp.int32, (8, rank), 0)
    height = rank // bricks
    for i in range(3):
        plus, minus = sums[2 * i], sums[2 * i + 1]
        diagonal = jnp.sum(jnp.where(row == col, minus, 0.0), axis=0, keepdims=True)
        vectors = vectors + jnp.where(block_row == 5 + i, diagonal, 0.0)
        packed = jnp.where(col >= row, plus, minus) * WEIGHT_V
        start = 8 + i * height
        out_ref[:, start : start + height, :] = packed.reshape(bricks, height, rank)
    out_ref[:, :8, :] = jnp.broadcast_to((vectors * WEIGHT_V)[None], (bricks, 8, rank))


def maxwell_kernel(
    brick_ref,
    cells_ref,
    integrals_ref,
    nodes_ref,
    first_ref,
    across_ref,
    part_ref,
    line_ref,
    state_ref,
    vectors_ref,
):
    bricks, cells, rank = cells_ref.shape
    groups, rows = nodes_ref.shape[0], across_ref.shape[1]
    total = bricks * cells
    brick = brick_ref[0]
    k_flat = jnp.concatenate([cells_ref[slot_of(i ^ brick)] for i in range(bricks)], axis=0)
    integrals = integrals_ref[0]
    for i in range(1, bricks):
        integrals = integrals + integrals_ref[i]
    height = integrals.shape[0] - 8
    part_ref[:, cells:, :] = jnp.broadcast_to(integrals[8:][None], (bricks, height, rank))
    vectors_ref[...] = integrals[:8]
    moments = contract(integrals[:8], k_flat, 1, 1)
    density, drift, temper = cell_state([moments[i : i + 1] for i in range(5)])
    slope = -0.5 / temper
    amplitude = density * jnp.exp(-1.5 * jnp.log(2.0 * math.pi * temper))
    first = jnp.broadcast_to(first_ref[:, :1], (groups, total))
    line = amplitude * jnp.exp((first - drift[0]) ** 2 * slope)
    state = jnp.concatenate([drift[1], drift[2], slope] + [amplitude] * 5, axis=0)
    state_ref[...] = state
    both = jnp.concatenate([line, state], axis=0).T
    line_cols = both[:, :groups]
    line_ref[...] = line_cols
    distance = (across_ref[0:1, :] - both[:, groups : groups + 1]) ** 2
    distance = distance + (across_ref[1:2, :] - both[:, groups + 1 : groups + 2]) ** 2
    high, low = two_parts(jnp.exp(distance * both[:, groups + 2 : groups + 3]))
    lhs = jnp.concatenate([high, high, low], axis=1)
    result = jnp.zeros((total, rank), jnp.float32)
    for group in range(0, groups, 2):
        node_high, node_low = two_parts(
            jnp.concatenate([nodes_ref[i, :rows] for i in (group, group + 1)], axis=1)
        )
        product = lax.dot_general(
            lhs,
            jnp.concatenate([node_high, node_low, node_high], axis=0),
            (((1,), (0,)), ((), ())),
            preferred_element_type=jnp.float32,
        )
        result = result + line_cols[:, group : group + 1] * product[:, :rank]
        result = result + line_cols[:, group + 1 : group + 2] * product[:, rank:]
    part_ref[:, :cells, :] = result.reshape(bricks, cells, rank)


def products_kernel(
    brick_ref, parts_ref, pieces_ref, chosen_ref, work_ref, *, cells_x, cells_y, cells_z
):
    bricks, _, rank = parts_ref.shape
    height = rank // bricks
    cells = cells_x * cells_y * cells_z
    total = bricks * cells
    advanced = parts_ref[:, :cells, :].reshape(total, rank)
    last_plane = parts_ref[:, cells - cells // cells_x : cells, :].reshape(-1, rank)
    start = pl.multiple_of(brick_ref[0] * height, height)
    chosen_row = lax.broadcasted_iota(jnp.int32, (height, rank), 0) + start
    chosen_col = lax.broadcasted_iota(jnp.int32, (height, rank), 1)
    chosen_ref[...] = contract(jnp.where(chosen_row == chosen_col, 1.0, 0.0), last_plane, 1, 1)
    row = lax.broadcasted_iota(jnp.int32, (total, rank), 0)
    plane = cells_y * cells_z

    def shifted(amount):
        return pltpu.roll(advanced, amount % total, 0)

    along_x = jnp.where(row // plane % cells_x < cells_x - 1, shifted(-plane), 0.0)
    wrap = cells - (cells_y - 1) * cells_z
    along_y = jnp.where(row // cells_z % cells_y > 0, shifted(cells_z), shifted(wrap))
    along_z = jnp.where(row % cells_z > 0, shifted(1), shifted(1 - cells_z))
    left_high, left_low = two_parts(advanced)
    high, low = two_parts(jnp.concatenate([along_x, along_y, along_z], axis=1))
    work_ref[:, :rank] = contract(advanced, advanced, 0, 0)
    work_ref[:, rank:] = lax.dot_general(
        jnp.concatenate([left_high, left_high, left_low], axis=0),
        jnp.concatenate([high, low, high], axis=0),
        (((0,), (0,)), ((), ())),
        preferred_element_type=jnp.float32,
    )
    own = work_ref[pl.ds(start, height), :]
    for i in range(4):
        pieces_ref[i * height : (i + 1) * height, :] = own[:, i * rank : (i + 1) * rank]
    projected = parts_ref[0, cells:, :]
    for i in range(1, bricks):
        projected = projected + parts_ref[i, cells:, :]
    pieces_ref[4 * height :, :] = projected


def back_kernel(parts_ref, line_ref, state_ref, across_ref, out_ref):
    bricks, _, rank = parts_ref.shape
    groups, rows, _ = out_ref.shape
    total = line_ref.shape[0]
    cells = total // bricks
    advanced = parts_ref[:, :cells, :].reshape(total, rank)
    distance = (across_ref[:, 0:1] - state_ref[0:1, :]) ** 2
    distance = distance + (across_ref[:, 1:2] - state_ref[1:2, :]) ** 2
    high, low = two_parts(jnp.exp(distance * state_ref[2:3, :]))
    lhs = jnp.concatenate([high, high, low], axis=1)
    for group in range(0, groups, 2):
        scaled = [line_ref[:, i : i + 1] * advanced for i in (group, group + 1)]
        part_high, part_low = two_parts(jnp.concatenate(scaled, axis=1))
        product = lax.dot_general(
            lhs,
            jnp.concatenate([part_high, part_low, part_high], axis=0),
            (((1,), (0,)), ((), ())),
            preferred_element_type=jnp.float32,
        )
        out_ref[group] = product[:, :rank]
        out_ref[group + 1] = product[:, rank:]


def advance_kernel(
    parts_ref,
    steps_ref,
    cells_ref,
    vectors_ref,
    payload_ref,
    advanced_ref,
    transport_ref,
    *,
    time_step,
):
    cells, rank = cells_ref.shape
    bricks = parts_ref.shape[0]
    height = rank // bricks
    maxwell_proj = parts_ref[0, :cells, :]
    for i in range(1, bricks):
        maxwell_proj = maxwell_proj + parts_ref[i, :cells, :]
    maxwell_proj = maxwell_proj * WEIGHT_V
    flux = jnp.zeros((cells, rank), jnp.float32)
    row = lax.broadcasted_iota(jnp.int32, (rank, rank), 0)
    col = lax.broadcasted_iota(jnp.int32, (rank, rank), 1)
    for i in range(3):
        start = cells + i * height
        packed = parts_ref[:, start : start + height, :].reshape(rank, rank)
        turned = packed.T
        plus = jnp.where(col >= row, packed, turned)
        minus = jnp.where(col < row, packed, turned)
        minus = jnp.where(col == row, vectors_ref[5 + i : 6 + i, :], minus)
        transport_ref[2 * i] = plus
        transport_ref[2 * i + 1] = minus
        flux = flux + contract(steps_ref[2 * i], plus, 1, 0)
        flux = flux + contract(steps_ref[2 * i + 1], minus, 1, 0)
    own = cells_ref[...]
    advanced = own - time_step * flux + COLLIDE * (maxwell_proj - own)
    advanced_ref[...] = advanced
    payload_ref[:, :cells, :] = jnp.broadcast_to(advanced[None], (bricks, cells, rank))
    projected = contract(advanced, maxwell_proj, 0, 0)
    payload_ref[:, cells:, :] = projected.reshape(bricks, height, rank)


def middle_kernel(
    brick_ref,
    pieces_ref,
    transport_ref,
    basis_ref,
    advanced_ref,
    speeds_ref,
    basis_x_ref,
    velocity_ref,
    inverse_ref,
    work_ref,
    upper_ref,
    *,
    lengths,
    time_step,
    weight_x,
):
    bricks, _, rank = pieces_ref.shape
    rows = basis_ref.shape[0]
    height = rank // bricks
    masks = [j ^ brick_ref[0] for j in range(bricks)]
    slots = [slot_of(mask) for mask in masks]

    def piece(ref, i):
        if ref is transport_ref:
            return ref[i]
        rows_of = [ref[slot, i * height : (i + 1) * height, :] for slot in slots]
        return jnp.concatenate(rows_of, axis=0)

    factor_into(piece(pieces_ref, 0) * weight_x, work_ref, upper_ref, inverse_ref)
    upper, inverse = upper_ref[...], inverse_ref[...]
    basis_x_ref[...] = contract(advanced_ref[...], inverse, 1, 1)
    change = jnp.zeros((rank, rank), jnp.float32)
    turned = []
    for i in range(3):
        shift = piece(pieces_ref, 1 + i) * weight_x
        straight = contract(inverse, shift, 1, 0)
        crossed = contract(inverse, shift, 1, 1)
        if i == 0:
            straight, crossed = crossed, straight
        turned.append(contract(straight, inverse, 1, 1))
        change = change + lengths[i] * (
            contract_three(upper - straight, piece(transport_ref, 2 * i), 1, 0)
            + contract_three(crossed - upper, piece(transport_ref, 2 * i + 1), 1, 0)
        )
    projected = contract(inverse, piece(pieces_ref, 4) * weight_x, 1, 0)
    middle = upper + time_step * change - COLLIDE * (projected - upper)
    now = contract(basis_ref[...], middle, 1, 1)
    drift_sum = jnp.zeros((rows, rank), jnp.float32)
    for i in range(3):
        speed = jnp.broadcast_to(speeds_ref[:, i : i + 1], (rows, rank)) * lengths[i]
        minus = contract_three(now, turned[i], 1, 1)
        plus = contract_three(now, turned[i], 1, 0)
        drift_sum = drift_sum + jnp.maximum(speed, 0.0) * (now - minus)
        drift_sum = drift_sum + jnp.minimum(speed, 0.0) * (plus - now)
    velocity_ref[...] = now - time_step * drift_sum - COLLIDE * now


def update_kernel(back_ref, velocity_ref, inverse_ref, updated_ref, gram_ref, *, weight_x):
    back = back_ref[0]
    for i in range(1, back_ref.shape[0]):
        back = back + back_ref[i]
    back_proj = contract(back * weight_x, inverse_ref[...], 1, 1)
    updated = velocity_ref[...] + COLLIDE * back_proj
    updated_ref[...] = updated
    gram_ref[...] = contract(updated, updated, 0, 0) * WEIGHT_V


def last_kernel(gram_ref, velocity_ref, coupling_ref, basis_ref, work_ref, upper_ref, inverse_ref):
    factor_into(gram_ref[...], work_ref, upper_ref, inverse_ref)
    coupling_ref[...] = upper_ref[...].T
    basis_ref[...] = contract(velocity_ref[...], inverse_ref[...], 1, 1)


def f32(*shape):
    return jax.ShapeDtypeStruct(shape, jnp.float32)


def factor_scratch(rank):
    shapes = ((rank, 2 * rank), (rank, rank), (rank, rank))
    return [pltpu.VMEM(shape, jnp.float32) for shape in shapes]


def local(k_coeffs, v_basis):
    cells_x, cells_y, cells_z, rank = k_coeffs.shape
    cells = cells_x * cells_y * cells_z
    slabs, bricks = lax.axis_size("slab"), lax.axis_size("brick")
    devices = slabs * bricks
    slab, brick = lax.axis_index("slab"), lax.axis_index("brick")
    lengths = (cells_x * slabs, cells_y * bricks, cells_z)
    time_step = CFL / (VMAX * sum(lengths))
    weight_x = 1.0 / (lengths[0] * lengths[1] * lengths[2])
    rows = v_basis.shape[0]
    slab_cells = cells * bricks
    half = slab_cells // cells_x
    height = rank // bricks
    up = [(i, (i + 1) % slabs) for i in range(slabs)]
    own_cells = k_coeffs.reshape(cells, rank)

    own_ids = (slab * bricks + brick) * rows + jnp.arange(rows, dtype=jnp.int32)
    own_velocity = velocities(own_ids)
    ones = jnp.ones_like(own_velocity[0])
    slab_owner = jnp.arange(slabs, dtype=jnp.int32)[:, None] * bricks + brick
    slab_velocity = velocities(slab_owner * rows + jnp.arange(rows, dtype=jnp.int32)[None])
    weights = jnp.stack(
        [jnp.ones_like(slab_velocity[0]), slab_velocity[0], slab_velocity[1], slab_velocity[2]]
        + [jnp.sum(slab_velocity * slab_velocity, axis=0)]
        + [jnp.zeros_like(slab_velocity[0])] * 3,
        axis=1,
    )
    plane = cells // cells_x
    vector_specs = [pl.BlockSpec(memory_space=pltpu.SMEM)]
    whole = pl.BlockSpec(memory_space=pltpu.VMEM)
    nodes = exchange(
        pl.pallas_call(
            repeat_kernel,
            out_shape=f32(slabs, rows + plane, rank),
            in_specs=vector_specs + [whole] * 2,
            out_specs=pl.BlockSpec(memory_space=pl.ANY),
            scratch_shapes=[pltpu.SemaphoreType.DMA((2, slabs))],
            name="repeat",
            compiler_params=pltpu.CompilerParams(vmem_limit_bytes=VMEM_BYTES),
        )(((slab + slabs - 1) % slabs).astype(jnp.int32)[None], v_basis, own_cells),
        "slab",
    )
    k_slab = gather_relative(own_cells, "brick", BRICK_GROUPS)
    below, above = ((slab + shift) % slabs for shift in (slabs - 1, 1))
    k_below, k_above = (
        lax.dynamic_slice(nodes, (peer, rows, 0), (1, plane, rank)).reshape(k_coeffs[:1].shape)
        for peer in (below, above)
    )

    across = velocities(brick * rows + jnp.arange(rows, dtype=jnp.int32))
    columns = [f(across[i]) for i in (1, 2) for f in (lambda v: jnp.maximum(v, 0.0), lambda v: jnp.minimum(v, 0.0))]
    columns = jnp.stack(columns + [jnp.zeros_like(ones)] * 4, axis=1)
    owner = jnp.arange(slabs, dtype=jnp.int32) * bricks + brick
    first_velocity = velocities(owner * rows)[0]
    first_speeds = jnp.broadcast_to(first_velocity[:, None], (slabs, rank))
    transport_part = pl.pallas_call(
        transport_kernel, out_shape=f32(bricks, 8 + 3 * height, rank), name="transport", compiler_params=pltpu.CompilerParams(vmem_limit_bytes=VMEM_BYTES)
    )(nodes, columns, first_speeds, weights)
    integrals = exchange(transport_part, "brick")
    k_slab, _ = lax.optimization_barrier((k_slab, transport_part))

    brick_id = brick.astype(jnp.int32)[None]
    payload, line, state, vectors = pl.pallas_call(
        maxwell_kernel,
        out_shape=(
            f32(bricks, cells + 3 * height, rank),
            f32(slab_cells, slabs),
            f32(8, slab_cells),
            f32(8, rank),
        ),
        in_specs=vector_specs + [whole] * 5,
        name="maxwell", compiler_params=pltpu.CompilerParams(vmem_limit_bytes=VMEM_BYTES),
    )(brick_id, k_slab, integrals, nodes, first_speeds, across[1:])
    second = exchange(payload, "brick")

    slab_grid = k_slab.reshape(bricks, cells_x, cells_y, cells_z, rank)
    left = slot_of(((brick - 1) % bricks) ^ brick)
    right = slot_of(((brick + 1) % bricks) ^ brick)
    left = lax.dynamic_index_in_dim(slab_grid, left, 0, keepdims=False)
    right = lax.dynamic_index_in_dim(slab_grid, right, 0, keepdims=False)
    lower = [
        jnp.concatenate([k_below, k_coeffs[:-1]], axis=0),
        jnp.concatenate([left[:, -1:], k_coeffs[:, :-1]], axis=1),
        jnp.roll(k_coeffs, 1, axis=2),
    ]
    upper = [
        jnp.concatenate([k_coeffs[1:], k_above], axis=0),
        jnp.concatenate([k_coeffs[:, 1:], right[:, :1]], axis=1),
        jnp.roll(k_coeffs, -1, axis=2),
    ]
    steps = []
    for axis_id in range(3):
        steps.append(((k_coeffs - lower[axis_id]) * lengths[axis_id]).reshape(cells, rank))
        steps.append(((upper[axis_id] - k_coeffs) * lengths[axis_id]).reshape(cells, rank))
    payload, advanced, transport = pl.pallas_call(
        functools.partial(advance_kernel, time_step=time_step),
        out_shape=(
            f32(bricks, cells + height, rank),
            f32(cells, rank),
            f32(6, rank, rank),
        ),
        name="advance", compiler_params=pltpu.CompilerParams(vmem_limit_bytes=VMEM_BYTES),
    )(second, jnp.stack(steps), own_cells, vectors)
    third = exchange(payload, "brick")

    pieces, chosen = pl.pallas_call(
        functools.partial(products_kernel, cells_x=cells_x, cells_y=cells_y, cells_z=cells_z),
        out_shape=(f32(5 * height, rank), f32(height, half)),
        in_specs=vector_specs + [whole],
        scratch_shapes=[pltpu.VMEM((rank, 4 * rank), jnp.float32)],
        name="products",
        compiler_params=pltpu.CompilerParams(vmem_limit_bytes=VMEM_BYTES),
    )(brick_id, third)
    chosen, third_after = lax.optimization_barrier((chosen, third))
    chosen_below = lax.ppermute(chosen, "slab", up)
    first_plane = third[:, : cells // cells_x].reshape(half, rank)

    back = pl.pallas_call(back_kernel, out_shape=f32(slabs, rows, rank), name="back", compiler_params=pltpu.CompilerParams(vmem_limit_bytes=VMEM_BYTES))(
        third_after, line, state, across[1:].T
    )

    pieces = pieces + jnp.pad(
        contract(chosen_below, first_plane, 1, 0), ((height, 3 * height), (0, 0))
    )
    pieces, back = lax.optimization_barrier((pieces, back))
    fourth = exchange(back, "slab")
    both = ("slab", "brick")
    lower_x, upper_x, cross_x = (from_peer(pieces, both, mask) for mask in (8, 16, 24))
    reduced = jnp.stack([pieces + upper_x, lower_x + cross_x])
    reduced = sum_over(reduced, both, ((32, 64, 96),))
    reduced = gather_more(reduced, both, ((2, 4, 6), (1,)))

    speeds = jnp.stack(list(own_velocity) + [jnp.zeros_like(ones)] * 5, axis=1)
    basis_new, velocity_part, inverse = pl.pallas_call(
        functools.partial(
            middle_kernel, lengths=lengths, time_step=time_step, weight_x=weight_x
        ),
        out_shape=(f32(cells, rank), f32(rows, rank), f32(rank, rank)),
        in_specs=vector_specs + [whole] * 5,
        scratch_shapes=factor_scratch(rank)[:2],
        name="middle",
        compiler_params=pltpu.CompilerParams(vmem_limit_bytes=VMEM_BYTES),
    )(brick_id, reduced, transport, v_basis, advanced, speeds)
    velocity_new, gram_part = pl.pallas_call(
        functools.partial(update_kernel, weight_x=weight_x),
        out_shape=(f32(rows, rank), f32(rank, rank)),
        name="update",
        compiler_params=pltpu.CompilerParams(vmem_limit_bytes=VMEM_BYTES),
    )(fourth, velocity_part, inverse)
    gram_v = sum_over(gram_part, ("slab", "brick"), ALL_GROUPS)
    coupling, vbasis_new = pl.pallas_call(
        last_kernel,
        out_shape=(f32(rank, rank), f32(rows, rank)),
        scratch_shapes=factor_scratch(rank),
        name="last", compiler_params=pltpu.CompilerParams(vmem_limit_bytes=VMEM_BYTES),
    )(gram_v, velocity_new)
    return (basis_new.reshape(cells_x, cells_y, cells_z, rank), coupling, vbasis_new)


def solution(mesh):
    placed = (P("slab", "brick", None, None), P(("slab", "brick"), None))
    return jax.shard_map(
        local,
        mesh=mesh,
        in_specs=placed,
        out_specs=(P("slab", "brick", None, None), P(), P(("slab", "brick"), None)),
        check_vma=False,
    )
```

```python
import functools
import math

import jax
import jax.numpy as jnp
from jax import lax
from jax.experimental import pallas as pl
from jax.experimental.pallas import tpu as pltpu
from jax.sharding import PartitionSpec as P

NVX = 32


CFL = 0.9
VMAX = 6.0
COLLIDE = 0.3
RHO_MIN = 0.25
TEMP_MIN = 0.25
PRECISE = lax.Precision.HIGHEST
FINE = lax.Precision.HIGH
SPACING = 2.0 * VMAX / NVX
WEIGHT_V = SPACING**3
PANEL = 16
VMEM_BYTES = 24 * 2**20


def contract(left, right, left_dim, right_dim, precision=PRECISE):
    return lax.dot_general(
        left, right, (((left_dim,), (right_dim,)), ((), ())), precision=precision
    )


def exchange(array, axis):
    return lax.all_to_all(array, axis, 0, 0, tiled=True)


def to_all(array, axis):
    copies = lax.axis_size(axis)
    return exchange(jnp.broadcast_to(array[None], (copies,) + array.shape), axis)


def velocities(indices):
    coords = jnp.stack([indices // (NVX * NVX), indices // NVX % NVX, indices % NVX])
    return -VMAX + (coords.astype(jnp.float32) + 0.5) * SPACING


def cell_state(moments):
    density = jnp.maximum(moments[0], RHO_MIN)
    drift = [moments[axis_id] / density for axis_id in (1, 2, 3)]
    square = drift[0] * drift[0] + drift[1] * drift[1] + drift[2] * drift[2]
    temper = jnp.maximum((moments[4] / density - square) / 3.0, TEMP_MIN)
    return density, drift, temper


def from_peer(values, axis, mask):
    axes = axis if isinstance(axis, tuple) else (axis,)
    peers = math.prod(lax.axis_size(name) for name in axes)
    return lax.ppermute(values, axis, [(i, i ^ mask) for i in range(peers)])


def sum_over(array, axis, groups):
    for masks in groups:
        parts = [array] + [from_peer(array, axis, mask) for mask in masks]
        array = sum_pairs(parts)
    return array


def sum_pairs(parts):
    if len(parts) == 1:
        return parts[0]
    half = len(parts) // 2
    return sum_pairs(parts[:half]) + sum_pairs(parts[half:])


def gather_relative(array, axis, groups):
    return gather_more(array[None], axis, groups)


def gather_more(array, axis, groups):
    for masks in groups:
        array = jnp.concatenate([array] + [from_peer(array, axis, mask) for mask in masks], axis=0)
    return array


BRICK_GROUPS = ((1,), (2, 4, 6), (8,))
ALL_GROUPS = ((1,), (2, 4, 6), (8, 16, 24), (32, 64, 96))


def three_parts(array):
    high = array.astype(jnp.bfloat16).astype(jnp.float32)
    rest = array - high
    middle = rest.astype(jnp.bfloat16).astype(jnp.float32)
    return high, middle, rest - middle


def two_parts(array):
    high = array.astype(jnp.bfloat16)
    return high, (array - high.astype(jnp.float32)).astype(jnp.bfloat16)


def factor_into(gram, work_ref, upper_ref, inverse_ref):
    size = gram.shape[0]
    rows = lax.broadcasted_iota(jnp.int32, (size, size), 0)
    cols = lax.broadcasted_iota(jnp.int32, (size, size), 1)
    work_ref[:, :size] = gram
    work_ref[:, size:] = jnp.where(rows == cols, 1.0, 0.0)
    panel_row = lax.broadcasted_iota(jnp.int32, (PANEL, size), 0)
    panel_col = lax.broadcasted_iota(jnp.int32, (PANEL, size), 1)
    for start in range(0, size, PANEL):
        stop = start + PANEL
        panel = work_ref[start:stop, :]
        spread = [
            jnp.broadcast_to(panel[:, start + t : start + t + 1], (PANEL, size))
            for t in range(PANEL)
        ]
        pivots = jnp.zeros((PANEL, size), jnp.float32)
        for t in range(PANEL):
            pivot = jnp.broadcast_to(spread[t][t : t + 1, :], (PANEL, size))
            pivots = jnp.where(panel_row == t, pivot, pivots)
            if t == PANEL - 1:
                break
            ratio = jnp.where(panel_row > t, spread[t] * (1.0 / pivot), 0.0)
            for u in range(t + 1, PANEL):
                spread[u] = spread[u] - ratio * jnp.broadcast_to(
                    spread[u][t : t + 1, :], (PANEL, size)
                )
            panel = panel - jnp.concatenate([ratio, ratio], axis=1) * jnp.broadcast_to(
                panel[t : t + 1, :], (PANEL, 2 * size)
            )
        scale = lax.rsqrt(pivots)
        panel = panel * jnp.concatenate([scale, scale], axis=1)
        left = jnp.where(panel_col >= panel_row + start, panel[:, :size], 0.0)
        right = panel[:, size:]
        upper_ref[start:stop, :] = left
        inverse_ref[start:stop, :] = right
        if stop < size:
            high, middle, low = three_parts(jnp.concatenate([left, right], axis=1))
            lhs = [high, high, middle, middle, high, low]
            rhs = [high, middle, high, middle, low, high]
            update = lax.dot_general(
                jnp.concatenate([part[:, :size] for part in lhs], axis=0).astype(jnp.bfloat16),
                jnp.concatenate(rhs, axis=0).astype(jnp.bfloat16),
                (((0,), (0,)), ((), ())),
                preferred_element_type=jnp.float32,
            )
            work_ref[stop:, :] = work_ref[stop:, :] - update[stop:, :]


def repeat_kernel(below_ref, source_ref, cells_ref, out_ref, sems):
    rows = source_ref.shape[0]
    plane = out_ref.shape[1] - rows
    last = cells_ref.shape[0] - plane
    copies = []
    for i in range(out_ref.shape[0]):
        start = pl.multiple_of(jnp.where(below_ref[0] == i, 0, last), 8)
        copies.append(pltpu.make_async_copy(source_ref, out_ref.at[i, :rows], sems.at[0, i]))
        copies.append(
            pltpu.make_async_copy(
                cells_ref.at[pl.ds(start, plane)], out_ref.at[i, rows:], sems.at[1, i]
            )
        )
    for copy in copies:
        copy.start()
    for copy in copies:
        copy.wait()


def contract_three(left, right, left_dim, right_dim):
    left_high, left_low = two_parts(left)
    right_high, right_low = two_parts(right)
    dims = (((left_dim,), (right_dim,)), ((), ()))

    def product(one, other):
        return lax.dot_general(one, other, dims, preferred_element_type=jnp.float32)

    small = product(left_high, right_low) + product(left_low, right_high)
    return product(left_high, right_high) + small


def transport_kernel(nodes_ref, columns_ref, speeds_ref, weights_ref, out_ref):
    groups, _, rank = nodes_ref.shape
    rows = columns_ref.shape[0]
    bricks = out_ref.shape[0]
    factors = [jnp.broadcast_to(columns_ref[:, i : i + 1], (rows, rank)) for i in range(4)]
    sums = [jnp.zeros((rank, rank), jnp.float32) for _ in range(6)]
    vectors = jnp.zeros((8, rank), jnp.float32)
    for group in range(groups):
        nodes = nodes_ref[group, :rows]
        weighted = jnp.concatenate([nodes] + [nodes * factor for factor in factors], axis=1)
        high, low = two_parts(weighted)
        node_high, node_low = high[:, :rank], low[:, :rank]
        product = lax.dot_general(
            jnp.concatenate([node_high, node_high, node_low], axis=0),
            jnp.concatenate([high, low, high], axis=0),
            (((0,), (0,)), ((), ())),
            preferred_element_type=jnp.float32,
        )
        vectors = vectors + contract(weights_ref[group], nodes, 1, 0)
        plain = product[:, :rank]
        speed = jnp.broadcast_to(speeds_ref[group : group + 1, :], (rank, rank))
        sums[0] = sums[0] + jnp.maximum(speed, 0.0) * plain
        sums[1] = sums[1] + jnp.minimum(speed, 0.0) * plain
        for i in range(4):
            sums[2 + i] = sums[2 + i] + product[:, (i + 1) * rank : (i + 2) * rank]
    row = lax.broadcasted_iota(jnp.int32, (rank, rank), 0)
    col = lax.broadcasted_iota(jnp.int32, (rank, rank), 1)
    block_row = lax.broadcasted_iota(jnp.int32, (8, rank), 0)
    height = rank // bricks
    for i in range(3):
        plus, minus = sums[2 * i], sums[2 * i + 1]
        diagonal = jnp.sum(jnp.where(row == col, minus, 0.0), axis=0, keepdims=True)
        vectors = vectors + jnp.where(block_row == 5 + i, diagonal, 0.0)
        packed = jnp.where(col >= row, plus, minus) * WEIGHT_V
        start = 8 + i * height
        out_ref[:, start : start + height, :] = packed.reshape(bricks, height, rank)
    out_ref[:, :8, :] = jnp.broadcast_to((vectors * WEIGHT_V)[None], (bricks, 8, rank))


def maxwell_kernel(
    brick_ref,
    cells_ref,
    integrals_ref,
    nodes_ref,
    first_ref,
    across_ref,
    part_ref,
    line_ref,
    state_ref,
    vectors_ref,
):
    bricks, cells, rank = cells_ref.shape
    groups, rows = nodes_ref.shape[0], across_ref.shape[1]
    total = bricks * cells
    brick = brick_ref[0]
    k_flat = jnp.concatenate([cells_ref[i ^ brick] for i in range(bricks)], axis=0)
    integrals = integrals_ref[0]
    for i in range(1, bricks):
        integrals = integrals + integrals_ref[i]
    height = integrals.shape[0] - 8
    part_ref[:, cells:, :] = jnp.broadcast_to(integrals[8:][None], (bricks, height, rank))
    vectors_ref[...] = integrals[:8]
    moments = contract(integrals[:8], k_flat, 1, 1)
    density, drift, temper = cell_state([moments[i : i + 1] for i in range(5)])
    slope = -0.5 / temper
    amplitude = density * jnp.exp(-1.5 * jnp.log(2.0 * math.pi * temper))
    first = jnp.broadcast_to(first_ref[:, :1], (groups, total))
    line = amplitude * jnp.exp((first - drift[0]) ** 2 * slope)
    state = jnp.concatenate([drift[1], drift[2], slope] + [amplitude] * 5, axis=0)
    state_ref[...] = state
    both = jnp.concatenate([line, state], axis=0).T
    line_cols = both[:, :groups]
    line_ref[...] = line_cols
    distance = (across_ref[0:1, :] - both[:, groups : groups + 1]) ** 2
    distance = distance + (across_ref[1:2, :] - both[:, groups + 1 : groups + 2]) ** 2
    high, low = two_parts(jnp.exp(distance * both[:, groups + 2 : groups + 3]))
    lhs = jnp.concatenate([high, high, low], axis=1)
    result = jnp.zeros((total, rank), jnp.float32)
    for group in range(0, groups, 2):
        node_high, node_low = two_parts(
            jnp.concatenate([nodes_ref[i, :rows] for i in (group, group + 1)], axis=1)
        )
        product = lax.dot_general(
            lhs,
            jnp.concatenate([node_high, node_low, node_high], axis=0),
            (((1,), (0,)), ((), ())),
            preferred_element_type=jnp.float32,
        )
        result = result + line_cols[:, group : group + 1] * product[:, :rank]
        result = result + line_cols[:, group + 1 : group + 2] * product[:, rank:]
    part_ref[:, :cells, :] = result.reshape(bricks, cells, rank)


def products_kernel(
    brick_ref, parts_ref, pieces_ref, chosen_ref, work_ref, *, cells_x, cells_y, cells_z
):
    bricks, _, rank = parts_ref.shape
    height = rank // bricks
    cells = cells_x * cells_y * cells_z
    total = bricks * cells
    advanced = parts_ref[:, :cells, :].reshape(total, rank)
    last_plane = parts_ref[:, cells - cells // cells_x : cells, :].reshape(-1, rank)
    start = pl.multiple_of(brick_ref[0] * height, height)
    chosen_row = lax.broadcasted_iota(jnp.int32, (height, rank), 0) + start
    chosen_col = lax.broadcasted_iota(jnp.int32, (height, rank), 1)
    chosen_ref[...] = contract(jnp.where(chosen_row == chosen_col, 1.0, 0.0), last_plane, 1, 1)
    row = lax.broadcasted_iota(jnp.int32, (total, rank), 0)
    plane = cells_y * cells_z

    def shifted(amount):
        return pltpu.roll(advanced, amount % total, 0)

    along_x = jnp.where(row // plane % cells_x < cells_x - 1, shifted(-plane), 0.0)
    wrap = cells - (cells_y - 1) * cells_z
    along_y = jnp.where(row // cells_z % cells_y > 0, shifted(cells_z), shifted(wrap))
    along_z = jnp.where(row % cells_z > 0, shifted(1), shifted(1 - cells_z))
    left_high, left_low = two_parts(advanced)
    high, low = two_parts(jnp.concatenate([along_x, along_y, along_z], axis=1))
    work_ref[:, :rank] = contract(advanced, advanced, 0, 0)
    work_ref[:, rank:] = lax.dot_general(
        jnp.concatenate([left_high, left_high, left_low], axis=0),
        jnp.concatenate([high, low, high], axis=0),
        (((0,), (0,)), ((), ())),
        preferred_element_type=jnp.float32,
    )
    own = work_ref[pl.ds(start, height), :]
    for i in range(4):
        pieces_ref[i * height : (i + 1) * height, :] = own[:, i * rank : (i + 1) * rank]
    projected = parts_ref[0, cells:, :]
    for i in range(1, bricks):
        projected = projected + parts_ref[i, cells:, :]
    pieces_ref[4 * height :, :] = projected


def back_kernel(parts_ref, line_ref, state_ref, across_ref, out_ref):
    bricks, _, rank = parts_ref.shape
    groups, rows, _ = out_ref.shape
    total = line_ref.shape[0]
    cells = total // bricks
    advanced = parts_ref[:, :cells, :].reshape(total, rank)
    distance = (across_ref[:, 0:1] - state_ref[0:1, :]) ** 2
    distance = distance + (across_ref[:, 1:2] - state_ref[1:2, :]) ** 2
    high, low = two_parts(jnp.exp(distance * state_ref[2:3, :]))
    lhs = jnp.concatenate([high, high, low], axis=1)
    for group in range(0, groups, 2):
        scaled = [line_ref[:, i : i + 1] * advanced for i in (group, group + 1)]
        part_high, part_low = two_parts(jnp.concatenate(scaled, axis=1))
        product = lax.dot_general(
            lhs,
            jnp.concatenate([part_high, part_low, part_high], axis=0),
            (((1,), (0,)), ((), ())),
            preferred_element_type=jnp.float32,
        )
        out_ref[group] = product[:, :rank]
        out_ref[group + 1] = product[:, rank:]


def advance_kernel(
    parts_ref,
    steps_ref,
    cells_ref,
    vectors_ref,
    payload_ref,
    advanced_ref,
    transport_ref,
    *,
    time_step,
):
    cells, rank = cells_ref.shape
    bricks = parts_ref.shape[0]
    height = rank // bricks
    maxwell_proj = parts_ref[0, :cells, :]
    for i in range(1, bricks):
        maxwell_proj = maxwell_proj + parts_ref[i, :cells, :]
    maxwell_proj = maxwell_proj * WEIGHT_V
    flux = jnp.zeros((cells, rank), jnp.float32)
    row = lax.broadcasted_iota(jnp.int32, (rank, rank), 0)
    col = lax.broadcasted_iota(jnp.int32, (rank, rank), 1)
    for i in range(3):
        start = cells + i * height
        packed = parts_ref[:, start : start + height, :].reshape(rank, rank)
        turned = packed.T
        plus = jnp.where(col >= row, packed, turned)
        minus = jnp.where(col < row, packed, turned)
        minus = jnp.where(col == row, vectors_ref[5 + i : 6 + i, :], minus)
        transport_ref[2 * i] = plus
        transport_ref[2 * i + 1] = minus
        flux = flux + contract(steps_ref[2 * i], plus, 1, 0)
        flux = flux + contract(steps_ref[2 * i + 1], minus, 1, 0)
    own = cells_ref[...]
    advanced = own - time_step * flux + COLLIDE * (maxwell_proj - own)
    advanced_ref[...] = advanced
    payload_ref[:, :cells, :] = jnp.broadcast_to(advanced[None], (bricks, cells, rank))
    projected = contract(advanced, maxwell_proj, 0, 0)
    payload_ref[:, cells:, :] = projected.reshape(bricks, height, rank)


def middle_kernel(
    brick_ref,
    pieces_ref,
    transport_ref,
    basis_ref,
    advanced_ref,
    speeds_ref,
    basis_x_ref,
    velocity_ref,
    inverse_ref,
    work_ref,
    upper_ref,
    *,
    lengths,
    time_step,
    weight_x,
):
    bricks, _, rank = pieces_ref.shape
    rows = basis_ref.shape[0]
    height = rank // bricks
    masks = [j ^ brick_ref[0] for j in range(bricks)]
    slots = [((m >> 1) & 3) * 4 + (m & 1) * 2 + (m >> 3) for m in masks]

    def piece(ref, i):
        if ref is transport_ref:
            return ref[i]
        rows_of = [ref[slot, i * height : (i + 1) * height, :] for slot in slots]
        return jnp.concatenate(rows_of, axis=0)

    factor_into(piece(pieces_ref, 0) * weight_x, work_ref, upper_ref, inverse_ref)
    upper, inverse = upper_ref[...], inverse_ref[...]
    basis_x_ref[...] = contract(advanced_ref[...], inverse, 1, 1)
    change = jnp.zeros((rank, rank), jnp.float32)
    turned = []
    for i in range(3):
        shift = piece(pieces_ref, 1 + i) * weight_x
        straight = contract(inverse, shift, 1, 0)
        crossed = contract(inverse, shift, 1, 1)
        if i == 0:
            straight, crossed = crossed, straight
        turned.append(contract(straight, inverse, 1, 1))
        change = change + lengths[i] * (
            contract_three(upper - straight, piece(transport_ref, 2 * i), 1, 0)
            + contract_three(crossed - upper, piece(transport_ref, 2 * i + 1), 1, 0)
        )
    projected = contract(inverse, piece(pieces_ref, 4) * weight_x, 1, 0)
    middle = upper + time_step * change - COLLIDE * (projected - upper)
    now = contract(basis_ref[...], middle, 1, 1)
    drift_sum = jnp.zeros((rows, rank), jnp.float32)
    for i in range(3):
        speed = jnp.broadcast_to(speeds_ref[:, i : i + 1], (rows, rank)) * lengths[i]
        minus = contract_three(now, turned[i], 1, 1)
        plus = contract_three(now, turned[i], 1, 0)
        drift_sum = drift_sum + jnp.maximum(speed, 0.0) * (now - minus)
        drift_sum = drift_sum + jnp.minimum(speed, 0.0) * (plus - now)
    velocity_ref[...] = now - time_step * drift_sum - COLLIDE * now


def update_kernel(back_ref, velocity_ref, inverse_ref, updated_ref, gram_ref, *, weight_x):
    back = back_ref[0]
    for i in range(1, back_ref.shape[0]):
        back = back + back_ref[i]
    back_proj = contract(back * weight_x, inverse_ref[...], 1, 1)
    updated = velocity_ref[...] + COLLIDE * back_proj
    updated_ref[...] = updated
    gram_ref[...] = contract(updated, updated, 0, 0) * WEIGHT_V


def last_kernel(gram_ref, velocity_ref, coupling_ref, basis_ref, work_ref, upper_ref, inverse_ref):
    factor_into(gram_ref[...], work_ref, upper_ref, inverse_ref)
    coupling_ref[...] = upper_ref[...].T
    basis_ref[...] = contract(velocity_ref[...], inverse_ref[...], 1, 1)


def f32(*shape):
    return jax.ShapeDtypeStruct(shape, jnp.float32)


def factor_scratch(rank):
    shapes = ((rank, 2 * rank), (rank, rank), (rank, rank))
    return [pltpu.VMEM(shape, jnp.float32) for shape in shapes]


def local(k_coeffs, v_basis):
    cells_x, cells_y, cells_z, rank = k_coeffs.shape
    cells = cells_x * cells_y * cells_z
    slabs, bricks = lax.axis_size("slab"), lax.axis_size("brick")
    devices = slabs * bricks
    slab, brick = lax.axis_index("slab"), lax.axis_index("brick")
    lengths = (cells_x * slabs, cells_y * bricks, cells_z)
    time_step = CFL / (VMAX * sum(lengths))
    weight_x = 1.0 / (lengths[0] * lengths[1] * lengths[2])
    rows = v_basis.shape[0]
    slab_cells = cells * bricks
    half = slab_cells // cells_x
    height = rank // bricks
    up = [(i, (i + 1) % slabs) for i in range(slabs)]
    own_cells = k_coeffs.reshape(cells, rank)

    own_ids = (slab * bricks + brick) * rows + jnp.arange(rows, dtype=jnp.int32)
    own_velocity = velocities(own_ids)
    ones = jnp.ones_like(own_velocity[0])
    slab_owner = jnp.arange(slabs, dtype=jnp.int32)[:, None] * bricks + brick
    slab_velocity = velocities(slab_owner * rows + jnp.arange(rows, dtype=jnp.int32)[None])
    weights = jnp.stack(
        [jnp.ones_like(slab_velocity[0]), slab_velocity[0], slab_velocity[1], slab_velocity[2]]
        + [jnp.sum(slab_velocity * slab_velocity, axis=0)]
        + [jnp.zeros_like(slab_velocity[0])] * 3,
        axis=1,
    )
    plane = cells // cells_x
    vector_specs = [pl.BlockSpec(memory_space=pltpu.SMEM)]
    whole = pl.BlockSpec(memory_space=pltpu.VMEM)
    nodes = exchange(
        pl.pallas_call(
            repeat_kernel,
            out_shape=f32(slabs, rows + plane, rank),
            in_specs=vector_specs + [whole] * 2,
            out_specs=pl.BlockSpec(memory_space=pl.ANY),
            scratch_shapes=[pltpu.SemaphoreType.DMA((2, slabs))],
            name="repeat",
            compiler_params=pltpu.CompilerParams(vmem_limit_bytes=VMEM_BYTES),
        )(((slab + slabs - 1) % slabs).astype(jnp.int32)[None], v_basis, own_cells),
        "slab",
    )
    k_part = gather_relative(own_cells, "brick", BRICK_GROUPS[:2])
    below, above = ((slab + shift) % slabs for shift in (slabs - 1, 1))
    k_below, k_above = (
        lax.dynamic_slice(nodes, (peer, rows, 0), (1, plane, rank)).reshape(k_coeffs[:1].shape)
        for peer in (below, above)
    )

    k_part, nodes = lax.optimization_barrier((k_part, nodes))
    k_slab = gather_more(k_part, "brick", BRICK_GROUPS[2:])

    across = velocities(brick * rows + jnp.arange(rows, dtype=jnp.int32))
    columns = [f(across[i]) for i in (1, 2) for f in (lambda v: jnp.maximum(v, 0.0), lambda v: jnp.minimum(v, 0.0))]
    columns = jnp.stack(columns + [jnp.zeros_like(ones)] * 4, axis=1)
    owner = jnp.arange(slabs, dtype=jnp.int32) * bricks + brick
    first_velocity = velocities(owner * rows)[0]
    first_speeds = jnp.broadcast_to(first_velocity[:, None], (slabs, rank))
    transport_part = pl.pallas_call(
        transport_kernel, out_shape=f32(bricks, 8 + 3 * height, rank), name="transport", compiler_params=pltpu.CompilerParams(vmem_limit_bytes=VMEM_BYTES)
    )(nodes, columns, first_speeds, weights)
    integrals = exchange(transport_part, "brick")

    brick_id = brick.astype(jnp.int32)[None]
    payload, line, state, vectors = pl.pallas_call(
        maxwell_kernel,
        out_shape=(
            f32(bricks, cells + 3 * height, rank),
            f32(slab_cells, slabs),
            f32(8, slab_cells),
            f32(8, rank),
        ),
        in_specs=vector_specs + [whole] * 5,
        name="maxwell", compiler_params=pltpu.CompilerParams(vmem_limit_bytes=VMEM_BYTES),
    )(brick_id, k_slab, integrals, nodes, first_speeds, across[1:])
    second = exchange(payload, "brick")

    slab_grid = k_slab.reshape(bricks, cells_x, cells_y, cells_z, rank)
    left = ((brick - 1) % bricks) ^ brick
    right = ((brick + 1) % bricks) ^ brick
    left = lax.dynamic_index_in_dim(slab_grid, left, 0, keepdims=False)
    right = lax.dynamic_index_in_dim(slab_grid, right, 0, keepdims=False)
    lower = [
        jnp.concatenate([k_below, k_coeffs[:-1]], axis=0),
        jnp.concatenate([left[:, -1:], k_coeffs[:, :-1]], axis=1),
        jnp.roll(k_coeffs, 1, axis=2),
    ]
    upper = [
        jnp.concatenate([k_coeffs[1:], k_above], axis=0),
        jnp.concatenate([k_coeffs[:, 1:], right[:, :1]], axis=1),
        jnp.roll(k_coeffs, -1, axis=2),
    ]
    steps = []
    for axis_id in range(3):
        steps.append(((k_coeffs - lower[axis_id]) * lengths[axis_id]).reshape(cells, rank))
        steps.append(((upper[axis_id] - k_coeffs) * lengths[axis_id]).reshape(cells, rank))
    payload, advanced, transport = pl.pallas_call(
        functools.partial(advance_kernel, time_step=time_step),
        out_shape=(
            f32(bricks, cells + height, rank),
            f32(cells, rank),
            f32(6, rank, rank),
        ),
        name="advance", compiler_params=pltpu.CompilerParams(vmem_limit_bytes=VMEM_BYTES),
    )(second, jnp.stack(steps), own_cells, vectors)
    third = exchange(payload, "brick")

    pieces, chosen = pl.pallas_call(
        functools.partial(products_kernel, cells_x=cells_x, cells_y=cells_y, cells_z=cells_z),
        out_shape=(f32(5 * height, rank), f32(height, half)),
        in_specs=vector_specs + [whole],
        scratch_shapes=[pltpu.VMEM((rank, 4 * rank), jnp.float32)],
        name="products",
        compiler_params=pltpu.CompilerParams(vmem_limit_bytes=VMEM_BYTES),
    )(brick_id, third)
    chosen, third_after = lax.optimization_barrier((chosen, third))
    chosen_below = lax.ppermute(chosen, "slab", up)
    first_plane = third[:, : cells // cells_x].reshape(half, rank)

    back = pl.pallas_call(back_kernel, out_shape=f32(slabs, rows, rank), name="back", compiler_params=pltpu.CompilerParams(vmem_limit_bytes=VMEM_BYTES))(
        third_after, line, state, across[1:].T
    )

    pieces = pieces + jnp.pad(
        contract(chosen_below, first_plane, 1, 0), ((height, 3 * height), (0, 0))
    )
    pieces, back = lax.optimization_barrier((pieces, back))
    fourth = exchange(back, "slab")
    both = ("slab", "brick")
    lower_x, upper_x, cross_x = (from_peer(pieces, both, mask) for mask in (8, 16, 24))
    reduced = jnp.stack([pieces + upper_x, lower_x + cross_x])
    reduced = sum_over(reduced, both, ((32, 64, 96),))
    reduced = gather_more(reduced, both, ((1,), (2, 4, 6)))

    speeds = jnp.stack(list(own_velocity) + [jnp.zeros_like(ones)] * 5, axis=1)
    basis_new, velocity_part, inverse = pl.pallas_call(
        functools.partial(
            middle_kernel, lengths=lengths, time_step=time_step, weight_x=weight_x
        ),
        out_shape=(f32(cells, rank), f32(rows, rank), f32(rank, rank)),
        in_specs=vector_specs + [whole] * 5,
        scratch_shapes=factor_scratch(rank)[:2],
        name="middle",
        compiler_params=pltpu.CompilerParams(vmem_limit_bytes=VMEM_BYTES),
    )(brick_id, reduced, transport, v_basis, advanced, speeds)
    velocity_new, gram_part = pl.pallas_call(
        functools.partial(update_kernel, weight_x=weight_x),
        out_shape=(f32(rows, rank), f32(rank, rank)),
        name="update",
        compiler_params=pltpu.CompilerParams(vmem_limit_bytes=VMEM_BYTES),
    )(fourth, velocity_part, inverse)
    gram_v = sum_over(gram_part, ("slab", "brick"), ALL_GROUPS)
    coupling, vbasis_new = pl.pallas_call(
        last_kernel,
        out_shape=(f32(rank, rank), f32(rows, rank)),
        scratch_shapes=factor_scratch(rank),
        name="last", compiler_params=pltpu.CompilerParams(vmem_limit_bytes=VMEM_BYTES),
    )(gram_v, velocity_new)
    return (basis_new.reshape(cells_x, cells_y, cells_z, rank), coupling, vbasis_new)


def solution(mesh):
    placed = (P("slab", "brick", None, None), P(("slab", "brick"), None))
    return jax.shard_map(
        local,
        mesh=mesh,
        in_specs=placed,
        out_specs=(P("slab", "brick", None, None), P(), P(("slab", "brick"), None)),
        check_vma=False,
    )
```

```python
import functools
import math

import jax
import jax.numpy as jnp
from jax import lax
from jax.experimental import pallas as pl
from jax.experimental.pallas import tpu as pltpu
from jax.sharding import PartitionSpec as P

NVX = 32


CFL = 0.9
VMAX = 6.0
COLLIDE = 0.3
RHO_MIN = 0.25
TEMP_MIN = 0.25
PRECISE = lax.Precision.HIGHEST
FINE = lax.Precision.HIGH
SPACING = 2.0 * VMAX / NVX
WEIGHT_V = SPACING**3
PANEL = 16
VMEM_BYTES = 24 * 2**20


def contract(left, right, left_dim, right_dim, precision=PRECISE):
    return lax.dot_general(
        left, right, (((left_dim,), (right_dim,)), ((), ())), precision=precision
    )


def exchange(array, axis):
    return lax.all_to_all(array, axis, 0, 0, tiled=True)


def to_all(array, axis):
    copies = lax.axis_size(axis)
    return exchange(jnp.broadcast_to(array[None], (copies,) + array.shape), axis)


def velocities(indices):
    coords = jnp.stack([indices // (NVX * NVX), indices // NVX % NVX, indices % NVX])
    return -VMAX + (coords.astype(jnp.float32) + 0.5) * SPACING


def cell_state(moments):
    density = jnp.maximum(moments[0], RHO_MIN)
    drift = [moments[axis_id] / density for axis_id in (1, 2, 3)]
    square = drift[0] * drift[0] + drift[1] * drift[1] + drift[2] * drift[2]
    temper = jnp.maximum((moments[4] / density - square) / 3.0, TEMP_MIN)
    return density, drift, temper


def from_peer(values, axis, mask):
    axes = axis if isinstance(axis, tuple) else (axis,)
    peers = math.prod(lax.axis_size(name) for name in axes)
    return lax.ppermute(values, axis, [(i, i ^ mask) for i in range(peers)])


def sum_over(array, axis, groups):
    for masks in groups:
        parts = [array] + [from_peer(array, axis, mask) for mask in masks]
        array = sum_pairs(parts)
    return array


def sum_pairs(parts):
    if len(parts) == 1:
        return parts[0]
    half = len(parts) // 2
    return sum_pairs(parts[:half]) + sum_pairs(parts[half:])


def gather_relative(array, axis, groups):
    return gather_more(array[None], axis, groups)


def gather_more(array, axis, groups):
    for masks in groups:
        far_first = masks[1:] + masks[:1]
        peers = {mask: from_peer(array, axis, mask) for mask in far_first}
        array = jnp.concatenate([array] + [peers[mask] for mask in masks], axis=0)
    return array


BRICK_GROUPS = ((1,), (2, 4, 6), (8,))
ALL_GROUPS = ((1,), (4, 6, 2), (16, 24, 8), (64, 96, 32))


def three_parts(array):
    high = array.astype(jnp.bfloat16).astype(jnp.float32)
    rest = array - high
    middle = rest.astype(jnp.bfloat16).astype(jnp.float32)
    return high, middle, rest - middle


def two_parts(array):
    high = array.astype(jnp.bfloat16)
    return high, (array - high.astype(jnp.float32)).astype(jnp.bfloat16)


def factor_into(gram, work_ref, upper_ref, inverse_ref):
    size = gram.shape[0]
    rows = lax.broadcasted_iota(jnp.int32, (size, size), 0)
    cols = lax.broadcasted_iota(jnp.int32, (size, size), 1)
    work_ref[:, :size] = gram
    work_ref[:, size:] = jnp.where(rows == cols, 1.0, 0.0)
    panel_row = lax.broadcasted_iota(jnp.int32, (PANEL, size), 0)
    panel_col = lax.broadcasted_iota(jnp.int32, (PANEL, size), 1)
    for start in range(0, size, PANEL):
        stop = start + PANEL
        panel = work_ref[start:stop, :]
        spread = [
            jnp.broadcast_to(panel[:, start + t : start + t + 1], (PANEL, size))
            for t in range(PANEL)
        ]
        pivots = jnp.zeros((PANEL, size), jnp.float32)
        for t in range(PANEL):
            pivot = jnp.broadcast_to(spread[t][t : t + 1, :], (PANEL, size))
            pivots = jnp.where(panel_row == t, pivot, pivots)
            if t == PANEL - 1:
                break
            ratio = jnp.where(panel_row > t, spread[t] * (1.0 / pivot), 0.0)
            for u in range(t + 1, PANEL):
                spread[u] = spread[u] - ratio * jnp.broadcast_to(
                    spread[u][t : t + 1, :], (PANEL, size)
                )
            panel = panel - jnp.concatenate([ratio, ratio], axis=1) * jnp.broadcast_to(
                panel[t : t + 1, :], (PANEL, 2 * size)
            )
        scale = lax.rsqrt(pivots)
        panel = panel * jnp.concatenate([scale, scale], axis=1)
        left = jnp.where(panel_col >= panel_row + start, panel[:, :size], 0.0)
        right = panel[:, size:]
        upper_ref[start:stop, :] = left
        inverse_ref[start:stop, :] = right
        if stop < size:
            high, middle, low = three_parts(jnp.concatenate([left, right], axis=1))
            lhs = [high, high, middle, middle, high, low]
            rhs = [high, middle, high, middle, low, high]
            update = lax.dot_general(
                jnp.concatenate([part[:, :size] for part in lhs], axis=0).astype(jnp.bfloat16),
                jnp.concatenate(rhs, axis=0).astype(jnp.bfloat16),
                (((0,), (0,)), ((), ())),
                preferred_element_type=jnp.float32,
            )
            work_ref[stop:, :] = work_ref[stop:, :] - update[stop:, :]


def repeat_kernel(below_ref, source_ref, cells_ref, out_ref, sems):
    rows = source_ref.shape[0]
    plane = out_ref.shape[1] - rows
    last = cells_ref.shape[0] - plane
    copies = []
    for i in range(out_ref.shape[0]):
        start = pl.multiple_of(jnp.where(below_ref[0] == i, 0, last), 8)
        copies.append(pltpu.make_async_copy(source_ref, out_ref.at[i, :rows], sems.at[0, i]))
        copies.append(
            pltpu.make_async_copy(
                cells_ref.at[pl.ds(start, plane)], out_ref.at[i, rows:], sems.at[1, i]
            )
        )
    for copy in copies:
        copy.start()
    for copy in copies:
        copy.wait()


def contract_three(left, right, left_dim, right_dim):
    left_high, left_low = two_parts(left)
    right_high, right_low = two_parts(right)
    dims = (((left_dim,), (right_dim,)), ((), ()))

    def product(one, other):
        return lax.dot_general(one, other, dims, preferred_element_type=jnp.float32)

    small = product(left_high, right_low) + product(left_low, right_high)
    return product(left_high, right_high) + small


def transport_kernel(nodes_ref, columns_ref, speeds_ref, weights_ref, out_ref):
    groups, _, rank = nodes_ref.shape
    rows = columns_ref.shape[0]
    bricks = out_ref.shape[0]
    factors = [jnp.broadcast_to(columns_ref[:, i : i + 1], (rows, rank)) for i in range(4)]
    sums = [jnp.zeros((rank, rank), jnp.float32) for _ in range(6)]
    vectors = jnp.zeros((8, rank), jnp.float32)
    for group in range(groups):
        nodes = nodes_ref[group, :rows]
        weighted = jnp.concatenate([nodes] + [nodes * factor for factor in factors], axis=1)
        high, low = two_parts(weighted)
        node_high, node_low = high[:, :rank], low[:, :rank]
        product = lax.dot_general(
            jnp.concatenate([node_high, node_high, node_low], axis=0),
            jnp.concatenate([high, low, high], axis=0),
            (((0,), (0,)), ((), ())),
            preferred_element_type=jnp.float32,
        )
        vectors = vectors + contract(weights_ref[group], nodes, 1, 0)
        plain = product[:, :rank]
        speed = jnp.broadcast_to(speeds_ref[group : group + 1, :], (rank, rank))
        sums[0] = sums[0] + jnp.maximum(speed, 0.0) * plain
        sums[1] = sums[1] + jnp.minimum(speed, 0.0) * plain
        for i in range(4):
            sums[2 + i] = sums[2 + i] + product[:, (i + 1) * rank : (i + 2) * rank]
    row = lax.broadcasted_iota(jnp.int32, (rank, rank), 0)
    col = lax.broadcasted_iota(jnp.int32, (rank, rank), 1)
    block_row = lax.broadcasted_iota(jnp.int32, (8, rank), 0)
    height = rank // bricks
    for i in range(3):
        plus, minus = sums[2 * i], sums[2 * i + 1]
        diagonal = jnp.sum(jnp.where(row == col, minus, 0.0), axis=0, keepdims=True)
        vectors = vectors + jnp.where(block_row == 5 + i, diagonal, 0.0)
        packed = jnp.where(col >= row, plus, minus) * WEIGHT_V
        start = 8 + i * height
        out_ref[:, start : start + height, :] = packed.reshape(bricks, height, rank)
    out_ref[:, :8, :] = jnp.broadcast_to((vectors * WEIGHT_V)[None], (bricks, 8, rank))


def maxwell_kernel(
    brick_ref,
    cells_ref,
    integrals_ref,
    nodes_ref,
    first_ref,
    across_ref,
    part_ref,
    line_ref,
    state_ref,
    vectors_ref,
):
    bricks, cells, rank = cells_ref.shape
    groups, rows = nodes_ref.shape[0], across_ref.shape[1]
    total = bricks * cells
    brick = brick_ref[0]
    k_flat = jnp.concatenate([cells_ref[i ^ brick] for i in range(bricks)], axis=0)
    integrals = integrals_ref[0]
    for i in range(1, bricks):
        integrals = integrals + integrals_ref[i]
    height = integrals.shape[0] - 8
    part_ref[:, cells:, :] = jnp.broadcast_to(integrals[8:][None], (bricks, height, rank))
    vectors_ref[...] = integrals[:8]
    moments = contract(integrals[:8], k_flat, 1, 1)
    density, drift, temper = cell_state([moments[i : i + 1] for i in range(5)])
    slope = -0.5 / temper
    amplitude = density * jnp.exp(-1.5 * jnp.log(2.0 * math.pi * temper))
    first = jnp.broadcast_to(first_ref[:, :1], (groups, total))
    line = amplitude * jnp.exp((first - drift[0]) ** 2 * slope)
    state = jnp.concatenate([drift[1], drift[2], slope] + [amplitude] * 5, axis=0)
    state_ref[...] = state
    both = jnp.concatenate([line, state], axis=0).T
    line_cols = both[:, :groups]
    line_ref[...] = line_cols
    distance = (across_ref[0:1, :] - both[:, groups : groups + 1]) ** 2
    distance = distance + (across_ref[1:2, :] - both[:, groups + 1 : groups + 2]) ** 2
    high, low = two_parts(jnp.exp(distance * both[:, groups + 2 : groups + 3]))
    lhs = jnp.concatenate([high, high, low], axis=1)
    result = jnp.zeros((total, rank), jnp.float32)
    for group in range(0, groups, 2):
        node_high, node_low = two_parts(
            jnp.concatenate([nodes_ref[i, :rows] for i in (group, group + 1)], axis=1)
        )
        product = lax.dot_general(
            lhs,
            jnp.concatenate([node_high, node_low, node_high], axis=0),
            (((1,), (0,)), ((), ())),
            preferred_element_type=jnp.float32,
        )
        result = result + line_cols[:, group : group + 1] * product[:, :rank]
        result = result + line_cols[:, group + 1 : group + 2] * product[:, rank:]
    part_ref[:, :cells, :] = result.reshape(bricks, cells, rank)


def products_kernel(
    brick_ref, parts_ref, pieces_ref, chosen_ref, work_ref, *, cells_x, cells_y, cells_z
):
    bricks, _, rank = parts_ref.shape
    height = rank // bricks
    cells = cells_x * cells_y * cells_z
    total = bricks * cells
    advanced = parts_ref[:, :cells, :].reshape(total, rank)
    last_plane = parts_ref[:, cells - cells // cells_x : cells, :].reshape(-1, rank)
    start = pl.multiple_of(brick_ref[0] * height, height)
    chosen_row = lax.broadcasted_iota(jnp.int32, (height, rank), 0) + start
    chosen_col = lax.broadcasted_iota(jnp.int32, (height, rank), 1)
    chosen_ref[...] = contract(jnp.where(chosen_row == chosen_col, 1.0, 0.0), last_plane, 1, 1)
    row = lax.broadcasted_iota(jnp.int32, (total, rank), 0)
    plane = cells_y * cells_z

    def shifted(amount):
        return pltpu.roll(advanced, amount % total, 0)

    along_x = jnp.where(row // plane % cells_x < cells_x - 1, shifted(-plane), 0.0)
    wrap = cells - (cells_y - 1) * cells_z
    along_y = jnp.where(row // cells_z % cells_y > 0, shifted(cells_z), shifted(wrap))
    along_z = jnp.where(row % cells_z > 0, shifted(1), shifted(1 - cells_z))
    left_high, left_low = two_parts(advanced)
    high, low = two_parts(jnp.concatenate([along_x, along_y, along_z], axis=1))
    work_ref[:, :rank] = contract(advanced, advanced, 0, 0)
    work_ref[:, rank:] = lax.dot_general(
        jnp.concatenate([left_high, left_high, left_low], axis=0),
        jnp.concatenate([high, low, high], axis=0),
        (((0,), (0,)), ((), ())),
        preferred_element_type=jnp.float32,
    )
    own = work_ref[pl.ds(start, height), :]
    for i in range(4):
        pieces_ref[i * height : (i + 1) * height, :] = own[:, i * rank : (i + 1) * rank]
    projected = parts_ref[0, cells:, :]
    for i in range(1, bricks):
        projected = projected + parts_ref[i, cells:, :]
    pieces_ref[4 * height :, :] = projected


def back_kernel(parts_ref, line_ref, state_ref, across_ref, out_ref):
    bricks, _, rank = parts_ref.shape
    groups, rows, _ = out_ref.shape
    total = line_ref.shape[0]
    cells = total // bricks
    advanced = parts_ref[:, :cells, :].reshape(total, rank)
    distance = (across_ref[:, 0:1] - state_ref[0:1, :]) ** 2
    distance = distance + (across_ref[:, 1:2] - state_ref[1:2, :]) ** 2
    high, low = two_parts(jnp.exp(distance * state_ref[2:3, :]))
    lhs = jnp.concatenate([high, high, low], axis=1)
    for group in range(0, groups, 2):
        scaled = [line_ref[:, i : i + 1] * advanced for i in (group, group + 1)]
        part_high, part_low = two_parts(jnp.concatenate(scaled, axis=1))
        product = lax.dot_general(
            lhs,
            jnp.concatenate([part_high, part_low, part_high], axis=0),
            (((1,), (0,)), ((), ())),
            preferred_element_type=jnp.float32,
        )
        out_ref[group] = product[:, :rank]
        out_ref[group + 1] = product[:, rank:]


def advance_kernel(
    parts_ref,
    steps_ref,
    cells_ref,
    vectors_ref,
    payload_ref,
    advanced_ref,
    transport_ref,
    *,
    time_step,
):
    cells, rank = cells_ref.shape
    bricks = parts_ref.shape[0]
    height = rank // bricks
    maxwell_proj = parts_ref[0, :cells, :]
    for i in range(1, bricks):
        maxwell_proj = maxwell_proj + parts_ref[i, :cells, :]
    maxwell_proj = maxwell_proj * WEIGHT_V
    flux = jnp.zeros((cells, rank), jnp.float32)
    row = lax.broadcasted_iota(jnp.int32, (rank, rank), 0)
    col = lax.broadcasted_iota(jnp.int32, (rank, rank), 1)
    for i in range(3):
        start = cells + i * height
        packed = parts_ref[:, start : start + height, :].reshape(rank, rank)
        turned = packed.T
        plus = jnp.where(col >= row, packed, turned)
        minus = jnp.where(col < row, packed, turned)
        minus = jnp.where(col == row, vectors_ref[5 + i : 6 + i, :], minus)
        transport_ref[2 * i] = plus
        transport_ref[2 * i + 1] = minus
        flux = flux + contract(steps_ref[2 * i], plus, 1, 0)
        flux = flux + contract(steps_ref[2 * i + 1], minus, 1, 0)
    own = cells_ref[...]
    advanced = own - time_step * flux + COLLIDE * (maxwell_proj - own)
    advanced_ref[...] = advanced
    payload_ref[:, :cells, :] = jnp.broadcast_to(advanced[None], (bricks, cells, rank))
    projected = contract(advanced, maxwell_proj, 0, 0)
    payload_ref[:, cells:, :] = projected.reshape(bricks, height, rank)


def middle_kernel(
    brick_ref,
    pieces_ref,
    transport_ref,
    basis_ref,
    advanced_ref,
    speeds_ref,
    basis_x_ref,
    velocity_ref,
    inverse_ref,
    work_ref,
    upper_ref,
    *,
    lengths,
    time_step,
    weight_x,
):
    bricks, _, rank = pieces_ref.shape
    rows = basis_ref.shape[0]
    height = rank // bricks
    masks = [j ^ brick_ref[0] for j in range(bricks)]
    slots = [((m >> 1) & 3) * 4 + (m & 1) * 2 + (m >> 3) for m in masks]

    def piece(ref, i):
        if ref is transport_ref:
            return ref[i]
        rows_of = [ref[slot, i * height : (i + 1) * height, :] for slot in slots]
        return jnp.concatenate(rows_of, axis=0)

    factor_into(piece(pieces_ref, 0) * weight_x, work_ref, upper_ref, inverse_ref)
    upper, inverse = upper_ref[...], inverse_ref[...]
    basis_x_ref[...] = contract(advanced_ref[...], inverse, 1, 1)
    change = jnp.zeros((rank, rank), jnp.float32)
    turned = []
    for i in range(3):
        shift = piece(pieces_ref, 1 + i) * weight_x
        straight = contract(inverse, shift, 1, 0)
        crossed = contract(inverse, shift, 1, 1)
        if i == 0:
            straight, crossed = crossed, straight
        turned.append(contract(straight, inverse, 1, 1))
        change = change + lengths[i] * (
            contract_three(upper - straight, piece(transport_ref, 2 * i), 1, 0)
            + contract_three(crossed - upper, piece(transport_ref, 2 * i + 1), 1, 0)
        )
    projected = contract(inverse, piece(pieces_ref, 4) * weight_x, 1, 0)
    middle = upper + time_step * change - COLLIDE * (projected - upper)
    now = contract(basis_ref[...], middle, 1, 1)
    drift_sum = jnp.zeros((rows, rank), jnp.float32)
    for i in range(3):
        speed = jnp.broadcast_to(speeds_ref[:, i : i + 1], (rows, rank)) * lengths[i]
        minus = contract_three(now, turned[i], 1, 1)
        plus = contract_three(now, turned[i], 1, 0)
        drift_sum = drift_sum + jnp.maximum(speed, 0.0) * (now - minus)
        drift_sum = drift_sum + jnp.minimum(speed, 0.0) * (plus - now)
    velocity_ref[...] = now - time_step * drift_sum - COLLIDE * now


def update_kernel(back_ref, velocity_ref, inverse_ref, updated_ref, gram_ref, *, weight_x):
    back = back_ref[0]
    for i in range(1, back_ref.shape[0]):
        back = back + back_ref[i]
    back_proj = contract(back * weight_x, inverse_ref[...], 1, 1)
    updated = velocity_ref[...] + COLLIDE * back_proj
    updated_ref[...] = updated
    gram_ref[...] = contract(updated, updated, 0, 0) * WEIGHT_V


def last_kernel(gram_ref, velocity_ref, coupling_ref, basis_ref, work_ref, upper_ref, inverse_ref):
    factor_into(gram_ref[...], work_ref, upper_ref, inverse_ref)
    coupling_ref[...] = upper_ref[...].T
    basis_ref[...] = contract(velocity_ref[...], inverse_ref[...], 1, 1)


def f32(*shape):
    return jax.ShapeDtypeStruct(shape, jnp.float32)


def factor_scratch(rank):
    shapes = ((rank, 2 * rank), (rank, rank), (rank, rank))
    return [pltpu.VMEM(shape, jnp.float32) for shape in shapes]


def local(k_coeffs, v_basis):
    cells_x, cells_y, cells_z, rank = k_coeffs.shape
    cells = cells_x * cells_y * cells_z
    slabs, bricks = lax.axis_size("slab"), lax.axis_size("brick")
    devices = slabs * bricks
    slab, brick = lax.axis_index("slab"), lax.axis_index("brick")
    lengths = (cells_x * slabs, cells_y * bricks, cells_z)
    time_step = CFL / (VMAX * sum(lengths))
    weight_x = 1.0 / (lengths[0] * lengths[1] * lengths[2])
    rows = v_basis.shape[0]
    slab_cells = cells * bricks
    half = slab_cells // cells_x
    height = rank // bricks
    up = [(i, (i + 1) % slabs) for i in range(slabs)]
    own_cells = k_coeffs.reshape(cells, rank)

    own_ids = (slab * bricks + brick) * rows + jnp.arange(rows, dtype=jnp.int32)
    own_velocity = velocities(own_ids)
    ones = jnp.ones_like(own_velocity[0])
    slab_owner = jnp.arange(slabs, dtype=jnp.int32)[:, None] * bricks + brick
    slab_velocity = velocities(slab_owner * rows + jnp.arange(rows, dtype=jnp.int32)[None])
    weights = jnp.stack(
        [jnp.ones_like(slab_velocity[0]), slab_velocity[0], slab_velocity[1], slab_velocity[2]]
        + [jnp.sum(slab_velocity * slab_velocity, axis=0)]
        + [jnp.zeros_like(slab_velocity[0])] * 3,
        axis=1,
    )
    plane = cells // cells_x
    vector_specs = [pl.BlockSpec(memory_space=pltpu.SMEM)]
    whole = pl.BlockSpec(memory_space=pltpu.VMEM)
    nodes = exchange(
        pl.pallas_call(
            repeat_kernel,
            out_shape=f32(slabs, rows + plane, rank),
            in_specs=vector_specs + [whole] * 2,
            out_specs=pl.BlockSpec(memory_space=pl.ANY),
            scratch_shapes=[pltpu.SemaphoreType.DMA((2, slabs))],
            name="repeat",
            compiler_params=pltpu.CompilerParams(vmem_limit_bytes=VMEM_BYTES),
        )(((slab + slabs - 1) % slabs).astype(jnp.int32)[None], v_basis, own_cells),
        "slab",
    )
    k_part = gather_relative(own_cells, "brick", BRICK_GROUPS[:2])
    below, above = ((slab + shift) % slabs for shift in (slabs - 1, 1))
    k_below, k_above = (
        lax.dynamic_slice(nodes, (peer, rows, 0), (1, plane, rank)).reshape(k_coeffs[:1].shape)
        for peer in (below, above)
    )

    k_part, nodes = lax.optimization_barrier((k_part, nodes))
    k_slab = gather_more(k_part, "brick", BRICK_GROUPS[2:])

    across = velocities(brick * rows + jnp.arange(rows, dtype=jnp.int32))
    columns = [f(across[i]) for i in (1, 2) for f in (lambda v: jnp.maximum(v, 0.0), lambda v: jnp.minimum(v, 0.0))]
    columns = jnp.stack(columns + [jnp.zeros_like(ones)] * 4, axis=1)
    owner = jnp.arange(slabs, dtype=jnp.int32) * bricks + brick
    first_velocity = velocities(owner * rows)[0]
    first_speeds = jnp.broadcast_to(first_velocity[:, None], (slabs, rank))
    transport_part = pl.pallas_call(
        transport_kernel, out_shape=f32(bricks, 8 + 3 * height, rank), name="transport", compiler_params=pltpu.CompilerParams(vmem_limit_bytes=VMEM_BYTES)
    )(nodes, columns, first_speeds, weights)
    integrals = exchange(transport_part, "brick")

    brick_id = brick.astype(jnp.int32)[None]
    payload, line, state, vectors = pl.pallas_call(
        maxwell_kernel,
        out_shape=(
            f32(bricks, cells + 3 * height, rank),
            f32(slab_cells, slabs),
            f32(8, slab_cells),
            f32(8, rank),
        ),
        in_specs=vector_specs + [whole] * 5,
        name="maxwell", compiler_params=pltpu.CompilerParams(vmem_limit_bytes=VMEM_BYTES),
    )(brick_id, k_slab, integrals, nodes, first_speeds, across[1:])
    second = exchange(payload, "brick")

    slab_grid = k_slab.reshape(bricks, cells_x, cells_y, cells_z, rank)
    left = ((brick - 1) % bricks) ^ brick
    right = ((brick + 1) % bricks) ^ brick
    left = lax.dynamic_index_in_dim(slab_grid, left, 0, keepdims=False)
    right = lax.dynamic_index_in_dim(slab_grid, right, 0, keepdims=False)
    lower = [
        jnp.concatenate([k_below, k_coeffs[:-1]], axis=0),
        jnp.concatenate([left[:, -1:], k_coeffs[:, :-1]], axis=1),
        jnp.roll(k_coeffs, 1, axis=2),
    ]
    upper = [
        jnp.concatenate([k_coeffs[1:], k_above], axis=0),
        jnp.concatenate([k_coeffs[:, 1:], right[:, :1]], axis=1),
        jnp.roll(k_coeffs, -1, axis=2),
    ]
    steps = []
    for axis_id in range(3):
        steps.append(((k_coeffs - lower[axis_id]) * lengths[axis_id]).reshape(cells, rank))
        steps.append(((upper[axis_id] - k_coeffs) * lengths[axis_id]).reshape(cells, rank))
    payload, advanced, transport = pl.pallas_call(
        functools.partial(advance_kernel, time_step=time_step),
        out_shape=(
            f32(bricks, cells + height, rank),
            f32(cells, rank),
            f32(6, rank, rank),
        ),
        name="advance", compiler_params=pltpu.CompilerParams(vmem_limit_bytes=VMEM_BYTES),
    )(second, jnp.stack(steps), own_cells, vectors)
    third = exchange(payload, "brick")

    pieces, chosen = pl.pallas_call(
        functools.partial(products_kernel, cells_x=cells_x, cells_y=cells_y, cells_z=cells_z),
        out_shape=(f32(5 * height, rank), f32(height, half)),
        in_specs=vector_specs + [whole],
        scratch_shapes=[pltpu.VMEM((rank, 4 * rank), jnp.float32)],
        name="products",
        compiler_params=pltpu.CompilerParams(vmem_limit_bytes=VMEM_BYTES),
    )(brick_id, third)
    chosen, third_after = lax.optimization_barrier((chosen, third))
    chosen_below = lax.ppermute(chosen, "slab", up)
    first_plane = third[:, : cells // cells_x].reshape(half, rank)

    back = pl.pallas_call(back_kernel, out_shape=f32(slabs, rows, rank), name="back", compiler_params=pltpu.CompilerParams(vmem_limit_bytes=VMEM_BYTES))(
        third_after, line, state, across[1:].T
    )

    pieces = pieces + jnp.pad(
        contract(chosen_below, first_plane, 1, 0), ((height, 3 * height), (0, 0))
    )
    pieces, back = lax.optimization_barrier((pieces, back))
    fourth = exchange(back, "slab")
    both = ("slab", "brick")
    lower_x, upper_x, cross_x = (from_peer(pieces, both, mask) for mask in (8, 16, 24))
    reduced = jnp.stack([pieces + upper_x, lower_x + cross_x])
    reduced = sum_over(reduced, both, ((32, 64, 96),))
    reduced = gather_more(reduced, both, ((1,), (2, 4, 6)))

    speeds = jnp.stack(list(own_velocity) + [jnp.zeros_like(ones)] * 5, axis=1)
    basis_new, velocity_part, inverse = pl.pallas_call(
        functools.partial(
            middle_kernel, lengths=lengths, time_step=time_step, weight_x=weight_x
        ),
        out_shape=(f32(cells, rank), f32(rows, rank), f32(rank, rank)),
        in_specs=vector_specs + [whole] * 5,
        scratch_shapes=factor_scratch(rank)[:2],
        name="middle",
        compiler_params=pltpu.CompilerParams(vmem_limit_bytes=VMEM_BYTES),
    )(brick_id, reduced, transport, v_basis, advanced, speeds)
    velocity_new, gram_part = pl.pallas_call(
        functools.partial(update_kernel, weight_x=weight_x),
        out_shape=(f32(rows, rank), f32(rank, rank)),
        name="update",
        compiler_params=pltpu.CompilerParams(vmem_limit_bytes=VMEM_BYTES),
    )(fourth, velocity_part, inverse)
    gram_v = sum_over(gram_part, ("slab", "brick"), ALL_GROUPS)
    coupling, vbasis_new = pl.pallas_call(
        last_kernel,
        out_shape=(f32(rank, rank), f32(rows, rank)),
        scratch_shapes=factor_scratch(rank),
        name="last", compiler_params=pltpu.CompilerParams(vmem_limit_bytes=VMEM_BYTES),
    )(gram_v, velocity_new)
    return (basis_new.reshape(cells_x, cells_y, cells_z, rank), coupling, vbasis_new)


def solution(mesh):
    placed = (P("slab", "brick", None, None), P(("slab", "brick"), None))
    return jax.shard_map(
        local,
        mesh=mesh,
        in_specs=placed,
        out_specs=(P("slab", "brick", None, None), P(), P(("slab", "brick"), None)),
        check_vma=False,
    )
```

```python
import functools
import math

import jax
import jax.numpy as jnp
from jax import lax
from jax.experimental import pallas as pl
from jax.experimental.pallas import tpu as pltpu
from jax.sharding import PartitionSpec as P

NVX = 32


CFL = 0.9
VMAX = 6.0
COLLIDE = 0.3
RHO_MIN = 0.25
TEMP_MIN = 0.25
PRECISE = lax.Precision.HIGHEST
FINE = lax.Precision.HIGH
SPACING = 2.0 * VMAX / NVX
WEIGHT_V = SPACING**3
PANEL = 16
VMEM_BYTES = 24 * 2**20


def contract(left, right, left_dim, right_dim, precision=PRECISE):
    return lax.dot_general(
        left, right, (((left_dim,), (right_dim,)), ((), ())), precision=precision
    )


def exchange(array, axis):
    return lax.all_to_all(array, axis, 0, 0, tiled=True)


def to_all(array, axis):
    copies = lax.axis_size(axis)
    return exchange(jnp.broadcast_to(array[None], (copies,) + array.shape), axis)


def velocities(indices):
    coords = jnp.stack([indices // (NVX * NVX), indices // NVX % NVX, indices % NVX])
    return -VMAX + (coords.astype(jnp.float32) + 0.5) * SPACING


def cell_state(moments):
    density = jnp.maximum(moments[0], RHO_MIN)
    drift = [moments[axis_id] / density for axis_id in (1, 2, 3)]
    square = drift[0] * drift[0] + drift[1] * drift[1] + drift[2] * drift[2]
    temper = jnp.maximum((moments[4] / density - square) / 3.0, TEMP_MIN)
    return density, drift, temper


def from_peer(values, axis, mask):
    axes = axis if isinstance(axis, tuple) else (axis,)
    peers = math.prod(lax.axis_size(name) for name in axes)
    return lax.ppermute(values, axis, [(i, i ^ mask) for i in range(peers)])


def sum_over(array, axis, groups):
    for masks in groups:
        parts = [array] + [from_peer(array, axis, mask) for mask in masks]
        array = sum_pairs(parts)
    return array


def sum_pairs(parts):
    if len(parts) == 1:
        return parts[0]
    half = len(parts) // 2
    return sum_pairs(parts[:half]) + sum_pairs(parts[half:])


def gather_relative(array, axis, groups):
    return gather_more(array[None], axis, groups)


def gather_more(array, axis, groups):
    for masks in groups:
        array = jnp.concatenate([array] + [from_peer(array, axis, mask) for mask in masks], axis=0)
    return array


BRICK_GROUPS = ((1,), (2, 4, 6), (8,))
ALL_GROUPS = ((1,), (4, 6, 2), (16, 24, 8), (64, 96, 32))


def three_parts(array):
    high = array.astype(jnp.bfloat16).astype(jnp.float32)
    rest = array - high
    middle = rest.astype(jnp.bfloat16).astype(jnp.float32)
    return high, middle, rest - middle


def two_parts(array):
    high = array.astype(jnp.bfloat16)
    return high, (array - high.astype(jnp.float32)).astype(jnp.bfloat16)


def factor_into(gram, work_ref, upper_ref, inverse_ref):
    size = gram.shape[0]
    rows = lax.broadcasted_iota(jnp.int32, (size, size), 0)
    cols = lax.broadcasted_iota(jnp.int32, (size, size), 1)
    work_ref[:, :size] = gram
    work_ref[:, size:] = jnp.where(rows == cols, 1.0, 0.0)
    panel_row = lax.broadcasted_iota(jnp.int32, (PANEL, size), 0)
    panel_col = lax.broadcasted_iota(jnp.int32, (PANEL, size), 1)
    for start in range(0, size, PANEL):
        stop = start + PANEL
        panel = work_ref[start:stop, :]
        spread = [
            jnp.broadcast_to(panel[:, start + t : start + t + 1], (PANEL, size))
            for t in range(PANEL)
        ]
        pivots = jnp.zeros((PANEL, size), jnp.float32)
        for t in range(PANEL):
            pivot = jnp.broadcast_to(spread[t][t : t + 1, :], (PANEL, size))
            pivots = jnp.where(panel_row == t, pivot, pivots)
            if t == PANEL - 1:
                break
            ratio = jnp.where(panel_row > t, spread[t] * (1.0 / pivot), 0.0)
            for u in range(t + 1, PANEL):
                spread[u] = spread[u] - ratio * jnp.broadcast_to(
                    spread[u][t : t + 1, :], (PANEL, size)
                )
            panel = panel - jnp.concatenate([ratio, ratio], axis=1) * jnp.broadcast_to(
                panel[t : t + 1, :], (PANEL, 2 * size)
            )
        scale = lax.rsqrt(pivots)
        panel = panel * jnp.concatenate([scale, scale], axis=1)
        left = jnp.where(panel_col >= panel_row + start, panel[:, :size], 0.0)
        right = panel[:, size:]
        upper_ref[start:stop, :] = left
        inverse_ref[start:stop, :] = right
        if stop < size:
            high, middle, low = three_parts(jnp.concatenate([left, right], axis=1))
            lhs = [high, high, middle, middle, high, low]
            rhs = [high, middle, high, middle, low, high]
            update = lax.dot_general(
                jnp.concatenate([part[:, :size] for part in lhs], axis=0).astype(jnp.bfloat16),
                jnp.concatenate(rhs, axis=0).astype(jnp.bfloat16),
                (((0,), (0,)), ((), ())),
                preferred_element_type=jnp.float32,
            )
            work_ref[stop:, :] = work_ref[stop:, :] - update[stop:, :]


def repeat_kernel(below_ref, source_ref, cells_ref, out_ref, nodes_ref, planes_ref, sems):
    rows = source_ref.shape[0]
    plane = out_ref.shape[1] - rows
    last = cells_ref.shape[0] - plane
    groups = out_ref.shape[0]
    fetch_nodes = pltpu.make_async_copy(source_ref, nodes_ref, sems.at[0, groups])
    fetch_planes = pltpu.make_async_copy(cells_ref, planes_ref, sems.at[1, groups])
    fetch_nodes.start()
    fetch_planes.start()
    to_nodes, to_planes = [], []
    for i in range(groups):
        start = pl.multiple_of(jnp.where(below_ref[0] == i, 0, last), 8)
        to_nodes.append(pltpu.make_async_copy(nodes_ref, out_ref.at[i, :rows], sems.at[0, i]))
        to_planes.append(
            pltpu.make_async_copy(
                planes_ref.at[pl.ds(start, plane)], out_ref.at[i, rows:], sems.at[1, i]
            )
        )
    fetch_nodes.wait()
    for copy in to_nodes:
        copy.start()
    fetch_planes.wait()
    for copy in to_planes:
        copy.start()
    for copy in to_nodes + to_planes:
        copy.wait()


def contract_three(left, right, left_dim, right_dim):
    left_high, left_low = two_parts(left)
    right_high, right_low = two_parts(right)
    dims = (((left_dim,), (right_dim,)), ((), ()))

    def product(one, other):
        return lax.dot_general(one, other, dims, preferred_element_type=jnp.float32)

    small = product(left_high, right_low) + product(left_low, right_high)
    return product(left_high, right_high) + small


def transport_kernel(nodes_ref, columns_ref, speeds_ref, weights_ref, out_ref):
    groups, _, rank = nodes_ref.shape
    rows = columns_ref.shape[0]
    bricks = out_ref.shape[0]
    factors = [jnp.broadcast_to(columns_ref[:, i : i + 1], (rows, rank)) for i in range(4)]
    sums = [jnp.zeros((rank, rank), jnp.float32) for _ in range(6)]
    vectors = jnp.zeros((8, rank), jnp.float32)
    for group in range(groups):
        nodes = nodes_ref[group, :rows]
        weighted = jnp.concatenate([nodes] + [nodes * factor for factor in factors], axis=1)
        high, low = two_parts(weighted)
        node_high, node_low = high[:, :rank], low[:, :rank]
        product = lax.dot_general(
            jnp.concatenate([node_high, node_high, node_low], axis=0),
            jnp.concatenate([high, low, high], axis=0),
            (((0,), (0,)), ((), ())),
            preferred_element_type=jnp.float32,
        )
        vectors = vectors + contract(weights_ref[group], nodes, 1, 0)
        plain = product[:, :rank]
        speed = jnp.broadcast_to(speeds_ref[group : group + 1, :], (rank, rank))
        sums[0] = sums[0] + jnp.maximum(speed, 0.0) * plain
        sums[1] = sums[1] + jnp.minimum(speed, 0.0) * plain
        for i in range(4):
            sums[2 + i] = sums[2 + i] + product[:, (i + 1) * rank : (i + 2) * rank]
    row = lax.broadcasted_iota(jnp.int32, (rank, rank), 0)
    col = lax.broadcasted_iota(jnp.int32, (rank, rank), 1)
    block_row = lax.broadcasted_iota(jnp.int32, (8, rank), 0)
    height = rank // bricks
    for i in range(3):
        plus, minus = sums[2 * i], sums[2 * i + 1]
        diagonal = jnp.sum(jnp.where(row == col, minus, 0.0), axis=0, keepdims=True)
        vectors = vectors + jnp.where(block_row == 5 + i, diagonal, 0.0)
        packed = jnp.where(col >= row, plus, minus) * WEIGHT_V
        start = 8 + i * height
        out_ref[:, start : start + height, :] = packed.reshape(bricks, height, rank)
    out_ref[:, :8, :] = jnp.broadcast_to((vectors * WEIGHT_V)[None], (bricks, 8, rank))


def maxwell_kernel(
    brick_ref,
    cells_ref,
    integrals_ref,
    nodes_ref,
    first_ref,
    across_ref,
    part_ref,
    line_ref,
    state_ref,
    vectors_ref,
):
    bricks, cells, rank = cells_ref.shape
    groups, rows = nodes_ref.shape[0], across_ref.shape[1]
    total = bricks * cells
    brick = brick_ref[0]
    k_flat = jnp.concatenate([cells_ref[i ^ brick] for i in range(bricks)], axis=0)
    integrals = integrals_ref[0]
    for i in range(1, bricks):
        integrals = integrals + integrals_ref[i]
    height = integrals.shape[0] - 8
    part_ref[:, cells:, :] = jnp.broadcast_to(integrals[8:][None], (bricks, height, rank))
    vectors_ref[...] = integrals[:8]
    moments = contract(integrals[:8], k_flat, 1, 1)
    density, drift, temper = cell_state([moments[i : i + 1] for i in range(5)])
    slope = -0.5 / temper
    amplitude = density * jnp.exp(-1.5 * jnp.log(2.0 * math.pi * temper))
    first = jnp.broadcast_to(first_ref[:, :1], (groups, total))
    line = amplitude * jnp.exp((first - drift[0]) ** 2 * slope)
    state = jnp.concatenate([drift[1], drift[2], slope] + [amplitude] * 5, axis=0)
    state_ref[...] = state
    both = jnp.concatenate([line, state], axis=0).T
    line_cols = both[:, :groups]
    line_ref[...] = line_cols
    distance = (across_ref[0:1, :] - both[:, groups : groups + 1]) ** 2
    distance = distance + (across_ref[1:2, :] - both[:, groups + 1 : groups + 2]) ** 2
    high, low = two_parts(jnp.exp(distance * both[:, groups + 2 : groups + 3]))
    lhs = jnp.concatenate([high, high, low], axis=1)
    result = jnp.zeros((total, rank), jnp.float32)
    for group in range(0, groups, 2):
        node_high, node_low = two_parts(
            jnp.concatenate([nodes_ref[i, :rows] for i in (group, group + 1)], axis=1)
        )
        product = lax.dot_general(
            lhs,
            jnp.concatenate([node_high, node_low, node_high], axis=0),
            (((1,), (0,)), ((), ())),
            preferred_element_type=jnp.float32,
        )
        result = result + line_cols[:, group : group + 1] * product[:, :rank]
        result = result + line_cols[:, group + 1 : group + 2] * product[:, rank:]
    part_ref[:, :cells, :] = result.reshape(bricks, cells, rank)


def products_kernel(
    brick_ref, parts_ref, pieces_ref, chosen_ref, work_ref, *, cells_x, cells_y, cells_z
):
    bricks, _, rank = parts_ref.shape
    height = rank // bricks
    cells = cells_x * cells_y * cells_z
    total = bricks * cells
    advanced = parts_ref[:, :cells, :].reshape(total, rank)
    last_plane = parts_ref[:, cells - cells // cells_x : cells, :].reshape(-1, rank)
    start = pl.multiple_of(brick_ref[0] * height, height)
    chosen_row = lax.broadcasted_iota(jnp.int32, (height, rank), 0) + start
    chosen_col = lax.broadcasted_iota(jnp.int32, (height, rank), 1)
    chosen_ref[...] = contract(jnp.where(chosen_row == chosen_col, 1.0, 0.0), last_plane, 1, 1)
    row = lax.broadcasted_iota(jnp.int32, (total, rank), 0)
    plane = cells_y * cells_z

    def shifted(amount):
        return pltpu.roll(advanced, amount % total, 0)

    along_x = jnp.where(row // plane % cells_x < cells_x - 1, shifted(-plane), 0.0)
    wrap = cells - (cells_y - 1) * cells_z
    along_y = jnp.where(row // cells_z % cells_y > 0, shifted(cells_z), shifted(wrap))
    along_z = jnp.where(row % cells_z > 0, shifted(1), shifted(1 - cells_z))
    left_high, left_low = two_parts(advanced)
    high, low = two_parts(jnp.concatenate([along_x, along_y, along_z], axis=1))
    work_ref[:, :rank] = contract(advanced, advanced, 0, 0)
    work_ref[:, rank:] = lax.dot_general(
        jnp.concatenate([left_high, left_high, left_low], axis=0),
        jnp.concatenate([high, low, high], axis=0),
        (((0,), (0,)), ((), ())),
        preferred_element_type=jnp.float32,
    )
    own = work_ref[pl.ds(start, height), :]
    for i in range(4):
        pieces_ref[i * height : (i + 1) * height, :] = own[:, i * rank : (i + 1) * rank]
    projected = parts_ref[0, cells:, :]
    for i in range(1, bricks):
        projected = projected + parts_ref[i, cells:, :]
    pieces_ref[4 * height :, :] = projected


def back_kernel(parts_ref, line_ref, state_ref, across_ref, out_ref):
    bricks, _, rank = parts_ref.shape
    groups, rows, _ = out_ref.shape
    total = line_ref.shape[0]
    cells = total // bricks
    advanced = parts_ref[:, :cells, :].reshape(total, rank)
    distance = (across_ref[:, 0:1] - state_ref[0:1, :]) ** 2
    distance = distance + (across_ref[:, 1:2] - state_ref[1:2, :]) ** 2
    high, low = two_parts(jnp.exp(distance * state_ref[2:3, :]))
    lhs = jnp.concatenate([high, high, low], axis=1)
    for group in range(0, groups, 2):
        scaled = [line_ref[:, i : i + 1] * advanced for i in (group, group + 1)]
        part_high, part_low = two_parts(jnp.concatenate(scaled, axis=1))
        product = lax.dot_general(
            lhs,
            jnp.concatenate([part_high, part_low, part_high], axis=0),
            (((1,), (0,)), ((), ())),
            preferred_element_type=jnp.float32,
        )
        out_ref[group] = product[:, :rank]
        out_ref[group + 1] = product[:, rank:]


def advance_kernel(
    parts_ref,
    steps_ref,
    cells_ref,
    vectors_ref,
    payload_ref,
    advanced_ref,
    transport_ref,
    *,
    time_step,
):
    cells, rank = cells_ref.shape
    bricks = parts_ref.shape[0]
    height = rank // bricks
    maxwell_proj = parts_ref[0, :cells, :]
    for i in range(1, bricks):
        maxwell_proj = maxwell_proj + parts_ref[i, :cells, :]
    maxwell_proj = maxwell_proj * WEIGHT_V
    flux = jnp.zeros((cells, rank), jnp.float32)
    row = lax.broadcasted_iota(jnp.int32, (rank, rank), 0)
    col = lax.broadcasted_iota(jnp.int32, (rank, rank), 1)
    for i in range(3):
        start = cells + i * height
        packed = parts_ref[:, start : start + height, :].reshape(rank, rank)
        turned = packed.T
        plus = jnp.where(col >= row, packed, turned)
        minus = jnp.where(col < row, packed, turned)
        minus = jnp.where(col == row, vectors_ref[5 + i : 6 + i, :], minus)
        transport_ref[2 * i] = plus
        transport_ref[2 * i + 1] = minus
        flux = flux + contract(steps_ref[2 * i], plus, 1, 0)
        flux = flux + contract(steps_ref[2 * i + 1], minus, 1, 0)
    own = cells_ref[...]
    advanced = own - time_step * flux + COLLIDE * (maxwell_proj - own)
    advanced_ref[...] = advanced
    payload_ref[:, :cells, :] = jnp.broadcast_to(advanced[None], (bricks, cells, rank))
    projected = contract(advanced, maxwell_proj, 0, 0)
    payload_ref[:, cells:, :] = projected.reshape(bricks, height, rank)


def middle_kernel(
    brick_ref,
    pieces_ref,
    transport_ref,
    basis_ref,
    advanced_ref,
    speeds_ref,
    basis_x_ref,
    velocity_ref,
    inverse_ref,
    work_ref,
    upper_ref,
    *,
    lengths,
    time_step,
    weight_x,
):
    bricks, _, rank = pieces_ref.shape
    rows = basis_ref.shape[0]
    height = rank // bricks
    masks = [j ^ brick_ref[0] for j in range(bricks)]
    depths = [(m >> 1) & 3 for m in masks]
    depths = [jnp.where(depth == 0, 0, (depth + 1) % 3 + 1) for depth in depths]
    slots = [depth * 4 + (m & 1) * 2 + (m >> 3) for depth, m in zip(depths, masks)]

    def piece(ref, i):
        if ref is transport_ref:
            return ref[i]
        rows_of = [ref[slot, i * height : (i + 1) * height, :] for slot in slots]
        return jnp.concatenate(rows_of, axis=0)

    factor_into(piece(pieces_ref, 0) * weight_x, work_ref, upper_ref, inverse_ref)
    upper, inverse = upper_ref[...], inverse_ref[...]
    basis_x_ref[...] = contract(advanced_ref[...], inverse, 1, 1)
    change = jnp.zeros((rank, rank), jnp.float32)
    turned = []
    for i in range(3):
        shift = piece(pieces_ref, 1 + i) * weight_x
        straight = contract(inverse, shift, 1, 0)
        crossed = contract(inverse, shift, 1, 1)
        if i == 0:
            straight, crossed = crossed, straight
        turned.append(contract(straight, inverse, 1, 1))
        change = change + lengths[i] * (
            contract_three(upper - straight, piece(transport_ref, 2 * i), 1, 0)
            + contract_three(crossed - upper, piece(transport_ref, 2 * i + 1), 1, 0)
        )
    projected = contract(inverse, piece(pieces_ref, 4) * weight_x, 1, 0)
    middle = upper + time_step * change - COLLIDE * (projected - upper)
    now = contract(basis_ref[...], middle, 1, 1)
    drift_sum = jnp.zeros((rows, rank), jnp.float32)
    for i in range(3):
        speed = jnp.broadcast_to(speeds_ref[:, i : i + 1], (rows, rank)) * lengths[i]
        minus = contract_three(now, turned[i], 1, 1)
        plus = contract_three(now, turned[i], 1, 0)
        drift_sum = drift_sum + jnp.maximum(speed, 0.0) * (now - minus)
        drift_sum = drift_sum + jnp.minimum(speed, 0.0) * (plus - now)
    velocity_ref[...] = now - time_step * drift_sum - COLLIDE * now


def update_kernel(back_ref, velocity_ref, inverse_ref, updated_ref, packed_ref, *, weight_x):
    back = back_ref[0]
    for i in range(1, back_ref.shape[0]):
        back = back + back_ref[i]
    back_proj = contract(back * weight_x, inverse_ref[...], 1, 1)
    updated = velocity_ref[...] + COLLIDE * back_proj
    updated_ref[...] = updated
    gram = contract(updated, updated, 0, 0) * WEIGHT_V
    half = gram.shape[0] // 2
    row = lax.broadcasted_iota(jnp.int32, (half, 2 * half), 0)
    col = lax.broadcasted_iota(jnp.int32, (half, 2 * half), 1)
    second = pltpu.roll(gram[half:], half, 1)
    diagonal = jnp.sum(jnp.where(row == col, second, 0.0), axis=0, keepdims=True)
    packed_ref[:half, :] = jnp.where(col < row, second, gram[:half])
    packed_ref[half:, :] = jnp.broadcast_to(diagonal, (8, 2 * half))


def last_kernel(packed_ref, velocity_ref, coupling_ref, basis_ref, work_ref, upper_ref, inverse_ref):
    half = packed_ref.shape[1] // 2
    packed = packed_ref[:half, :]
    row = lax.broadcasted_iota(jnp.int32, (half, 2 * half), 0)
    col = lax.broadcasted_iota(jnp.int32, (half, 2 * half), 1)
    turned = jnp.concatenate([packed, jnp.zeros_like(packed)], axis=0).T[:half]
    second = jnp.where(col < row, packed, turned)
    second = jnp.where(col == row, packed_ref[half : half + 1, :], second)
    gram = jnp.concatenate(
        [jnp.where(col >= row, packed, turned), pltpu.roll(second, half, 1)], axis=0
    )
    factor_into(gram, work_ref, upper_ref, inverse_ref)
    coupling_ref[...] = upper_ref[...].T
    basis_ref[...] = contract(velocity_ref[...], inverse_ref[...], 1, 1)


def f32(*shape):
    return jax.ShapeDtypeStruct(shape, jnp.float32)


def factor_scratch(rank):
    shapes = ((rank, 2 * rank), (rank, rank), (rank, rank))
    return [pltpu.VMEM(shape, jnp.float32) for shape in shapes]


def local(k_coeffs, v_basis):
    cells_x, cells_y, cells_z, rank = k_coeffs.shape
    cells = cells_x * cells_y * cells_z
    slabs, bricks = lax.axis_size("slab"), lax.axis_size("brick")
    devices = slabs * bricks
    slab, brick = lax.axis_index("slab"), lax.axis_index("brick")
    lengths = (cells_x * slabs, cells_y * bricks, cells_z)
    time_step = CFL / (VMAX * sum(lengths))
    weight_x = 1.0 / (lengths[0] * lengths[1] * lengths[2])
    rows = v_basis.shape[0]
    slab_cells = cells * bricks
    half = slab_cells // cells_x
    height = rank // bricks
    up = [(i, (i + 1) % slabs) for i in range(slabs)]
    own_cells = k_coeffs.reshape(cells, rank)

    own_ids = (slab * bricks + brick) * rows + jnp.arange(rows, dtype=jnp.int32)
    own_velocity = velocities(own_ids)
    ones = jnp.ones_like(own_velocity[0])
    slab_owner = jnp.arange(slabs, dtype=jnp.int32)[:, None] * bricks + brick
    slab_velocity = velocities(slab_owner * rows + jnp.arange(rows, dtype=jnp.int32)[None])
    weights = jnp.stack(
        [jnp.ones_like(slab_velocity[0]), slab_velocity[0], slab_velocity[1], slab_velocity[2]]
        + [jnp.sum(slab_velocity * slab_velocity, axis=0)]
        + [jnp.zeros_like(slab_velocity[0])] * 3,
        axis=1,
    )
    plane = cells // cells_x
    vector_specs = [pl.BlockSpec(memory_space=pltpu.SMEM)]
    whole = pl.BlockSpec(memory_space=pltpu.VMEM)
    nodes = exchange(
        pl.pallas_call(
            repeat_kernel,
            out_shape=f32(slabs, rows + plane, rank),
            in_specs=vector_specs + [pl.BlockSpec(memory_space=pltpu.HBM)] * 2,
            out_specs=pl.BlockSpec(memory_space=pl.ANY),
            scratch_shapes=[
                pltpu.VMEM((rows, rank), jnp.float32),
                pltpu.VMEM((cells, rank), jnp.float32),
                pltpu.SemaphoreType.DMA((2, slabs + 1)),
            ],
            name="repeat",
            compiler_params=pltpu.CompilerParams(vmem_limit_bytes=VMEM_BYTES),
        )(((slab + slabs - 1) % slabs).astype(jnp.int32)[None], v_basis, own_cells),
        "slab",
    )
    k_part = gather_relative(own_cells, "brick", BRICK_GROUPS[:2])
    below, above = ((slab + shift) % slabs for shift in (slabs - 1, 1))
    k_below, k_above = (
        lax.dynamic_slice(nodes, (peer, rows, 0), (1, plane, rank)).reshape(k_coeffs[:1].shape)
        for peer in (below, above)
    )

    k_part, nodes = lax.optimization_barrier((k_part, nodes))
    k_slab = gather_more(k_part, "brick", BRICK_GROUPS[2:])

    across = velocities(brick * rows + jnp.arange(rows, dtype=jnp.int32))
    columns = [f(across[i]) for i in (1, 2) for f in (lambda v: jnp.maximum(v, 0.0), lambda v: jnp.minimum(v, 0.0))]
    columns = jnp.stack(columns + [jnp.zeros_like(ones)] * 4, axis=1)
    owner = jnp.arange(slabs, dtype=jnp.int32) * bricks + brick
    first_velocity = velocities(owner * rows)[0]
    first_speeds = jnp.broadcast_to(first_velocity[:, None], (slabs, rank))
    transport_part = pl.pallas_call(
        transport_kernel, out_shape=f32(bricks, 8 + 3 * height, rank), name="transport", compiler_params=pltpu.CompilerParams(vmem_limit_bytes=VMEM_BYTES)
    )(nodes, columns, first_speeds, weights)
    integrals = exchange(transport_part, "brick")

    brick_id = brick.astype(jnp.int32)[None]
    payload, line, state, vectors = pl.pallas_call(
        maxwell_kernel,
        out_shape=(
            f32(bricks, cells + 3 * height, rank),
            f32(slab_cells, slabs),
            f32(8, slab_cells),
            f32(8, rank),
        ),
        in_specs=vector_specs + [whole] * 5,
        name="maxwell", compiler_params=pltpu.CompilerParams(vmem_limit_bytes=VMEM_BYTES),
    )(brick_id, k_slab, integrals, nodes, first_speeds, across[1:])
    second = exchange(payload, "brick")

    slab_grid = k_slab.reshape(bricks, cells_x, cells_y, cells_z, rank)
    left = ((brick - 1) % bricks) ^ brick
    right = ((brick + 1) % bricks) ^ brick
    left = lax.dynamic_index_in_dim(slab_grid, left, 0, keepdims=False)
    right = lax.dynamic_index_in_dim(slab_grid, right, 0, keepdims=False)
    lower = [
        jnp.concatenate([k_below, k_coeffs[:-1]], axis=0),
        jnp.concatenate([left[:, -1:], k_coeffs[:, :-1]], axis=1),
        jnp.roll(k_coeffs, 1, axis=2),
    ]
    upper = [
        jnp.concatenate([k_coeffs[1:], k_above], axis=0),
        jnp.concatenate([k_coeffs[:, 1:], right[:, :1]], axis=1),
        jnp.roll(k_coeffs, -1, axis=2),
    ]
    steps = []
    for axis_id in range(3):
        steps.append(((k_coeffs - lower[axis_id]) * lengths[axis_id]).reshape(cells, rank))
        steps.append(((upper[axis_id] - k_coeffs) * lengths[axis_id]).reshape(cells, rank))
    payload, advanced, transport = pl.pallas_call(
        functools.partial(advance_kernel, time_step=time_step),
        out_shape=(
            f32(bricks, cells + height, rank),
            f32(cells, rank),
            f32(6, rank, rank),
        ),
        name="advance", compiler_params=pltpu.CompilerParams(vmem_limit_bytes=VMEM_BYTES),
    )(second, jnp.stack(steps), own_cells, vectors)
    third = exchange(payload, "brick")

    pieces, chosen = pl.pallas_call(
        functools.partial(products_kernel, cells_x=cells_x, cells_y=cells_y, cells_z=cells_z),
        out_shape=(f32(5 * height, rank), f32(height, half)),
        in_specs=vector_specs + [whole],
        scratch_shapes=[pltpu.VMEM((rank, 4 * rank), jnp.float32)],
        name="products",
        compiler_params=pltpu.CompilerParams(vmem_limit_bytes=VMEM_BYTES),
    )(brick_id, third)
    chosen, third_after = lax.optimization_barrier((chosen, third))
    chosen_below = lax.ppermute(chosen, "slab", up)
    first_plane = third[:, : cells // cells_x].reshape(half, rank)

    back = pl.pallas_call(back_kernel, out_shape=f32(slabs, rows, rank), name="back", compiler_params=pltpu.CompilerParams(vmem_limit_bytes=VMEM_BYTES))(
        third_after, line, state, across[1:].T
    )

    pieces = pieces + jnp.pad(
        contract(chosen_below, first_plane, 1, 0), ((height, 3 * height), (0, 0))
    )
    pieces, back = lax.optimization_barrier((pieces, back))
    fourth = exchange(back, "slab")
    both = ("slab", "brick")
    lower_x, upper_x, cross_x = (from_peer(pieces, both, mask) for mask in (8, 16, 24))
    reduced = jnp.stack([pieces + upper_x, lower_x + cross_x])
    reduced = sum_over(reduced, both, ((32, 64, 96),))
    reduced = gather_more(reduced, both, ((1,), (4, 6, 2)))

    speeds = jnp.stack(list(own_velocity) + [jnp.zeros_like(ones)] * 5, axis=1)
    basis_new, velocity_part, inverse = pl.pallas_call(
        functools.partial(
            middle_kernel, lengths=lengths, time_step=time_step, weight_x=weight_x
        ),
        out_shape=(f32(cells, rank), f32(rows, rank), f32(rank, rank)),
        in_specs=vector_specs + [whole] * 5,
        scratch_shapes=factor_scratch(rank)[:2],
        name="middle",
        compiler_params=pltpu.CompilerParams(vmem_limit_bytes=VMEM_BYTES),
    )(brick_id, reduced, transport, v_basis, advanced, speeds)
    velocity_new, gram_part = pl.pallas_call(
        functools.partial(update_kernel, weight_x=weight_x),
        out_shape=(f32(rows, rank), f32(rank // 2 + 8, rank)),
        name="update",
        compiler_params=pltpu.CompilerParams(vmem_limit_bytes=VMEM_BYTES),
    )(fourth, velocity_part, inverse)
    gram_v = sum_over(gram_part, ("slab", "brick"), ALL_GROUPS)
    coupling, vbasis_new = pl.pallas_call(
        last_kernel,
        out_shape=(f32(rank, rank), f32(rows, rank)),
        scratch_shapes=factor_scratch(rank),
        name="last", compiler_params=pltpu.CompilerParams(vmem_limit_bytes=VMEM_BYTES),
    )(gram_v, velocity_new)
    return (basis_new.reshape(cells_x, cells_y, cells_z, rank), coupling, vbasis_new)


def solution(mesh):
    placed = (P("slab", "brick", None, None), P(("slab", "brick"), None))
    return jax.shard_map(
        local,
        mesh=mesh,
        in_specs=placed,
        out_specs=(P("slab", "brick", None, None), P(), P(("slab", "brick"), None)),
        check_vma=False,
    )
```

```python
import functools
import math

import jax
import jax.numpy as jnp
from jax import lax
from jax.experimental import pallas as pl
from jax.experimental.pallas import tpu as pltpu
from jax.sharding import PartitionSpec as P

NVX = 32


CFL = 0.9
VMAX = 6.0
COLLIDE = 0.3
RHO_MIN = 0.25
TEMP_MIN = 0.25
PRECISE = lax.Precision.HIGHEST
FINE = lax.Precision.HIGH
SPACING = 2.0 * VMAX / NVX
WEIGHT_V = SPACING**3
PANEL = 16
VMEM_BYTES = 24 * 2**20


def contract(left, right, left_dim, right_dim, precision=PRECISE):
    return lax.dot_general(
        left, right, (((left_dim,), (right_dim,)), ((), ())), precision=precision
    )


def exchange(array, axis):
    return lax.all_to_all(array, axis, 0, 0, tiled=True)


def to_all(array, axis):
    copies = lax.axis_size(axis)
    return exchange(jnp.broadcast_to(array[None], (copies,) + array.shape), axis)


def velocities(indices):
    coords = jnp.stack([indices // (NVX * NVX), indices // NVX % NVX, indices % NVX])
    return -VMAX + (coords.astype(jnp.float32) + 0.5) * SPACING


def cell_state(moments):
    density = jnp.maximum(moments[0], RHO_MIN)
    drift = [moments[axis_id] / density for axis_id in (1, 2, 3)]
    square = drift[0] * drift[0] + drift[1] * drift[1] + drift[2] * drift[2]
    temper = jnp.maximum((moments[4] / density - square) / 3.0, TEMP_MIN)
    return density, drift, temper


def from_peer(values, axis, mask):
    axes = axis if isinstance(axis, tuple) else (axis,)
    peers = math.prod(lax.axis_size(name) for name in axes)
    return lax.ppermute(values, axis, [(i, i ^ mask) for i in range(peers)])


def sum_over(array, axis, groups):
    for masks in groups:
        parts = [array] + [from_peer(array, axis, mask) for mask in masks]
        array = sum_pairs(parts)
    return array


def sum_pairs(parts):
    if len(parts) == 1:
        return parts[0]
    half = len(parts) // 2
    return sum_pairs(parts[:half]) + sum_pairs(parts[half:])


def gather_relative(array, axis, groups):
    return gather_more(array[None], axis, groups)


def gather_more(array, axis, groups):
    for masks in groups:
        array = jnp.concatenate([array] + [from_peer(array, axis, mask) for mask in masks], axis=0)
    return array


BRICK_GROUPS = ((1,), (2, 4, 6), (8,))
ALL_GROUPS = ((1,), (4, 2, 6), (16, 8, 24), (64, 32, 96))


def three_parts(array):
    high = array.astype(jnp.bfloat16).astype(jnp.float32)
    rest = array - high
    middle = rest.astype(jnp.bfloat16).astype(jnp.float32)
    return high, middle, rest - middle


def two_parts(array):
    high = array.astype(jnp.bfloat16)
    return high, (array - high.astype(jnp.float32)).astype(jnp.bfloat16)


def factor_into(gram, work_ref, upper_ref, inverse_ref):
    size = gram.shape[0]
    rows = lax.broadcasted_iota(jnp.int32, (size, size), 0)
    cols = lax.broadcasted_iota(jnp.int32, (size, size), 1)
    work_ref[:, :size] = gram
    work_ref[:, size:] = jnp.where(rows == cols, 1.0, 0.0)
    panel_row = lax.broadcasted_iota(jnp.int32, (PANEL, size), 0)
    panel_col = lax.broadcasted_iota(jnp.int32, (PANEL, size), 1)
    for start in range(0, size, PANEL):
        stop = start + PANEL
        panel = work_ref[start:stop, :]
        spread = [
            jnp.broadcast_to(panel[:, start + t : start + t + 1], (PANEL, size))
            for t in range(PANEL)
        ]
        pivots = jnp.zeros((PANEL, size), jnp.float32)
        for t in range(PANEL):
            pivot = jnp.broadcast_to(spread[t][t : t + 1, :], (PANEL, size))
            pivots = jnp.where(panel_row == t, pivot, pivots)
            if t == PANEL - 1:
                break
            ratio = jnp.where(panel_row > t, spread[t] * (1.0 / pivot), 0.0)
            for u in range(t + 1, PANEL):
                spread[u] = spread[u] - ratio * jnp.broadcast_to(
                    spread[u][t : t + 1, :], (PANEL, size)
                )
            panel = panel - jnp.concatenate([ratio, ratio], axis=1) * jnp.broadcast_to(
                panel[t : t + 1, :], (PANEL, 2 * size)
            )
        scale = lax.rsqrt(pivots)
        panel = panel * jnp.concatenate([scale, scale], axis=1)
        left = jnp.where(panel_col >= panel_row + start, panel[:, :size], 0.0)
        right = panel[:, size:]
        upper_ref[start:stop, :] = left
        inverse_ref[start:stop, :] = right
        if stop < size:
            high, middle, low = three_parts(jnp.concatenate([left, right], axis=1))
            lhs = [high, high, middle, middle, high, low]
            rhs = [high, middle, high, middle, low, high]
            update = lax.dot_general(
                jnp.concatenate([part[:, :size] for part in lhs], axis=0).astype(jnp.bfloat16),
                jnp.concatenate(rhs, axis=0).astype(jnp.bfloat16),
                (((0,), (0,)), ((), ())),
                preferred_element_type=jnp.float32,
            )
            work_ref[stop:, :] = work_ref[stop:, :] - update[stop:, :]


def repeat_kernel(below_ref, source_ref, cells_ref, out_ref, sems):
    rows = source_ref.shape[0]
    plane = out_ref.shape[1] - rows
    last = cells_ref.shape[0] - plane
    copies = []
    for i in range(out_ref.shape[0]):
        start = pl.multiple_of(jnp.where(below_ref[0] == i, 0, last), 8)
        copies.append(pltpu.make_async_copy(source_ref, out_ref.at[i, :rows], sems.at[0, i]))
        copies.append(
            pltpu.make_async_copy(
                cells_ref.at[pl.ds(start, plane)], out_ref.at[i, rows:], sems.at[1, i]
            )
        )
    for copy in copies:
        copy.start()
    for copy in copies:
        copy.wait()


def contract_three(left, right, left_dim, right_dim):
    left_high, left_low = two_parts(left)
    right_high, right_low = two_parts(right)
    dims = (((left_dim,), (right_dim,)), ((), ()))

    def product(one, other):
        return lax.dot_general(one, other, dims, preferred_element_type=jnp.float32)

    small = product(left_high, right_low) + product(left_low, right_high)
    return product(left_high, right_high) + small


def transport_kernel(nodes_ref, columns_ref, speeds_ref, weights_ref, out_ref):
    groups, _, rank = nodes_ref.shape
    rows = columns_ref.shape[0]
    bricks = out_ref.shape[0]
    factors = [jnp.broadcast_to(columns_ref[:, i : i + 1], (rows, rank)) for i in range(4)]
    sums = [jnp.zeros((rank, rank), jnp.float32) for _ in range(6)]
    vectors = jnp.zeros((8, rank), jnp.float32)
    for group in range(groups):
        nodes = nodes_ref[group, :rows]
        weighted = jnp.concatenate([nodes] + [nodes * factor for factor in factors], axis=1)
        high, low = two_parts(weighted)
        node_high, node_low = high[:, :rank], low[:, :rank]
        product = lax.dot_general(
            jnp.concatenate([node_high, node_high, node_low], axis=0),
            jnp.concatenate([high, low, high], axis=0),
            (((0,), (0,)), ((), ())),
            preferred_element_type=jnp.float32,
        )
        vectors = vectors + contract(weights_ref[group], nodes, 1, 0)
        plain = product[:, :rank]
        speed = jnp.broadcast_to(speeds_ref[group : group + 1, :], (rank, rank))
        sums[0] = sums[0] + jnp.maximum(speed, 0.0) * plain
        sums[1] = sums[1] + jnp.minimum(speed, 0.0) * plain
        for i in range(4):
            sums[2 + i] = sums[2 + i] + product[:, (i + 1) * rank : (i + 2) * rank]
    row = lax.broadcasted_iota(jnp.int32, (rank, rank), 0)
    col = lax.broadcasted_iota(jnp.int32, (rank, rank), 1)
    block_row = lax.broadcasted_iota(jnp.int32, (8, rank), 0)
    height = rank // bricks
    for i in range(3):
        plus, minus = sums[2 * i], sums[2 * i + 1]
        diagonal = jnp.sum(jnp.where(row == col, minus, 0.0), axis=0, keepdims=True)
        vectors = vectors + jnp.where(block_row == 5 + i, diagonal, 0.0)
        packed = jnp.where(col >= row, plus, minus) * WEIGHT_V
        start = 8 + i * height
        out_ref[:, start : start + height, :] = packed.reshape(bricks, height, rank)
    out_ref[:, :8, :] = jnp.broadcast_to((vectors * WEIGHT_V)[None], (bricks, 8, rank))


def maxwell_kernel(
    brick_ref,
    cells_ref,
    integrals_ref,
    nodes_ref,
    first_ref,
    across_ref,
    part_ref,
    line_ref,
    state_ref,
    vectors_ref,
):
    bricks, cells, rank = cells_ref.shape
    groups, rows = nodes_ref.shape[0], across_ref.shape[1]
    total = bricks * cells
    brick = brick_ref[0]
    k_flat = jnp.concatenate([cells_ref[i ^ brick] for i in range(bricks)], axis=0)
    integrals = integrals_ref[0]
    for i in range(1, bricks):
        integrals = integrals + integrals_ref[i]
    height = integrals.shape[0] - 8
    part_ref[:, cells:, :] = jnp.broadcast_to(integrals[8:][None], (bricks, height, rank))
    vectors_ref[...] = integrals[:8]
    moments = contract(integrals[:8], k_flat, 1, 1)
    density, drift, temper = cell_state([moments[i : i + 1] for i in range(5)])
    slope = -0.5 / temper
    amplitude = density * jnp.exp(-1.5 * jnp.log(2.0 * math.pi * temper))
    first = jnp.broadcast_to(first_ref[:, :1], (groups, total))
    line = amplitude * jnp.exp((first - drift[0]) ** 2 * slope)
    state = jnp.concatenate([drift[1], drift[2], slope] + [amplitude] * 5, axis=0)
    state_ref[...] = state
    both = jnp.concatenate([line, state], axis=0).T
    line_cols = both[:, :groups]
    line_ref[...] = line_cols
    distance = (across_ref[0:1, :] - both[:, groups : groups + 1]) ** 2
    distance = distance + (across_ref[1:2, :] - both[:, groups + 1 : groups + 2]) ** 2
    high, low = two_parts(jnp.exp(distance * both[:, groups + 2 : groups + 3]))
    lhs = jnp.concatenate([high, high, low], axis=1)
    result = jnp.zeros((total, rank), jnp.float32)
    for group in range(0, groups, 2):
        node_high, node_low = two_parts(
            jnp.concatenate([nodes_ref[i, :rows] for i in (group, group + 1)], axis=1)
        )
        product = lax.dot_general(
            lhs,
            jnp.concatenate([node_high, node_low, node_high], axis=0),
            (((1,), (0,)), ((), ())),
            preferred_element_type=jnp.float32,
        )
        result = result + line_cols[:, group : group + 1] * product[:, :rank]
        result = result + line_cols[:, group + 1 : group + 2] * product[:, rank:]
    part_ref[:, :cells, :] = result.reshape(bricks, cells, rank)


def products_kernel(
    brick_ref, parts_ref, pieces_ref, chosen_ref, work_ref, *, cells_x, cells_y, cells_z
):
    bricks, _, rank = parts_ref.shape
    height = rank // bricks
    cells = cells_x * cells_y * cells_z
    total = bricks * cells
    advanced = parts_ref[:, :cells, :].reshape(total, rank)
    last_plane = parts_ref[:, cells - cells // cells_x : cells, :].reshape(-1, rank)
    start = pl.multiple_of(brick_ref[0] * height, height)
    chosen_row = lax.broadcasted_iota(jnp.int32, (height, rank), 0) + start
    chosen_col = lax.broadcasted_iota(jnp.int32, (height, rank), 1)
    chosen_ref[...] = contract(jnp.where(chosen_row == chosen_col, 1.0, 0.0), last_plane, 1, 1)
    row = lax.broadcasted_iota(jnp.int32, (total, rank), 0)
    plane = cells_y * cells_z

    def shifted(amount):
        return pltpu.roll(advanced, amount % total, 0)

    along_x = jnp.where(row // plane % cells_x < cells_x - 1, shifted(-plane), 0.0)
    wrap = cells - (cells_y - 1) * cells_z
    along_y = jnp.where(row // cells_z % cells_y > 0, shifted(cells_z), shifted(wrap))
    along_z = jnp.where(row % cells_z > 0, shifted(1), shifted(1 - cells_z))
    left_high, left_low = two_parts(advanced)
    high, low = two_parts(jnp.concatenate([along_x, along_y, along_z], axis=1))
    work_ref[:, :rank] = contract(advanced, advanced, 0, 0)
    work_ref[:, rank:] = lax.dot_general(
        jnp.concatenate([left_high, left_high, left_low], axis=0),
        jnp.concatenate([high, low, high], axis=0),
        (((0,), (0,)), ((), ())),
        preferred_element_type=jnp.float32,
    )
    own = work_ref[pl.ds(start, height), :]
    for i in range(4):
        pieces_ref[i * height : (i + 1) * height, :] = own[:, i * rank : (i + 1) * rank]
    projected = parts_ref[0, cells:, :]
    for i in range(1, bricks):
        projected = projected + parts_ref[i, cells:, :]
    pieces_ref[4 * height :, :] = projected


def back_kernel(parts_ref, line_ref, state_ref, across_ref, out_ref):
    bricks, _, rank = parts_ref.shape
    groups, rows, _ = out_ref.shape
    total = line_ref.shape[0]
    cells = total // bricks
    advanced = parts_ref[:, :cells, :].reshape(total, rank)
    distance = (across_ref[:, 0:1] - state_ref[0:1, :]) ** 2
    distance = distance + (across_ref[:, 1:2] - state_ref[1:2, :]) ** 2
    high, low = two_parts(jnp.exp(distance * state_ref[2:3, :]))
    lhs = jnp.concatenate([high, high, low], axis=1)
    for group in range(0, groups, 2):
        scaled = [line_ref[:, i : i + 1] * advanced for i in (group, group + 1)]
        part_high, part_low = two_parts(jnp.concatenate(scaled, axis=1))
        product = lax.dot_general(
            lhs,
            jnp.concatenate([part_high, part_low, part_high], axis=0),
            (((1,), (0,)), ((), ())),
            preferred_element_type=jnp.float32,
        )
        out_ref[group] = product[:, :rank]
        out_ref[group + 1] = product[:, rank:]


def advance_kernel(
    parts_ref,
    steps_ref,
    cells_ref,
    vectors_ref,
    payload_ref,
    advanced_ref,
    transport_ref,
    *,
    time_step,
):
    cells, rank = cells_ref.shape
    bricks = parts_ref.shape[0]
    height = rank // bricks
    maxwell_proj = parts_ref[0, :cells, :]
    for i in range(1, bricks):
        maxwell_proj = maxwell_proj + parts_ref[i, :cells, :]
    maxwell_proj = maxwell_proj * WEIGHT_V
    flux = jnp.zeros((cells, rank), jnp.float32)
    row = lax.broadcasted_iota(jnp.int32, (rank, rank), 0)
    col = lax.broadcasted_iota(jnp.int32, (rank, rank), 1)
    for i in range(3):
        start = cells + i * height
        packed = parts_ref[:, start : start + height, :].reshape(rank, rank)
        turned = packed.T
        plus = jnp.where(col >= row, packed, turned)
        minus = jnp.where(col < row, packed, turned)
        minus = jnp.where(col == row, vectors_ref[5 + i : 6 + i, :], minus)
        transport_ref[2 * i] = plus
        transport_ref[2 * i + 1] = minus
        flux = flux + contract(steps_ref[2 * i], plus, 1, 0)
        flux = flux + contract(steps_ref[2 * i + 1], minus, 1, 0)
    own = cells_ref[...]
    advanced = own - time_step * flux + COLLIDE * (maxwell_proj - own)
    advanced_ref[...] = advanced
    payload_ref[:, :cells, :] = jnp.broadcast_to(advanced[None], (bricks, cells, rank))
    projected = contract(advanced, maxwell_proj, 0, 0)
    payload_ref[:, cells:, :] = projected.reshape(bricks, height, rank)


def middle_kernel(
    brick_ref,
    pieces_ref,
    transport_ref,
    basis_ref,
    advanced_ref,
    speeds_ref,
    basis_x_ref,
    velocity_ref,
    inverse_ref,
    work_ref,
    upper_ref,
    *,
    lengths,
    time_step,
    weight_x,
):
    bricks, _, rank = pieces_ref.shape
    rows = basis_ref.shape[0]
    height = rank // bricks
    masks = [j ^ brick_ref[0] for j in range(bricks)]
    slots = [((m >> 1) & 1) * 8 + ((m >> 2) & 1) * 4 + (m & 1) * 2 + (m >> 3) for m in masks]

    def piece(ref, i):
        if ref is transport_ref:
            return ref[i]
        rows_of = [ref[slot, i * height : (i + 1) * height, :] for slot in slots]
        return jnp.concatenate(rows_of, axis=0)

    factor_into(piece(pieces_ref, 0) * weight_x, work_ref, upper_ref, inverse_ref)
    upper, inverse = upper_ref[...], inverse_ref[...]
    basis_x_ref[...] = contract(advanced_ref[...], inverse, 1, 1)
    change = jnp.zeros((rank, rank), jnp.float32)
    turned = []
    for i in range(3):
        shift = piece(pieces_ref, 1 + i) * weight_x
        straight = contract(inverse, shift, 1, 0)
        crossed = contract(inverse, shift, 1, 1)
        if i == 0:
            straight, crossed = crossed, straight
        turned.append(contract(straight, inverse, 1, 1))
        change = change + lengths[i] * (
            contract_three(upper - straight, piece(transport_ref, 2 * i), 1, 0)
            + contract_three(crossed - upper, piece(transport_ref, 2 * i + 1), 1, 0)
        )
    projected = contract(inverse, piece(pieces_ref, 4) * weight_x, 1, 0)
    middle = upper + time_step * change - COLLIDE * (projected - upper)
    now = contract(basis_ref[...], middle, 1, 1)
    drift_sum = jnp.zeros((rows, rank), jnp.float32)
    for i in range(3):
        speed = jnp.broadcast_to(speeds_ref[:, i : i + 1], (rows, rank)) * lengths[i]
        minus = contract_three(now, turned[i], 1, 1)
        plus = contract_three(now, turned[i], 1, 0)
        drift_sum = drift_sum + jnp.maximum(speed, 0.0) * (now - minus)
        drift_sum = drift_sum + jnp.minimum(speed, 0.0) * (plus - now)
    velocity_ref[...] = now - time_step * drift_sum - COLLIDE * now


def update_kernel(back_ref, velocity_ref, inverse_ref, updated_ref, packed_ref, *, weight_x):
    back = back_ref[0]
    for i in range(1, back_ref.shape[0]):
        back = back + back_ref[i]
    back_proj = contract(back * weight_x, inverse_ref[...], 1, 1)
    updated = velocity_ref[...] + COLLIDE * back_proj
    updated_ref[...] = updated
    gram = contract(updated, updated, 0, 0) * WEIGHT_V
    half = gram.shape[0] // 2
    row = lax.broadcasted_iota(jnp.int32, (half, 2 * half), 0)
    col = lax.broadcasted_iota(jnp.int32, (half, 2 * half), 1)
    second = pltpu.roll(gram[half:], half, 1)
    diagonal = jnp.sum(jnp.where(row == col, second, 0.0), axis=0, keepdims=True)
    packed_ref[:half, :] = jnp.where(col < row, second, gram[:half])
    packed_ref[half:, :] = jnp.broadcast_to(diagonal, (8, 2 * half))


def last_kernel(packed_ref, velocity_ref, coupling_ref, basis_ref, work_ref, upper_ref, inverse_ref):
    half = packed_ref.shape[1] // 2
    packed = packed_ref[:half, :]
    row = lax.broadcasted_iota(jnp.int32, (half, 2 * half), 0)
    col = lax.broadcasted_iota(jnp.int32, (half, 2 * half), 1)
    turned = jnp.concatenate([packed, jnp.zeros_like(packed)], axis=0).T[:half]
    second = jnp.where(col < row, packed, turned)
    second = jnp.where(col == row, packed_ref[half : half + 1, :], second)
    gram = jnp.concatenate(
        [jnp.where(col >= row, packed, turned), pltpu.roll(second, half, 1)], axis=0
    )
    factor_into(gram, work_ref, upper_ref, inverse_ref)
    coupling_ref[...] = upper_ref[...].T
    basis_ref[...] = contract(velocity_ref[...], inverse_ref[...], 1, 1)


def f32(*shape):
    return jax.ShapeDtypeStruct(shape, jnp.float32)


def factor_scratch(rank):
    shapes = ((rank, 2 * rank), (rank, rank), (rank, rank))
    return [pltpu.VMEM(shape, jnp.float32) for shape in shapes]


def local(k_coeffs, v_basis):
    cells_x, cells_y, cells_z, rank = k_coeffs.shape
    cells = cells_x * cells_y * cells_z
    slabs, bricks = lax.axis_size("slab"), lax.axis_size("brick")
    devices = slabs * bricks
    slab, brick = lax.axis_index("slab"), lax.axis_index("brick")
    lengths = (cells_x * slabs, cells_y * bricks, cells_z)
    time_step = CFL / (VMAX * sum(lengths))
    weight_x = 1.0 / (lengths[0] * lengths[1] * lengths[2])
    rows = v_basis.shape[0]
    slab_cells = cells * bricks
    half = slab_cells // cells_x
    height = rank // bricks
    up = [(i, (i + 1) % slabs) for i in range(slabs)]
    own_cells = k_coeffs.reshape(cells, rank)

    own_ids = (slab * bricks + brick) * rows + jnp.arange(rows, dtype=jnp.int32)
    own_velocity = velocities(own_ids)
    ones = jnp.ones_like(own_velocity[0])
    slab_owner = jnp.arange(slabs, dtype=jnp.int32)[:, None] * bricks + brick
    slab_velocity = velocities(slab_owner * rows + jnp.arange(rows, dtype=jnp.int32)[None])
    weights = jnp.stack(
        [jnp.ones_like(slab_velocity[0]), slab_velocity[0], slab_velocity[1], slab_velocity[2]]
        + [jnp.sum(slab_velocity * slab_velocity, axis=0)]
        + [jnp.zeros_like(slab_velocity[0])] * 3,
        axis=1,
    )
    plane = cells // cells_x
    vector_specs = [pl.BlockSpec(memory_space=pltpu.SMEM)]
    whole = pl.BlockSpec(memory_space=pltpu.VMEM)
    nodes = exchange(
        pl.pallas_call(
            repeat_kernel,
            out_shape=f32(slabs, rows + plane, rank),
            in_specs=vector_specs + [whole] * 2,
            out_specs=pl.BlockSpec(memory_space=pl.ANY),
            scratch_shapes=[pltpu.SemaphoreType.DMA((2, slabs))],
            name="repeat",
            compiler_params=pltpu.CompilerParams(vmem_limit_bytes=VMEM_BYTES),
        )(((slab + slabs - 1) % slabs).astype(jnp.int32)[None], v_basis, own_cells),
        "slab",
    )
    k_part = gather_relative(own_cells, "brick", BRICK_GROUPS[:2])
    below, above = ((slab + shift) % slabs for shift in (slabs - 1, 1))
    k_below, k_above = (
        lax.dynamic_slice(nodes, (peer, rows, 0), (1, plane, rank)).reshape(k_coeffs[:1].shape)
        for peer in (below, above)
    )

    k_part, nodes = lax.optimization_barrier((k_part, nodes))
    k_slab = gather_more(k_part, "brick", BRICK_GROUPS[2:])

    across = velocities(brick * rows + jnp.arange(rows, dtype=jnp.int32))
    columns = [f(across[i]) for i in (1, 2) for f in (lambda v: jnp.maximum(v, 0.0), lambda v: jnp.minimum(v, 0.0))]
    columns = jnp.stack(columns + [jnp.zeros_like(ones)] * 4, axis=1)
    owner = jnp.arange(slabs, dtype=jnp.int32) * bricks + brick
    first_velocity = velocities(owner * rows)[0]
    first_speeds = jnp.broadcast_to(first_velocity[:, None], (slabs, rank))
    transport_part = pl.pallas_call(
        transport_kernel, out_shape=f32(bricks, 8 + 3 * height, rank), name="transport", compiler_params=pltpu.CompilerParams(vmem_limit_bytes=VMEM_BYTES)
    )(nodes, columns, first_speeds, weights)
    integrals = exchange(transport_part, "brick")

    brick_id = brick.astype(jnp.int32)[None]
    payload, line, state, vectors = pl.pallas_call(
        maxwell_kernel,
        out_shape=(
            f32(bricks, cells + 3 * height, rank),
            f32(slab_cells, slabs),
            f32(8, slab_cells),
            f32(8, rank),
        ),
        in_specs=vector_specs + [whole] * 5,
        name="maxwell", compiler_params=pltpu.CompilerParams(vmem_limit_bytes=VMEM_BYTES),
    )(brick_id, k_slab, integrals, nodes, first_speeds, across[1:])
    second = exchange(payload, "brick")

    slab_grid = k_slab.reshape(bricks, cells_x, cells_y, cells_z, rank)
    left = ((brick - 1) % bricks) ^ brick
    right = ((brick + 1) % bricks) ^ brick
    left = lax.dynamic_index_in_dim(slab_grid, left, 0, keepdims=False)
    right = lax.dynamic_index_in_dim(slab_grid, right, 0, keepdims=False)
    lower = [
        jnp.concatenate([k_below, k_coeffs[:-1]], axis=0),
        jnp.concatenate([left[:, -1:], k_coeffs[:, :-1]], axis=1),
        jnp.roll(k_coeffs, 1, axis=2),
    ]
    upper = [
        jnp.concatenate([k_coeffs[1:], k_above], axis=0),
        jnp.concatenate([k_coeffs[:, 1:], right[:, :1]], axis=1),
        jnp.roll(k_coeffs, -1, axis=2),
    ]
    steps = []
    for axis_id in range(3):
        steps.append(((k_coeffs - lower[axis_id]) * lengths[axis_id]).reshape(cells, rank))
        steps.append(((upper[axis_id] - k_coeffs) * lengths[axis_id]).reshape(cells, rank))
    payload, advanced, transport = pl.pallas_call(
        functools.partial(advance_kernel, time_step=time_step),
        out_shape=(
            f32(bricks, cells + height, rank),
            f32(cells, rank),
            f32(6, rank, rank),
        ),
        name="advance", compiler_params=pltpu.CompilerParams(vmem_limit_bytes=VMEM_BYTES),
    )(second, jnp.stack(steps), own_cells, vectors)
    third = exchange(payload, "brick")

    pieces, chosen = pl.pallas_call(
        functools.partial(products_kernel, cells_x=cells_x, cells_y=cells_y, cells_z=cells_z),
        out_shape=(f32(5 * height, rank), f32(height, half)),
        in_specs=vector_specs + [whole],
        scratch_shapes=[pltpu.VMEM((rank, 4 * rank), jnp.float32)],
        name="products",
        compiler_params=pltpu.CompilerParams(vmem_limit_bytes=VMEM_BYTES),
    )(brick_id, third)
    chosen, third_after = lax.optimization_barrier((chosen, third))
    chosen_below = lax.ppermute(chosen, "slab", up)
    first_plane = third[:, : cells // cells_x].reshape(half, rank)

    back = pl.pallas_call(back_kernel, out_shape=f32(slabs, rows, rank), name="back", compiler_params=pltpu.CompilerParams(vmem_limit_bytes=VMEM_BYTES))(
        third_after, line, state, across[1:].T
    )

    pieces = pieces + jnp.pad(
        contract(chosen_below, first_plane, 1, 0), ((height, 3 * height), (0, 0))
    )
    pieces, back = lax.optimization_barrier((pieces, back))
    fourth = exchange(back, "slab")
    both = ("slab", "brick")
    lower_x, upper_x, cross_x = (from_peer(pieces, both, mask) for mask in (8, 16, 24))
    reduced = jnp.stack([pieces + upper_x, lower_x + cross_x])
    reduced = sum_over(reduced, both, ((96, 64, 32),))
    reduced = gather_more(reduced, both, ((1,), (4, 2, 6)))

    speeds = jnp.stack(list(own_velocity) + [jnp.zeros_like(ones)] * 5, axis=1)
    basis_new, velocity_part, inverse = pl.pallas_call(
        functools.partial(
            middle_kernel, lengths=lengths, time_step=time_step, weight_x=weight_x
        ),
        out_shape=(f32(cells, rank), f32(rows, rank), f32(rank, rank)),
        in_specs=vector_specs + [whole] * 5,
        scratch_shapes=factor_scratch(rank)[:2],
        name="middle",
        compiler_params=pltpu.CompilerParams(vmem_limit_bytes=VMEM_BYTES),
    )(brick_id, reduced, transport, v_basis, advanced, speeds)
    velocity_new, gram_part = pl.pallas_call(
        functools.partial(update_kernel, weight_x=weight_x),
        out_shape=(f32(rows, rank), f32(rank // 2 + 8, rank)),
        name="update",
        compiler_params=pltpu.CompilerParams(vmem_limit_bytes=VMEM_BYTES),
    )(fourth, velocity_part, inverse)
    gram_v = sum_over(gram_part, ("slab", "brick"), ALL_GROUPS)
    coupling, vbasis_new = pl.pallas_call(
        last_kernel,
        out_shape=(f32(rank, rank), f32(rows, rank)),
        scratch_shapes=factor_scratch(rank),
        name="last", compiler_params=pltpu.CompilerParams(vmem_limit_bytes=VMEM_BYTES),
    )(gram_v, velocity_new)
    return (basis_new.reshape(cells_x, cells_y, cells_z, rank), coupling, vbasis_new)


def solution(mesh):
    placed = (P("slab", "brick", None, None), P(("slab", "brick"), None))
    return jax.shard_map(
        local,
        mesh=mesh,
        in_specs=placed,
        out_specs=(P("slab", "brick", None, None), P(), P(("slab", "brick"), None)),
        check_vma=False,
    )
```

```python
import functools
import math

import jax
import jax.numpy as jnp
from jax import lax
from jax.experimental import pallas as pl
from jax.experimental.pallas import tpu as pltpu
from jax.sharding import PartitionSpec as P

NVX = 32


CFL = 0.9
VMAX = 6.0
COLLIDE = 0.3
RHO_MIN = 0.25
TEMP_MIN = 0.25
PRECISE = lax.Precision.HIGHEST
FINE = lax.Precision.HIGH
SPACING = 2.0 * VMAX / NVX
WEIGHT_V = SPACING**3
PANEL = 16
VMEM_BYTES = 24 * 2**20


def contract(left, right, left_dim, right_dim, precision=PRECISE):
    return lax.dot_general(
        left, right, (((left_dim,), (right_dim,)), ((), ())), precision=precision
    )


def exchange(array, axis):
    return lax.all_to_all(array, axis, 0, 0, tiled=True)


def to_all(array, axis):
    copies = lax.axis_size(axis)
    return exchange(jnp.broadcast_to(array[None], (copies,) + array.shape), axis)


def velocities(indices):
    coords = jnp.stack([indices // (NVX * NVX), indices // NVX % NVX, indices % NVX])
    return -VMAX + (coords.astype(jnp.float32) + 0.5) * SPACING


def cell_state(moments):
    density = jnp.maximum(moments[0], RHO_MIN)
    drift = [moments[axis_id] / density for axis_id in (1, 2, 3)]
    square = drift[0] * drift[0] + drift[1] * drift[1] + drift[2] * drift[2]
    temper = jnp.maximum((moments[4] / density - square) / 3.0, TEMP_MIN)
    return density, drift, temper


def from_peer(values, axis, mask):
    axes = axis if isinstance(axis, tuple) else (axis,)
    peers = math.prod(lax.axis_size(name) for name in axes)
    return lax.ppermute(values, axis, [(i, i ^ mask) for i in range(peers)])


def sum_over(array, axis, groups):
    for masks in groups:
        parts = [array] + [from_peer(array, axis, mask) for mask in masks]
        array = sum_pairs(parts)
    return array


def sum_pairs(parts):
    if len(parts) == 1:
        return parts[0]
    half = len(parts) // 2
    return sum_pairs(parts[:half]) + sum_pairs(parts[half:])


def gather_relative(array, axis, groups):
    return gather_more(array[None], axis, groups)


def gather_more(array, axis, groups):
    for masks in groups:
        array = jnp.concatenate([array] + [from_peer(array, axis, mask) for mask in masks], axis=0)
    return array


BRICK_GROUPS = ((1,), (2, 4, 6), (8,))
ALL_GROUPS = ((1,), (4, 6, 2), (16, 24, 8), (64, 96, 32))


def three_parts(array):
    high = array.astype(jnp.bfloat16).astype(jnp.float32)
    rest = array - high
    middle = rest.astype(jnp.bfloat16).astype(jnp.float32)
    return high, middle, rest - middle


def two_parts(array):
    high = array.astype(jnp.bfloat16)
    return high, (array - high.astype(jnp.float32)).astype(jnp.bfloat16)


def factor_into(gram, work_ref, upper_ref, inverse_ref):
    size = gram.shape[0]
    rows = lax.broadcasted_iota(jnp.int32, (size, size), 0)
    cols = lax.broadcasted_iota(jnp.int32, (size, size), 1)
    work_ref[:, :size] = gram
    work_ref[:, size:] = jnp.where(rows == cols, 1.0, 0.0)
    panel_row = lax.broadcasted_iota(jnp.int32, (PANEL, size), 0)
    panel_col = lax.broadcasted_iota(jnp.int32, (PANEL, size), 1)
    for start in range(0, size, PANEL):
        stop = start + PANEL
        panel = work_ref[start:stop, :]
        spread = [
            jnp.broadcast_to(panel[:, start + t : start + t + 1], (PANEL, size))
            for t in range(PANEL)
        ]
        pivots = jnp.zeros((PANEL, size), jnp.float32)
        for t in range(PANEL):
            pivot = jnp.broadcast_to(spread[t][t : t + 1, :], (PANEL, size))
            pivots = jnp.where(panel_row == t, pivot, pivots)
            if t == PANEL - 1:
                break
            ratio = jnp.where(panel_row > t, spread[t] * (1.0 / pivot), 0.0)
            for u in range(t + 1, PANEL):
                spread[u] = spread[u] - ratio * jnp.broadcast_to(
                    spread[u][t : t + 1, :], (PANEL, size)
                )
            panel = panel - jnp.concatenate([ratio, ratio], axis=1) * jnp.broadcast_to(
                panel[t : t + 1, :], (PANEL, 2 * size)
            )
        scale = lax.rsqrt(pivots)
        panel = panel * jnp.concatenate([scale, scale], axis=1)
        left = jnp.where(panel_col >= panel_row + start, panel[:, :size], 0.0)
        right = panel[:, size:]
        upper_ref[start:stop, :] = left
        inverse_ref[start:stop, :] = right
        if stop < size:
            high, middle, low = three_parts(jnp.concatenate([left, right], axis=1))
            lhs = [high, high, middle, middle, high, low]
            rhs = [high, middle, high, middle, low, high]
            update = lax.dot_general(
                jnp.concatenate([part[:, :size] for part in lhs], axis=0).astype(jnp.bfloat16),
                jnp.concatenate(rhs, axis=0).astype(jnp.bfloat16),
                (((0,), (0,)), ((), ())),
                preferred_element_type=jnp.float32,
            )
            work_ref[stop:, :] = work_ref[stop:, :] - update[stop:, :]


def repeat_kernel(below_ref, source_ref, cells_ref, out_ref, sems):
    rows = source_ref.shape[0]
    plane = out_ref.shape[1] - rows
    last = cells_ref.shape[0] - plane
    copies = []
    for i in range(out_ref.shape[0]):
        start = pl.multiple_of(jnp.where(below_ref[0] == i, 0, last), 8)
        copies.append(pltpu.make_async_copy(source_ref, out_ref.at[i, :rows], sems.at[0, i]))
        copies.append(
            pltpu.make_async_copy(
                cells_ref.at[pl.ds(start, plane)], out_ref.at[i, rows:], sems.at[1, i]
            )
        )
    for copy in copies:
        copy.start()
    for copy in copies:
        copy.wait()


def contract_three(left, right, left_dim, right_dim):
    left_high, left_low = two_parts(left)
    right_high, right_low = two_parts(right)
    dims = (((left_dim,), (right_dim,)), ((), ()))

    def product(one, other):
        return lax.dot_general(one, other, dims, preferred_element_type=jnp.float32)

    small = product(left_high, right_low) + product(left_low, right_high)
    return product(left_high, right_high) + small


def transport_kernel(nodes_ref, columns_ref, speeds_ref, weights_ref, out_ref):
    groups, _, rank = nodes_ref.shape
    rows = columns_ref.shape[0]
    bricks = out_ref.shape[0]
    factors = [jnp.broadcast_to(columns_ref[:, i : i + 1], (rows, rank)) for i in range(4)]
    sums = [jnp.zeros((rank, rank), jnp.float32) for _ in range(6)]
    vectors = jnp.zeros((8, rank), jnp.float32)
    for group in range(groups):
        nodes = nodes_ref[group, :rows]
        weighted = jnp.concatenate([nodes] + [nodes * factor for factor in factors], axis=1)
        high, low = two_parts(weighted)
        node_high, node_low = high[:, :rank], low[:, :rank]
        product = lax.dot_general(
            jnp.concatenate([node_high, node_high, node_low], axis=0),
            jnp.concatenate([high, low, high], axis=0),
            (((0,), (0,)), ((), ())),
            preferred_element_type=jnp.float32,
        )
        vectors = vectors + contract(weights_ref[group], nodes, 1, 0)
        plain = product[:, :rank]
        speed = jnp.broadcast_to(speeds_ref[group : group + 1, :], (rank, rank))
        sums[0] = sums[0] + jnp.maximum(speed, 0.0) * plain
        sums[1] = sums[1] + jnp.minimum(speed, 0.0) * plain
        for i in range(4):
            sums[2 + i] = sums[2 + i] + product[:, (i + 1) * rank : (i + 2) * rank]
    row = lax.broadcasted_iota(jnp.int32, (rank, rank), 0)
    col = lax.broadcasted_iota(jnp.int32, (rank, rank), 1)
    block_row = lax.broadcasted_iota(jnp.int32, (8, rank), 0)
    height = rank // bricks
    for i in range(3):
        plus, minus = sums[2 * i], sums[2 * i + 1]
        diagonal = jnp.sum(jnp.where(row == col, minus, 0.0), axis=0, keepdims=True)
        vectors = vectors + jnp.where(block_row == 5 + i, diagonal, 0.0)
        packed = jnp.where(col >= row, plus, minus) * WEIGHT_V
        start = 8 + i * height
        out_ref[:, start : start + height, :] = packed.reshape(bricks, height, rank)
    out_ref[:, :8, :] = jnp.broadcast_to((vectors * WEIGHT_V)[None], (bricks, 8, rank))


def maxwell_kernel(
    brick_ref,
    cells_ref,
    integrals_ref,
    nodes_ref,
    first_ref,
    across_ref,
    part_ref,
    line_ref,
    state_ref,
    vectors_ref,
):
    bricks, cells, rank = cells_ref.shape
    groups, rows = nodes_ref.shape[0], across_ref.shape[1]
    total = bricks * cells
    brick = brick_ref[0]
    k_flat = jnp.concatenate([cells_ref[i ^ brick] for i in range(bricks)], axis=0)
    integrals = integrals_ref[0]
    for i in range(1, bricks):
        integrals = integrals + integrals_ref[i]
    height = integrals.shape[0] - 8
    part_ref[:, cells:, :] = jnp.broadcast_to(integrals[8:][None], (bricks, height, rank))
    vectors_ref[...] = integrals[:8]
    moments = contract(integrals[:8], k_flat, 1, 1)
    density, drift, temper = cell_state([moments[i : i + 1] for i in range(5)])
    slope = -0.5 / temper
    amplitude = density * jnp.exp(-1.5 * jnp.log(2.0 * math.pi * temper))
    first = jnp.broadcast_to(first_ref[:, :1], (groups, total))
    line = amplitude * jnp.exp((first - drift[0]) ** 2 * slope)
    state = jnp.concatenate([drift[1], drift[2], slope] + [amplitude] * 5, axis=0)
    state_ref[...] = state
    both = jnp.concatenate([line, state], axis=0).T
    line_cols = both[:, :groups]
    line_ref[...] = line_cols
    distance = (across_ref[0:1, :] - both[:, groups : groups + 1]) ** 2
    distance = distance + (across_ref[1:2, :] - both[:, groups + 1 : groups + 2]) ** 2
    high, low = two_parts(jnp.exp(distance * both[:, groups + 2 : groups + 3]))
    lhs = jnp.concatenate([high, high, low], axis=1)
    result = jnp.zeros((total, rank), jnp.float32)
    for group in range(0, groups, 2):
        node_high, node_low = two_parts(
            jnp.concatenate([nodes_ref[i, :rows] for i in (group, group + 1)], axis=1)
        )
        product = lax.dot_general(
            lhs,
            jnp.concatenate([node_high, node_low, node_high], axis=0),
            (((1,), (0,)), ((), ())),
            preferred_element_type=jnp.float32,
        )
        result = result + line_cols[:, group : group + 1] * product[:, :rank]
        result = result + line_cols[:, group + 1 : group + 2] * product[:, rank:]
    part_ref[:, :cells, :] = result.reshape(bricks, cells, rank)


def products_kernel(
    brick_ref, parts_ref, pieces_ref, chosen_ref, work_ref, *, cells_x, cells_y, cells_z
):
    bricks, _, rank = parts_ref.shape
    height = rank // bricks
    cells = cells_x * cells_y * cells_z
    total = bricks * cells
    advanced = parts_ref[:, :cells, :].reshape(total, rank)
    last_plane = parts_ref[:, cells - cells // cells_x : cells, :].reshape(-1, rank)
    start = pl.multiple_of(brick_ref[0] * height, height)
    chosen_row = lax.broadcasted_iota(jnp.int32, (height, rank), 0) + start
    chosen_col = lax.broadcasted_iota(jnp.int32, (height, rank), 1)
    chosen_ref[...] = contract(jnp.where(chosen_row == chosen_col, 1.0, 0.0), last_plane, 1, 1)
    row = lax.broadcasted_iota(jnp.int32, (total, rank), 0)
    plane = cells_y * cells_z

    def shifted(amount):
        return pltpu.roll(advanced, amount % total, 0)

    along_x = jnp.where(row // plane % cells_x < cells_x - 1, shifted(-plane), 0.0)
    wrap = cells - (cells_y - 1) * cells_z
    along_y = jnp.where(row // cells_z % cells_y > 0, shifted(cells_z), shifted(wrap))
    along_z = jnp.where(row % cells_z > 0, shifted(1), shifted(1 - cells_z))
    left_high, left_low = two_parts(advanced)
    high, low = two_parts(jnp.concatenate([along_x, along_y, along_z], axis=1))
    work_ref[:, :rank] = contract(advanced, advanced, 0, 0)
    work_ref[:, rank:] = lax.dot_general(
        jnp.concatenate([left_high, left_high, left_low], axis=0),
        jnp.concatenate([high, low, high], axis=0),
        (((0,), (0,)), ((), ())),
        preferred_element_type=jnp.float32,
    )
    own = work_ref[pl.ds(start, height), :]
    for i in range(4):
        pieces_ref[i * height : (i + 1) * height, :] = own[:, i * rank : (i + 1) * rank]
    projected = parts_ref[0, cells:, :]
    for i in range(1, bricks):
        projected = projected + parts_ref[i, cells:, :]
    pieces_ref[4 * height :, :] = projected


def back_kernel(parts_ref, line_ref, state_ref, across_ref, out_ref):
    bricks, _, rank = parts_ref.shape
    groups, rows, _ = out_ref.shape
    total = line_ref.shape[0]
    cells = total // bricks
    advanced = parts_ref[:, :cells, :].reshape(total, rank)
    distance = (across_ref[:, 0:1] - state_ref[0:1, :]) ** 2
    distance = distance + (across_ref[:, 1:2] - state_ref[1:2, :]) ** 2
    high, low = two_parts(jnp.exp(distance * state_ref[2:3, :]))
    lhs = jnp.concatenate([high, high, low], axis=1)
    for group in range(0, groups, 2):
        scaled = [line_ref[:, i : i + 1] * advanced for i in (group, group + 1)]
        part_high, part_low = two_parts(jnp.concatenate(scaled, axis=1))
        product = lax.dot_general(
            lhs,
            jnp.concatenate([part_high, part_low, part_high], axis=0),
            (((1,), (0,)), ((), ())),
            preferred_element_type=jnp.float32,
        )
        out_ref[group] = product[:, :rank]
        out_ref[group + 1] = product[:, rank:]


def advance_kernel(
    parts_ref,
    steps_ref,
    cells_ref,
    vectors_ref,
    payload_ref,
    advanced_ref,
    transport_ref,
    *,
    time_step,
):
    cells, rank = cells_ref.shape
    bricks = parts_ref.shape[0]
    height = rank // bricks
    maxwell_proj = parts_ref[0, :cells, :]
    for i in range(1, bricks):
        maxwell_proj = maxwell_proj + parts_ref[i, :cells, :]
    maxwell_proj = maxwell_proj * WEIGHT_V
    flux = jnp.zeros((cells, rank), jnp.float32)
    row = lax.broadcasted_iota(jnp.int32, (rank, rank), 0)
    col = lax.broadcasted_iota(jnp.int32, (rank, rank), 1)
    for i in range(3):
        start = cells + i * height
        packed = parts_ref[:, start : start + height, :].reshape(rank, rank)
        turned = packed.T
        plus = jnp.where(col >= row, packed, turned)
        minus = jnp.where(col < row, packed, turned)
        minus = jnp.where(col == row, vectors_ref[5 + i : 6 + i, :], minus)
        transport_ref[2 * i] = plus
        transport_ref[2 * i + 1] = minus
        flux = flux + contract(steps_ref[2 * i], plus, 1, 0)
        flux = flux + contract(steps_ref[2 * i + 1], minus, 1, 0)
    own = cells_ref[...]
    advanced = own - time_step * flux + COLLIDE * (maxwell_proj - own)
    advanced_ref[...] = advanced
    payload_ref[:, :cells, :] = jnp.broadcast_to(advanced[None], (bricks, cells, rank))
    projected = contract(advanced, maxwell_proj, 0, 0)
    payload_ref[:, cells:, :] = projected.reshape(bricks, height, rank)


def middle_kernel(
    brick_ref,
    pieces_ref,
    transport_ref,
    basis_ref,
    advanced_ref,
    speeds_ref,
    basis_x_ref,
    velocity_ref,
    inverse_ref,
    work_ref,
    upper_ref,
    *,
    lengths,
    time_step,
    weight_x,
):
    bricks, _, rank = pieces_ref.shape
    rows = basis_ref.shape[0]
    height = rank // bricks
    masks = [j ^ brick_ref[0] for j in range(bricks)]
    slots = [((m >> 1) & 1) * 8 + ((m >> 2) & 1) * 4 + (m & 1) * 2 + (m >> 3) for m in masks]

    def piece(ref, i):
        if ref is transport_ref:
            return ref[i]
        rows_of = [ref[slot, i * height : (i + 1) * height, :] for slot in slots]
        return jnp.concatenate(rows_of, axis=0)

    factor_into(piece(pieces_ref, 0) * weight_x, work_ref, upper_ref, inverse_ref)
    upper, inverse = upper_ref[...], inverse_ref[...]
    basis_x_ref[...] = contract(advanced_ref[...], inverse, 1, 1)
    change = jnp.zeros((rank, rank), jnp.float32)
    turned = []
    for i in range(3):
        shift = piece(pieces_ref, 1 + i) * weight_x
        straight = contract(inverse, shift, 1, 0)
        crossed = contract(inverse, shift, 1, 1)
        if i == 0:
            straight, crossed = crossed, straight
        turned.append(contract(straight, inverse, 1, 1))
        change = change + lengths[i] * (
            contract_three(upper - straight, piece(transport_ref, 2 * i), 1, 0)
            + contract_three(crossed - upper, piece(transport_ref, 2 * i + 1), 1, 0)
        )
    projected = contract(inverse, piece(pieces_ref, 4) * weight_x, 1, 0)
    middle = upper + time_step * change - COLLIDE * (projected - upper)
    now = contract(basis_ref[...], middle, 1, 1)
    drift_sum = jnp.zeros((rows, rank), jnp.float32)
    for i in range(3):
        speed = jnp.broadcast_to(speeds_ref[:, i : i + 1], (rows, rank)) * lengths[i]
        minus = contract_three(now, turned[i], 1, 1)
        plus = contract_three(now, turned[i], 1, 0)
        drift_sum = drift_sum + jnp.maximum(speed, 0.0) * (now - minus)
        drift_sum = drift_sum + jnp.minimum(speed, 0.0) * (plus - now)
    velocity_ref[...] = now - time_step * drift_sum - COLLIDE * now


def update_kernel(back_ref, velocity_ref, inverse_ref, updated_ref, packed_ref, *, weight_x):
    back = back_ref[0]
    for i in range(1, back_ref.shape[0]):
        back = back + back_ref[i]
    back_proj = contract(back * weight_x, inverse_ref[...], 1, 1)
    updated = velocity_ref[...] + COLLIDE * back_proj
    updated_ref[...] = updated
    gram = contract(updated, updated, 0, 0) * WEIGHT_V
    half = gram.shape[0] // 2
    row = lax.broadcasted_iota(jnp.int32, (half, 2 * half), 0)
    col = lax.broadcasted_iota(jnp.int32, (half, 2 * half), 1)
    second = pltpu.roll(gram[half:], half, 1)
    diagonal = jnp.sum(jnp.where(row == col, second, 0.0), axis=0, keepdims=True)
    packed_ref[:half, :] = jnp.where(col < row, second, gram[:half])
    packed_ref[half:, :] = jnp.broadcast_to(diagonal, (8, 2 * half))


def last_kernel(packed_ref, velocity_ref, coupling_ref, basis_ref, work_ref, upper_ref, inverse_ref):
    half = packed_ref.shape[1] // 2
    packed = packed_ref[:half, :]
    row = lax.broadcasted_iota(jnp.int32, (half, 2 * half), 0)
    col = lax.broadcasted_iota(jnp.int32, (half, 2 * half), 1)
    turned = jnp.concatenate([packed, jnp.zeros_like(packed)], axis=0).T[:half]
    second = jnp.where(col < row, packed, turned)
    second = jnp.where(col == row, packed_ref[half : half + 1, :], second)
    gram = jnp.concatenate(
        [jnp.where(col >= row, packed, turned), pltpu.roll(second, half, 1)], axis=0
    )
    factor_into(gram, work_ref, upper_ref, inverse_ref)
    coupling_ref[...] = upper_ref[...].T
    basis_ref[...] = contract(velocity_ref[...], inverse_ref[...], 1, 1)


def f32(*shape):
    return jax.ShapeDtypeStruct(shape, jnp.float32)


def factor_scratch(rank):
    shapes = ((rank, 2 * rank), (rank, rank), (rank, rank))
    return [pltpu.VMEM(shape, jnp.float32) for shape in shapes]


def local(k_coeffs, v_basis):
    cells_x, cells_y, cells_z, rank = k_coeffs.shape
    cells = cells_x * cells_y * cells_z
    slabs, bricks = lax.axis_size("slab"), lax.axis_size("brick")
    devices = slabs * bricks
    slab, brick = lax.axis_index("slab"), lax.axis_index("brick")
    lengths = (cells_x * slabs, cells_y * bricks, cells_z)
    time_step = CFL / (VMAX * sum(lengths))
    weight_x = 1.0 / (lengths[0] * lengths[1] * lengths[2])
    rows = v_basis.shape[0]
    slab_cells = cells * bricks
    half = slab_cells // cells_x
    height = rank // bricks
    up = [(i, (i + 1) % slabs) for i in range(slabs)]
    own_cells = k_coeffs.reshape(cells, rank)

    own_ids = (slab * bricks + brick) * rows + jnp.arange(rows, dtype=jnp.int32)
    own_velocity = velocities(own_ids)
    ones = jnp.ones_like(own_velocity[0])
    slab_owner = jnp.arange(slabs, dtype=jnp.int32)[:, None] * bricks + brick
    slab_velocity = velocities(slab_owner * rows + jnp.arange(rows, dtype=jnp.int32)[None])
    weights = jnp.stack(
        [jnp.ones_like(slab_velocity[0]), slab_velocity[0], slab_velocity[1], slab_velocity[2]]
        + [jnp.sum(slab_velocity * slab_velocity, axis=0)]
        + [jnp.zeros_like(slab_velocity[0])] * 3,
        axis=1,
    )
    plane = cells // cells_x
    vector_specs = [pl.BlockSpec(memory_space=pltpu.SMEM)]
    whole = pl.BlockSpec(memory_space=pltpu.VMEM)
    nodes = exchange(
        pl.pallas_call(
            repeat_kernel,
            out_shape=f32(slabs, rows + plane, rank),
            in_specs=vector_specs + [whole] * 2,
            out_specs=pl.BlockSpec(memory_space=pl.ANY),
            scratch_shapes=[pltpu.SemaphoreType.DMA((2, slabs))],
            name="repeat",
            compiler_params=pltpu.CompilerParams(vmem_limit_bytes=VMEM_BYTES),
        )(((slab + slabs - 1) % slabs).astype(jnp.int32)[None], v_basis, own_cells),
        "slab",
    )
    k_part = gather_relative(own_cells, "brick", BRICK_GROUPS[:2])
    below, above = ((slab + shift) % slabs for shift in (slabs - 1, 1))
    k_below, k_above = (
        lax.dynamic_slice(nodes, (peer, rows, 0), (1, plane, rank)).reshape(k_coeffs[:1].shape)
        for peer in (below, above)
    )

    k_part, nodes = lax.optimization_barrier((k_part, nodes))
    k_slab = gather_more(k_part, "brick", BRICK_GROUPS[2:])

    across = velocities(brick * rows + jnp.arange(rows, dtype=jnp.int32))
    columns = [f(across[i]) for i in (1, 2) for f in (lambda v: jnp.maximum(v, 0.0), lambda v: jnp.minimum(v, 0.0))]
    columns = jnp.stack(columns + [jnp.zeros_like(ones)] * 4, axis=1)
    owner = jnp.arange(slabs, dtype=jnp.int32) * bricks + brick
    first_velocity = velocities(owner * rows)[0]
    first_speeds = jnp.broadcast_to(first_velocity[:, None], (slabs, rank))
    transport_part = pl.pallas_call(
        transport_kernel, out_shape=f32(bricks, 8 + 3 * height, rank), name="transport", compiler_params=pltpu.CompilerParams(vmem_limit_bytes=VMEM_BYTES)
    )(nodes, columns, first_speeds, weights)
    integrals = exchange(transport_part, "brick")

    brick_id = brick.astype(jnp.int32)[None]
    payload, line, state, vectors = pl.pallas_call(
        maxwell_kernel,
        out_shape=(
            f32(bricks, cells + 3 * height, rank),
            f32(slab_cells, slabs),
            f32(8, slab_cells),
            f32(8, rank),
        ),
        in_specs=vector_specs + [whole] * 5,
        name="maxwell", compiler_params=pltpu.CompilerParams(vmem_limit_bytes=VMEM_BYTES),
    )(brick_id, k_slab, integrals, nodes, first_speeds, across[1:])
    second = exchange(payload, "brick")

    slab_grid = k_slab.reshape(bricks, cells_x, cells_y, cells_z, rank)
    left = ((brick - 1) % bricks) ^ brick
    right = ((brick + 1) % bricks) ^ brick
    left = lax.dynamic_index_in_dim(slab_grid, left, 0, keepdims=False)
    right = lax.dynamic_index_in_dim(slab_grid, right, 0, keepdims=False)
    lower = [
        jnp.concatenate([k_below, k_coeffs[:-1]], axis=0),
        jnp.concatenate([left[:, -1:], k_coeffs[:, :-1]], axis=1),
        jnp.roll(k_coeffs, 1, axis=2),
    ]
    upper = [
        jnp.concatenate([k_coeffs[1:], k_above], axis=0),
        jnp.concatenate([k_coeffs[:, 1:], right[:, :1]], axis=1),
        jnp.roll(k_coeffs, -1, axis=2),
    ]
    steps = []
    for axis_id in range(3):
        steps.append(((k_coeffs - lower[axis_id]) * lengths[axis_id]).reshape(cells, rank))
        steps.append(((upper[axis_id] - k_coeffs) * lengths[axis_id]).reshape(cells, rank))
    payload, advanced, transport = pl.pallas_call(
        functools.partial(advance_kernel, time_step=time_step),
        out_shape=(
            f32(bricks, cells + height, rank),
            f32(cells, rank),
            f32(6, rank, rank),
        ),
        name="advance", compiler_params=pltpu.CompilerParams(vmem_limit_bytes=VMEM_BYTES),
    )(second, jnp.stack(steps), own_cells, vectors)
    third = exchange(payload, "brick")

    pieces, chosen = pl.pallas_call(
        functools.partial(products_kernel, cells_x=cells_x, cells_y=cells_y, cells_z=cells_z),
        out_shape=(f32(5 * height, rank), f32(height, half)),
        in_specs=vector_specs + [whole],
        scratch_shapes=[pltpu.VMEM((rank, 4 * rank), jnp.float32)],
        name="products",
        compiler_params=pltpu.CompilerParams(vmem_limit_bytes=VMEM_BYTES),
    )(brick_id, third)
    chosen, third_after = lax.optimization_barrier((chosen, third))
    chosen_below = lax.ppermute(chosen, "slab", up)
    first_plane = third[:, : cells // cells_x].reshape(half, rank)

    back = pl.pallas_call(back_kernel, out_shape=f32(slabs, rows, rank), name="back", compiler_params=pltpu.CompilerParams(vmem_limit_bytes=VMEM_BYTES))(
        third_after, line, state, across[1:].T
    )

    pieces = pieces + jnp.pad(
        contract(chosen_below, first_plane, 1, 0), ((height, 3 * height), (0, 0))
    )
    pieces, back = lax.optimization_barrier((pieces, back))
    fourth = exchange(back, "slab")
    both = ("slab", "brick")
    lower_x, upper_x, cross_x = (from_peer(pieces, both, mask) for mask in (8, 16, 24))
    reduced = jnp.stack([pieces + upper_x, lower_x + cross_x])
    reduced = sum_over(reduced, both, ((96, 64, 32),))
    reduced = gather_more(reduced, both, ((1,), (4, 2, 6)))

    speeds = jnp.stack(list(own_velocity) + [jnp.zeros_like(ones)] * 5, axis=1)
    basis_new, velocity_part, inverse = pl.pallas_call(
        functools.partial(
            middle_kernel, lengths=lengths, time_step=time_step, weight_x=weight_x
        ),
        out_shape=(f32(cells, rank), f32(rows, rank), f32(rank, rank)),
        in_specs=vector_specs + [whole] * 5,
        scratch_shapes=factor_scratch(rank)[:2],
        name="middle",
        compiler_params=pltpu.CompilerParams(vmem_limit_bytes=VMEM_BYTES),
    )(brick_id, reduced, transport, v_basis, advanced, speeds)
    velocity_new, gram_part = pl.pallas_call(
        functools.partial(update_kernel, weight_x=weight_x),
        out_shape=(f32(rows, rank), f32(rank // 2 + 8, rank)),
        name="update",
        compiler_params=pltpu.CompilerParams(vmem_limit_bytes=VMEM_BYTES),
    )(fourth, velocity_part, inverse)
    gram_v = sum_over(gram_part, ("slab", "brick"), ALL_GROUPS)
    coupling, vbasis_new = pl.pallas_call(
        last_kernel,
        out_shape=(f32(rank, rank), f32(rows, rank)),
        scratch_shapes=factor_scratch(rank),
        name="last", compiler_params=pltpu.CompilerParams(vmem_limit_bytes=VMEM_BYTES),
    )(gram_v, velocity_new)
    return (basis_new.reshape(cells_x, cells_y, cells_z, rank), coupling, vbasis_new)


def solution(mesh):
    placed = (P("slab", "brick", None, None), P(("slab", "brick"), None))
    return jax.shard_map(
        local,
        mesh=mesh,
        in_specs=placed,
        out_specs=(P("slab", "brick", None, None), P(), P(("slab", "brick"), None)),
        check_vma=False,
    )
```
